32 devices in a mesh: dp: 4 (over y, core), fsdp: 8 (over z, x).
Axes of the slice: x: 2, y: 2, z: 4, core: 2. Of those that a mesh axis runs over, the one named last changes fastest.
Arguments:
- series: float32 [4, 512, 720], P('dp', 'fsdp'), may hold values from -23 to 23
- observed: int32 [4, 512, 720], P('dp', 'fsdp'), may hold values 0 or 1
- targets: float32 [4, 512, 360], P('dp', 'fsdp'), may hold values from -23 to 23
- target_mask: int32 [4, 512, 360], P('dp', 'fsdp'), may hold values 0 or 1
- counts: int32 [4], P('dp'), may hold values from 64 to 512, as said below
- matrices: float32 [1703936], P(('dp', 'fsdp')), may hold values from -0.9375 to 0.9375
- feed_weights: float32 [1048576], P(('dp', 'fsdp')), may hold values from -0.3125 to 0.3125
- vectors: float32 [265216], P(('dp', 'fsdp')), may hold values from -5 to 5
- matrices_first: float32 [1703936], P(('dp', 'fsdp')), may hold values from -9.536743e-06 to 9.536743e-06
- matrices_second: float32 [1703936], P(('dp', 'fsdp')), may hold values from 3.313751e-14 to 1.3255004e-13
- feed_first: float32 [1048576], P(('dp', 'fsdp')), may hold values from -9.536743e-06 to 9.536743e-06
- feed_second: float32 [1048576], P(('dp', 'fsdp')), may hold values from 3.313751e-14 to 1.3255004e-13
- vectors_first: float32 [265216], P(('dp', 'fsdp')), may hold values from -3.8146973e-05 to 3.8146973e-05
- vectors_second: float32 [265216], P(('dp', 'fsdp')), may hold values from 5.302002e-13 to 2.1208007e-12
Outputs:
- grad_norm: float32 [], replicated
- new_matrices: float32 [1703936], P(('dp', 'fsdp'))
- new_matrices_first: float32 [1703936], P(('dp', 'fsdp'))
- new_matrices_second: float32 [1703936], P(('dp', 'fsdp'))
- new_feed: float32 [1048576], P(('dp', 'fsdp'))
- new_feed_first: float32 [1048576], P(('dp', 'fsdp'))
- new_feed_second: float32 [1048576], P(('dp', 'fsdp'))
- new_vectors: float32 [265216], P(('dp', 'fsdp'))
- new_vectors_first: float32 [265216], P(('dp', 'fsdp'))
- new_vectors_second: float32 [265216], P(('dp', 'fsdp'))
The draws below stay inside these ranges and needn't reach their ends.
Inputs may be any that keep to these rules, and one draw needn't show every extreme that they name: A series' variables occupy slots 0 to counts - 1, the other slots are padding; some series fills all 512 slots.
All inputs are finite; a program needn't handle non-finite values. No bound on the sum of `observed` or of `target_mask` on one device may be relied on, other than what follows from the above.
Results may differ from the reference program's by a relative error of at most 0.0003.
The reference program's roundings to bfloat16 on the way count: a program that leaves them out, or rounds other values in their place, can miss the bound.
Values may be sent and summed in bfloat16 or wider, within the bound.
A program may use at most 512 MiB of HBM per device.

```python
import math
import jax
import jax.numpy as jnp
from jax import lax

D = 256
HEADS = 8
FF = 512
ROUT = 10
SEGLEN = 12
PRED = 12
SEG = 60
NSQ = 26
VARS = 512
ITEMS = 4
HORIZ = 360
NVEC = 1036
NPARAM = 3017728


def rough_noise(key, array_shape):
    return jnp.clip(jax.random.normal(key, array_shape, jnp.float32), -5.0, 5.0)


def levels_and_spread(key):
    levels = jax.random.uniform(jax.random.fold_in(key, 21), (ITEMS, VARS, 1), jnp.float32, -3.0, 3.0)
    spread = jnp.exp(jax.random.uniform(jax.random.fold_in(key, 22), (ITEMS, VARS, 1), jnp.float32, math.log(0.5), math.log(4.0)))
    return (levels, spread)


def draw_series(key, part):
    levels, spread = levels_and_spread(key)
    return levels + spread * rough_noise(jax.random.fold_in(key, 23), (ITEMS, VARS, SEG * SEGLEN))


def draw_targets(key, part):
    levels, spread = levels_and_spread(key)
    return levels + spread * rough_noise(jax.random.fold_in(key, 24), (ITEMS, VARS, HORIZ))


def draw_counts(key, part):
    smallest = max(1, VARS // 8)
    random_counts = jax.random.randint(jax.random.fold_in(key, 11), (ITEMS,), smallest, VARS + 1, dtype=jnp.int32)
    chosen = jax.random.randint(jax.random.fold_in(key, 12), (), 0, ITEMS, dtype=jnp.int32)
    return jnp.where(jnp.arange(ITEMS, dtype=jnp.int32) == chosen, VARS, random_counts)


def draw_matrices(key, part):
    entries = NSQ * D * D
    random_part = rough_noise(jax.random.fold_in(key, 31), (entries,))
    which_matrix = jnp.arange(entries, dtype=jnp.int32) // (D * D)
    factor = jnp.where(which_matrix % 4 == 3, 3.0, 1.0) * jnp.where(which_matrix >= 24, 0.70710678, 1.0)
    return random_part * factor / math.sqrt(D)


def draw_feed_weights(key, part):
    entries = 8 * D * FF
    random_part = rough_noise(jax.random.fold_in(key, 32), (entries,))
    which_matrix = jnp.arange(entries, dtype=jnp.int32) // (D * FF)
    return random_part * jnp.where(which_matrix < 4, 1.0 / math.sqrt(D), 1.0 / math.sqrt(FF))


def draw_vectors(key, part):
    entries = NVEC * D
    random_part = rough_noise(jax.random.fold_in(key, 41), (entries,))
    gain_noise = jax.random.uniform(jax.random.fold_in(key, 42), (entries,), jnp.float32, -0.3, 0.3)
    row_index = jnp.arange(entries, dtype=jnp.int32) // D
    layer_start = SEGLEN + 1 + SEG
    inside = (row_index - layer_start) % 23
    in_layers = (row_index >= layer_start) & (row_index < layer_start + 46)
    gain_rows = in_layers & ((inside == 3) | (inside == 8) | (inside == 16) | (inside == 21))
    gain_rows = gain_rows | (row_index >= layer_start + 46) & (row_index < layer_start + 48)
    head_start = layer_start + 51
    router_start = head_start + PRED
    factor = jnp.where(row_index < SEGLEN, 1.0 / math.sqrt(SEGLEN), 0.3)
    factor = jnp.where((row_index > SEGLEN) & (row_index < layer_start), 0.5, factor)
    factor = jnp.where((row_index >= head_start) & (row_index < router_start), 1.0 / math.sqrt(D), factor)
    factor = jnp.where(row_index >= router_start, 1.0, factor)
    return jnp.where(gain_rows, 1.0 + gain_noise, random_part * factor)


def with_ends(array, stream_key, low, high):
    index_at = [jax.random.randint(jax.random.fold_in(stream_key, axis), (), 0, length) for axis, length in enumerate(array.shape)]
    main_axis = array.shape.index(max(array.shape))
    beside = index_at[:main_axis] + [(index_at[main_axis] + 1) % array.shape[main_axis]] + index_at[main_axis + 1:]
    return array.at[tuple(index_at)].set(low).at[tuple(beside)].set(high)


def steps_of(own_key, shape, split, low, largest):
    def one(axis_at, blocks):
        heights = jax.random.uniform(jax.random.fold_in(jax.random.fold_in(own_key, 6), axis_at), (blocks,), jnp.float32, low / len(split), largest / len(split))
        return jnp.repeat(jnp.exp(heights), shape[axis_at] // blocks).reshape((-1,) + (1,) * (len(shape) - axis_at - 1))

    gain = one(*split[0])
    for cut in split[1:]:
        gain = gain * one(*cut)
    return gain


def gaussian(stream_key, shape, deviation, bound, cuts=(), kind=jnp.bfloat16):
    values = jax.random.normal(stream_key, shape, jnp.float32) * deviation
    if len(cuts) > 0:
        values = steps_of(stream_key, shape, cuts, -0.22, 0.18) * values
    return jnp.clip(values, min=-bound, max=bound).astype(kind)


def setup_inputs(seed: int = 0) -> dict:
    splits = jax.random.split(jax.random.key(seed), 15)
    series = draw_series(jax.random.fold_in(splits[14], 71), 0)
    observed = with_ends((jax.random.randint(splits[1], (ITEMS, VARS, SEG * SEGLEN), 0, 10) < 9).astype(jnp.int32), jax.random.fold_in(splits[1], 1), 0, 1)
    targets = draw_targets(jax.random.fold_in(splits[14], 71), 0)
    target_mask = with_ends((jax.random.randint(splits[3], (ITEMS, VARS, HORIZ), 0, 10) < 9).astype(jnp.int32), jax.random.fold_in(splits[3], 1), 0, 1)
    counts = draw_counts(jax.random.fold_in(splits[14], 71), 0)
    matrices = draw_matrices(jax.random.fold_in(splits[14], 71), 0)
    feed_weights = draw_feed_weights(jax.random.fold_in(splits[14], 71), 0)
    vectors = draw_vectors(jax.random.fold_in(splits[14], 71), 0)
    matrices_first = gaussian(splits[8], (NSQ * D * D,), (0.11 * 0.01 / NPARAM ** 0.5), 9.5367431640625e-06, ((0, 32),), jnp.float32)
    matrices_second = jnp.clip(jnp.exp(math.log(1.325500446165348e-13) - 1.3862944 * jax.random.uniform(splits[9], (NSQ * D * D,), jnp.float32) ** steps_of(splits[9], (NSQ * D * D,), ((0, 32),), -0.2, 0.2)), 3.31375111541337e-14, 1.325500446165348e-13)
    feed_first = gaussian(splits[10], (8 * D * FF,), (0.11 * 0.01 / NPARAM ** 0.5), 9.5367431640625e-06, ((0, 32),), jnp.float32)
    feed_second = jnp.clip(jnp.exp(math.log(1.325500446165348e-13) - 1.3862944 * jax.random.uniform(splits[11], (8 * D * FF,), jnp.float32) ** steps_of(splits[11], (8 * D * FF,), ((0, 32),), -0.2, 0.2)), 3.31375111541337e-14, 1.325500446165348e-13)
    vectors_first = gaussian(splits[12], (NVEC * D,), (0.44 * 0.01 / NPARAM ** 0.5), 3.814697265625e-05, ((0, 32),), jnp.float32)
    vectors_second = jnp.clip(jnp.exp(math.log(2.120800713864557e-12) - 1.3862944 * jax.random.uniform(splits[13], (NVEC * D,), jnp.float32) ** steps_of(splits[13], (NVEC * D,), ((0, 32),), -0.2, 0.2)), 5.302001784661392e-13, 2.120800713864557e-12)
    return dict(series=series, observed=observed, targets=targets, target_mask=target_mask, counts=counts, matrices=matrices, feed_weights=feed_weights, vectors=vectors, matrices_first=matrices_first, matrices_second=matrices_second, feed_first=feed_first, feed_second=feed_second, vectors_first=vectors_first, vectors_second=vectors_second)


@jax.custom_vjp
def low(v):
    return lax.optimization_barrier(v.astype(jnp.bfloat16)).astype(jnp.float32)

@jax.custom_vjp
def low_back(v):
    return v

def low_keep(v):
    return (low(v), None)

def low_pass(kept, grad):
    return (grad,)

def back_keep(v):
    return (v, None)

def back_low(kept, grad):
    return (low(grad),)
low.defvjp(low_keep, low_pass)
low_back.defvjp(back_keep, back_low)
highest_score = lax.Precision.HIGHEST
negative = -1e+30
norm_eps = 1e-05
beta_one = 0.9
beta_two = 0.999
adam_eps = 1e-08
weight_decay = 0.01
learn_rate = 0.2
clip_norm = 0.01
step_count = 10.0

def dense(inputs, matrix):
    return jnp.einsum('...d,de->...e', inputs, matrix, precision=highest_score)

def layer_norm(inputs, norm_gain, norm_bias):
    center = inputs - lax.optimization_barrier(jnp.mean(inputs, -1, keepdims=True))
    spread = lax.optimization_barrier(jnp.mean(center * center, -1, keepdims=True))
    return center * lax.rsqrt(spread + norm_eps) * norm_gain + norm_bias

def feed_forward(inputs, w_up, b_up, w_down, b_down):
    return dense(jax.nn.gelu(dense(inputs, w_up) + b_up, approximate=False), w_down) + b_down

def split_heads(inputs):
    return inputs.reshape(inputs.shape[:-1] + (HEADS, inputs.shape[-1] // HEADS))

def unpack(matrices, feed_weights, vectors):
    square = matrices.reshape(NSQ, D, D)
    feed_pack = feed_weights.reshape(8, D * FF)
    return (square, feed_pack[:4].reshape(4, D, FF), feed_pack[4:].reshape(4, FF, D), vectors.reshape(NVEC, D))

def layer_rows(params, layer_index):
    first_row = SEGLEN + 1 + SEG + 23 * layer_index
    return (params[0][12 * layer_index:12 * layer_index + 12], params[3][first_row:first_row + 23])

def router_rows(params, layer_index):
    first_row = SEGLEN + SEG + 52 + PRED + layer_index * SEG * ROUT
    segments = SEG // (1 + layer_index)
    return params[3][first_row:first_row + segments * ROUT].reshape(segments, ROUT, D)

def normalize(series, observed):
    seen_mask = observed.astype(jnp.float32)
    counted = jnp.maximum(lax.optimization_barrier(jnp.sum(seen_mask, -1, keepdims=True)), 1.0)
    series_mean = lax.optimization_barrier(jnp.sum(seen_mask * series, -1, keepdims=True)) / counted
    center = (series - series_mean) * seen_mask
    series_scale = jnp.sqrt(lax.optimization_barrier(jnp.sum(center * center, -1, keepdims=True)) / counted + norm_eps)
    return (center / series_scale, series_mean, series_scale)

def embed(normed, params):
    vector_rows = params[3]
    pieces = normed.reshape(normed.shape[0], SEG, SEGLEN)
    tokens = jnp.einsum('vsl,ld->vsd', pieces, vector_rows[:SEGLEN], precision=highest_score)
    return tokens + vector_rows[SEGLEN] + vector_rows[SEGLEN + 1:SEGLEN + 1 + SEG]

def time_part(tokens, params, layer_index):
    layer_mats, layer_vecs = layer_rows(params, layer_index)
    score_factor = (D // HEADS) ** (-0.5)
    query_rows = split_heads(dense(tokens, layer_mats[0]) + layer_vecs[0])
    key_matrix = split_heads(dense(tokens, layer_mats[1]))
    value_rows = split_heads(dense(tokens, layer_mats[2]) + layer_vecs[1])
    attention_scores = jnp.einsum('vqhe,vkhe->vhqk', query_rows, key_matrix, precision=highest_score) * score_factor
    attention_weights = jax.nn.softmax(attention_scores, -1)
    mixed_output_rows = jnp.einsum('vhqk,vkhe->vqhe', attention_weights, value_rows, precision=highest_score).reshape(tokens.shape)
    hidden = layer_norm(tokens + dense(mixed_output_rows, layer_mats[3]) + layer_vecs[2], layer_vecs[3], layer_vecs[4])
    branch = feed_forward(hidden, params[1][2 * layer_index], layer_vecs[5:7].reshape(-1), params[2][2 * layer_index], layer_vecs[7])
    return layer_norm(hidden + branch, layer_vecs[8], layer_vecs[9])

def router_query(params, layer_index):
    layer_mats, layer_vecs = layer_rows(params, layer_index)
    return dense(router_rows(params, layer_index), layer_mats[4]) + layer_vecs[10]

def receive_part(dimension_sender, buffer, params, layer_index):
    layer_mats, layer_vecs = layer_rows(params, layer_index)
    score_factor = (D // HEADS) ** (-0.5)
    query_rows = split_heads(dense(dimension_sender, layer_mats[8]) + layer_vecs[13])
    key_matrix = split_heads(dense(buffer, layer_mats[9]))
    value_rows = split_heads(dense(buffer, layer_mats[10]) + layer_vecs[14])
    attention_scores = jnp.einsum('tmiq,muiq->tmiu', query_rows, key_matrix, precision=highest_score) * score_factor
    attention_weights = jax.nn.softmax(attention_scores, -1)
    mixed_output_rows = jnp.einsum('cfkj,fjky->cfky', attention_weights, value_rows, precision=highest_score).reshape(dimension_sender.shape)
    hidden = layer_norm(dimension_sender + dense(mixed_output_rows, layer_mats[11]) + layer_vecs[15], layer_vecs[16], layer_vecs[17])
    branch = feed_forward(hidden, params[1][2 * layer_index + 1], layer_vecs[18:20].reshape(-1), params[2][2 * layer_index + 1], layer_vecs[20])
    return layer_norm(hidden + branch, layer_vecs[21], layer_vecs[22])

def two_section(tokens, params, layer_index, present):
    dimension_sender = time_part(tokens, params, layer_index)
    layer_mats, layer_vecs = layer_rows(params, layer_index)
    score_factor = (D // HEADS) ** (-0.5)
    router_queries = split_heads(router_query(params, layer_index))
    key_matrix = split_heads(dense(dimension_sender, layer_mats[5]))
    value_rows = split_heads(dense(dimension_sender, layer_mats[6]) + layer_vecs[11])
    attention_scores = jnp.einsum('srhe,vshe->srhv', router_queries, key_matrix, precision=highest_score) * score_factor
    attention_weights = jax.nn.softmax(jnp.where(present, attention_scores, negative), -1)
    mixed_output_rows = jnp.einsum('srhv,vshe->srhe', attention_weights, value_rows, precision=highest_score)
    buffer = dense(mixed_output_rows.reshape(mixed_output_rows.shape[:2] + (D,)), layer_mats[7]) + layer_vecs[12]
    return receive_part(dimension_sender, buffer, params, layer_index)

def merge_segments(tokens, params):
    vector_rows = params[3]
    first_row = SEGLEN + SEG + 47
    paired = tokens.reshape(tokens.shape[0], tokens.shape[1] // 2, 2 * D)
    normed = layer_norm(paired, vector_rows[first_row:first_row + 2].reshape(-1), vector_rows[first_row + 2:first_row + 4].reshape(-1))
    return dense(normed, jnp.concatenate([params[0][24], params[0][25]], 0)) + vector_rows[first_row + 4]

def head_loss(tokens, params, series_mean, series_scale, targets, kept_mask):
    first_row = SEGLEN + SEG + 52
    predicted = jnp.einsum('vsd,pd->vsp', tokens, params[3][first_row:first_row + PRED], precision=highest_score)
    misfit = predicted.reshape(targets.shape) * series_scale + series_mean - targets
    return jnp.sum(kept_mask * misfit * misfit)

def item_loss(params, series, observed, targets, target_mask, var_count):
    present = jnp.arange(series.shape[0], dtype=jnp.int32) < var_count
    normed, series_mean, series_scale = normalize(series, observed)
    tokens = embed(normed, params)
    tokens = two_section(tokens, params, 0, present)
    tokens = merge_segments(tokens, params)
    tokens = two_section(tokens, params, 1, present)
    kept_mask = target_mask.astype(jnp.float32) * present[:, None].astype(jnp.float32)
    return head_loss(tokens, params, series_mean, series_scale, targets, kept_mask)

def adam_update(weight, first_moment, second_moment, gradient):
    first_new = beta_one * first_moment + (1.0 - beta_one) * gradient
    second_new = beta_two * second_moment + (1.0 - beta_two) * gradient * gradient
    corrected = first_new / (1.0 - beta_one ** step_count) / (jnp.sqrt(second_new / (1.0 - beta_two ** step_count)) + adam_eps)
    return (weight - learn_rate * (corrected + weight_decay * weight), first_new, second_new)

def reference(series, observed, targets, target_mask, counts, matrices, feed_weights, vectors, matrices_first, matrices_second, feed_first, feed_second, vectors_first, vectors_second):
    slot_index = jnp.arange(series.shape[1], dtype=jnp.int32)
    present_all = (slot_index[None, :] < counts[:, None]).astype(jnp.float32)
    target_total = jnp.maximum(jnp.sum(target_mask.astype(jnp.float32) * present_all[:, :, None]), 1.0)

    def loss_of(mat_master, feed_master, vec_master):
        params = unpack(low(mat_master), low(feed_master), low(vec_master))

        def per_item(item_data):
            return jax.checkpoint(item_loss)(params, item_data[0], item_data[1], item_data[2], item_data[3], item_data[4])
        return jnp.sum(lax.map(per_item, (series, observed, targets, target_mask, counts))) / target_total
    loss_value, pull_loss = jax.vjp(loss_of, matrices, feed_weights, vectors)
    weight_grads = pull_loss(jnp.ones_like(loss_value))
    square_sum = jnp.sum(weight_grads[0] * weight_grads[0]) + jnp.sum(weight_grads[1] * weight_grads[1]) + jnp.sum(weight_grads[2] * weight_grads[2])
    grad_norm = jnp.sqrt(square_sum)
    factor = clip_norm / jnp.maximum(grad_norm, clip_norm)
    mat_new = adam_update(matrices, matrices_first, matrices_second, weight_grads[0] * factor)
    feed_new = adam_update(feed_weights, feed_first, feed_second, weight_grads[1] * factor)
    vec_new = adam_update(vectors, vectors_first, vectors_second, weight_grads[2] * factor)
    return (grad_norm, mat_new[0], mat_new[1], mat_new[2], feed_new[0], feed_new[1], feed_new[2], vec_new[0], vec_new[1], vec_new[2])
```

```python
import functools
import jax
import jax.numpy as jnp
from jax import lax
from jax.experimental import pallas as pl
from jax.experimental.pallas import tpu as pltpu
from jax.sharding import PartitionSpec as P

D = 256
HEADS = 8
FF = 512
ROUT = 10
RPAD = 16
SEGLEN = 12
PRED = 12
PPAD = 16
SEG = 60
NSQ = 26
NVEC = 1036
HALF = 128
VB = 8

BF = jnp.bfloat16
F32 = jnp.float32
SCALE = (D // HEADS) ** (-0.5)
negative = -1e30
norm_eps = 1e-05
beta_one = 0.9
beta_two = 0.999
adam_eps = 1e-08
weight_decay = 0.01
learn_rate = 0.2
clip_norm = 0.01
step_count = 10.0
VMEM_LIMIT = 60 << 20


def split2(x):
    hi = x.astype(BF)
    return hi, (x - hi.astype(F32)).astype(BF)


def dots(a, b, ca, cb):
    return lax.dot_general(a, b, (((ca,), (cb,)), ((), ())), preferred_element_type=F32)


def mmw(x2, w):
    return dots(x2[0], w, 1, 0) + dots(x2[1], w, 1, 0)


def mmwt(x2, w):
    return dots(x2[0], w, 1, 1) + dots(x2[1], w, 1, 1)


def rows2(a2):
    return jnp.concatenate([a2[0], a2[1]], 0)


def nn3(a2, b2):
    m = a2[0].shape[0]
    both = dots(rows2(a2), b2[0], 1, 0)
    return both[:m] + both[m:] + dots(a2[0], b2[1], 1, 0)


def nt3(a2, b2):
    m = a2[0].shape[0]
    both = dots(rows2(a2), b2[0], 1, 1)
    return both[:m] + both[m:] + dots(a2[0], b2[1], 1, 1)


def tn3(a2, b2):
    n = b2[0].shape[1]
    both = dots(a2[0], jnp.concatenate([b2[0], b2[1]], 1), 0, 0)
    return both[:, :n] + both[:, n:] + dots(a2[1], b2[0], 0, 0)


def norm_fwd(z, gain, bias):
    center = z - jnp.mean(z, -1, keepdims=True)
    inv = lax.rsqrt(jnp.mean(center * center, -1, keepdims=True) + norm_eps)
    unit = center * inv
    return unit * gain + bias, unit, inv


def norm_bwd(dy, unit, inv, gain):
    t = dy * gain
    return inv * (t - jnp.mean(t, -1, keepdims=True) - unit * jnp.mean(t * unit, -1, keepdims=True))


def colsum(x):
    return jnp.sum(x.reshape(x.shape[0] // 8, 8, x.shape[1]), 0)


def gelu_cdf(u):
    return 0.5 + 0.5 * lax.erf(u * 0.7071067811865476)


def gelu_slope(u, cdf):
    return cdf + u * (jnp.exp(-0.5 * u * u) * 0.3989422804014327)


def halves(x):
    return x[:, :HALF], x[:, HALF:]


def lane_head(rows):
    return lax.broadcasted_iota(jnp.int32, (rows, HALF), 1) // 32


def spread_heads(x, zero):
    head = lane_head(x.shape[0])
    return jnp.concatenate([jnp.where(head == h, x, zero) for h in range(4)], 0)


def gather_heads(x, group):
    head = lane_head(group)
    out = x[3 * group :]
    for h in range(3):
        out = jnp.where(head == h, x[h * group : (h + 1) * group], out)
    return out


def ones_heads(group, count):
    row = lax.broadcasted_iota(jnp.int32, (4 * group, HALF), 0)
    lane = lax.broadcasted_iota(jnp.int32, (4 * group, HALF), 1)
    return jnp.where((row // group == lane // 32) & (row % group < count), 1.0, 0.0).astype(BF)


def group_max(s, group, count):
    lane = lax.broadcasted_iota(jnp.int32, (s.shape[0], HALF), 1)
    outs = []
    for t in range(s.shape[1] // HALF):
        part = s[:, t * HALF : (t + 1) * HALF]
        top = None
        for g in range(HALF // group):
            here = (lane // group == g)
            best = jnp.max(jnp.where((lane // group == g) & (lane % group < count), part, negative), -1, keepdims=True)
            top = jnp.broadcast_to(best, part.shape) if top is None else jnp.where(here, best, top)
        outs.append(jnp.where(lane % group < count, part - top, negative))
    return jnp.concatenate(outs, 1)


def time_attend(c, v, group, count, q_s, k_s, v_s, o_s, p_s, l_s):
    at = pl.ds(v, group, stride=VB)
    q2 = split2(q_s[c, at, :])
    k2 = split2(k_s[c, at, :])
    w2 = split2(v_s[c, at, :])
    zero = jnp.zeros((), BF)
    k_hi, k_lo = spread_heads(k2[0], zero), spread_heads(k2[1], zero)
    w_hi, w_lo = spread_heads(w2[0], zero), spread_heads(w2[1], zero)
    s = dots(jnp.concatenate(q2, 1), jnp.concatenate([k_hi, k_hi], 1), 1, 1) + dots(q2[0], k_lo, 1, 1)
    p = jnp.exp(group_max(s, group, count))
    p2 = split2(p)
    both = dots(rows2(p2), jnp.concatenate([w_hi, ones_heads(group, count)], 1), 1, 0)
    both = both[:group] + both[group:]
    total = both[:, HALF:]
    o_s[c, at, :] = (both[:, :HALF] + dots(p2[0], w_lo, 1, 0)) / total
    if p_s is not None:
        p_s[c, v] = p
        l_s[c, v] = total


def time_attend_back(c, v, group, count, q_s, k_s, v_s, o_s, p_s, l_s, do_s):
    at = pl.ds(v, group, stride=VB)
    q2 = split2(q_s[c, at, :])
    k2 = split2(k_s[c, at, :])
    w2 = split2(v_s[c, at, :])
    zero = jnp.zeros((), BF)
    k_hi, k_lo = spread_heads(k2[0], zero), spread_heads(k2[1], zero)
    w_hi, w_lo = spread_heads(w2[0], zero), spread_heads(w2[1], zero)
    d = do_s[c, at, :] / l_s[c, v]
    d2 = split2(d)
    e2 = split2(d * o_s[c, at, :])
    p = p_s[c, v]
    x2 = (jnp.concatenate([d2[0], e2[0]], 1), jnp.concatenate([d2[1], e2[1]], 1))
    both = dots(rows2(x2), jnp.concatenate([w_hi, -ones_heads(group, count)], 1), 1, 1)
    dp = both[:group] + both[group:] + dots(d2[0], w_lo, 1, 1)
    p2 = split2(p)
    s2 = split2(p * dp)
    both = dots(rows2(s2), k_hi, 1, 0)
    q_s[c, at, :] = both[:group] + both[group:] + dots(s2[0], k_lo, 1, 0)
    k_s[c, at, :] = gather_heads(tn3(s2, q2), group)
    v_s[c, at, :] = gather_heads(tn3(p2, d2), group)


def store_halves(ref, x):
    rows = x.shape[0]
    ref[0, :rows, :] = x[:, :HALF]
    ref[1, :rows, :] = x[:, HALF:]


def load_halves(ref, rows):
    return jnp.concatenate([ref[0, :rows, :], ref[1, :rows, :]], 1)


def zero_tail(ref, rows):
    tail = ref.shape[1] - rows
    ref[:, rows:, :] = jnp.zeros((2, tail, HALF), F32)


def time_forward(x, w, vec, count, group, q_s, k_s, v_s, o_s, p_s=None, l_s=None):
    rows = count * VB
    x2 = split2(x)
    store_halves(q_s, (mmw(x2, w["q"]) + vec[0:1]) * SCALE)
    store_halves(k_s, mmw(x2, w["k"]))
    store_halves(v_s, mmw(x2, w["v"]) + vec[1:2])
    for ref in (q_s, k_s, v_s):
        zero_tail(ref, rows)

    def one(v, carry):
        for c in range(2):
            time_attend(c, v, group, count, q_s, k_s, v_s, o_s, p_s, l_s)
        return carry

    lax.fori_loop(0, VB, one, 0)
    mixed = load_halves(o_s, rows)
    h, unit1, inv1 = norm_fwd(x + mmw(split2(mixed), w["o"]) + vec[2:3], vec[3:4], vec[4:5])
    bias_up = jnp.concatenate([vec[5:6], vec[6:7]], 1)
    u = mmw(split2(h), w["up"]) + bias_up
    cdf = gelu_cdf(u)
    z2 = h + mmw(split2(u * cdf), w["down"]) + vec[7:8]
    y, unit2, inv2 = norm_fwd(z2, vec[8:9], vec[9:10])
    return y, (x2, mixed, h, unit1, inv1, u, cdf, unit2, inv2)


def embed_block(pieces, emb, place):
    return mmw(split2(pieces), emb) + place


TIME_W = ("q", "k", "v", "o", "up", "down")


def time_fwd_kernel(first, count, group, *refs):
    if first:
        x_ref, emb_ref, place_ref = refs[:3]
        refs = refs[3:]
    else:
        x_ref = refs[0]
        refs = refs[1:]
    w = {name: refs[i][...] for i, name in enumerate(TIME_W)}
    vec_ref, y_ref, q_s, k_s, v_s, o_s = refs[6:]
    rows = count * VB
    if first:
        place = jnp.broadcast_to(place_ref[...], (count, VB, D)).reshape(rows, D)
        x = embed_block(x_ref[...].reshape(rows, 16), emb_ref[...], place)
    else:
        x = x_ref[...].reshape(rows, D)
    y, _ = time_forward(x, w, vec_ref[...], count, group, q_s, k_s, v_s, o_s)
    y_ref[...] = y.reshape(count, VB, D)


def whole(shape):
    return pl.BlockSpec(shape, lambda i: (0,) * len(shape))


def params_spec():
    return pltpu.CompilerParams(vmem_limit_bytes=VMEM_LIMIT)


def time_weight_specs():
    return [whole((D, D))] * 4 + [whole((D, FF)), whole((FF, D)), whole((24, D))]


def time_fwd(first, x, extra, weights, count):
    group = 64 if count > 32 else 32
    nv = x.shape[1]
    width = x.shape[2]
    specs = [pl.BlockSpec((count, VB, width), lambda i: (0, i, 0))]
    if first:
        specs += [whole((16, D)), whole((count, 1, D))]
    pad = group * VB
    return pl.pallas_call(
        functools.partial(time_fwd_kernel, first, count, group),
        grid=(nv // VB,),
        in_specs=specs + time_weight_specs(),
        out_specs=pl.BlockSpec((count, VB, D), lambda i: (0, i, 0)),
        out_shape=jax.ShapeDtypeStruct((count, nv, D), F32),
        scratch_shapes=[pltpu.VMEM((2, pad, HALF), F32)] * 4,
        compiler_params=params_spec(),
        name="time_fwd",
    )(x, *extra, *weights)


def time_bwd_kernel(first, count, group, *refs):
    if first:
        x_ref, emb_ref, place_ref = refs[:3]
        refs = refs[3:]
    else:
        x_ref = refs[0]
        refs = refs[1:]
    dy_ref = refs[0]
    w = {name: refs[1 + i][...] for i, name in enumerate(TIME_W)}
    vec_ref = refs[7]
    outs = refs[8:]
    n_out = 9 if first else 8
    g = dict(zip(TIME_W + ("rows",), outs[:7]))
    tail = outs[7:n_out]
    q_s, k_s, v_s, o_s, do_s, p_s, l_s = outs[n_out:]
    rows = count * VB
    step = pl.program_id(0)

    @pl.when(step == 0)
    def _():
        for ref in list(g.values()) + (list(tail) if first else []):
            ref[...] = jnp.zeros(ref.shape, F32)

    vec = vec_ref[...]
    if first:
        place = jnp.broadcast_to(place_ref[...], (count, VB, D)).reshape(rows, D)
        pieces = x_ref[...].reshape(rows, 16)
        x = embed_block(pieces, emb_ref[...], place)
    else:
        x = x_ref[...].reshape(rows, D)
    _, (x2, mixed, h, unit1, inv1, u, cdf, unit2, inv2) = time_forward(
        x, w, vec, count, group, q_s, k_s, v_s, o_s, p_s, l_s
    )
    dy = dy_ref[...].reshape(rows, D)
    g["rows"][8] += colsum(dy * unit2)
    g["rows"][9] += colsum(dy)
    dz2 = norm_bwd(dy, unit2, inv2, vec[8:9])
    g["rows"][7] += colsum(dz2)
    dz22 = split2(dz2)
    g["down"][...] += tn3(split2(u * cdf), dz22)
    du = mmwt(dz22, w["down"]) * gelu_slope(u, cdf)
    g["rows"][5] += colsum(du[:, :D])
    g["rows"][6] += colsum(du[:, D:])
    du2 = split2(du)
    g["up"][...] += tn3(split2(h), du2)
    dh = dz2 + mmwt(du2, w["up"])
    g["rows"][3] += colsum(dh * unit1)
    g["rows"][4] += colsum(dh)
    dz1 = norm_bwd(dh, unit1, inv1, vec[3:4])
    g["rows"][2] += colsum(dz1)
    dz12 = split2(dz1)
    g["o"][...] += tn3(split2(mixed), dz12)
    store_halves(do_s, mmwt(dz12, w["o"]))
    zero_tail(do_s, rows)

    def one(v, carry):
        for c in range(2):
            time_attend_back(c, v, group, count, q_s, k_s, v_s, o_s, p_s, l_s, do_s)
        return carry

    lax.fori_loop(0, VB, one, 0)
    dq = load_halves(q_s, rows) * SCALE
    g["rows"][0] += colsum(dq)
    dq2 = split2(dq)
    g["q"][...] += tn3(x2, dq2)
    dx = dz1 + mmwt(dq2, w["q"])
    dk2 = split2(load_halves(k_s, rows))
    g["k"][...] += tn3(x2, dk2)
    dx = dx + mmwt(dk2, w["k"])
    dv = load_halves(v_s, rows)
    g["rows"][1] += colsum(dv)
    dv2 = split2(dv)
    g["v"][...] += tn3(x2, dv2)
    dx = dx + mmwt(dv2, w["v"])
    if first:
        tail[0][...] += tn3(split2(pieces), split2(dx))
        tail[1][...] += dx
    else:
        tail[0][...] = dx.reshape(count, VB, D)


def time_bwd(first, x, extra, dy, weights, count):
    group = 64 if count > 32 else 32
    nv = x.shape[1]
    width = x.shape[2]
    pad = group * VB
    block = pl.BlockSpec((count, VB, D), lambda i: (0, i, 0))
    specs = [pl.BlockSpec((count, VB, width), lambda i: (0, i, 0))]
    if first:
        specs += [whole((16, D)), whole((count, 1, D))]
    grad_shapes = [(D, D)] * 4 + [(D, FF), (FF, D), (10, 8, D)]
    if first:
        grad_shapes += [(16, D), (count * VB, D)]
    out_specs = [whole(s) for s in grad_shapes]
    out_shape = [jax.ShapeDtypeStruct(s, F32) for s in grad_shapes]
    if not first:
        out_specs.append(block)
        out_shape.append(jax.ShapeDtypeStruct((count, nv, D), F32))
    return pl.pallas_call(
        functools.partial(time_bwd_kernel, first, count, group),
        grid=(nv // VB,),
        in_specs=specs + [block] + time_weight_specs(),
        out_specs=out_specs,
        out_shape=out_shape,
        scratch_shapes=[pltpu.VMEM((2, pad, HALF), F32)] * 5
        + [pltpu.VMEM((2, VB, group, 4 * group), F32), pltpu.VMEM((2, VB, group, HALF), F32)],
        compiler_params=params_spec(),
        name="time_bwd",
    )(x, *extra, dy, *weights)

SB_ROWS = 64


def head_rows():
    sub = lax.broadcasted_iota(jnp.int32, (8, D), 0)
    lane = lax.broadcasted_iota(jnp.int32, (8, D), 1)
    return jnp.where(sub == lane // 32, 1.0, 0.0).astype(F32)


def spread_rows(x):
    wide = jnp.broadcast_to(x[:, None, :], (RPAD, HEADS, D)) * head_rows()[None]
    return wide.reshape(RPAD * HEADS, D)


def gather_rows(x):
    return jnp.sum(x.reshape(RPAD, HEADS, D) * head_rows()[None], 1)


def valid_lane(rows):
    return lax.broadcasted_iota(jnp.int32, (rows, HALF), 1) < ROUT * HEADS


def router_reduce(x, op):
    for shift in (8, 16, 32, 64):
        x = op(x, pltpu.roll(x, shift, 1))
    return x


def merge_rows(y, pairs, vec):
    wide = y.reshape(pairs, 2, SB_ROWS, D)
    wide = jnp.concatenate([wide[:, 0].reshape(pairs * SB_ROWS, D), wide[:, 1].reshape(pairs * SB_ROWS, D)], 1)
    gain = jnp.concatenate([vec[0:1], vec[1:2]], 1)
    bias = jnp.concatenate([vec[2:3], vec[3:4]], 1)
    return norm_fwd(wide, gain, bias) + (gain,)


RECV_W = ("so", "rk", "rv", "rq", "ro", "up", "down")


def recv_forward(send, o_rows, w, vec, q_s, mix_s, p_s, kb_s, vb_s):
    sb = send.shape[0] // SB_ROWS
    send2 = split2(send)
    o2 = split2(o_rows)
    buf = mmw(o2, w["so"]) + vec[12:13]
    buf2 = split2(buf)
    kb_s[...] = mmw(buf2, w["rk"])
    vb_s[...] = mmw(buf2, w["rv"]) + vec[14:15]
    q_s[...] = (mmw(send2, w["rq"]) + vec[13:14]) * SCALE

    def one(s, carry):
        at = pl.ds(pl.multiple_of(s * SB_ROWS, SB_ROWS), SB_ROWS)
        ar = pl.ds(pl.multiple_of(s * RPAD, RPAD), RPAD)
        k2 = split2(spread_rows(kb_s[ar, :]))
        v2 = split2(spread_rows(vb_s[ar, :]))
        sc = jnp.where(valid_lane(SB_ROWS), nt3(split2(q_s[at, :]), k2), negative)
        p = jnp.exp(sc - router_reduce(sc, jnp.maximum))
        p = p / router_reduce(p, jnp.add)
        p_s[at, :] = p
        mix_s[at, :] = nn3(split2(p), v2)
        return carry

    lax.fori_loop(0, sb, one, 0)
    mixed = mix_s[...]
    g, unit3, inv3 = norm_fwd(send + mmw(split2(mixed), w["ro"]) + vec[15:16], vec[16:17], vec[17:18])
    u = mmw(split2(g), w["up"]) + jnp.concatenate([vec[18:19], vec[19:20]], 1)
    cdf = gelu_cdf(u)
    y, unit4, inv4 = norm_fwd(g + mmw(split2(u * cdf), w["down"]) + vec[20:21], vec[21:22], vec[22:23])
    return y, (send2, o2, buf2, mixed, g, unit3, inv3, u, cdf, unit4, inv4)


RECV_G = RECV_W + ("rows",)


def recv_backward(dy, kept, w, vec, g, q_s, do_s, p_s, kb_s, vb_s):
    send2, o2, buf2, mixed, gg, unit3, inv3, u, cdf, unit4, inv4 = kept
    sb = dy.shape[0] // SB_ROWS
    rows = g["rows"]
    rows[9] += colsum(dy * unit4)
    rows[10] += colsum(dy)
    dz4 = norm_bwd(dy, unit4, inv4, vec[21:22])
    rows[8] += colsum(dz4)
    dz42 = split2(dz4)
    g["down"][...] += tn3(split2(u * cdf), dz42)
    du = mmwt(dz42, w["down"]) * gelu_slope(u, cdf)
    rows[6] += colsum(du[:, :D])
    rows[7] += colsum(du[:, D:])
    du2 = split2(du)
    g["up"][...] += tn3(split2(gg), du2)
    dg = dz4 + mmwt(du2, w["up"])
    rows[4] += colsum(dg * unit3)
    rows[5] += colsum(dg)
    dz3 = norm_bwd(dg, unit3, inv3, vec[16:17])
    rows[3] += colsum(dz3)
    dz32 = split2(dz3)
    g["ro"][...] += tn3(split2(mixed), dz32)
    do_s[...] = mmwt(dz32, w["ro"])

    def one(s, carry):
        at = pl.ds(pl.multiple_of(s * SB_ROWS, SB_ROWS), SB_ROWS)
        ar = pl.ds(pl.multiple_of(s * RPAD, RPAD), RPAD)
        k2 = split2(spread_rows(kb_s[ar, :]))
        v2 = split2(spread_rows(vb_s[ar, :]))
        q2 = split2(q_s[at, :])
        d2 = split2(do_s[at, :])
        p = p_s[at, :]
        dp = nt3(d2, v2)
        ds = p * (dp - router_reduce(p * dp, jnp.add))
        s2 = split2(ds)
        kb_s[ar, :] = gather_rows(tn3(s2, q2))
        vb_s[ar, :] = gather_rows(tn3(split2(p), d2))
        q_s[at, :] = nn3(s2, k2)
        return carry

    lax.fori_loop(0, sb, one, 0)
    dq = q_s[...] * SCALE
    rows[1] += colsum(dq)
    dq2 = split2(dq)
    g["rq"][...] += tn3(send2, dq2)
    dsend = dz3 + mmwt(dq2, w["rq"])
    dk2 = split2(kb_s[...])
    dv = vb_s[...]
    dv2 = split2(dv)
    rows[2] += colsum(dv)
    g["rk"][...] += tn3(buf2, dk2)
    g["rv"][...] += tn3(buf2, dv2)
    dbuf = mmwt(dk2, w["rk"]) + mmwt(dv2, w["rv"])
    rows[0] += colsum(dbuf)
    dbuf2 = split2(dbuf)
    g["so"][...] += tn3(o2, dbuf2)
    return dsend, mmwt(dbuf2, w["so"])


def recv_scratch(sb):
    return [
        pltpu.VMEM((sb * SB_ROWS, D), F32),
        pltpu.VMEM((sb * SB_ROWS, D), F32),
        pltpu.VMEM((sb * SB_ROWS, HALF), F32),
        pltpu.VMEM((sb * RPAD, D), F32),
        pltpu.VMEM((sb * RPAD, D), F32),
    ]


def recv_weight_specs():
    return [whole((D, D))] * 5 + [whole((D, FF)), whole((FF, D)), whole((24, D))]


def seg_block(sb, rows=SB_ROWS, width=D):
    return pl.BlockSpec((sb, rows, width), lambda i: (i, 0, 0))


def recv_fwd_kernel(sb, send_ref, o_ref, *refs):
    w = {n: refs[i][...] for i, n in enumerate(RECV_W)}
    vec_ref, mvec_ref, mw_ref, out_ref = refs[7:11]
    q_s, mix_s, p_s, kb_s, vb_s = refs[11:]
    y, _ = recv_forward(
        send_ref[...].reshape(sb * SB_ROWS, D), o_ref[...].reshape(sb * RPAD, D), w, vec_ref[...], q_s, mix_s, p_s, kb_s, vb_s
    )
    mvec = mvec_ref[...]
    wide, _, _, _ = merge_rows(y, sb // 2, mvec)
    out_ref[...] = (mmw(split2(wide), mw_ref[...]) + mvec[4:5]).reshape(sb // 2, SB_ROWS, D)


def recv_fwd(send, o, weights, mvec, mw, sb):
    n = send.shape[0]
    return pl.pallas_call(
        functools.partial(recv_fwd_kernel, sb),
        grid=(n // sb,),
        in_specs=[seg_block(sb), seg_block(sb, RPAD)] + recv_weight_specs() + [whole((8, D)), whole((2 * D, D))],
        out_specs=seg_block(sb // 2),
        out_shape=jax.ShapeDtypeStruct((n // 2, SB_ROWS, D), F32),
        scratch_shapes=recv_scratch(sb),
        compiler_params=params_spec(),
        name="recv_fwd",
    )(send, o, *weights, mvec, mw)


def recv_bwd_kernel(sb, send_ref, o_ref, dx_ref, *refs):
    w = {n: refs[i][...] for i, n in enumerate(RECV_W)}
    vec_ref, mvec_ref, mw_ref, dsend_ref, do_ref = refs[7:12]
    g = dict(zip(RECV_G, refs[12:20]))
    dmw_ref, dmv_ref = refs[20:22]
    q_s, mix_s, p_s, kb_s, vb_s = refs[22:]

    @pl.when(pl.program_id(0) == 0)
    def _():
        for ref in list(g.values()) + [dmw_ref, dmv_ref]:
            ref[...] = jnp.zeros(ref.shape, F32)

    vec = vec_ref[...]
    y, kept = recv_forward(
        send_ref[...].reshape(sb * SB_ROWS, D), o_ref[...].reshape(sb * RPAD, D), w, vec, q_s, mix_s, p_s, kb_s, vb_s
    )
    pairs = sb // 2
    wide, unit, inv, gain = merge_rows(y, pairs, mvec_ref[...])
    dx = dx_ref[...].reshape(pairs * SB_ROWS, D)
    dmv_ref[4] += colsum(dx)
    dx2 = split2(dx)
    dmw_ref[...] += tn3(split2(wide), dx2)
    dn = mmwt(dx2, mw_ref[...])
    part = colsum(dn * unit)
    dmv_ref[0] += part[:, :D]
    dmv_ref[1] += part[:, D:]
    part = colsum(dn)
    dmv_ref[2] += part[:, :D]
    dmv_ref[3] += part[:, D:]
    dwide = norm_bwd(dn, unit, inv, gain)
    left = dwide[:, :D].reshape(pairs, 1, SB_ROWS, D)
    right = dwide[:, D:].reshape(pairs, 1, SB_ROWS, D)
    dy = jnp.concatenate([left, right], 1).reshape(sb * SB_ROWS, D)
    dsend, do = recv_backward(dy, kept, w, vec, g, q_s, mix_s, p_s, kb_s, vb_s)
    dsend_ref[...] = dsend.reshape(sb, SB_ROWS, D)
    do_ref[...] = do.reshape(sb, RPAD, D)


RECV_GRADS = [(D, D)] * 5 + [(D, FF), (FF, D), (11, 8, D)]


def recv_bwd(send, o, dx, weights, mvec, mw, sb):
    n = send.shape[0]
    shapes = RECV_GRADS + [(2 * D, D), (5, 8, D)]
    return pl.pallas_call(
        functools.partial(recv_bwd_kernel, sb),
        grid=(n // sb,),
        in_specs=[seg_block(sb), seg_block(sb, RPAD), seg_block(sb // 2)]
        + recv_weight_specs()
        + [whole((8, D)), whole((2 * D, D))],
        out_specs=[seg_block(sb), seg_block(sb, RPAD)] + [whole(s) for s in shapes],
        out_shape=[jax.ShapeDtypeStruct((n, SB_ROWS, D), F32), jax.ShapeDtypeStruct((n, RPAD, D), F32)]
        + [jax.ShapeDtypeStruct(s, F32) for s in shapes],
        scratch_shapes=recv_scratch(sb),
        compiler_params=params_spec(),
        name="recv_bwd",
    )(send, o, dx, *weights, mvec, mw)


def tail_kernel(sb, send_ref, o_ref, tgt_ref, kept_ref, scale_ref, mean_ref, *refs):
    w = {n: refs[i][...] for i, n in enumerate(RECV_W)}
    vec_ref, head_ref, dsend_ref, do_ref = refs[7:11]
    g = dict(zip(RECV_G, refs[11:19]))
    dhead_ref = refs[19]
    q_s, mix_s, p_s, kb_s, vb_s = refs[20:]

    @pl.when(pl.program_id(0) == 0)
    def _():
        for ref in list(g.values()) + [dhead_ref]:
            ref[...] = jnp.zeros(ref.shape, F32)

    vec = vec_ref[...]
    rows = sb * SB_ROWS
    y, kept = recv_forward(
        send_ref[...].reshape(rows, D), o_ref[...].reshape(sb * RPAD, D), w, vec, q_s, mix_s, p_s, kb_s, vb_s
    )
    head = head_ref[...]
    y2 = split2(y)
    scale = jnp.broadcast_to(scale_ref[...][None], (sb, SB_ROWS, PPAD)).reshape(rows, PPAD)
    mean = jnp.broadcast_to(mean_ref[...][None], (sb, SB_ROWS, PPAD)).reshape(rows, PPAD)
    misfit = mmwt(y2, head) * scale + mean - tgt_ref[...].reshape(rows, PPAD)
    dpred = kept_ref[...].reshape(rows, PPAD) * misfit * scale
    dpred2 = split2(dpred)
    dhead_ref[...] += tn3(dpred2, y2)
    dy = mmw(dpred2, head)
    dsend, do = recv_backward(dy, kept, w, vec, g, q_s, mix_s, p_s, kb_s, vb_s)
    dsend_ref[...] = dsend.reshape(sb, SB_ROWS, D)
    do_ref[...] = do.reshape(sb, RPAD, D)


def tail(send, o, tgt, kept, scale, mean, weights, head, sb):
    n = send.shape[0]
    shapes = RECV_GRADS + [(PPAD, D)]
    return pl.pallas_call(
        functools.partial(tail_kernel, sb),
        grid=(n // sb,),
        in_specs=[seg_block(sb), seg_block(sb, RPAD), seg_block(sb, SB_ROWS, PPAD), seg_block(sb, SB_ROWS, PPAD)]
        + [whole((SB_ROWS, PPAD))] * 2
        + recv_weight_specs()
        + [whole((PPAD, D))],
        out_specs=[seg_block(sb), seg_block(sb, RPAD)] + [whole(s) for s in shapes],
        out_shape=[jax.ShapeDtypeStruct((n, SB_ROWS, D), F32), jax.ShapeDtypeStruct((n, RPAD, D), F32)]
        + [jax.ShapeDtypeStruct(s, F32) for s in shapes],
        scratch_shapes=recv_scratch(sb),
        compiler_params=params_spec(),
        name="tail",
    )(send, o, tgt, kept, scale, mean, *weights, head)


SEND_W = ("sq", "sk", "sv")


def send_project(dim2, r_rows, w, vec, k_s, v_s, q_s):
    k_s[...] = mmw(dim2, w["sk"])
    v_s[...] = mmw(dim2, w["sv"]) + vec[11:12]
    r2 = split2(r_rows)
    q_s[...] = (mmw(r2, w["sq"]) + vec[10:11]) * SCALE
    return r2


def send_fwd_kernel(sb, dim_ref, r_ref, here_ref, *refs):
    w = {n: refs[i][...] for i, n in enumerate(SEND_W)}
    vec_ref, o_ref, lse_ref, k_s, v_s, q_s = refs[3:]
    dim2 = split2(dim_ref[...].reshape(sb * SB_ROWS, D))
    send_project(dim2, r_ref[...].reshape(sb * RPAD, D), w, vec_ref[...], k_s, v_s, q_s)
    here = here_ref[...] > 0.5

    def one(s, carry):
        at = pl.ds(pl.multiple_of(s * SB_ROWS, SB_ROWS), SB_ROWS)
        ar = pl.ds(pl.multiple_of(s * RPAD, RPAD), RPAD)
        q2 = split2(spread_rows(q_s[ar, :]))
        sc = jnp.where(here, nt3(split2(k_s[at, :]), q2), negative)
        top = jnp.max(sc, 0, keepdims=True)
        p = jnp.where(here, jnp.exp(sc - top), 0.0)
        total = jnp.sum(p, 0, keepdims=True)
        safe = jnp.where(total > 0.0, total, 1.0)
        o_ref[s] = gather_rows(tn3(split2(p / safe), split2(v_s[at, :])))
        lse_ref[s] = jnp.where(total > 0.0, top + jnp.log(safe), negative)
        return carry

    lax.fori_loop(0, sb, one, 0)


def send_weight_specs():
    return [whole((D, D))] * 3 + [whole((24, D))]


def send_scratch(sb):
    return [
        pltpu.VMEM((sb * SB_ROWS, D), F32),
        pltpu.VMEM((sb * SB_ROWS, D), F32),
        pltpu.VMEM((sb * RPAD, D), F32),
    ]


def send_fwd(dim, routers, here, weights, sb):
    n = dim.shape[0]
    return pl.pallas_call(
        functools.partial(send_fwd_kernel, sb),
        grid=(n // sb,),
        in_specs=[seg_block(sb), seg_block(sb, RPAD), whole((SB_ROWS, HALF))] + send_weight_specs(),
        out_specs=[seg_block(sb, RPAD), seg_block(sb, 1, HALF)],
        out_shape=[jax.ShapeDtypeStruct((n, RPAD, D), F32), jax.ShapeDtypeStruct((n, 1, HALF), F32)],
        scratch_shapes=send_scratch(sb),
        compiler_params=params_spec(),
        name="send_fwd",
    )(dim, routers, here, *weights)


def send_bwd_kernel(sb, dim_ref, dpart_ref, r_ref, o_ref, lse_ref, do_ref, here_ref, *refs):
    w = {n: refs[i][...] for i, n in enumerate(SEND_W)}
    vec_ref, ddim_ref, dr_ref = refs[3:6]
    dsq_ref, dsk_ref, dsv_ref, rows = refs[6:10]
    k_s, v_s, q_s = refs[10:]

    @pl.when(pl.program_id(0) == 0)
    def _():
        for ref in (dsq_ref, dsk_ref, dsv_ref, rows):
            ref[...] = jnp.zeros(ref.shape, F32)

    dim2 = split2(dim_ref[...].reshape(sb * SB_ROWS, D))
    r2 = send_project(dim2, r_ref[...].reshape(sb * RPAD, D), w, vec_ref[...], k_s, v_s, q_s)
    here = (here_ref[...] > 0.5) & valid_lane(SB_ROWS)

    def one(s, carry):
        at = pl.ds(pl.multiple_of(s * SB_ROWS, SB_ROWS), SB_ROWS)
        ar = pl.ds(pl.multiple_of(s * RPAD, RPAD), RPAD)
        q2 = split2(spread_rows(q_s[ar, :]))
        k2 = split2(k_s[at, :])
        p = jnp.where(here, jnp.exp(nt3(k2, q2) - lse_ref[s]), 0.0)
        dwide = spread_rows(do_ref[s])
        d2 = split2(dwide)
        owide = jnp.broadcast_to(o_ref[s][:, None, :], (RPAD, HEADS, D)).reshape(RPAD * HEADS, D)
        e2 = split2(dwide * owide)
        one_row = jnp.ones((8, D), BF)
        mean = (dots(one_row, e2[0], 1, 1) + dots(one_row, e2[1], 1, 1))[0:1]
        dp = nt3(split2(v_s[at, :]), d2)
        s2 = split2(p * (dp - mean))
        q_s[ar, :] = gather_rows(tn3(s2, k2))
        k_s[at, :] = nn3(s2, q2)
        v_s[at, :] = nn3(split2(p), d2)
        return carry

    lax.fori_loop(0, sb, one, 0)
    dk2 = split2(k_s[...])
    dv = v_s[...]
    dv2 = split2(dv)
    rows[1] += colsum(dv)
    dsk_ref[...] += tn3(dim2, dk2)
    dsv_ref[...] += tn3(dim2, dv2)
    out = dpart_ref[...].reshape(sb * SB_ROWS, D) + mmwt(dk2, w["sk"]) + mmwt(dv2, w["sv"])
    ddim_ref[...] = out.reshape(sb, SB_ROWS, D)
    dq = q_s[...] * SCALE
    rows[0] += colsum(dq)
    dq2 = split2(dq)
    dsq_ref[...] += tn3(r2, dq2)
    dr_ref[...] = mmwt(dq2, w["sq"]).reshape(sb, RPAD, D)


def send_bwd(dim, dpart, routers, o, lse, do, here, weights, sb):
    n = dim.shape[0]
    shapes = [(D, D)] * 3 + [(2, 8, D)]
    return pl.pallas_call(
        functools.partial(send_bwd_kernel, sb),
        grid=(n // sb,),
        in_specs=[seg_block(sb), seg_block(sb), seg_block(sb, RPAD), seg_block(sb, RPAD), seg_block(sb, 1, HALF), seg_block(sb, RPAD), whole((SB_ROWS, HALF))]
        + send_weight_specs(),
        out_specs=[seg_block(sb), seg_block(sb, RPAD)] + [whole(s) for s in shapes],
        out_shape=[jax.ShapeDtypeStruct((n, SB_ROWS, D), F32), jax.ShapeDtypeStruct((n, RPAD, D), F32)]
        + [jax.ShapeDtypeStruct(s, F32) for s in shapes],
        scratch_shapes=send_scratch(sb),
        compiler_params=params_spec(),
        name="send_bwd",
    )(dim, dpart, routers, o, lse, do, here, *weights)


def merge_stats(o, lse, axis):
    every_o = lax.all_gather(o, axis)
    every_l = lax.all_gather(lse, axis)
    top = jnp.max(every_l, 0)
    total = top + jnp.log(jnp.sum(jnp.exp(every_l - top), 0))
    share = jnp.exp(every_l - total)
    n = o.shape[0]
    share = jnp.repeat(share.reshape(share.shape[0], n, RPAD, HEADS), D // HEADS, -1)
    return jnp.sum(every_o * share, 0), total


def series_stats(series, observed):
    seen = observed.astype(F32)
    counted = jnp.maximum(jnp.sum(seen, -1, keepdims=True), 1.0)
    mean = jnp.sum(seen * series, -1, keepdims=True) / counted
    center = (series - mean) * seen
    scale = jnp.sqrt(jnp.sum(center * center, -1, keepdims=True) / counted + norm_eps)
    return center / scale, mean, scale


def adam_update(weight, first_moment, second_moment, gradient):
    first_new = beta_one * first_moment + (1.0 - beta_one) * gradient
    second_new = beta_two * second_moment + (1.0 - beta_two) * gradient * gradient
    corrected = (
        first_new
        / (1.0 - beta_one**step_count)
        / (jnp.sqrt(second_new / (1.0 - beta_two**step_count)) + adam_eps)
    )
    return (weight - learn_rate * (corrected + weight_decay * weight), first_new, second_new)


def segment_major(x, width):
    nv = x.shape[0]
    x = x.reshape(nv, -1, 12).transpose(1, 0, 2)
    return jnp.pad(x, ((0, 0), (0, 0), (0, width - 12)))


def pad_rows(x, rows):
    return jnp.pad(x, ((0, rows - x.shape[0]), (0, 0)))


def gradient_parts(series, observed, targets, target_mask, present, square, up, down, vectors):
    nv = series.shape[0]
    normed, mean, scale = series_stats(series, observed)
    pieces = segment_major(normed, 16)
    factor = 2.0 / (1 << 20)
    kept = segment_major(target_mask.astype(F32) * present[:, None] * factor, PPAD)
    tgt = segment_major(targets, PPAD)
    scale16 = jnp.broadcast_to(scale, (nv, PPAD))
    mean16 = jnp.broadcast_to(mean, (nv, PPAD))
    here = jnp.broadcast_to(present[:, None], (nv, HALF))

    emb = pad_rows(vectors[:12], 16).astype(BF)
    place = (vectors[12:13] + vectors[13:73])[:, None, :]
    layer_start = SEGLEN + 1 + SEG
    vecs = [pad_rows(vectors[layer_start + 23 * l : layer_start + 23 * l + 23], 24) for l in range(2)]
    merge_at = layer_start + 46
    mvec = pad_rows(vectors[merge_at : merge_at + 5], 8)
    mw = square[24:26].reshape(2 * D, D)
    head = pad_rows(vectors[merge_at + 5 : merge_at + 17], PPAD).astype(BF)
    router_at = merge_at + 17
    routers = []
    for l, n in ((0, SEG), (1, SEG // 2)):
        r = vectors[router_at + l * SEG * ROUT : router_at + l * SEG * ROUT + n * ROUT].reshape(n, ROUT, D)
        routers.append(jnp.pad(r, ((0, 0), (0, RPAD - ROUT), (0, 0))))
    time_w = [
        (*[square[12 * l + i] for i in (0, 1, 2, 3)], up[2 * l], down[2 * l], vecs[l]) for l in range(2)
    ]
    send_w = [(*[square[12 * l + i] for i in (4, 5, 6)], vecs[l]) for l in range(2)]
    recv_w = [
        (*[square[12 * l + i] for i in (7, 9, 10, 8, 11)], up[2 * l + 1], down[2 * l + 1], vecs[l]) for l in range(2)
    ]

    sb0, sb1 = 4, 6
    dim0 = time_fwd(True, pieces, (emb, place), time_w[0], SEG)
    o0, lse0 = send_fwd(dim0, routers[0], here, send_w[0], sb0)
    o0, lse0 = merge_stats(o0, lse0, "fsdp")
    x1 = recv_fwd(dim0, o0, recv_w[0], mvec, mw, sb0)
    dim1 = time_fwd(False, x1, (), time_w[1], SEG // 2)
    o1, lse1 = send_fwd(dim1, routers[1], here, send_w[1], sb1)
    o1, lse1 = merge_stats(o1, lse1, "fsdp")
    out = tail(dim1, o1, tgt, kept, scale16, mean16, recv_w[1], head, sb1)
    ddim1, do1, grecv1, dhead = out[0], out[1], out[2:10], out[10]
    do1 = lax.psum(do1, "fsdp")
    out = send_bwd(dim1, ddim1, routers[1], o1, lse1, do1, here, send_w[1], sb1)
    ddim1, dr1, gsend1 = out[0], out[1], out[2:]
    out = time_bwd(False, x1, (), ddim1, time_w[1], SEG // 2)
    gtime1, dx1 = out[:7], out[7]
    out = recv_bwd(dim0, o0, dx1, recv_w[0], mvec, mw, sb0)
    ddim0, do0, grecv0, dmw, dmv = out[0], out[1], out[2:10], out[10], out[11]
    do0 = lax.psum(do0, "fsdp")
    out = send_bwd(dim0, ddim0, routers[0], o0, lse0, do0, here, send_w[0], sb0)
    ddim0, dr0, gsend0 = out[0], out[1], out[2:]
    out = time_bwd(True, pieces, (emb, place), ddim0, time_w[0], SEG)
    gtime0, demb, dplace = out[:7], out[7], out[8]

    mats, ups, downs, rows = [], [], [], []
    for gt, gs, gr in ((gtime0, gsend0, grecv0), (gtime1, gsend1, grecv1)):
        mats += [gt[0], gt[1], gt[2], gt[3], gs[0], gs[1], gs[2], gr[0], gr[3], gr[1], gr[2], gr[4]]
        ups += [gt[4], gr[5]]
        downs += [gt[5], gr[6]]
        rt, rs, rr = gt[6].sum(1), gs[3].sum(1), gr[7].sum(1)
        rows += [rt, rs, rr]
    mats += [dmw]
    dplace = dplace.reshape(SEG, VB, D).sum(1)
    vec = jnp.concatenate(
        [demb[:12], dplace.sum(0, keepdims=True), dplace]
        + rows
        + [dmv.sum(1), dhead[:12]]
        + [dr[:, :ROUT].reshape(-1, D) for dr in (dr0, dr1)],
        0,
    )
    return jnp.concatenate(mats, 0), jnp.concatenate(ups, 0), jnp.concatenate(downs, 0), vec


def on_device(series, observed, targets, target_mask, counts, matrices, feed_weights, vectors, matrices_first, matrices_second, feed_first, feed_second, vectors_first, vectors_second):
    everywhere = ("dp", "fsdp")
    local_vars = series.shape[1]
    slot = lax.axis_index("fsdp") * local_vars + jnp.arange(local_vars, dtype=jnp.int32)
    present = (slot < counts[0]).astype(F32)
    square = lax.all_gather(matrices.astype(BF), everywhere, axis=0, tiled=True).reshape(NSQ, D, D)
    feed = lax.all_gather(feed_weights.astype(BF), everywhere, axis=0, tiled=True)
    up = feed[: 4 * D * FF].reshape(4, D, FF)
    down = feed[4 * D * FF :].reshape(4, FF, D)
    vecs = lax.all_gather(vectors.astype(BF), everywhere, axis=0, tiled=True).astype(F32).reshape(NVEC, D)
    g_mat, g_up, g_down, g_vec = gradient_parts(
        series[0], observed[0], targets[0], target_mask[0], present, square, up, down, vecs
    )
    flat = (g_mat.reshape(-1), jnp.concatenate([g_up.reshape(-1), g_down.reshape(-1)]), g_vec.reshape(-1))
    shards = [lax.psum_scatter(f, everywhere, scatter_dimension=0, tiled=True) for f in flat]
    kept = jnp.sum(target_mask[0].astype(F32) * present[:, None])
    squares = sum(jnp.sum(s * s) for s in shards)
    sums = lax.psum(jnp.stack([squares, kept]), everywhere)
    upscale = (1 << 20) / jnp.maximum(sums[1], 1.0)
    grad_norm = jnp.sqrt(sums[0]) * upscale
    factor = upscale * (clip_norm / jnp.maximum(grad_norm, clip_norm))
    new = (
        adam_update(matrices, matrices_first, matrices_second, shards[0] * factor)
        + adam_update(feed_weights, feed_first, feed_second, shards[1] * factor)
        + adam_update(vectors, vectors_first, vectors_second, shards[2] * factor)
    )
    return (grad_norm,) + new


def solution(mesh):
    both = P(("dp", "fsdp"))
    data = P("dp", "fsdp", None)
    return jax.shard_map(
        on_device,
        mesh=mesh,
        in_specs=(data,) * 4 + (P("dp"),) + (both,) * 9,
        out_specs=(P(),) + (both,) * 9,
        check_vma=False,
    )
```

```python
import functools
import jax
import jax.numpy as jnp
from jax import lax
from jax.experimental import pallas as pl
from jax.experimental.pallas import tpu as pltpu
from jax.sharding import PartitionSpec as P

D = 256
HEADS = 8
FF = 512
ROUT = 10
RPAD = 16
SEGLEN = 12
PRED = 12
PPAD = 16
SEG = 60
NSQ = 26
NVEC = 1036
HALF = 128
VB = 8

BF = jnp.bfloat16
F32 = jnp.float32
SCALE = (D // HEADS) ** (-0.5)
negative = -1e30
norm_eps = 1e-05
beta_one = 0.9
beta_two = 0.999
adam_eps = 1e-08
weight_decay = 0.01
learn_rate = 0.2
clip_norm = 0.01
step_count = 10.0
VMEM_LIMIT = 60 << 20


def split2(x):
    hi = x.astype(BF)
    return hi, (x - hi.astype(F32)).astype(BF)


def dots(a, b, ca, cb):
    return lax.dot_general(a, b, (((ca,), (cb,)), ((), ())), preferred_element_type=F32)


def mmw(x2, w):
    return dots(x2[0], w, 1, 0) + dots(x2[1], w, 1, 0)


def mmwt(x2, w):
    return dots(x2[0], w, 1, 1) + dots(x2[1], w, 1, 1)


def rows2(a2):
    return jnp.concatenate([a2[0], a2[1]], 0)


def nn3(a2, b2):
    m = a2[0].shape[0]
    both = dots(rows2(a2), b2[0], 1, 0)
    return both[:m] + both[m:] + dots(a2[0], b2[1], 1, 0)


def nt3(a2, b2):
    m = a2[0].shape[0]
    both = dots(rows2(a2), b2[0], 1, 1)
    return both[:m] + both[m:] + dots(a2[0], b2[1], 1, 1)


def tn3(a2, b2):
    n = b2[0].shape[1]
    both = dots(a2[0], jnp.concatenate([b2[0], b2[1]], 1), 0, 0)
    return both[:, :n] + both[:, n:] + dots(a2[1], b2[0], 0, 0)


def norm_fwd(z, gain, bias):
    center = z - jnp.mean(z, -1, keepdims=True)
    inv = lax.rsqrt(jnp.mean(center * center, -1, keepdims=True) + norm_eps)
    unit = center * inv
    return unit * gain + bias, unit, inv


def norm_bwd(dy, unit, inv, gain):
    t = dy * gain
    return inv * (t - jnp.mean(t, -1, keepdims=True) - unit * jnp.mean(t * unit, -1, keepdims=True))


def colsum(x):
    return jnp.sum(x.reshape(x.shape[0] // 8, 8, x.shape[1]), 0)


def gelu_cdf(u):
    return 0.5 + 0.5 * lax.erf(u * 0.7071067811865476)


def gelu_slope(u, cdf):
    return cdf + u * (jnp.exp(-0.5 * u * u) * 0.3989422804014327)


def halves(x):
    return x[:, :HALF], x[:, HALF:]


def lane_head(rows):
    return lax.broadcasted_iota(jnp.int32, (rows, HALF), 1) // 32


def spread_heads(x, zero):
    head = lane_head(x.shape[0])
    return jnp.concatenate([jnp.where(head == h, x, zero) for h in range(4)], 0)


def gather_heads(x, group):
    head = lane_head(group)
    out = x[3 * group :]
    for h in range(3):
        out = jnp.where(head == h, x[h * group : (h + 1) * group], out)
    return out


def ones_heads(group, count):
    row = lax.broadcasted_iota(jnp.int32, (4 * group, HALF), 0)
    lane = lax.broadcasted_iota(jnp.int32, (4 * group, HALF), 1)
    return jnp.where((row // group == lane // 32) & (row % group < count), 1.0, 0.0).astype(BF)


def group_max(s, group, count):
    lane = lax.broadcasted_iota(jnp.int32, (s.shape[0], HALF), 1)
    outs = []
    for t in range(s.shape[1] // HALF):
        part = s[:, t * HALF : (t + 1) * HALF]
        top = None
        for g in range(HALF // group):
            here = (lane // group == g)
            best = jnp.max(jnp.where((lane // group == g) & (lane % group < count), part, negative), -1, keepdims=True)
            top = jnp.broadcast_to(best, part.shape) if top is None else jnp.where(here, best, top)
        outs.append(jnp.where(lane % group < count, part - top, negative))
    return jnp.concatenate(outs, 1)


def time_attend(c, v, group, count, q_s, k_s, v_s, o_s, p_s, l_s):
    at = pl.ds(v, group, stride=VB)
    q2 = split2(q_s[c, at, :])
    k2 = split2(k_s[c, at, :])
    w2 = split2(v_s[c, at, :])
    zero = jnp.zeros((), BF)
    k_hi, k_lo = spread_heads(k2[0], zero), spread_heads(k2[1], zero)
    w_hi, w_lo = spread_heads(w2[0], zero), spread_heads(w2[1], zero)
    s = dots(jnp.concatenate(q2, 1), jnp.concatenate([k_hi, k_hi], 1), 1, 1) + dots(q2[0], k_lo, 1, 1)
    p = jnp.exp(group_max(s, group, count))
    p2 = split2(p)
    both = dots(rows2(p2), jnp.concatenate([w_hi, ones_heads(group, count)], 1), 1, 0)
    both = both[:group] + both[group:]
    total = both[:, HALF:]
    o_s[c, at, :] = (both[:, :HALF] + dots(p2[0], w_lo, 1, 0)) / total
    if p_s is not None:
        p_s[c, v] = p
        l_s[c, v] = total


def time_attend_back(c, v, group, count, q_s, k_s, v_s, o_s, p_s, l_s, do_s):
    at = pl.ds(v, group, stride=VB)
    q2 = split2(q_s[c, at, :])
    k2 = split2(k_s[c, at, :])
    w2 = split2(v_s[c, at, :])
    zero = jnp.zeros((), BF)
    k_hi, k_lo = spread_heads(k2[0], zero), spread_heads(k2[1], zero)
    w_hi, w_lo = spread_heads(w2[0], zero), spread_heads(w2[1], zero)
    d = do_s[c, at, :] / l_s[c, v]
    d2 = split2(d)
    e2 = split2(d * o_s[c, at, :])
    p = p_s[c, v]
    x2 = (jnp.concatenate([d2[0], e2[0]], 1), jnp.concatenate([d2[1], e2[1]], 1))
    both = dots(rows2(x2), jnp.concatenate([w_hi, -ones_heads(group, count)], 1), 1, 1)
    dp = both[:group] + both[group:] + dots(d2[0], w_lo, 1, 1)
    p2 = split2(p)
    s2 = split2(p * dp)
    both = dots(rows2(s2), k_hi, 1, 0)
    q_s[c, at, :] = both[:group] + both[group:] + dots(s2[0], k_lo, 1, 0)
    k_s[c, at, :] = gather_heads(tn3(s2, q2), group)
    v_s[c, at, :] = gather_heads(tn3(p2, d2), group)


def store_halves(ref, x):
    rows = x.shape[0]
    ref[0, :rows, :] = x[:, :HALF]
    ref[1, :rows, :] = x[:, HALF:]


def load_halves(ref, rows):
    return jnp.concatenate([ref[0, :rows, :], ref[1, :rows, :]], 1)


def zero_tail(ref, rows):
    tail = ref.shape[1] - rows
    ref[:, rows:, :] = jnp.zeros((2, tail, HALF), F32)


def time_forward(x, w, vec, count, group, q_s, k_s, v_s, o_s, p_s=None, l_s=None):
    rows = count * VB
    x2 = split2(x)
    store_halves(q_s, (mmw(x2, w["q"]) + vec[0:1]) * SCALE)
    store_halves(k_s, mmw(x2, w["k"]))
    store_halves(v_s, mmw(x2, w["v"]) + vec[1:2])
    for ref in (q_s, k_s, v_s):
        zero_tail(ref, rows)

    def one(v, carry):
        for c in range(2):
            time_attend(c, v, group, count, q_s, k_s, v_s, o_s, p_s, l_s)
        return carry

    lax.fori_loop(0, VB, one, 0)
    mixed = load_halves(o_s, rows)
    h, unit1, inv1 = norm_fwd(x + mmw(split2(mixed), w["o"]) + vec[2:3], vec[3:4], vec[4:5])
    bias_up = jnp.concatenate([vec[5:6], vec[6:7]], 1)
    u = mmw(split2(h), w["up"]) + bias_up
    cdf = gelu_cdf(u)
    z2 = h + mmw(split2(u * cdf), w["down"]) + vec[7:8]
    y, unit2, inv2 = norm_fwd(z2, vec[8:9], vec[9:10])
    return y, (x2, mixed, h, unit1, inv1, u, cdf, unit2, inv2)


def embed_block(pieces, emb, place):
    return mmw(split2(pieces), emb) + place


TIME_W = ("q", "k", "v", "o", "up", "down")


def time_fwd_kernel(first, count, group, *refs):
    if first:
        x_ref, emb_ref, place_ref = refs[:3]
        refs = refs[3:]
    else:
        x_ref = refs[0]
        refs = refs[1:]
    w = {name: refs[i][...] for i, name in enumerate(TIME_W)}
    vec_ref, y_ref, q_s, k_s, v_s, o_s = refs[6:]
    rows = count * VB
    if first:
        place = jnp.broadcast_to(place_ref[...], (count, VB, D)).reshape(rows, D)
        x = embed_block(x_ref[...].reshape(rows, 16), emb_ref[...], place)
    else:
        x = x_ref[...].reshape(rows, D)
    y, _ = time_forward(x, w, vec_ref[...], count, group, q_s, k_s, v_s, o_s)
    y_ref[...] = y.reshape(count, VB, D)


def whole(shape):
    return pl.BlockSpec(shape, lambda i: (0,) * len(shape))


def params_spec():
    return pltpu.CompilerParams(vmem_limit_bytes=VMEM_LIMIT)


def time_weight_specs():
    return [whole((D, D))] * 4 + [whole((D, FF)), whole((FF, D)), whole((24, D))]


def time_fwd(first, x, extra, weights, count):
    group = 64 if count > 32 else 32
    nv = x.shape[1]
    width = x.shape[2]
    specs = [pl.BlockSpec((count, VB, width), lambda i: (0, i, 0))]
    if first:
        specs += [whole((16, D)), whole((count, 1, D))]
    pad = group * VB
    return pl.pallas_call(
        functools.partial(time_fwd_kernel, first, count, group),
        grid=(nv // VB,),
        in_specs=specs + time_weight_specs(),
        out_specs=pl.BlockSpec((count, VB, D), lambda i: (0, i, 0)),
        out_shape=jax.ShapeDtypeStruct((count, nv, D), F32),
        scratch_shapes=[pltpu.VMEM((2, pad, HALF), F32)] * 4,
        compiler_params=params_spec(),
        name="time_fwd",
    )(x, *extra, *weights)


def time_bwd_kernel(first, count, group, *refs):
    if first:
        x_ref, emb_ref, place_ref = refs[:3]
        refs = refs[3:]
    else:
        x_ref = refs[0]
        refs = refs[1:]
    dy_ref = refs[0]
    w = {name: refs[1 + i][...] for i, name in enumerate(TIME_W)}
    vec_ref = refs[7]
    outs = refs[8:]
    n_out = 9 if first else 8
    g = dict(zip(TIME_W + ("rows",), outs[:7]))
    tail = outs[7:n_out]
    q_s, k_s, v_s, o_s, do_s, p_s, l_s = outs[n_out:]
    rows = count * VB
    step = pl.program_id(0)

    @pl.when(step == 0)
    def _():
        for ref in list(g.values()) + (list(tail) if first else []):
            ref[...] = jnp.zeros(ref.shape, F32)

    vec = vec_ref[...]
    if first:
        place = jnp.broadcast_to(place_ref[...], (count, VB, D)).reshape(rows, D)
        pieces = x_ref[...].reshape(rows, 16)
        x = embed_block(pieces, emb_ref[...], place)
    else:
        x = x_ref[...].reshape(rows, D)
    _, (x2, mixed, h, unit1, inv1, u, cdf, unit2, inv2) = time_forward(
        x, w, vec, count, group, q_s, k_s, v_s, o_s, p_s, l_s
    )
    dy = dy_ref[...].reshape(rows, D)
    g["rows"][8] += colsum(dy * unit2)
    g["rows"][9] += colsum(dy)
    dz2 = norm_bwd(dy, unit2, inv2, vec[8:9])
    g["rows"][7] += colsum(dz2)
    dz22 = split2(dz2)
    g["down"][...] += tn3(split2(u * cdf), dz22)
    du = mmwt(dz22, w["down"]) * gelu_slope(u, cdf)
    g["rows"][5] += colsum(du[:, :D])
    g["rows"][6] += colsum(du[:, D:])
    du2 = split2(du)
    g["up"][...] += tn3(split2(h), du2)
    dh = dz2 + mmwt(du2, w["up"])
    g["rows"][3] += colsum(dh * unit1)
    g["rows"][4] += colsum(dh)
    dz1 = norm_bwd(dh, unit1, inv1, vec[3:4])
    g["rows"][2] += colsum(dz1)
    dz12 = split2(dz1)
    g["o"][...] += tn3(split2(mixed), dz12)
    store_halves(do_s, mmwt(dz12, w["o"]))
    zero_tail(do_s, rows)

    def one(v, carry):
        for c in range(2):
            time_attend_back(c, v, group, count, q_s, k_s, v_s, o_s, p_s, l_s, do_s)
        return carry

    lax.fori_loop(0, VB, one, 0)
    dq = load_halves(q_s, rows) * SCALE
    g["rows"][0] += colsum(dq)
    dq2 = split2(dq)
    g["q"][...] += tn3(x2, dq2)
    dx = dz1 + mmwt(dq2, w["q"])
    dk2 = split2(load_halves(k_s, rows))
    g["k"][...] += tn3(x2, dk2)
    dx = dx + mmwt(dk2, w["k"])
    dv = load_halves(v_s, rows)
    g["rows"][1] += colsum(dv)
    dv2 = split2(dv)
    g["v"][...] += tn3(x2, dv2)
    dx = dx + mmwt(dv2, w["v"])
    if first:
        tail[0][...] += tn3(split2(pieces), split2(dx))
        tail[1][...] += dx
    else:
        tail[0][...] = dx.reshape(count, VB, D)


def time_bwd(first, x, extra, dy, weights, count):
    group = 64 if count > 32 else 32
    nv = x.shape[1]
    width = x.shape[2]
    pad = group * VB
    block = pl.BlockSpec((count, VB, D), lambda i: (0, i, 0))
    specs = [pl.BlockSpec((count, VB, width), lambda i: (0, i, 0))]
    if first:
        specs += [whole((16, D)), whole((count, 1, D))]
    grad_shapes = [(D, D)] * 4 + [(D, FF), (FF, D), (10, 8, D)]
    if first:
        grad_shapes += [(16, D), (count * VB, D)]
    out_specs = [whole(s) for s in grad_shapes]
    out_shape = [jax.ShapeDtypeStruct(s, F32) for s in grad_shapes]
    if not first:
        out_specs.append(block)
        out_shape.append(jax.ShapeDtypeStruct((count, nv, D), F32))
    return pl.pallas_call(
        functools.partial(time_bwd_kernel, first, count, group),
        grid=(nv // VB,),
        in_specs=specs + [block] + time_weight_specs(),
        out_specs=out_specs,
        out_shape=out_shape,
        scratch_shapes=[pltpu.VMEM((2, pad, HALF), F32)] * 5
        + [pltpu.VMEM((2, VB, group, 4 * group), F32), pltpu.VMEM((2, VB, group, HALF), F32)],
        compiler_params=params_spec(),
        name="time_bwd",
    )(x, *extra, dy, *weights)

SB_ROWS = 64


def head_rows():
    sub = lax.broadcasted_iota(jnp.int32, (8, D), 0)
    lane = lax.broadcasted_iota(jnp.int32, (8, D), 1)
    return jnp.where(sub == lane // 32, 1.0, 0.0).astype(F32)


def spread_rows(x):
    wide = jnp.broadcast_to(x[:, None, :], (RPAD, HEADS, D)) * head_rows()[None]
    return wide.reshape(RPAD * HEADS, D)


def gather_rows(x):
    return jnp.sum(x.reshape(RPAD, HEADS, D) * head_rows()[None], 1)


PACK = 24


def pack_rows(x, last=None):
    last = jnp.zeros((1, HALF), F32) if last is None else last
    return jnp.concatenate([x[:ROUT, :HALF], x[:ROUT, HALF:], last, jnp.zeros((PACK - 2 * ROUT - 1, HALF), F32)], 0)


def unpack_rows(x):
    x = jnp.concatenate([x[:ROUT], x[ROUT : 2 * ROUT]], 1)
    return jnp.concatenate([x, jnp.zeros((RPAD - ROUT, D), F32)], 0)


def unpack_block(ref, sb):
    return jnp.concatenate([unpack_rows(ref[s]) for s in range(sb)], 0)


def pack_block(ref, x, sb):
    for s in range(sb):
        ref[s] = pack_rows(x[s * RPAD : (s + 1) * RPAD])


def valid_lane(rows):
    return lax.broadcasted_iota(jnp.int32, (rows, HALF), 1) < ROUT * HEADS


def router_reduce(x, op):
    for shift in (8, 16, 32, 64):
        x = op(x, pltpu.roll(x, shift, 1))
    return x


def merge_rows(y, pairs, vec):
    wide = y.reshape(pairs, 2, SB_ROWS, D)
    wide = jnp.concatenate([wide[:, 0].reshape(pairs * SB_ROWS, D), wide[:, 1].reshape(pairs * SB_ROWS, D)], 1)
    gain = jnp.concatenate([vec[0:1], vec[1:2]], 1)
    bias = jnp.concatenate([vec[2:3], vec[3:4]], 1)
    return norm_fwd(wide, gain, bias) + (gain,)


RECV_W = ("so", "rk", "rv", "rq", "ro", "up", "down")


def recv_forward(send, o_rows, w, vec, q_s, mix_s, p_s, kb_s, vb_s):
    sb = send.shape[0] // SB_ROWS
    send2 = split2(send)
    o2 = split2(o_rows)
    buf = mmw(o2, w["so"]) + vec[12:13]
    buf2 = split2(buf)
    kb_s[...] = mmw(buf2, w["rk"])
    vb_s[...] = mmw(buf2, w["rv"]) + vec[14:15]
    q_s[...] = (mmw(send2, w["rq"]) + vec[13:14]) * SCALE

    def one(s, carry):
        at = pl.ds(pl.multiple_of(s * SB_ROWS, SB_ROWS), SB_ROWS)
        ar = pl.ds(pl.multiple_of(s * RPAD, RPAD), RPAD)
        k2 = split2(spread_rows(kb_s[ar, :]))
        v2 = split2(spread_rows(vb_s[ar, :]))
        sc = jnp.where(valid_lane(SB_ROWS), nt3(split2(q_s[at, :]), k2), negative)
        p = jnp.exp(sc - router_reduce(sc, jnp.maximum))
        p = p / router_reduce(p, jnp.add)
        p_s[at, :] = p
        mix_s[at, :] = nn3(split2(p), v2)
        return carry

    lax.fori_loop(0, sb, one, 0)
    mixed = mix_s[...]
    g, unit3, inv3 = norm_fwd(send + mmw(split2(mixed), w["ro"]) + vec[15:16], vec[16:17], vec[17:18])
    u = mmw(split2(g), w["up"]) + jnp.concatenate([vec[18:19], vec[19:20]], 1)
    cdf = gelu_cdf(u)
    y, unit4, inv4 = norm_fwd(g + mmw(split2(u * cdf), w["down"]) + vec[20:21], vec[21:22], vec[22:23])
    return y, (send2, o2, buf2, mixed, g, unit3, inv3, u, cdf, unit4, inv4)


RECV_G = RECV_W + ("rows",)


def recv_backward(dy, kept, w, vec, g, q_s, do_s, p_s, kb_s, vb_s):
    send2, o2, buf2, mixed, gg, unit3, inv3, u, cdf, unit4, inv4 = kept
    sb = dy.shape[0] // SB_ROWS
    rows = g["rows"]
    rows[9] += colsum(dy * unit4)
    rows[10] += colsum(dy)
    dz4 = norm_bwd(dy, unit4, inv4, vec[21:22])
    rows[8] += colsum(dz4)
    dz42 = split2(dz4)
    g["down"][...] += tn3(split2(u * cdf), dz42)
    du = mmwt(dz42, w["down"]) * gelu_slope(u, cdf)
    rows[6] += colsum(du[:, :D])
    rows[7] += colsum(du[:, D:])
    du2 = split2(du)
    g["up"][...] += tn3(split2(gg), du2)
    dg = dz4 + mmwt(du2, w["up"])
    rows[4] += colsum(dg * unit3)
    rows[5] += colsum(dg)
    dz3 = norm_bwd(dg, unit3, inv3, vec[16:17])
    rows[3] += colsum(dz3)
    dz32 = split2(dz3)
    g["ro"][...] += tn3(split2(mixed), dz32)
    do_s[...] = mmwt(dz32, w["ro"])

    def one(s, carry):
        at = pl.ds(pl.multiple_of(s * SB_ROWS, SB_ROWS), SB_ROWS)
        ar = pl.ds(pl.multiple_of(s * RPAD, RPAD), RPAD)
        k2 = split2(spread_rows(kb_s[ar, :]))
        v2 = split2(spread_rows(vb_s[ar, :]))
        q2 = split2(q_s[at, :])
        d2 = split2(do_s[at, :])
        p = p_s[at, :]
        dp = nt3(d2, v2)
        ds = p * (dp - router_reduce(p * dp, jnp.add))
        s2 = split2(ds)
        kb_s[ar, :] = gather_rows(tn3(s2, q2))
        vb_s[ar, :] = gather_rows(tn3(split2(p), d2))
        q_s[at, :] = nn3(s2, k2)
        return carry

    lax.fori_loop(0, sb, one, 0)
    dq = q_s[...] * SCALE
    rows[1] += colsum(dq)
    dq2 = split2(dq)
    g["rq"][...] += tn3(send2, dq2)
    dsend = dz3 + mmwt(dq2, w["rq"])
    dk2 = split2(kb_s[...])
    dv = vb_s[...]
    dv2 = split2(dv)
    rows[2] += colsum(dv)
    g["rk"][...] += tn3(buf2, dk2)
    g["rv"][...] += tn3(buf2, dv2)
    dbuf = mmwt(dk2, w["rk"]) + mmwt(dv2, w["rv"])
    rows[0] += colsum(dbuf)
    dbuf2 = split2(dbuf)
    g["so"][...] += tn3(o2, dbuf2)
    return dsend, mmwt(dbuf2, w["so"])


def recv_scratch(sb):
    return [
        pltpu.VMEM((sb * SB_ROWS, D), F32),
        pltpu.VMEM((sb * SB_ROWS, D), F32),
        pltpu.VMEM((sb * SB_ROWS, HALF), F32),
        pltpu.VMEM((sb * RPAD, D), F32),
        pltpu.VMEM((sb * RPAD, D), F32),
    ]


def recv_weight_specs():
    return [whole((D, D))] * 5 + [whole((D, FF)), whole((FF, D)), whole((24, D))]


def seg_block(sb, rows=SB_ROWS, width=D):
    return pl.BlockSpec((sb, rows, width), lambda i: (i, 0, 0))


def pack_spec(sb):
    return seg_block(sb, PACK, HALF)


def recv_fwd_kernel(sb, send_ref, o_ref, *refs):
    w = {n: refs[i][...] for i, n in enumerate(RECV_W)}
    vec_ref, mvec_ref, mw_ref, out_ref = refs[7:11]
    q_s, mix_s, p_s, kb_s, vb_s = refs[11:]
    y, _ = recv_forward(
        send_ref[...].reshape(sb * SB_ROWS, D), unpack_block(o_ref, sb), w, vec_ref[...], q_s, mix_s, p_s, kb_s, vb_s
    )
    mvec = mvec_ref[...]
    wide, _, _, _ = merge_rows(y, sb // 2, mvec)
    out_ref[...] = (mmw(split2(wide), mw_ref[...]) + mvec[4:5]).reshape(sb // 2, SB_ROWS, D)


def recv_fwd(send, o, weights, mvec, mw, sb):
    n = send.shape[0]
    return pl.pallas_call(
        functools.partial(recv_fwd_kernel, sb),
        grid=(n // sb,),
        in_specs=[seg_block(sb), pack_spec(sb)] + recv_weight_specs() + [whole((8, D)), whole((2 * D, D))],
        out_specs=seg_block(sb // 2),
        out_shape=jax.ShapeDtypeStruct((n // 2, SB_ROWS, D), F32),
        scratch_shapes=recv_scratch(sb),
        compiler_params=params_spec(),
        name="recv_fwd",
    )(send, o, *weights, mvec, mw)


def recv_bwd_kernel(sb, send_ref, o_ref, dx_ref, *refs):
    w = {n: refs[i][...] for i, n in enumerate(RECV_W)}
    vec_ref, mvec_ref, mw_ref, dsend_ref, do_ref = refs[7:12]
    g = dict(zip(RECV_G, refs[12:20]))
    dmw_ref, dmv_ref = refs[20:22]
    q_s, mix_s, p_s, kb_s, vb_s = refs[22:]

    @pl.when(pl.program_id(0) == 0)
    def _():
        for ref in list(g.values()) + [dmw_ref, dmv_ref]:
            ref[...] = jnp.zeros(ref.shape, F32)

    vec = vec_ref[...]
    y, kept = recv_forward(
        send_ref[...].reshape(sb * SB_ROWS, D), unpack_block(o_ref, sb), w, vec, q_s, mix_s, p_s, kb_s, vb_s
    )
    pairs = sb // 2
    wide, unit, inv, gain = merge_rows(y, pairs, mvec_ref[...])
    dx = dx_ref[...].reshape(pairs * SB_ROWS, D)
    dmv_ref[4] += colsum(dx)
    dx2 = split2(dx)
    dmw_ref[...] += tn3(split2(wide), dx2)
    dn = mmwt(dx2, mw_ref[...])
    part = colsum(dn * unit)
    dmv_ref[0] += part[:, :D]
    dmv_ref[1] += part[:, D:]
    part = colsum(dn)
    dmv_ref[2] += part[:, :D]
    dmv_ref[3] += part[:, D:]
    dwide = norm_bwd(dn, unit, inv, gain)
    left = dwide[:, :D].reshape(pairs, 1, SB_ROWS, D)
    right = dwide[:, D:].reshape(pairs, 1, SB_ROWS, D)
    dy = jnp.concatenate([left, right], 1).reshape(sb * SB_ROWS, D)
    dsend, do = recv_backward(dy, kept, w, vec, g, q_s, mix_s, p_s, kb_s, vb_s)
    dsend_ref[...] = dsend.reshape(sb, SB_ROWS, D)
    pack_block(do_ref, do, sb)


RECV_GRADS = [(D, D)] * 5 + [(D, FF), (FF, D), (11, 8, D)]


def recv_bwd(send, o, dx, weights, mvec, mw, sb):
    n = send.shape[0]
    shapes = RECV_GRADS + [(2 * D, D), (5, 8, D)]
    return pl.pallas_call(
        functools.partial(recv_bwd_kernel, sb),
        grid=(n // sb,),
        in_specs=[seg_block(sb), pack_spec(sb), seg_block(sb // 2)]
        + recv_weight_specs()
        + [whole((8, D)), whole((2 * D, D))],
        out_specs=[seg_block(sb), pack_spec(sb)] + [whole(s) for s in shapes],
        out_shape=[jax.ShapeDtypeStruct((n, SB_ROWS, D), F32), jax.ShapeDtypeStruct(o.shape, F32)]
        + [jax.ShapeDtypeStruct(s, F32) for s in shapes],
        scratch_shapes=recv_scratch(sb),
        compiler_params=params_spec(),
        name="recv_bwd",
    )(send, o, dx, *weights, mvec, mw)


def tail_kernel(sb, send_ref, o_ref, tgt_ref, kept_ref, scale_ref, mean_ref, *refs):
    w = {n: refs[i][...] for i, n in enumerate(RECV_W)}
    vec_ref, head_ref, dsend_ref, do_ref = refs[7:11]
    g = dict(zip(RECV_G, refs[11:19]))
    dhead_ref = refs[19]
    q_s, mix_s, p_s, kb_s, vb_s = refs[20:]

    @pl.when(pl.program_id(0) == 0)
    def _():
        for ref in list(g.values()) + [dhead_ref]:
            ref[...] = jnp.zeros(ref.shape, F32)

    vec = vec_ref[...]
    rows = sb * SB_ROWS
    y, kept = recv_forward(
        send_ref[...].reshape(rows, D), unpack_block(o_ref, sb), w, vec, q_s, mix_s, p_s, kb_s, vb_s
    )
    head = head_ref[...]
    y2 = split2(y)
    scale = jnp.broadcast_to(scale_ref[...][None], (sb, SB_ROWS, PPAD)).reshape(rows, PPAD)
    mean = jnp.broadcast_to(mean_ref[...][None], (sb, SB_ROWS, PPAD)).reshape(rows, PPAD)
    misfit = mmwt(y2, head) * scale + mean - tgt_ref[...].reshape(rows, PPAD)
    dpred = kept_ref[...].reshape(rows, PPAD) * misfit * scale
    dpred2 = split2(dpred)
    dhead_ref[...] += tn3(dpred2, y2)
    dy = mmw(dpred2, head)
    dsend, do = recv_backward(dy, kept, w, vec, g, q_s, mix_s, p_s, kb_s, vb_s)
    dsend_ref[...] = dsend.reshape(sb, SB_ROWS, D)
    pack_block(do_ref, do, sb)


def tail(send, o, tgt, kept, scale, mean, weights, head, sb):
    n = send.shape[0]
    shapes = RECV_GRADS + [(PPAD, D)]
    return pl.pallas_call(
        functools.partial(tail_kernel, sb),
        grid=(n // sb,),
        in_specs=[seg_block(sb), pack_spec(sb), seg_block(sb, SB_ROWS, PPAD), seg_block(sb, SB_ROWS, PPAD)]
        + [whole((SB_ROWS, PPAD))] * 2
        + recv_weight_specs()
        + [whole((PPAD, D))],
        out_specs=[seg_block(sb), pack_spec(sb)] + [whole(s) for s in shapes],
        out_shape=[jax.ShapeDtypeStruct((n, SB_ROWS, D), F32), jax.ShapeDtypeStruct(o.shape, F32)]
        + [jax.ShapeDtypeStruct(s, F32) for s in shapes],
        scratch_shapes=recv_scratch(sb),
        compiler_params=params_spec(),
        name="tail",
    )(send, o, tgt, kept, scale, mean, *weights, head)


SEND_W = ("sq", "sk", "sv")


def send_project(dim2, r_rows, w, vec, k_s, v_s, q_s):
    k_s[...] = mmw(dim2, w["sk"])
    v_s[...] = mmw(dim2, w["sv"]) + vec[11:12]
    r2 = split2(r_rows)
    q_s[...] = (mmw(r2, w["sq"]) + vec[10:11]) * SCALE
    return r2


def send_fwd_kernel(sb, dim_ref, r_ref, here_ref, *refs):
    w = {n: refs[i][...] for i, n in enumerate(SEND_W)}
    vec_ref, o_ref, k_s, v_s, q_s = refs[3:]
    dim2 = split2(dim_ref[...].reshape(sb * SB_ROWS, D))
    send_project(dim2, r_ref[...].reshape(sb * RPAD, D), w, vec_ref[...], k_s, v_s, q_s)
    here = here_ref[...] > 0.5

    def one(s, carry):
        at = pl.ds(pl.multiple_of(s * SB_ROWS, SB_ROWS), SB_ROWS)
        ar = pl.ds(pl.multiple_of(s * RPAD, RPAD), RPAD)
        q2 = split2(spread_rows(q_s[ar, :]))
        sc = jnp.where(here, nt3(split2(k_s[at, :]), q2), negative)
        top = jnp.max(sc, 0, keepdims=True)
        p = jnp.where(here, jnp.exp(sc - top), 0.0)
        total = jnp.sum(p, 0, keepdims=True)
        safe = jnp.where(total > 0.0, total, 1.0)
        lse = jnp.where(total > 0.0, top + jnp.log(safe), negative)
        o_ref[s] = pack_rows(gather_rows(tn3(split2(p / safe), split2(v_s[at, :]))), lse)
        return carry

    lax.fori_loop(0, sb, one, 0)


def send_weight_specs():
    return [whole((D, D))] * 3 + [whole((24, D))]


def send_scratch(sb):
    return [
        pltpu.VMEM((sb * SB_ROWS, D), F32),
        pltpu.VMEM((sb * SB_ROWS, D), F32),
        pltpu.VMEM((sb * RPAD, D), F32),
    ]


def send_fwd(dim, routers, here, weights, sb, npad):
    n = dim.shape[0]
    return pl.pallas_call(
        functools.partial(send_fwd_kernel, sb),
        grid=(n // sb,),
        in_specs=[seg_block(sb), seg_block(sb, RPAD), whole((SB_ROWS, HALF))] + send_weight_specs(),
        out_specs=pack_spec(sb),
        out_shape=jax.ShapeDtypeStruct((npad, PACK, HALF), F32),
        scratch_shapes=send_scratch(sb),
        compiler_params=params_spec(),
        name="send_fwd",
    )(dim, routers, here, *weights)


def send_bwd_kernel(sb, dim_ref, dpart_ref, r_ref, o_ref, do_ref, here_ref, *refs):
    w = {n: refs[i][...] for i, n in enumerate(SEND_W)}
    vec_ref, ddim_ref, dr_ref = refs[3:6]
    dsq_ref, dsk_ref, dsv_ref, rows = refs[6:10]
    k_s, v_s, q_s = refs[10:]

    @pl.when(pl.program_id(0) == 0)
    def _():
        for ref in (dsq_ref, dsk_ref, dsv_ref, rows):
            ref[...] = jnp.zeros(ref.shape, F32)

    dim2 = split2(dim_ref[...].reshape(sb * SB_ROWS, D))
    r2 = send_project(dim2, r_ref[...].reshape(sb * RPAD, D), w, vec_ref[...], k_s, v_s, q_s)
    here = (here_ref[...] > 0.5) & valid_lane(SB_ROWS)

    def one(s, carry):
        at = pl.ds(pl.multiple_of(s * SB_ROWS, SB_ROWS), SB_ROWS)
        ar = pl.ds(pl.multiple_of(s * RPAD, RPAD), RPAD)
        q2 = split2(spread_rows(q_s[ar, :]))
        k2 = split2(k_s[at, :])
        p = jnp.where(here, jnp.exp(nt3(k2, q2) - o_ref[s][2 * ROUT : 2 * ROUT + 1]), 0.0)
        dwide = spread_rows(unpack_rows(do_ref[s]))
        d2 = split2(dwide)
        owide = jnp.broadcast_to(unpack_rows(o_ref[s])[:, None, :], (RPAD, HEADS, D)).reshape(RPAD * HEADS, D)
        e2 = split2(dwide * owide)
        one_row = jnp.ones((8, D), BF)
        mean = (dots(one_row, e2[0], 1, 1) + dots(one_row, e2[1], 1, 1))[0:1]
        dp = nt3(split2(v_s[at, :]), d2)
        s2 = split2(p * (dp - mean))
        q_s[ar, :] = gather_rows(tn3(s2, k2))
        k_s[at, :] = nn3(s2, q2)
        v_s[at, :] = nn3(split2(p), d2)
        return carry

    lax.fori_loop(0, sb, one, 0)
    dk2 = split2(k_s[...])
    dv = v_s[...]
    dv2 = split2(dv)
    rows[1] += colsum(dv)
    dsk_ref[...] += tn3(dim2, dk2)
    dsv_ref[...] += tn3(dim2, dv2)
    out = dpart_ref[...].reshape(sb * SB_ROWS, D) + mmwt(dk2, w["sk"]) + mmwt(dv2, w["sv"])
    ddim_ref[...] = out.reshape(sb, SB_ROWS, D)
    dq = q_s[...] * SCALE
    rows[0] += colsum(dq)
    dq2 = split2(dq)
    dsq_ref[...] += tn3(r2, dq2)
    dr_ref[...] = mmwt(dq2, w["sq"]).reshape(sb, RPAD, D)


def send_bwd(dim, dpart, routers, o, do, here, weights, sb):
    n = dim.shape[0]
    shapes = [(D, D)] * 3 + [(2, 8, D)]
    return pl.pallas_call(
        functools.partial(send_bwd_kernel, sb),
        grid=(n // sb,),
        in_specs=[seg_block(sb), seg_block(sb), seg_block(sb, RPAD), pack_spec(sb), pack_spec(sb), whole((SB_ROWS, HALF))]
        + send_weight_specs(),
        out_specs=[seg_block(sb), seg_block(sb, RPAD)] + [whole(s) for s in shapes],
        out_shape=[jax.ShapeDtypeStruct((n, SB_ROWS, D), F32), jax.ShapeDtypeStruct((n, RPAD, D), F32)]
        + [jax.ShapeDtypeStruct(s, F32) for s in shapes],
        scratch_shapes=send_scratch(sb),
        compiler_params=params_spec(),
        name="send_bwd",
    )(dim, dpart, routers, o, do, here, *weights)

MESH = pl.DeviceIdType.MESH
ANY = pl.BlockSpec(memory_space=pl.ANY)
INVMEM = pl.BlockSpec(memory_space=pltpu.VMEM)


def grid_sizes():
    nf = lax.axis_size("fsdp")
    nx = 1
    while 2 * nx * nx < nf:
        nx *= 2
    return lax.axis_size("dp") // 2, nf // nx, nx


class Place:
    def __init__(self):
        self.ny, self.nz, self.nx = grid_sizes()
        dp, fs = lax.axis_index("dp"), lax.axis_index("fsdp")
        self.core, self.y = lax.rem(dp, 2), lax.div(dp, 2)
        self.x, self.z = lax.rem(fs, self.nx), lax.div(fs, self.nx)

    def at(self, y=None, core=None, z=None, x=None):
        y = self.y if y is None else y
        core = self.core if core is None else core
        z = self.z if z is None else z
        x = self.x if x is None else x
        return (y * 2 + core, z * self.nx + x)

    def other(self):
        return 1 - self.core

    def next_x(self, k):
        return lax.rem(self.x + k, self.nx)

    def next_y(self, k):
        return lax.rem(self.y + k, self.ny)

    def next_z(self, k):
        return lax.rem(self.z + k, self.nz)

    def neighbours(self):
        out = [self.at(core=self.other())]
        out += [self.at(x=self.next_x(k)) for k in range(1, self.nx)]
        out += [self.at(y=self.next_y(k)) for k in range(1, self.ny)]
        out += [self.at(z=self.next_z(k)) for k in range(1, self.nz)]
        return out


def greet(devices):
    barrier = pltpu.get_barrier_semaphore()
    for device in devices:
        pl.semaphore_signal(barrier, inc=1, device_id=device, device_id_type=MESH)
    pl.semaphore_wait(barrier, len(devices))


def remote(src, dst, send, recv, device):
    return pltpu.make_async_remote_copy(
        src_ref=src, dst_ref=dst, send_sem=send, recv_sem=recv, device_id=device, device_id_type=MESH
    )


def gather_kernel(n, *refs):
    shards, outs = refs[:n], refs[n : 2 * n]
    send, recv, local = refs[2 * n :]
    me = Place()
    y, c, z, x = me.y, me.core, me.z, me.x
    m = me.nx
    greet(me.neighbours())
    copies, slot = [], [0]

    def push(src, dst, device):
        copy = remote(src, dst, send.at[slot[0]], recv.at[slot[0]], device)
        slot[0] += 1
        copy.start()
        return copy

    own = [pltpu.make_async_copy(shards[j], outs[j].at[y, c, z, x], local.at[j]) for j in range(n)]
    for copy in own:
        copy.start()
    first = [
        push(shards[j], outs[j].at[y, c, z, x], me.at(z=me.next_z(k))) for j in range(n) for k in range(1, me.nz)
    ]
    for copy in own:
        copy.wait()
    for copy in first:
        copy.wait()
    base = slot[0]

    def rest(by_core):
        slot[0] = base
        shared, started = [], []
        sibling = me.at(core=1 - by_core)
        second = []
        for j in range(n):
            piece = outs[j].at[y, by_core, :, x]
            for k in range(1, m):
                peer = me.at(x=me.next_x(k)) if by_core == 0 else me.at(y=me.next_y(k))
                second.append(push(piece, piece, peer))
            shared.append(push(piece, piece, sibling))
        for copy in second:
            copy.wait()
        third = []
        for j in range(n):
            wide = outs[j].at[y, by_core] if by_core == 0 else outs[j].at[:, by_core, :, x]
            for k in range(1, m):
                peer = me.at(y=me.next_y(k)) if by_core == 0 else me.at(x=me.next_x(k))
                third.append(push(wide, wide, peer))
            for k in range(1, m):
                piece = outs[j].at[y, by_core, :, me.next_x(k)] if by_core == 0 else outs[j].at[me.next_y(k), by_core, :, x]
                shared.append(push(piece, piece, sibling))
        for copy in third:
            copy.wait()
        for j in range(n):
            for k in range(1, m):
                wide = outs[j].at[me.next_y(k), by_core] if by_core == 0 else outs[j].at[:, by_core, :, me.next_x(k)]
                shared.append(push(wide, wide, sibling))
        for copy in shared:
            copy.wait()

    for by_core in (0, 1):
        pl.when(c == by_core)(functools.partial(rest, by_core))


def gather_all(shards):
    ny, nz, nx = grid_sizes()
    n = len(shards)
    count = n * ((nz - 1) + (nx - 1) + 1 + (nx - 1) * 3)
    return pl.pallas_call(
        functools.partial(gather_kernel, n),
        in_specs=[ANY] * n,
        out_specs=[ANY] * n,
        out_shape=[jax.ShapeDtypeStruct((ny, 2, nz, nx) + s.shape, s.dtype) for s in shards],
        scratch_shapes=[pltpu.SemaphoreType.DMA((count,)), pltpu.SemaphoreType.DMA((count,)), pltpu.SemaphoreType.DMA((n,))],
        compiler_params=pltpu.CompilerParams(collective_id=0, has_side_effects=True, vmem_limit_bytes=16 << 20),
        name="gather_all",
    )(*shards)


def add_into(acc, at, terms, rows):
    total = acc[at]
    for ref, index in terms:
        total = total + ref[index]
    acc[at] = total


def scatter_kernel(n, *refs):
    grads, tile_ref = refs[:n], refs[n]
    outs, stat_ref = refs[n + 1 : 2 * n + 1], refs[2 * n + 1]
    acc, r1, r2, r3, r4 = (refs[2 * n + 2 + i * n : 2 * n + 2 + (i + 1) * n] for i in range(5))
    tc, tx, ty, tz, send, recv, local = refs[7 * n + 2 :]
    me = Place()
    y, c, z, x = me.y, me.core, me.z, me.x
    ny, nz, nx, m = me.ny, me.nz, me.nx, me.nx
    greet(me.neighbours())
    slot = [0]

    def push(src, dst, device):
        copy = remote(src, dst, send.at[slot[0]], recv.at[slot[0]], device)
        slot[0] += 1
        copy.start()
        return copy

    stage, own = [], []
    for j in range(n):
        stage.append([push(grads[j].at[:, me.other(), :, k], r1[j].at[:, k], me.at(core=me.other())) for k in range(nx)])
        mine = [
            pltpu.make_async_copy(grads[j].at[:, c, :, k], acc[j].at[:, k], local.at[j * nx + k]) for k in range(nx)
        ]
        for copy in mine:
            copy.start()
        own.append(mine)
    base = slot[0]

    def rest(by_core):
        slot[0] = base
        two, three, four = [], [], []
        for j in range(n):
            for copy in own[j] + stage[j]:
                copy.wait()

            def add1(i, carry):
                at = (lax.div(i, nx * nz), lax.rem(lax.div(i, nz), nx), lax.rem(i, nz))
                add_into(acc[j], at, [(r1[j], at)], None)
                return carry

            lax.fori_loop(0, ny * nx * nz, add1, 0)
            if by_core == 0:
                two.append([push(acc[j].at[:, me.next_x(k)], r2[j].at[k - 1], me.at(x=me.next_x(k))) for k in range(1, m)])
            else:
                two.append([push(acc[j].at[me.next_y(k)], r2[j].at[k - 1], me.at(y=me.next_y(k))) for k in range(1, m)])
        for j in range(n):
            for copy in two[j]:
                copy.wait()

            def add2(i, carry):
                a, b = lax.div(i, nz), lax.rem(i, nz)
                at = (a, x, b) if by_core == 0 else (y, a, b)
                add_into(acc[j], at, [(r2[j], (k, a, b)) for k in range(m - 1)], None)
                return carry

            lax.fori_loop(0, m * nz, add2, 0)
            if by_core == 0:
                three.append([push(acc[j].at[me.next_y(k), x], r3[j].at[k - 1], me.at(y=me.next_y(k))) for k in range(1, m)])
            else:
                three.append([push(acc[j].at[y, me.next_x(k)], r3[j].at[k - 1], me.at(x=me.next_x(k))) for k in range(1, m)])
        for j in range(n):
            for copy in three[j]:
                copy.wait()

            def add3(i, carry):
                add_into(acc[j], (y, x, i), [(r3[j], (k, i)) for k in range(m - 1)], None)
                return carry

            lax.fori_loop(0, nz, add3, 0)
            four.append(
                [push(acc[j].at[y, x, me.next_z(k)], r4[j].at[k - 1], me.at(z=me.next_z(k))) for k in range(1, nz)]
            )
        squares = jnp.zeros((8, HALF), F32)
        for j in range(n):
            for copy in four[j]:
                copy.wait()
            total = acc[j][y, x, z]
            for k in range(nz - 1):
                total = total + r4[j][k]
            outs[j][...] = total
            sq = colsum_any(total * total)
            squares = squares + sq[:, :HALF] + sq[:, HALF:]
        tc[c] = jnp.concatenate([squares, tile_ref[...]], 0)

    for by_core in (0, 1):
        pl.when(c == by_core)(functools.partial(rest, by_core))

    slot[0] = base + n * ((m - 1) * 2 + nz - 1)
    push(tc.at[c], tc.at[c], me.at(core=me.other())).wait()
    tx[x] = tc[0] + tc[1]
    for copy in [push(tx.at[x], tx.at[x], me.at(x=me.next_x(k))) for k in range(1, nx)]:
        copy.wait()
    ty[y] = functools.reduce(jnp.add, [tx[k] for k in range(nx)])
    for copy in [push(ty.at[y], ty.at[y], me.at(y=me.next_y(k))) for k in range(1, ny)]:
        copy.wait()
    tz[z] = functools.reduce(jnp.add, [ty[k] for k in range(ny)])
    for copy in [push(tz.at[z], tz.at[z], me.at(z=me.next_z(k))) for k in range(1, nz)]:
        copy.wait()
    stat_ref[...] = functools.reduce(jnp.add, [tz[k] for k in range(nz)])


def colsum_any(x):
    rows = x.shape[0]
    even = rows // 8 * 8
    out = colsum(x[:even]) if even else jnp.zeros((8, x.shape[1]), F32)
    if rows > even:
        out = out + jnp.pad(x[even:], ((0, 8 - rows + even), (0, 0)))
    return out


def scatter_sum(grads, tile):
    ny, nz, nx = grid_sizes()
    n = len(grads)
    shapes = [g.shape[-2:] for g in grads]
    count = n * nx + n * ((nx - 1) * 2 + nz - 1) + 1 + (nx - 1) + (ny - 1) + (nz - 1)

    def buffers(*lead):
        return [pltpu.VMEM(lead + s, F32) for s in shapes]

    return pl.pallas_call(
        functools.partial(scatter_kernel, n),
        in_specs=[ANY] * n + [INVMEM],
        out_specs=[INVMEM] * (n + 1),
        out_shape=[jax.ShapeDtypeStruct(s, F32) for s in shapes] + [jax.ShapeDtypeStruct((16, HALF), F32)],
        scratch_shapes=buffers(ny, nx, nz)
        + buffers(ny, nx, nz)
        + buffers(nx - 1, nx, nz)
        + buffers(nx - 1, nz)
        + buffers(nz - 1)
        + [pltpu.VMEM((k, 16, HALF), F32) for k in (2, nx, ny, nz)]
        + [pltpu.SemaphoreType.DMA((count,)), pltpu.SemaphoreType.DMA((count,)), pltpu.SemaphoreType.DMA((n * nx,))],
        compiler_params=pltpu.CompilerParams(collective_id=1, has_side_effects=True, vmem_limit_bytes=VMEM_LIMIT),
        name="scatter_sum",
    )(*grads, tile)


def group_kernel(stats, per, in_ref, out_ref, got, result, send, recv, local):
    nf = lax.axis_size("fsdp")
    dp, f = lax.axis_index("dp"), lax.axis_index("fsdp")
    peers = [lax.rem(f + k, nf) for k in range(1, nf)]
    greet([(dp, p) for p in peers])

    def part(ref, who):
        return ref.at[pl.ds(pl.multiple_of(who * per, per), per)]

    own = pltpu.make_async_copy(part(in_ref, f), got.at[f], local)
    own.start()
    copies = [
        remote(part(in_ref, p), got.at[f], send.at[k], recv.at[k], (dp, p)) for k, p in enumerate(peers)
    ]
    for copy in copies:
        copy.start()
    own.wait()
    for copy in copies:
        copy.wait()
    if stats:
        row = lax.broadcasted_iota(jnp.int32, (PACK, HALF), 0)
        lane = lax.broadcasted_iota(jnp.int32, (PACK, HALF), 1)
        router = jnp.where(row < ROUT, row, row - ROUT)
        pick = (lane // 8 == router) & (row < 2 * ROUT)
        src = lax.broadcasted_iota(jnp.int32, (HALF, D), 0)
        dst = lax.broadcasted_iota(jnp.int32, (HALF, D), 1)
        widen = jnp.where(src % 8 == dst // 32, 1.0, 0.0).astype(BF)

        def one(s, carry):
            lse = [got[d, s, 2 * ROUT : 2 * ROUT + 1, :] for d in range(nf)]
            top = functools.reduce(jnp.maximum, lse)
            total = top + jnp.log(functools.reduce(jnp.add, [jnp.exp(l - top) for l in lse]))
            out = jnp.where(row == 2 * ROUT, total, 0.0)
            share = jnp.concatenate([jnp.where(pick, jnp.exp(l - total), 0.0) for l in lse], 0)
            wide = mmw(split2(share), widen)
            for d in range(nf):
                w = wide[d * PACK : (d + 1) * PACK]
                w = jnp.where(row < ROUT, w[:, :HALF], w[:, HALF:])
                out = out + jnp.where(row < 2 * ROUT, w * got[d, s], 0.0)
            result[s] = out
            return carry

        lax.fori_loop(0, per, one, 0)
    else:
        result[...] = functools.reduce(jnp.add, [got[d] for d in range(nf)])
    own = pltpu.make_async_copy(result, part(out_ref, f), local)
    own.start()
    copies = [
        remote(result, part(out_ref, f), send.at[nf - 1 + k], recv.at[nf - 1 + k], (dp, p)) for k, p in enumerate(peers)
    ]
    for copy in copies:
        copy.start()
    own.wait()
    for copy in copies:
        copy.wait()


def group_combine(packed, stats, cid):
    nf = lax.axis_size("fsdp")
    per = packed.shape[0] // nf
    return pl.pallas_call(
        functools.partial(group_kernel, stats, per),
        in_specs=[INVMEM],
        out_specs=INVMEM,
        out_shape=jax.ShapeDtypeStruct(packed.shape, F32),
        scratch_shapes=[
            pltpu.VMEM((nf, per, PACK, HALF), F32),
            pltpu.VMEM((per, PACK, HALF), F32),
            pltpu.SemaphoreType.DMA((2 * nf - 2,)),
            pltpu.SemaphoreType.DMA((2 * nf - 2,)),
            pltpu.SemaphoreType.DMA,
        ],
        compiler_params=pltpu.CompilerParams(collective_id=cid, has_side_effects=True, vmem_limit_bytes=32 << 20),
        name="group_stats" if stats else "group_sum",
    )(packed)


def series_stats(series, observed):
    seen = observed.astype(F32)
    counted = jnp.maximum(jnp.sum(seen, -1, keepdims=True), 1.0)
    mean = jnp.sum(seen * series, -1, keepdims=True) / counted
    center = (series - mean) * seen
    scale = jnp.sqrt(jnp.sum(center * center, -1, keepdims=True) / counted + norm_eps)
    return center / scale, mean, scale


def adam_update(weight, first_moment, second_moment, gradient):
    first_new = beta_one * first_moment + (1.0 - beta_one) * gradient
    second_new = beta_two * second_moment + (1.0 - beta_two) * gradient * gradient
    corrected = (
        first_new
        / (1.0 - beta_one**step_count)
        / (jnp.sqrt(second_new / (1.0 - beta_two**step_count)) + adam_eps)
    )
    return (weight - learn_rate * (corrected + weight_decay * weight), first_new, second_new)


def segment_major(x, width):
    nv = x.shape[0]
    x = x.reshape(nv, -1, 12).transpose(1, 0, 2)
    return jnp.pad(x, ((0, 0), (0, 0), (0, width - 12)))


def pad_rows(x, rows):
    return jnp.pad(x, ((0, rows - x.shape[0]), (0, 0)))


def gradient_parts(series, observed, targets, target_mask, present, square, up, down, vectors, combine, nf):
    nv = series.shape[0]
    normed, mean, scale = series_stats(series, observed)
    pieces = segment_major(normed, 16)
    factor = 2.0 / (1 << 20)
    kept = segment_major(target_mask.astype(F32) * present[:, None] * factor, PPAD)
    tgt = segment_major(targets, PPAD)
    scale16 = jnp.broadcast_to(scale, (nv, PPAD))
    mean16 = jnp.broadcast_to(mean, (nv, PPAD))
    here = jnp.broadcast_to(present[:, None], (nv, HALF))

    emb = pad_rows(vectors[:12], 16).astype(BF)
    place = (vectors[12:13] + vectors[13:73])[:, None, :]
    layer_start = SEGLEN + 1 + SEG
    vecs = [pad_rows(vectors[layer_start + 23 * l : layer_start + 23 * l + 23], 24) for l in range(2)]
    merge_at = layer_start + 46
    mvec = pad_rows(vectors[merge_at : merge_at + 5], 8)
    mw = square[24:26].reshape(2 * D, D)
    head = pad_rows(vectors[merge_at + 5 : merge_at + 17], PPAD).astype(BF)
    router_at = merge_at + 17
    routers = []
    for l, n in ((0, SEG), (1, SEG // 2)):
        r = vectors[router_at + l * SEG * ROUT : router_at + l * SEG * ROUT + n * ROUT].reshape(n, ROUT, D)
        routers.append(jnp.pad(r, ((0, 0), (0, RPAD - ROUT), (0, 0))))
    time_w = [
        (*[square[12 * l + i] for i in (0, 1, 2, 3)], up[2 * l], down[2 * l], vecs[l]) for l in range(2)
    ]
    send_w = [(*[square[12 * l + i] for i in (4, 5, 6)], vecs[l]) for l in range(2)]
    recv_w = [
        (*[square[12 * l + i] for i in (7, 9, 10, 8, 11)], up[2 * l + 1], down[2 * l + 1], vecs[l]) for l in range(2)
    ]

    sb0, sb1 = 4, 6
    dim0 = time_fwd(True, pieces, (emb, place), time_w[0], SEG)
    o0 = send_fwd(dim0, routers[0], here, send_w[0], sb0, -(-SEG // nf) * nf)
    o0 = combine(o0, True, 2)
    x1 = recv_fwd(dim0, o0, recv_w[0], mvec, mw, sb0)
    dim1 = time_fwd(False, x1, (), time_w[1], SEG // 2)
    o1 = send_fwd(dim1, routers[1], here, send_w[1], sb1, -(-SEG // 2 // nf) * nf)
    o1 = combine(o1, True, 3)
    out = tail(dim1, o1, tgt, kept, scale16, mean16, recv_w[1], head, sb1)
    ddim1, do1, grecv1, dhead = out[0], out[1], out[2:10], out[10]
    do1 = combine(do1, False, 4)
    out = send_bwd(dim1, ddim1, routers[1], o1, do1, here, send_w[1], sb1)
    ddim1, dr1, gsend1 = out[0], out[1], out[2:]
    out = time_bwd(False, x1, (), ddim1, time_w[1], SEG // 2)
    gtime1, dx1 = out[:7], out[7]
    out = recv_bwd(dim0, o0, dx1, recv_w[0], mvec, mw, sb0)
    ddim0, do0, grecv0, dmw, dmv = out[0], out[1], out[2:10], out[10], out[11]
    do0 = combine(do0, False, 5)
    out = send_bwd(dim0, ddim0, routers[0], o0, do0, here, send_w[0], sb0)
    ddim0, dr0, gsend0 = out[0], out[1], out[2:]
    out = time_bwd(True, pieces, (emb, place), ddim0, time_w[0], SEG)
    gtime0, demb, dplace = out[:7], out[7], out[8]

    mats, ups, downs, rows = [], [], [], []
    for gt, gs, gr in ((gtime0, gsend0, grecv0), (gtime1, gsend1, grecv1)):
        mats += [gt[0], gt[1], gt[2], gt[3], gs[0], gs[1], gs[2], gr[0], gr[3], gr[1], gr[2], gr[4]]
        ups += [gt[4], gr[5]]
        downs += [gt[5], gr[6]]
        rt, rs, rr = gt[6].sum(1), gs[3].sum(1), gr[7].sum(1)
        rows += [rt, rs, rr]
    mats += [dmw]
    dplace = dplace.reshape(SEG, VB, D).sum(1)
    vec = jnp.concatenate(
        [demb[:12], dplace.sum(0, keepdims=True), dplace]
        + rows
        + [dmv.sum(1), dhead[:12]]
        + [dr[:, :ROUT].reshape(-1, D) for dr in (dr0, dr1)],
        0,
    )
    return jnp.concatenate(mats, 0), jnp.concatenate(ups, 0), jnp.concatenate(downs, 0), vec


def on_device(series, observed, targets, target_mask, counts, matrices, feed_weights, vectors, matrices_first, matrices_second, feed_first, feed_second, vectors_first, vectors_second):
    local_vars = series.shape[1]
    nf = lax.axis_size("fsdp")
    devices = nf * lax.axis_size("dp")
    slot = lax.axis_index("fsdp") * local_vars + jnp.arange(local_vars, dtype=jnp.int32)
    present = (slot < counts[0]).astype(F32)
    own_rows = NVEC * D // devices
    vec_rows = -(-own_rows // D)

    def as_rows(x):
        return x.reshape(-1, D)

    def pad_flat(x):
        return jnp.pad(x, [(0, 0)] * (x.ndim - 1) + [(0, vec_rows * D - own_rows)])

    square, feed, vecs = gather_all(
        [as_rows(matrices.astype(BF)), as_rows(feed_weights.astype(BF)), as_rows(pad_flat(vectors.astype(BF)))]
    )
    square = square.reshape(NSQ, D, D)
    feed = feed.reshape(-1, D)
    up = feed[: 4 * FF].reshape(4, D, FF)
    down = feed[4 * FF :].reshape(4, FF, D)
    vecs = vecs.reshape(devices, -1)[:, :own_rows].reshape(NVEC, D).astype(F32)
    g_mat, g_up, g_down, g_vec = gradient_parts(
        series[0], observed[0], targets[0], target_mask[0], present, square, up, down, vecs, group_combine, nf
    )
    g_feed = jnp.concatenate([g_up.reshape(-1, D), g_down], 0)
    g_vec = pad_flat(g_vec.reshape(devices, own_rows))
    ny, nz, nx = grid_sizes()
    lead = (ny, 2, nz, nx)
    kept = target_mask[0].astype(F32) * present[:, None]
    tile = jnp.pad(jnp.sum(kept).reshape(1, 1), ((0, 7), (0, HALF - 1)))
    s_mat, s_feed, s_vec, sums = scatter_sum(
        [g_mat.reshape(lead + (-1, D)), g_feed.reshape(lead + (-1, D)), g_vec.reshape(lead + (-1, D))], tile
    )
    shards = (s_mat.reshape(-1), s_feed.reshape(-1), s_vec.reshape(-1)[:own_rows])
    upscale = (1 << 20) / jnp.maximum(jnp.sum(sums[8:]), 1.0)
    grad_norm = jnp.sqrt(jnp.sum(sums[:8])) * upscale
    factor = upscale * (clip_norm / jnp.maximum(grad_norm, clip_norm))
    new = (
        adam_update(matrices, matrices_first, matrices_second, shards[0] * factor)
        + adam_update(feed_weights, feed_first, feed_second, shards[1] * factor)
        + adam_update(vectors, vectors_first, vectors_second, shards[2] * factor)
    )
    return (grad_norm,) + new


def solution(mesh):
    both = P(("dp", "fsdp"))
    data = P("dp", "fsdp", None)
    return jax.shard_map(
        on_device,
        mesh=mesh,
        in_specs=(data,) * 4 + (P("dp"),) + (both,) * 9,
        out_specs=(P(),) + (both,) * 9,
        check_vma=False,
    )
```

```python
import functools
import jax
import jax.numpy as jnp
from jax import lax
from jax.experimental import pallas as pl
from jax.experimental.pallas import tpu as pltpu
from jax.sharding import PartitionSpec as P

D = 256
HEADS = 8
FF = 512
ROUT = 10
RPAD = 16
SEGLEN = 12
PRED = 12
PPAD = 16
SEG = 60
NSQ = 26
NVEC = 1036
HALF = 128
VB = 8
UNROLL = 4
UNROLL_BACK = 4

BF = jnp.bfloat16
F32 = jnp.float32
SCALE = (D // HEADS) ** (-0.5)
negative = -1e30
norm_eps = 1e-05
beta_one = 0.9
beta_two = 0.999
adam_eps = 1e-08
weight_decay = 0.01
learn_rate = 0.2
clip_norm = 0.01
step_count = 10.0
VMEM_LIMIT = 60 << 20


def split2(x):
    hi = x.astype(BF)
    return hi, (x - hi.astype(F32)).astype(BF)


def dots(a, b, ca, cb):
    return lax.dot_general(a, b, (((ca,), (cb,)), ((), ())), preferred_element_type=F32)


def mmw(x2, w):
    return dots(x2[0], w, 1, 0) + dots(x2[1], w, 1, 0)


def mmwt(x2, w):
    return dots(x2[0], w, 1, 1) + dots(x2[1], w, 1, 1)


def rows2(a2):
    return jnp.concatenate([a2[0], a2[1]], 0)


def nn3(a2, b2):
    m = a2[0].shape[0]
    both = dots(rows2(a2), b2[0], 1, 0)
    return both[:m] + both[m:] + dots(a2[0], b2[1], 1, 0)


def nt3(a2, b2):
    m = a2[0].shape[0]
    both = dots(rows2(a2), b2[0], 1, 1)
    return both[:m] + both[m:] + dots(a2[0], b2[1], 1, 1)


def tn3(a2, b2):
    n = b2[0].shape[1]
    both = dots(a2[0], jnp.concatenate([b2[0], b2[1]], 1), 0, 0)
    return both[:, :n] + both[:, n:] + dots(a2[1], b2[0], 0, 0)


def norm_fwd(z, gain, bias):
    center = z - jnp.mean(z, -1, keepdims=True)
    inv = lax.rsqrt(jnp.mean(center * center, -1, keepdims=True) + norm_eps)
    unit = center * inv
    return unit * gain + bias, unit, inv


def norm_bwd(dy, unit, inv, gain):
    t = dy * gain
    return inv * (t - jnp.mean(t, -1, keepdims=True) - unit * jnp.mean(t * unit, -1, keepdims=True))


def colsum(x):
    return jnp.sum(x.reshape(x.shape[0] // 8, 8, x.shape[1]), 0)


def gelu_cdf(u):
    return 0.5 + 0.5 * lax.erf(u * 0.7071067811865476)


def gelu_slope(u, cdf):
    return cdf + u * (jnp.exp(-0.5 * u * u) * 0.3989422804014327)


def halves(x):
    return x[:, :HALF], x[:, HALF:]


def lane_head(rows):
    return lax.broadcasted_iota(jnp.int32, (rows, HALF), 1) // 32


def spread_heads(x, zero):
    head = lane_head(x.shape[0])
    return jnp.concatenate([jnp.where(head == h, x, zero) for h in range(4)], 0)


def gather_heads(x, group):
    head = lane_head(group)
    out = x[3 * group :]
    for h in range(3):
        out = jnp.where(head == h, x[h * group : (h + 1) * group], out)
    return out


def ones_heads(group, count):
    row = lax.broadcasted_iota(jnp.int32, (4 * group, HALF), 0)
    lane = lax.broadcasted_iota(jnp.int32, (4 * group, HALF), 1)
    return jnp.where((row // group == lane // 32) & (row % group < count), 1.0, 0.0).astype(BF)


def group_max(s, group, count):
    lane = lax.broadcasted_iota(jnp.int32, (s.shape[0], HALF), 1)
    outs = []
    for t in range(s.shape[1] // HALF):
        part = s[:, t * HALF : (t + 1) * HALF]
        top = None
        for g in range(HALF // group):
            here = (lane // group == g)
            best = jnp.max(jnp.where((lane // group == g) & (lane % group < count), part, negative), -1, keepdims=True)
            top = jnp.broadcast_to(best, part.shape) if top is None else jnp.where(here, best, top)
        outs.append(jnp.where(lane % group < count, part - top, negative))
    return jnp.concatenate(outs, 1)


def time_parts(units, group, ref):
    return [split2(ref[c, pl.ds(v, group, stride=VB), :]) for c, v in units]


def spread2(x2):
    zero = jnp.zeros((), BF)
    return spread_heads(x2[0], zero), spread_heads(x2[1], zero)


def time_attend(units, group, count, q_s, k_s, v_s, o_s, p_s, l_s):
    q = time_parts(units, group, q_s)
    k = [spread2(x2) for x2 in time_parts(units, group, k_s)]
    scores = [
        dots(jnp.concatenate(q2, 1), jnp.concatenate([k2[0], k2[0]], 1), 1, 1) + dots(q2[0], k2[1], 1, 1)
        for q2, k2 in zip(q, k)
    ]
    probs = [jnp.exp(group_max(s, group, count)) for s in scores]
    probs2 = [split2(p) for p in probs]
    w = [spread2(x2) for x2 in time_parts(units, group, v_s)]
    ones = ones_heads(group, count)
    both = [dots(rows2(p2), jnp.concatenate([w2[0], ones], 1), 1, 0) for p2, w2 in zip(probs2, w)]
    both = [b[:group] + b[group:] for b in both]
    mixed = [(b[:, :HALF] + dots(p2[0], w2[1], 1, 0)) / b[:, HALF:] for b, p2, w2 in zip(both, probs2, w)]
    for (c, v), o, p, b in zip(units, mixed, probs, both):
        o_s[c, pl.ds(v, group, stride=VB), :] = o
        if p_s is not None:
            p_s[c, v] = p
            l_s[c, v] = b[:, HALF:]


def time_attend_back(units, group, count, q_s, k_s, v_s, o_s, p_s, l_s, do_s):
    d = [do_s[c, pl.ds(v, group, stride=VB), :] / l_s[c, v] for c, v in units]
    e2 = [split2(x * o_s[c, pl.ds(v, group, stride=VB), :]) for x, (c, v) in zip(d, units)]
    d2 = [split2(x) for x in d]
    w = [spread2(x2) for x2 in time_parts(units, group, v_s)]
    ones = -ones_heads(group, count)
    both = [
        dots(
            jnp.concatenate([jnp.concatenate([a[0], b[0]], 1), jnp.concatenate([a[1], b[1]], 1)], 0),
            jnp.concatenate([w2[0], ones], 1),
            1,
            1,
        )
        for a, b, w2 in zip(d2, e2, w)
    ]
    dp = [b[:group] + b[group:] + dots(a[0], w2[1], 1, 1) for b, a, w2 in zip(both, d2, w)]
    probs = [p_s[c, v] for c, v in units]
    s2 = [split2(p * x) for p, x in zip(probs, dp)]
    p2 = [split2(p) for p in probs]
    k = [spread2(x2) for x2 in time_parts(units, group, k_s)]
    both = [dots(rows2(a), k2[0], 1, 0) for a, k2 in zip(s2, k)]
    dq = [b[:group] + b[group:] + dots(a[0], k2[1], 1, 0) for b, a, k2 in zip(both, s2, k)]
    q = time_parts(units, group, q_s)
    dk = [gather_heads(tn3(a, q2), group) for a, q2 in zip(s2, q)]
    dv = [gather_heads(tn3(a, x), group) for a, x in zip(p2, d2)]
    for (c, v), x, y, z in zip(units, dq, dk, dv):
        at = pl.ds(v, group, stride=VB)
        q_s[c, at, :] = x
        k_s[c, at, :] = y
        v_s[c, at, :] = z


def store_halves(ref, x):
    rows = x.shape[0]
    ref[0, :rows, :] = x[:, :HALF]
    ref[1, :rows, :] = x[:, HALF:]


def load_halves(ref, rows):
    return jnp.concatenate([ref[0, :rows, :], ref[1, :rows, :]], 1)


def zero_tail(ref, rows):
    tail = ref.shape[1] - rows
    ref[:, rows:, :] = jnp.zeros((2, tail, HALF), F32)


def time_forward(x, w, vec, count, group, q_s, k_s, v_s, o_s, p_s=None, l_s=None):
    rows = count * VB
    x2 = split2(x)
    store_halves(q_s, (mmw(x2, w["q"]) + vec[0:1]) * SCALE)
    store_halves(k_s, mmw(x2, w["k"]))
    store_halves(v_s, mmw(x2, w["v"]) + vec[1:2])
    for ref in (q_s, k_s, v_s):
        zero_tail(ref, rows)

    def some(i, carry):
        units = [(c, i * UNROLL + k) for k in range(UNROLL) for c in range(2)]
        time_attend(units, group, count, q_s, k_s, v_s, o_s, p_s, l_s)
        return carry

    lax.fori_loop(0, VB // UNROLL, some, 0)
    mixed = load_halves(o_s, rows)
    h, unit1, inv1 = norm_fwd(x + mmw(split2(mixed), w["o"]) + vec[2:3], vec[3:4], vec[4:5])
    bias_up = jnp.concatenate([vec[5:6], vec[6:7]], 1)
    u = mmw(split2(h), w["up"]) + bias_up
    cdf = gelu_cdf(u)
    z2 = h + mmw(split2(u * cdf), w["down"]) + vec[7:8]
    y, unit2, inv2 = norm_fwd(z2, vec[8:9], vec[9:10])
    return y, (x2, mixed, h, unit1, inv1, u, cdf, unit2, inv2)


def embed_block(pieces, emb, place):
    return mmw(split2(pieces), emb) + place


TIME_W = ("q", "k", "v", "o", "up", "down")


def time_fwd_kernel(first, count, group, *refs):
    if first:
        x_ref, emb_ref, place_ref = refs[:3]
        refs = refs[3:]
    else:
        x_ref = refs[0]
        refs = refs[1:]
    w = {name: refs[i][...] for i, name in enumerate(TIME_W)}
    vec_ref, y_ref, q_s, k_s, v_s, o_s = refs[6:]
    rows = count * VB
    if first:
        place = jnp.broadcast_to(place_ref[...], (count, VB, D)).reshape(rows, D)
        x = embed_block(x_ref[...].reshape(rows, 16), emb_ref[...], place)
    else:
        x = x_ref[...].reshape(rows, D)
    y, _ = time_forward(x, w, vec_ref[...], count, group, q_s, k_s, v_s, o_s)
    y_ref[...] = y.reshape(count, VB, D)


def whole(shape):
    return pl.BlockSpec(shape, lambda i: (0,) * len(shape))


def params_spec():
    return pltpu.CompilerParams(vmem_limit_bytes=VMEM_LIMIT)


def time_weight_specs():
    return [whole((D, D))] * 4 + [whole((D, FF)), whole((FF, D)), whole((24, D))]


def time_fwd(first, x, extra, weights, count):
    group = 64 if count > 32 else 32
    nv = x.shape[1]
    width = x.shape[2]
    specs = [pl.BlockSpec((count, VB, width), lambda i: (0, i, 0))]
    if first:
        specs += [whole((16, D)), whole((count, 1, D))]
    pad = group * VB
    return pl.pallas_call(
        functools.partial(time_fwd_kernel, first, count, group),
        grid=(nv // VB,),
        in_specs=specs + time_weight_specs(),
        out_specs=pl.BlockSpec((count, VB, D), lambda i: (0, i, 0)),
        out_shape=jax.ShapeDtypeStruct((count, nv, D), F32),
        scratch_shapes=[pltpu.VMEM((2, pad, HALF), F32)] * 4,
        compiler_params=params_spec(),
        name="time_fwd",
    )(x, *extra, *weights)


def time_bwd_kernel(first, count, group, *refs):
    if first:
        x_ref, emb_ref, place_ref = refs[:3]
        refs = refs[3:]
    else:
        x_ref = refs[0]
        refs = refs[1:]
    dy_ref = refs[0]
    w = {name: refs[1 + i][...] for i, name in enumerate(TIME_W)}
    vec_ref = refs[7]
    outs = refs[8:]
    n_out = 9 if first else 8
    g = dict(zip(TIME_W + ("rows",), outs[:7]))
    tail = outs[7:n_out]
    q_s, k_s, v_s, o_s, do_s, p_s, l_s = outs[n_out:]
    rows = count * VB
    step = pl.program_id(0)

    @pl.when(step == 0)
    def _():
        for ref in list(g.values()) + (list(tail) if first else []):
            ref[...] = jnp.zeros(ref.shape, F32)

    vec = vec_ref[...]
    if first:
        place = jnp.broadcast_to(place_ref[...], (count, VB, D)).reshape(rows, D)
        pieces = x_ref[...].reshape(rows, 16)
        x = embed_block(pieces, emb_ref[...], place)
    else:
        x = x_ref[...].reshape(rows, D)
    _, (x2, mixed, h, unit1, inv1, u, cdf, unit2, inv2) = time_forward(
        x, w, vec, count, group, q_s, k_s, v_s, o_s, p_s, l_s
    )
    dy = dy_ref[...].reshape(rows, D)
    g["rows"][8] += colsum(dy * unit2)
    g["rows"][9] += colsum(dy)
    dz2 = norm_bwd(dy, unit2, inv2, vec[8:9])
    g["rows"][7] += colsum(dz2)
    dz22 = split2(dz2)
    g["down"][...] += tn3(split2(u * cdf), dz22)
    du = mmwt(dz22, w["down"]) * gelu_slope(u, cdf)
    g["rows"][5] += colsum(du[:, :D])
    g["rows"][6] += colsum(du[:, D:])
    du2 = split2(du)
    g["up"][...] += tn3(split2(h), du2)
    dh = dz2 + mmwt(du2, w["up"])
    g["rows"][3] += colsum(dh * unit1)
    g["rows"][4] += colsum(dh)
    dz1 = norm_bwd(dh, unit1, inv1, vec[3:4])
    g["rows"][2] += colsum(dz1)
    dz12 = split2(dz1)
    g["o"][...] += tn3(split2(mixed), dz12)
    store_halves(do_s, mmwt(dz12, w["o"]))
    zero_tail(do_s, rows)

    def some(i, carry):
        units = [(c, i * UNROLL_BACK + k) for k in range(UNROLL_BACK) for c in range(2)]
        time_attend_back(units, group, count, q_s, k_s, v_s, o_s, p_s, l_s, do_s)
        return carry

    lax.fori_loop(0, VB // UNROLL_BACK, some, 0)
    dq = load_halves(q_s, rows) * SCALE
    g["rows"][0] += colsum(dq)
    dq2 = split2(dq)
    g["q"][...] += tn3(x2, dq2)
    dx = dz1 + mmwt(dq2, w["q"])
    dk2 = split2(load_halves(k_s, rows))
    g["k"][...] += tn3(x2, dk2)
    dx = dx + mmwt(dk2, w["k"])
    dv = load_halves(v_s, rows)
    g["rows"][1] += colsum(dv)
    dv2 = split2(dv)
    g["v"][...] += tn3(x2, dv2)
    dx = dx + mmwt(dv2, w["v"])
    if first:
        tail[0][...] += tn3(split2(pieces), split2(dx))
        tail[1][...] += dx
    else:
        tail[0][...] = dx.reshape(count, VB, D)


def time_bwd(first, x, extra, dy, weights, count):
    group = 64 if count > 32 else 32
    nv = x.shape[1]
    width = x.shape[2]
    pad = group * VB
    block = pl.BlockSpec((count, VB, D), lambda i: (0, i, 0))
    specs = [pl.BlockSpec((count, VB, width), lambda i: (0, i, 0))]
    if first:
        specs += [whole((16, D)), whole((count, 1, D))]
    grad_shapes = [(D, D)] * 4 + [(D, FF), (FF, D), (10, 8, D)]
    if first:
        grad_shapes += [(16, D), (count * VB, D)]
    out_specs = [whole(s) for s in grad_shapes]
    out_shape = [jax.ShapeDtypeStruct(s, F32) for s in grad_shapes]
    if not first:
        out_specs.append(block)
        out_shape.append(jax.ShapeDtypeStruct((count, nv, D), F32))
    return pl.pallas_call(
        functools.partial(time_bwd_kernel, first, count, group),
        grid=(nv // VB,),
        in_specs=specs + [block] + time_weight_specs(),
        out_specs=out_specs,
        out_shape=out_shape,
        scratch_shapes=[pltpu.VMEM((2, pad, HALF), F32)] * 5
        + [pltpu.VMEM((2, VB, group, 4 * group), F32), pltpu.VMEM((2, VB, group, HALF), F32)],
        compiler_params=params_spec(),
        name="time_bwd",
    )(x, *extra, dy, *weights)

SB_ROWS = 64


def head_rows():
    sub = lax.broadcasted_iota(jnp.int32, (8, D), 0)
    lane = lax.broadcasted_iota(jnp.int32, (8, D), 1)
    return jnp.where(sub == lane // 32, 1.0, 0.0).astype(F32)


def spread_rows(x):
    wide = jnp.broadcast_to(x[:, None, :], (RPAD, HEADS, D)) * head_rows()[None]
    return wide.reshape(RPAD * HEADS, D)


def gather_rows(x):
    return jnp.sum(x.reshape(RPAD, HEADS, D) * head_rows()[None], 1)


PACK = 24


def pack_rows(x, last=None):
    last = jnp.zeros((1, HALF), F32) if last is None else last
    return jnp.concatenate([x[:ROUT, :HALF], x[:ROUT, HALF:], last, jnp.zeros((PACK - 2 * ROUT - 1, HALF), F32)], 0)


def unpack_rows(x):
    x = jnp.concatenate([x[:ROUT], x[ROUT : 2 * ROUT]], 1)
    return jnp.concatenate([x, jnp.zeros((RPAD - ROUT, D), F32)], 0)


def unpack_block(ref, sb):
    return jnp.concatenate([unpack_rows(ref[s]) for s in range(sb)], 0)


def pack_block(ref, x, sb):
    for s in range(sb):
        ref[s] = pack_rows(x[s * RPAD : (s + 1) * RPAD])


def valid_lane(rows):
    return lax.broadcasted_iota(jnp.int32, (rows, HALF), 1) < ROUT * HEADS


def router_reduce(x, op):
    for shift in (8, 16, 32, 64):
        x = op(x, pltpu.roll(x, shift, 1))
    return x


def merge_rows(y, pairs, vec):
    wide = y.reshape(pairs, 2, SB_ROWS, D)
    wide = jnp.concatenate([wide[:, 0].reshape(pairs * SB_ROWS, D), wide[:, 1].reshape(pairs * SB_ROWS, D)], 1)
    gain = jnp.concatenate([vec[0:1], vec[1:2]], 1)
    bias = jnp.concatenate([vec[2:3], vec[3:4]], 1)
    return norm_fwd(wide, gain, bias) + (gain,)


RECV_W = ("so", "rk", "rv", "rq", "ro", "up", "down")


def recv_forward(send, o_rows, w, vec):
    sb = send.shape[0] // SB_ROWS
    send2 = split2(send)
    o2 = split2(o_rows)
    buf = mmw(o2, w["so"]) + vec[12:13]
    buf2 = split2(buf)
    kb = mmw(buf2, w["rk"])
    vb = mmw(buf2, w["rv"]) + vec[14:15]
    q = (mmw(send2, w["rq"]) + vec[13:14]) * SCALE

    segs = range(sb)
    k = [split2(spread_rows(kb[s * RPAD : (s + 1) * RPAD])) for s in segs]
    v = [split2(spread_rows(vb[s * RPAD : (s + 1) * RPAD])) for s in segs]
    ok = valid_lane(SB_ROWS)
    scores = [jnp.where(ok, nt3(split2(q[s * SB_ROWS : (s + 1) * SB_ROWS]), k[s]), negative) for s in segs]
    probs = [jnp.exp(sc - router_reduce(sc, jnp.maximum)) for sc in scores]
    probs = [p / router_reduce(p, jnp.add) for p in probs]
    mixed = jnp.concatenate([nn3(split2(p), v2) for p, v2 in zip(probs, v)], 0)
    g, unit3, inv3 = norm_fwd(send + mmw(split2(mixed), w["ro"]) + vec[15:16], vec[16:17], vec[17:18])
    u = mmw(split2(g), w["up"]) + jnp.concatenate([vec[18:19], vec[19:20]], 1)
    cdf = gelu_cdf(u)
    y, unit4, inv4 = norm_fwd(g + mmw(split2(u * cdf), w["down"]) + vec[20:21], vec[21:22], vec[22:23])
    return y, (send2, o2, buf2, mixed, g, unit3, inv3, u, cdf, unit4, inv4, q, k, v, probs)


RECV_G = RECV_W + ("rows",)


def recv_backward(dy, kept, w, vec, g):
    send2, o2, buf2, mixed, gg, unit3, inv3, u, cdf, unit4, inv4, q, k, v, probs = kept
    sb = dy.shape[0] // SB_ROWS
    rows = g["rows"]
    rows[9] += colsum(dy * unit4)
    rows[10] += colsum(dy)
    dz4 = norm_bwd(dy, unit4, inv4, vec[21:22])
    rows[8] += colsum(dz4)
    dz42 = split2(dz4)
    g["down"][...] += tn3(split2(u * cdf), dz42)
    du = mmwt(dz42, w["down"]) * gelu_slope(u, cdf)
    rows[6] += colsum(du[:, :D])
    rows[7] += colsum(du[:, D:])
    du2 = split2(du)
    g["up"][...] += tn3(split2(gg), du2)
    dg = dz4 + mmwt(du2, w["up"])
    rows[4] += colsum(dg * unit3)
    rows[5] += colsum(dg)
    dz3 = norm_bwd(dg, unit3, inv3, vec[16:17])
    rows[3] += colsum(dz3)
    dz32 = split2(dz3)
    g["ro"][...] += tn3(split2(mixed), dz32)
    do = mmwt(dz32, w["ro"])
    segs = range(sb)
    d = [split2(do[s * SB_ROWS : (s + 1) * SB_ROWS]) for s in segs]
    dp = [nt3(d2, v2) for d2, v2 in zip(d, v)]
    ds = [split2(p * (x - router_reduce(p * x, jnp.add))) for p, x in zip(probs, dp)]
    dq = jnp.concatenate([nn3(s2, k2) for s2, k2 in zip(ds, k)], 0) * SCALE
    q = [split2(q[s * SB_ROWS : (s + 1) * SB_ROWS]) for s in segs]
    dk = jnp.concatenate([gather_rows(tn3(s2, q2)) for s2, q2 in zip(ds, q)], 0)
    dv = jnp.concatenate([gather_rows(tn3(split2(p), d2)) for p, d2 in zip(probs, d)], 0)
    rows[1] += colsum(dq)
    dq2 = split2(dq)
    g["rq"][...] += tn3(send2, dq2)
    dsend = dz3 + mmwt(dq2, w["rq"])
    dk2 = split2(dk)
    dv2 = split2(dv)
    rows[2] += colsum(dv)
    g["rk"][...] += tn3(buf2, dk2)
    g["rv"][...] += tn3(buf2, dv2)
    dbuf = mmwt(dk2, w["rk"]) + mmwt(dv2, w["rv"])
    rows[0] += colsum(dbuf)
    dbuf2 = split2(dbuf)
    g["so"][...] += tn3(o2, dbuf2)
    return dsend, mmwt(dbuf2, w["so"])


def recv_weight_specs():
    return [whole((D, D))] * 5 + [whole((D, FF)), whole((FF, D)), whole((24, D))]


def seg_block(sb, rows=SB_ROWS, width=D):
    return pl.BlockSpec((sb, rows, width), lambda i: (i, 0, 0))


def pack_spec(sb):
    return seg_block(sb, PACK, HALF)


def recv_fwd_kernel(sb, send_ref, o_ref, *refs):
    w = {n: refs[i][...] for i, n in enumerate(RECV_W)}
    vec_ref, mvec_ref, mw_ref, out_ref = refs[7:11]
    y, _ = recv_forward(
        send_ref[...].reshape(sb * SB_ROWS, D), unpack_block(o_ref, sb), w, vec_ref[...]
    )
    mvec = mvec_ref[...]
    wide, _, _, _ = merge_rows(y, sb // 2, mvec)
    out_ref[...] = (mmw(split2(wide), mw_ref[...]) + mvec[4:5]).reshape(sb // 2, SB_ROWS, D)


def recv_fwd(send, o, weights, mvec, mw, sb):
    n = send.shape[0]
    return pl.pallas_call(
        functools.partial(recv_fwd_kernel, sb),
        grid=(n // sb,),
        in_specs=[seg_block(sb), pack_spec(sb)] + recv_weight_specs() + [whole((8, D)), whole((2 * D, D))],
        out_specs=seg_block(sb // 2),
        out_shape=jax.ShapeDtypeStruct((n // 2, SB_ROWS, D), F32),
        compiler_params=params_spec(),
        name="recv_fwd",
    )(send, o, *weights, mvec, mw)


def recv_bwd_kernel(sb, send_ref, o_ref, dx_ref, *refs):
    w = {n: refs[i][...] for i, n in enumerate(RECV_W)}
    vec_ref, mvec_ref, mw_ref, dsend_ref, do_ref = refs[7:12]
    g = dict(zip(RECV_G, refs[12:20]))
    dmw_ref, dmv_ref = refs[20:22]

    @pl.when(pl.program_id(0) == 0)
    def _():
        for ref in list(g.values()) + [dmw_ref, dmv_ref]:
            ref[...] = jnp.zeros(ref.shape, F32)

    vec = vec_ref[...]
    y, kept = recv_forward(
        send_ref[...].reshape(sb * SB_ROWS, D), unpack_block(o_ref, sb), w, vec
    )
    pairs = sb // 2
    wide, unit, inv, gain = merge_rows(y, pairs, mvec_ref[...])
    dx = dx_ref[...].reshape(pairs * SB_ROWS, D)
    dmv_ref[4] += colsum(dx)
    dx2 = split2(dx)
    dmw_ref[...] += tn3(split2(wide), dx2)
    dn = mmwt(dx2, mw_ref[...])
    part = colsum(dn * unit)
    dmv_ref[0] += part[:, :D]
    dmv_ref[1] += part[:, D:]
    part = colsum(dn)
    dmv_ref[2] += part[:, :D]
    dmv_ref[3] += part[:, D:]
    dwide = norm_bwd(dn, unit, inv, gain)
    left = dwide[:, :D].reshape(pairs, 1, SB_ROWS, D)
    right = dwide[:, D:].reshape(pairs, 1, SB_ROWS, D)
    dy = jnp.concatenate([left, right], 1).reshape(sb * SB_ROWS, D)
    dsend, do = recv_backward(dy, kept, w, vec, g)
    dsend_ref[...] = dsend.reshape(sb, SB_ROWS, D)
    pack_block(do_ref, do, sb)


RECV_GRADS = [(D, D)] * 5 + [(D, FF), (FF, D), (11, 8, D)]


def recv_bwd(send, o, dx, weights, mvec, mw, sb):
    n = send.shape[0]
    shapes = RECV_GRADS + [(2 * D, D), (5, 8, D)]
    return pl.pallas_call(
        functools.partial(recv_bwd_kernel, sb),
        grid=(n // sb,),
        in_specs=[seg_block(sb), pack_spec(sb), seg_block(sb // 2)]
        + recv_weight_specs()
        + [whole((8, D)), whole((2 * D, D))],
        out_specs=[seg_block(sb), pack_spec(sb)] + [whole(s) for s in shapes],
        out_shape=[jax.ShapeDtypeStruct((n, SB_ROWS, D), F32), jax.ShapeDtypeStruct(o.shape, F32)]
        + [jax.ShapeDtypeStruct(s, F32) for s in shapes],
        compiler_params=params_spec(),
        name="recv_bwd",
    )(send, o, dx, *weights, mvec, mw)


def tail_kernel(sb, send_ref, o_ref, tgt_ref, kept_ref, scale_ref, mean_ref, *refs):
    w = {n: refs[i][...] for i, n in enumerate(RECV_W)}
    vec_ref, head_ref, dsend_ref, do_ref = refs[7:11]
    g = dict(zip(RECV_G, refs[11:19]))
    dhead_ref = refs[19]

    @pl.when(pl.program_id(0) == 0)
    def _():
        for ref in list(g.values()) + [dhead_ref]:
            ref[...] = jnp.zeros(ref.shape, F32)

    vec = vec_ref[...]
    rows = sb * SB_ROWS
    y, kept = recv_forward(
        send_ref[...].reshape(rows, D), unpack_block(o_ref, sb), w, vec
    )
    head = head_ref[...]
    y2 = split2(y)
    scale = jnp.broadcast_to(scale_ref[...][None], (sb, SB_ROWS, PPAD)).reshape(rows, PPAD)
    mean = jnp.broadcast_to(mean_ref[...][None], (sb, SB_ROWS, PPAD)).reshape(rows, PPAD)
    misfit = mmwt(y2, head) * scale + mean - tgt_ref[...].reshape(rows, PPAD)
    dpred = kept_ref[...].reshape(rows, PPAD) * misfit * scale
    dpred2 = split2(dpred)
    dhead_ref[...] += tn3(dpred2, y2)
    dy = mmw(dpred2, head)
    dsend, do = recv_backward(dy, kept, w, vec, g)
    dsend_ref[...] = dsend.reshape(sb, SB_ROWS, D)
    pack_block(do_ref, do, sb)


def tail(send, o, tgt, kept, scale, mean, weights, head, sb):
    n = send.shape[0]
    shapes = RECV_GRADS + [(PPAD, D)]
    return pl.pallas_call(
        functools.partial(tail_kernel, sb),
        grid=(n // sb,),
        in_specs=[seg_block(sb), pack_spec(sb), seg_block(sb, SB_ROWS, PPAD), seg_block(sb, SB_ROWS, PPAD)]
        + [whole((SB_ROWS, PPAD))] * 2
        + recv_weight_specs()
        + [whole((PPAD, D))],
        out_specs=[seg_block(sb), pack_spec(sb)] + [whole(s) for s in shapes],
        out_shape=[jax.ShapeDtypeStruct((n, SB_ROWS, D), F32), jax.ShapeDtypeStruct(o.shape, F32)]
        + [jax.ShapeDtypeStruct(s, F32) for s in shapes],
        compiler_params=params_spec(),
        name="tail",
    )(send, o, tgt, kept, scale, mean, *weights, head)


SEND_W = ("sq", "sk", "sv")


def send_project(dim2, r_rows, w, vec):
    r2 = split2(r_rows)
    sb = r_rows.shape[0] // RPAD
    k = mmw(dim2, w["sk"])
    v = mmw(dim2, w["sv"]) + vec[11:12]
    q = (mmw(r2, w["sq"]) + vec[10:11]) * SCALE
    k = [split2(k[s * SB_ROWS : (s + 1) * SB_ROWS]) for s in range(sb)]
    v = [split2(v[s * SB_ROWS : (s + 1) * SB_ROWS]) for s in range(sb)]
    q = [split2(spread_rows(q[s * RPAD : (s + 1) * RPAD])) for s in range(sb)]
    return r2, k, v, q


def send_fwd_kernel(sb, dim_ref, r_ref, here_ref, *refs):
    w = {n: refs[i][...] for i, n in enumerate(SEND_W)}
    vec_ref, o_ref = refs[3:]
    dim2 = split2(dim_ref[...].reshape(sb * SB_ROWS, D))
    _, k, v, q = send_project(dim2, r_ref[...].reshape(sb * RPAD, D), w, vec_ref[...])
    here = here_ref[...] > 0.5
    scores = [jnp.where(here, nt3(k2, q2), negative) for k2, q2 in zip(k, q)]
    tops = [jnp.max(sc, 0, keepdims=True) for sc in scores]
    probs = [jnp.where(here, jnp.exp(sc - top), 0.0) for sc, top in zip(scores, tops)]
    totals = [jnp.sum(p, 0, keepdims=True) for p in probs]
    safe = [jnp.where(t > 0.0, t, 1.0) for t in totals]
    mixed = [gather_rows(tn3(split2(p / t), v2)) for p, t, v2 in zip(probs, safe, v)]
    for s in range(sb):
        lse = jnp.where(totals[s] > 0.0, tops[s] + jnp.log(safe[s]), negative)
        o_ref[s] = pack_rows(mixed[s], lse)


def send_weight_specs():
    return [whole((D, D))] * 3 + [whole((24, D))]


def send_fwd(dim, routers, here, weights, sb, npad):
    n = dim.shape[0]
    return pl.pallas_call(
        functools.partial(send_fwd_kernel, sb),
        grid=(n // sb,),
        in_specs=[seg_block(sb), seg_block(sb, RPAD), whole((SB_ROWS, HALF))] + send_weight_specs(),
        out_specs=pack_spec(sb),
        out_shape=jax.ShapeDtypeStruct((npad, PACK, HALF), F32),
        compiler_params=params_spec(),
        name="send_fwd",
    )(dim, routers, here, *weights)


def send_bwd_kernel(sb, dim_ref, dpart_ref, r_ref, o_ref, do_ref, here_ref, *refs):
    w = {n: refs[i][...] for i, n in enumerate(SEND_W)}
    vec_ref, ddim_ref, dr_ref = refs[3:6]
    dsq_ref, dsk_ref, dsv_ref, rows = refs[6:10]

    @pl.when(pl.program_id(0) == 0)
    def _():
        for ref in (dsq_ref, dsk_ref, dsv_ref, rows):
            ref[...] = jnp.zeros(ref.shape, F32)

    dim2 = split2(dim_ref[...].reshape(sb * SB_ROWS, D))
    r2, k, v, q = send_project(dim2, r_ref[...].reshape(sb * RPAD, D), w, vec_ref[...])
    here = (here_ref[...] > 0.5) & valid_lane(SB_ROWS)
    segs = range(sb)
    scores = [nt3(k2, q2) for k2, q2 in zip(k, q)]
    probs = [jnp.where(here, jnp.exp(scores[s] - o_ref[s][2 * ROUT : 2 * ROUT + 1]), 0.0) for s in segs]
    dwide = [spread_rows(unpack_rows(do_ref[s])) for s in segs]
    owide = [
        jnp.broadcast_to(unpack_rows(o_ref[s])[:, None, :], (RPAD, HEADS, D)).reshape(RPAD * HEADS, D) for s in segs
    ]
    e = [split2(a * b) for a, b in zip(dwide, owide)]
    d = [split2(a) for a in dwide]
    one_row = jnp.ones((8, D), BF)
    means = [(dots(one_row, e2[0], 1, 1) + dots(one_row, e2[1], 1, 1))[0:1] for e2 in e]
    dp = [nt3(v2, d2) for v2, d2 in zip(v, d)]
    ds = [split2(p * (x - mean)) for p, x, mean in zip(probs, dp, means)]
    dk = jnp.concatenate([nn3(s2, q2) for s2, q2 in zip(ds, q)], 0)
    dv = jnp.concatenate([nn3(split2(p), d2) for p, d2 in zip(probs, d)], 0)
    dq = jnp.concatenate([gather_rows(tn3(s2, k2)) for s2, k2 in zip(ds, k)], 0) * SCALE
    dk2 = split2(dk)
    dv2 = split2(dv)
    rows[1] += colsum(dv)
    dsk_ref[...] += tn3(dim2, dk2)
    dsv_ref[...] += tn3(dim2, dv2)
    out = dpart_ref[...].reshape(sb * SB_ROWS, D) + mmwt(dk2, w["sk"]) + mmwt(dv2, w["sv"])
    ddim_ref[...] = out.reshape(sb, SB_ROWS, D)
    rows[0] += colsum(dq)
    dq2 = split2(dq)
    dsq_ref[...] += tn3(r2, dq2)
    dr_ref[...] = mmwt(dq2, w["sq"]).reshape(sb, RPAD, D)


def send_bwd(dim, dpart, routers, o, do, here, weights, sb):
    n = dim.shape[0]
    shapes = [(D, D)] * 3 + [(2, 8, D)]
    return pl.pallas_call(
        functools.partial(send_bwd_kernel, sb),
        grid=(n // sb,),
        in_specs=[seg_block(sb), seg_block(sb), seg_block(sb, RPAD), pack_spec(sb), pack_spec(sb), whole((SB_ROWS, HALF))]
        + send_weight_specs(),
        out_specs=[seg_block(sb), seg_block(sb, RPAD)] + [whole(s) for s in shapes],
        out_shape=[jax.ShapeDtypeStruct((n, SB_ROWS, D), F32), jax.ShapeDtypeStruct((n, RPAD, D), F32)]
        + [jax.ShapeDtypeStruct(s, F32) for s in shapes],
        compiler_params=params_spec(),
        name="send_bwd",
    )(dim, dpart, routers, o, do, here, *weights)

MESH = pl.DeviceIdType.MESH
ANY = pl.BlockSpec(memory_space=pl.ANY)
INVMEM = pl.BlockSpec(memory_space=pltpu.VMEM)


def grid_sizes():
    nf = lax.axis_size("fsdp")
    nx = 1
    while 2 * nx * nx < nf:
        nx *= 2
    return lax.axis_size("dp") // 2, nf // nx, nx


class Place:
    def __init__(self):
        self.ny, self.nz, self.nx = grid_sizes()
        dp, fs = lax.axis_index("dp"), lax.axis_index("fsdp")
        self.core, self.y = lax.rem(dp, 2), lax.div(dp, 2)
        self.x, self.z = lax.rem(fs, self.nx), lax.div(fs, self.nx)

    def at(self, y=None, core=None, z=None, x=None):
        y = self.y if y is None else y
        core = self.core if core is None else core
        z = self.z if z is None else z
        x = self.x if x is None else x
        return (y * 2 + core, z * self.nx + x)

    def other(self):
        return 1 - self.core

    def next_x(self, k):
        return lax.rem(self.x + k, self.nx)

    def next_y(self, k):
        return lax.rem(self.y + k, self.ny)

    def next_z(self, k):
        return lax.rem(self.z + k, self.nz)

    def neighbours(self):
        out = [self.at(core=self.other())]
        out += [self.at(x=self.next_x(k)) for k in range(1, self.nx)]
        out += [self.at(y=self.next_y(k)) for k in range(1, self.ny)]
        out += [self.at(z=self.next_z(k)) for k in range(1, self.nz)]
        return out


def greet(devices):
    barrier = pltpu.get_barrier_semaphore()
    for device in devices:
        pl.semaphore_signal(barrier, inc=1, device_id=device, device_id_type=MESH)
    pl.semaphore_wait(barrier, len(devices))


def remote(src, dst, send, recv, device):
    return pltpu.make_async_remote_copy(
        src_ref=src, dst_ref=dst, send_sem=send, recv_sem=recv, device_id=device, device_id_type=MESH
    )


def gather_kernel(n, *refs):
    shards, outs = refs[:n], refs[n : 2 * n]
    send, recv, local = refs[2 * n :]
    me = Place()
    y, c, z, x = me.y, me.core, me.z, me.x
    m = me.nx
    greet(me.neighbours())
    copies, slot = [], [0]

    def push(src, dst, device):
        copy = remote(src, dst, send.at[slot[0]], recv.at[slot[0]], device)
        slot[0] += 1
        copy.start()
        return copy

    own = [pltpu.make_async_copy(shards[j], outs[j].at[y, c, z, x], local.at[j]) for j in range(n)]
    for copy in own:
        copy.start()
    first = [
        push(shards[j], outs[j].at[y, c, z, x], me.at(z=me.next_z(k))) for j in range(n) for k in range(1, me.nz)
    ]
    for copy in own:
        copy.wait()
    for copy in first:
        copy.wait()
    base = slot[0]

    def rest(by_core):
        slot[0] = base
        shared, started = [], []
        sibling = me.at(core=1 - by_core)
        second = []
        for j in range(n):
            piece = outs[j].at[y, by_core, :, x]
            for k in range(1, m):
                peer = me.at(x=me.next_x(k)) if by_core == 0 else me.at(y=me.next_y(k))
                second.append(push(piece, piece, peer))
            shared.append(push(piece, piece, sibling))
        for copy in second:
            copy.wait()
        third = []
        for j in range(n):
            wide = outs[j].at[y, by_core] if by_core == 0 else outs[j].at[:, by_core, :, x]
            for k in range(1, m):
                peer = me.at(y=me.next_y(k)) if by_core == 0 else me.at(x=me.next_x(k))
                third.append(push(wide, wide, peer))
            for k in range(1, m):
                piece = outs[j].at[y, by_core, :, me.next_x(k)] if by_core == 0 else outs[j].at[me.next_y(k), by_core, :, x]
                shared.append(push(piece, piece, sibling))
        for copy in third:
            copy.wait()
        for j in range(n):
            for k in range(1, m):
                wide = outs[j].at[me.next_y(k), by_core] if by_core == 0 else outs[j].at[:, by_core, :, me.next_x(k)]
                shared.append(push(wide, wide, sibling))
        for copy in shared:
            copy.wait()

    for by_core in (0, 1):
        pl.when(c == by_core)(functools.partial(rest, by_core))


def gather_all(shards):
    ny, nz, nx = grid_sizes()
    n = len(shards)
    count = n * ((nz - 1) + (nx - 1) + 1 + (nx - 1) * 3)
    return pl.pallas_call(
        functools.partial(gather_kernel, n),
        in_specs=[ANY] * n,
        out_specs=[ANY] * n,
        out_shape=[jax.ShapeDtypeStruct((ny, 2, nz, nx) + s.shape, s.dtype) for s in shards],
        scratch_shapes=[pltpu.SemaphoreType.DMA((count,)), pltpu.SemaphoreType.DMA((count,)), pltpu.SemaphoreType.DMA((n,))],
        compiler_params=pltpu.CompilerParams(collective_id=0, has_side_effects=True, vmem_limit_bytes=16 << 20),
        name="gather_all",
    )(*shards)


def add_into(acc, at, terms, rows):
    total = acc[at]
    for ref, index in terms:
        total = total + ref[index]
    acc[at] = total


def scatter_kernel(n, *refs):
    grads, tile_ref = refs[:n], refs[n]
    outs, stat_ref = refs[n + 1 : 2 * n + 1], refs[2 * n + 1]
    acc, r1, r2, r3, r4 = (refs[2 * n + 2 + i * n : 2 * n + 2 + (i + 1) * n] for i in range(5))
    tc, tx, ty, tz, send, recv, local = refs[7 * n + 2 :]
    me = Place()
    y, c, z, x = me.y, me.core, me.z, me.x
    ny, nz, nx, m = me.ny, me.nz, me.nx, me.nx
    greet(me.neighbours())
    slot = [0]

    def push(src, dst, device):
        copy = remote(src, dst, send.at[slot[0]], recv.at[slot[0]], device)
        slot[0] += 1
        copy.start()
        return copy

    stage, own = [], []
    for j in range(n):
        stage.append([push(grads[j].at[:, me.other(), :, k], r1[j].at[:, k], me.at(core=me.other())) for k in range(nx)])
        mine = [
            pltpu.make_async_copy(grads[j].at[:, c, :, k], acc[j].at[:, k], local.at[j * nx + k]) for k in range(nx)
        ]
        for copy in mine:
            copy.start()
        own.append(mine)
    base = slot[0]

    def rest(by_core):
        slot[0] = base
        two, three, four = [], [], []
        for j in range(n):
            for copy in own[j] + stage[j]:
                copy.wait()

            def add1(i, carry):
                at = (lax.div(i, nx * nz), lax.rem(lax.div(i, nz), nx), lax.rem(i, nz))
                add_into(acc[j], at, [(r1[j], at)], None)
                return carry

            lax.fori_loop(0, ny * nx * nz, add1, 0)
            if by_core == 0:
                two.append([push(acc[j].at[:, me.next_x(k)], r2[j].at[k - 1], me.at(x=me.next_x(k))) for k in range(1, m)])
            else:
                two.append([push(acc[j].at[me.next_y(k)], r2[j].at[k - 1], me.at(y=me.next_y(k))) for k in range(1, m)])
        for j in range(n):
            for copy in two[j]:
                copy.wait()

            def add2(i, carry):
                a, b = lax.div(i, nz), lax.rem(i, nz)
                at = (a, x, b) if by_core == 0 else (y, a, b)
                add_into(acc[j], at, [(r2[j], (k, a, b)) for k in range(m - 1)], None)
                return carry

            lax.fori_loop(0, m * nz, add2, 0)
            if by_core == 0:
                three.append([push(acc[j].at[me.next_y(k), x], r3[j].at[k - 1], me.at(y=me.next_y(k))) for k in range(1, m)])
            else:
                three.append([push(acc[j].at[y, me.next_x(k)], r3[j].at[k - 1], me.at(x=me.next_x(k))) for k in range(1, m)])
        for j in range(n):
            for copy in three[j]:
                copy.wait()

            def add3(i, carry):
                add_into(acc[j], (y, x, i), [(r3[j], (k, i)) for k in range(m - 1)], None)
                return carry

            lax.fori_loop(0, nz, add3, 0)
            four.append(
                [push(acc[j].at[y, x, me.next_z(k)], r4[j].at[k - 1], me.at(z=me.next_z(k))) for k in range(1, nz)]
            )
        squares = jnp.zeros((8, HALF), F32)
        for j in range(n):
            for copy in four[j]:
                copy.wait()
            total = acc[j][y, x, z]
            for k in range(nz - 1):
                total = total + r4[j][k]
            outs[j][...] = total
            sq = colsum_any(total * total)
            squares = squares + sq[:, :HALF] + sq[:, HALF:]
        tc[c] = jnp.concatenate([squares, tile_ref[...]], 0)

    for by_core in (0, 1):
        pl.when(c == by_core)(functools.partial(rest, by_core))

    slot[0] = base + n * ((m - 1) * 2 + nz - 1)
    push(tc.at[c], tc.at[c], me.at(core=me.other())).wait()
    tx[x] = tc[0] + tc[1]
    for copy in [push(tx.at[x], tx.at[x], me.at(x=me.next_x(k))) for k in range(1, nx)]:
        copy.wait()
    ty[y] = functools.reduce(jnp.add, [tx[k] for k in range(nx)])
    for copy in [push(ty.at[y], ty.at[y], me.at(y=me.next_y(k))) for k in range(1, ny)]:
        copy.wait()
    tz[z] = functools.reduce(jnp.add, [ty[k] for k in range(ny)])
    for copy in [push(tz.at[z], tz.at[z], me.at(z=me.next_z(k))) for k in range(1, nz)]:
        copy.wait()
    stat_ref[...] = functools.reduce(jnp.add, [tz[k] for k in range(nz)])


def colsum_any(x):
    rows = x.shape[0]
    even = rows // 8 * 8
    out = colsum(x[:even]) if even else jnp.zeros((8, x.shape[1]), F32)
    if rows > even:
        out = out + jnp.pad(x[even:], ((0, 8 - rows + even), (0, 0)))
    return out


def scatter_sum(grads, tile):
    ny, nz, nx = grid_sizes()
    n = len(grads)
    shapes = [g.shape[-2:] for g in grads]
    count = n * nx + n * ((nx - 1) * 2 + nz - 1) + 1 + (nx - 1) + (ny - 1) + (nz - 1)

    def buffers(*lead):
        return [pltpu.VMEM(lead + s, F32) for s in shapes]

    return pl.pallas_call(
        functools.partial(scatter_kernel, n),
        in_specs=[ANY] * n + [INVMEM],
        out_specs=[INVMEM] * (n + 1),
        out_shape=[jax.ShapeDtypeStruct(s, F32) for s in shapes] + [jax.ShapeDtypeStruct((16, HALF), F32)],
        scratch_shapes=buffers(ny, nx, nz)
        + buffers(ny, nx, nz)
        + buffers(nx - 1, nx, nz)
        + buffers(nx - 1, nz)
        + buffers(nz - 1)
        + [pltpu.VMEM((k, 16, HALF), F32) for k in (2, nx, ny, nz)]
        + [pltpu.SemaphoreType.DMA((count,)), pltpu.SemaphoreType.DMA((count,)), pltpu.SemaphoreType.DMA((n * nx,))],
        compiler_params=pltpu.CompilerParams(collective_id=1, has_side_effects=True, vmem_limit_bytes=VMEM_LIMIT),
        name="scatter_sum",
    )(*grads, tile)


def group_kernel(stats, per, in_ref, out_ref, got, result, send, recv, local):
    nf = lax.axis_size("fsdp")
    dp, f = lax.axis_index("dp"), lax.axis_index("fsdp")
    peers = [lax.rem(f + k, nf) for k in range(1, nf)]
    greet([(dp, p) for p in peers])

    def part(ref, who):
        return ref.at[pl.ds(pl.multiple_of(who * per, per), per)]

    own = pltpu.make_async_copy(part(in_ref, f), got.at[f], local)
    own.start()
    copies = [
        remote(part(in_ref, p), got.at[f], send.at[k], recv.at[k], (dp, p)) for k, p in enumerate(peers)
    ]
    for copy in copies:
        copy.start()
    own.wait()
    for copy in copies:
        copy.wait()
    if stats:
        row = lax.broadcasted_iota(jnp.int32, (PACK, HALF), 0)
        lane = lax.broadcasted_iota(jnp.int32, (PACK, HALF), 1)
        router = jnp.where(row < ROUT, row, row - ROUT)
        pick = (lane // 8 == router) & (row < 2 * ROUT)
        src = lax.broadcasted_iota(jnp.int32, (HALF, D), 0)
        dst = lax.broadcasted_iota(jnp.int32, (HALF, D), 1)
        widen = jnp.where(src % 8 == dst // 32, 1.0, 0.0).astype(BF)

        def one(s, carry):
            lse = [got[d, s, 2 * ROUT : 2 * ROUT + 1, :] for d in range(nf)]
            top = functools.reduce(jnp.maximum, lse)
            total = top + jnp.log(functools.reduce(jnp.add, [jnp.exp(l - top) for l in lse]))
            out = jnp.where(row == 2 * ROUT, total, 0.0)
            share = jnp.concatenate([jnp.where(pick, jnp.exp(l - total), 0.0) for l in lse], 0)
            wide = mmw(split2(share), widen)
            for d in range(nf):
                w = wide[d * PACK : (d + 1) * PACK]
                w = jnp.where(row < ROUT, w[:, :HALF], w[:, HALF:])
                out = out + jnp.where(row < 2 * ROUT, w * got[d, s], 0.0)
            result[s] = out
            return carry

        lax.fori_loop(0, per, one, 0)
    else:
        result[...] = functools.reduce(jnp.add, [got[d] for d in range(nf)])
    own = pltpu.make_async_copy(result, part(out_ref, f), local)
    own.start()
    copies = [
        remote(result, part(out_ref, f), send.at[nf - 1 + k], recv.at[nf - 1 + k], (dp, p)) for k, p in enumerate(peers)
    ]
    for copy in copies:
        copy.start()
    own.wait()
    for copy in copies:
        copy.wait()


def group_combine(packed, stats, cid):
    nf = lax.axis_size("fsdp")
    per = packed.shape[0] // nf
    return pl.pallas_call(
        functools.partial(group_kernel, stats, per),
        in_specs=[INVMEM],
        out_specs=INVMEM,
        out_shape=jax.ShapeDtypeStruct(packed.shape, F32),
        scratch_shapes=[
            pltpu.VMEM((nf, per, PACK, HALF), F32),
            pltpu.VMEM((per, PACK, HALF), F32),
            pltpu.SemaphoreType.DMA((2 * nf - 2,)),
            pltpu.SemaphoreType.DMA((2 * nf - 2,)),
            pltpu.SemaphoreType.DMA,
        ],
        compiler_params=pltpu.CompilerParams(collective_id=cid, has_side_effects=True, vmem_limit_bytes=32 << 20),
        name="group_stats" if stats else "group_sum",
    )(packed)


def series_stats(series, observed):
    seen = observed.astype(F32)
    counted = jnp.maximum(jnp.sum(seen, -1, keepdims=True), 1.0)
    mean = jnp.sum(seen * series, -1, keepdims=True) / counted
    center = (series - mean) * seen
    scale = jnp.sqrt(jnp.sum(center * center, -1, keepdims=True) / counted + norm_eps)
    return center / scale, mean, scale


def adam_update(weight, first_moment, second_moment, gradient):
    first_new = beta_one * first_moment + (1.0 - beta_one) * gradient
    second_new = beta_two * second_moment + (1.0 - beta_two) * gradient * gradient
    corrected = (
        first_new
        / (1.0 - beta_one**step_count)
        / (jnp.sqrt(second_new / (1.0 - beta_two**step_count)) + adam_eps)
    )
    return (weight - learn_rate * (corrected + weight_decay * weight), first_new, second_new)


def segment_major(x, width):
    nv = x.shape[0]
    x = x.reshape(nv, -1, 12).transpose(1, 0, 2)
    return jnp.pad(x, ((0, 0), (0, 0), (0, width - 12)))


def pad_rows(x, rows):
    return jnp.pad(x, ((0, rows - x.shape[0]), (0, 0)))


def gradient_parts(series, observed, targets, target_mask, present, square, up, down, vectors, combine, nf):
    nv = series.shape[0]
    normed, mean, scale = series_stats(series, observed)
    pieces = segment_major(normed, 16)
    factor = 2.0 / (1 << 20)
    kept = segment_major(target_mask.astype(F32) * present[:, None] * factor, PPAD)
    tgt = segment_major(targets, PPAD)
    scale16 = jnp.broadcast_to(scale, (nv, PPAD))
    mean16 = jnp.broadcast_to(mean, (nv, PPAD))
    here = jnp.broadcast_to(present[:, None], (nv, HALF))

    emb = pad_rows(vectors[:12], 16).astype(BF)
    place = (vectors[12:13] + vectors[13:73])[:, None, :]
    layer_start = SEGLEN + 1 + SEG
    vecs = [pad_rows(vectors[layer_start + 23 * l : layer_start + 23 * l + 23], 24) for l in range(2)]
    merge_at = layer_start + 46
    mvec = pad_rows(vectors[merge_at : merge_at + 5], 8)
    mw = square[24:26].reshape(2 * D, D)
    head = pad_rows(vectors[merge_at + 5 : merge_at + 17], PPAD).astype(BF)
    router_at = merge_at + 17
    routers = []
    for l, n in ((0, SEG), (1, SEG // 2)):
        r = vectors[router_at + l * SEG * ROUT : router_at + l * SEG * ROUT + n * ROUT].reshape(n, ROUT, D)
        routers.append(jnp.pad(r, ((0, 0), (0, RPAD - ROUT), (0, 0))))
    time_w = [
        (*[square[12 * l + i] for i in (0, 1, 2, 3)], up[2 * l], down[2 * l], vecs[l]) for l in range(2)
    ]
    send_w = [(*[square[12 * l + i] for i in (4, 5, 6)], vecs[l]) for l in range(2)]
    recv_w = [
        (*[square[12 * l + i] for i in (7, 9, 10, 8, 11)], up[2 * l + 1], down[2 * l + 1], vecs[l]) for l in range(2)
    ]

    sb0, sb1 = 4, 6
    dim0 = time_fwd(True, pieces, (emb, place), time_w[0], SEG)
    o0 = send_fwd(dim0, routers[0], here, send_w[0], sb0, -(-SEG // nf) * nf)
    o0 = combine(o0, True, 2)
    x1 = recv_fwd(dim0, o0, recv_w[0], mvec, mw, sb0)
    dim1 = time_fwd(False, x1, (), time_w[1], SEG // 2)
    o1 = send_fwd(dim1, routers[1], here, send_w[1], sb1, -(-SEG // 2 // nf) * nf)
    o1 = combine(o1, True, 3)
    out = tail(dim1, o1, tgt, kept, scale16, mean16, recv_w[1], head, sb1)
    ddim1, do1, grecv1, dhead = out[0], out[1], out[2:10], out[10]
    do1 = combine(do1, False, 4)
    out = send_bwd(dim1, ddim1, routers[1], o1, do1, here, send_w[1], sb1)
    ddim1, dr1, gsend1 = out[0], out[1], out[2:]
    out = time_bwd(False, x1, (), ddim1, time_w[1], SEG // 2)
    gtime1, dx1 = out[:7], out[7]
    out = recv_bwd(dim0, o0, dx1, recv_w[0], mvec, mw, sb0)
    ddim0, do0, grecv0, dmw, dmv = out[0], out[1], out[2:10], out[10], out[11]
    do0 = combine(do0, False, 5)
    out = send_bwd(dim0, ddim0, routers[0], o0, do0, here, send_w[0], sb0)
    ddim0, dr0, gsend0 = out[0], out[1], out[2:]
    out = time_bwd(True, pieces, (emb, place), ddim0, time_w[0], SEG)
    gtime0, demb, dplace = out[:7], out[7], out[8]

    mats, ups, downs, rows = [], [], [], []
    for gt, gs, gr in ((gtime0, gsend0, grecv0), (gtime1, gsend1, grecv1)):
        mats += [gt[0], gt[1], gt[2], gt[3], gs[0], gs[1], gs[2], gr[0], gr[3], gr[1], gr[2], gr[4]]
        ups += [gt[4], gr[5]]
        downs += [gt[5], gr[6]]
        rt, rs, rr = gt[6].sum(1), gs[3].sum(1), gr[7].sum(1)
        rows += [rt, rs, rr]
    mats += [dmw]
    dplace = dplace.reshape(SEG, VB, D).sum(1)
    vec = jnp.concatenate(
        [demb[:12], dplace.sum(0, keepdims=True), dplace]
        + rows
        + [dmv.sum(1), dhead[:12]]
        + [dr[:, :ROUT].reshape(-1, D) for dr in (dr0, dr1)],
        0,
    )
    return jnp.concatenate(mats, 0), jnp.concatenate(ups, 0), jnp.concatenate(downs, 0), vec


def on_device(series, observed, targets, target_mask, counts, matrices, feed_weights, vectors, matrices_first, matrices_second, feed_first, feed_second, vectors_first, vectors_second):
    local_vars = series.shape[1]
    nf = lax.axis_size("fsdp")
    devices = nf * lax.axis_size("dp")
    slot = lax.axis_index("fsdp") * local_vars + jnp.arange(local_vars, dtype=jnp.int32)
    present = (slot < counts[0]).astype(F32)
    own_rows = NVEC * D // devices
    vec_rows = -(-own_rows // D)

    def as_rows(x):
        return x.reshape(-1, D)

    def pad_flat(x):
        return jnp.pad(x, [(0, 0)] * (x.ndim - 1) + [(0, vec_rows * D - own_rows)])

    square, feed, vecs = gather_all(
        [as_rows(matrices.astype(BF)), as_rows(feed_weights.astype(BF)), as_rows(pad_flat(vectors.astype(BF)))]
    )
    square = square.reshape(NSQ, D, D)
    feed = feed.reshape(-1, D)
    up = feed[: 4 * FF].reshape(4, D, FF)
    down = feed[4 * FF :].reshape(4, FF, D)
    vecs = vecs.reshape(devices, -1)[:, :own_rows].reshape(NVEC, D).astype(F32)
    g_mat, g_up, g_down, g_vec = gradient_parts(
        series[0], observed[0], targets[0], target_mask[0], present, square, up, down, vecs, group_combine, nf
    )
    g_feed = jnp.concatenate([g_up.reshape(-1, D), g_down], 0)
    g_vec = pad_flat(g_vec.reshape(devices, own_rows))
    ny, nz, nx = grid_sizes()
    lead = (ny, 2, nz, nx)
    kept = target_mask[0].astype(F32) * present[:, None]
    tile = jnp.pad(jnp.sum(kept).reshape(1, 1), ((0, 7), (0, HALF - 1)))
    s_mat, s_feed, s_vec, sums = scatter_sum(
        [g_mat.reshape(lead + (-1, D)), g_feed.reshape(lead + (-1, D)), g_vec.reshape(lead + (-1, D))], tile
    )
    shards = (s_mat.reshape(-1), s_feed.reshape(-1), s_vec.reshape(-1)[:own_rows])
    upscale = (1 << 20) / jnp.maximum(jnp.sum(sums[8:]), 1.0)
    grad_norm = jnp.sqrt(jnp.sum(sums[:8])) * upscale
    factor = upscale * (clip_norm / jnp.maximum(grad_norm, clip_norm))
    new = (
        adam_update(matrices, matrices_first, matrices_second, shards[0] * factor)
        + adam_update(feed_weights, feed_first, feed_second, shards[1] * factor)
        + adam_update(vectors, vectors_first, vectors_second, shards[2] * factor)
    )
    return (grad_norm,) + new


def solution(mesh):
    both = P(("dp", "fsdp"))
    data = P("dp", "fsdp", None)
    return jax.shard_map(
        on_device,
        mesh=mesh,
        in_specs=(data,) * 4 + (P("dp"),) + (both,) * 9,
        out_specs=(P(),) + (both,) * 9,
        check_vma=False,
    )
```

```python
import functools
import jax
import jax.numpy as jnp
from jax import lax
from jax.experimental import pallas as pl
from jax.experimental.pallas import tpu as pltpu
from jax.sharding import PartitionSpec as P

D = 256
HEADS = 8
FF = 512
ROUT = 10
RPAD = 16
SEGLEN = 12
PRED = 12
PPAD = 16
SEG = 60
NSQ = 26
NVEC = 1036
HALF = 128
VB = 8
UNROLL = 8
UNROLL_BACK = 8

BF = jnp.bfloat16
F32 = jnp.float32
SCALE = (D // HEADS) ** (-0.5)
negative = -1e30
norm_eps = 1e-05
beta_one = 0.9
beta_two = 0.999
adam_eps = 1e-08
weight_decay = 0.01
learn_rate = 0.2
clip_norm = 0.01
step_count = 10.0
VMEM_LIMIT = 60 << 20


def split2(x):
    hi = x.astype(BF)
    return hi, (x - hi.astype(F32)).astype(BF)


def dots(a, b, ca, cb):
    return lax.dot_general(a, b, (((ca,), (cb,)), ((), ())), preferred_element_type=F32)


def mmw(x2, w):
    return dots(x2[0], w, 1, 0) + dots(x2[1], w, 1, 0)


def mmwt(x2, w):
    return dots(x2[0], w, 1, 1) + dots(x2[1], w, 1, 1)


def rows2(a2):
    return jnp.concatenate([a2[0], a2[1]], 0)


def nn3(a2, b2):
    m = a2[0].shape[0]
    both = dots(rows2(a2), b2[0], 1, 0)
    return both[:m] + both[m:] + dots(a2[0], b2[1], 1, 0)


def nt3(a2, b2):
    m = a2[0].shape[0]
    both = dots(rows2(a2), b2[0], 1, 1)
    return both[:m] + both[m:] + dots(a2[0], b2[1], 1, 1)


def tn3(a2, b2):
    n = b2[0].shape[1]
    both = dots(a2[0], jnp.concatenate([b2[0], b2[1]], 1), 0, 0)
    return both[:, :n] + both[:, n:] + dots(a2[1], b2[0], 0, 0)


def norm_fwd(z, gain, bias):
    center = z - jnp.mean(z, -1, keepdims=True)
    inv = lax.rsqrt(jnp.mean(center * center, -1, keepdims=True) + norm_eps)
    unit = center * inv
    return unit * gain + bias, unit, inv


def norm_bwd(dy, unit, inv, gain):
    t = dy * gain
    return inv * (t - jnp.mean(t, -1, keepdims=True) - unit * jnp.mean(t * unit, -1, keepdims=True))


def colsum(x):
    return jnp.sum(x.reshape(x.shape[0] // 8, 8, x.shape[1]), 0)


def gelu_cdf(u):
    return 0.5 + 0.5 * lax.erf(u * 0.7071067811865476)


def gelu_slope(u, cdf):
    return cdf + u * (jnp.exp(-0.5 * u * u) * 0.3989422804014327)


def halves(x):
    return x[:, :HALF], x[:, HALF:]


def lane_head(rows):
    return lax.broadcasted_iota(jnp.int32, (rows, HALF), 1) // 32


def spread_heads(x, zero):
    head = lane_head(x.shape[0])
    return jnp.concatenate([jnp.where(head == h, x, zero) for h in range(4)], 0)


def gather_heads(x, group):
    head = lane_head(group)
    out = x[3 * group :]
    for h in range(3):
        out = jnp.where(head == h, x[h * group : (h + 1) * group], out)
    return out


def ones_heads(group, count):
    row = lax.broadcasted_iota(jnp.int32, (4 * group, HALF), 0)
    lane = lax.broadcasted_iota(jnp.int32, (4 * group, HALF), 1)
    return jnp.where((row // group == lane // 32) & (row % group < count), 1.0, 0.0).astype(BF)


def group_max(s, group, count):
    lane = lax.broadcasted_iota(jnp.int32, (s.shape[0], HALF), 1)
    outs = []
    for t in range(s.shape[1] // HALF):
        part = s[:, t * HALF : (t + 1) * HALF]
        top = None
        for g in range(HALF // group):
            here = (lane // group == g)
            best = jnp.max(jnp.where((lane // group == g) & (lane % group < count), part, negative), -1, keepdims=True)
            top = jnp.broadcast_to(best, part.shape) if top is None else jnp.where(here, best, top)
        outs.append(jnp.where(lane % group < count, part - top, negative))
    return jnp.concatenate(outs, 1)


def time_parts(units, group, ref):
    return [split2(ref[c, pl.ds(v, group, stride=VB), :]) for c, v in units]


def spread2(x2):
    zero = jnp.zeros((), BF)
    return spread_heads(x2[0], zero), spread_heads(x2[1], zero)


def time_attend(units, group, count, q_s, k_s, v_s, o_s, p_s, l_s):
    q = time_parts(units, group, q_s)
    k = [spread2(x2) for x2 in time_parts(units, group, k_s)]
    scores = [
        dots(jnp.concatenate(q2, 1), jnp.concatenate([k2[0], k2[0]], 1), 1, 1) + dots(q2[0], k2[1], 1, 1)
        for q2, k2 in zip(q, k)
    ]
    probs = [jnp.exp(group_max(s, group, count)) for s in scores]
    probs2 = [split2(p) for p in probs]
    w = [spread2(x2) for x2 in time_parts(units, group, v_s)]
    ones = ones_heads(group, count)
    both = [dots(rows2(p2), jnp.concatenate([w2[0], ones], 1), 1, 0) for p2, w2 in zip(probs2, w)]
    both = [b[:group] + b[group:] for b in both]
    inv = [1.0 / b[:, HALF:] for b in both]
    mixed = [(b[:, :HALF] + dots(p2[0], w2[1], 1, 0)) * i for b, p2, w2, i in zip(both, probs2, w, inv)]
    for (c, v), o, p, i in zip(units, mixed, probs, inv):
        o_s[c, pl.ds(v, group, stride=VB), :] = o
        p_s[c, v] = p
        l_s[c, v] = i


def time_attend_back(units, group, count, q_s, k_s, v_s, o_s, p_s, l_s, do_s, dq_s, dk_s, dv_s):
    d = [do_s[c, pl.ds(v, group, stride=VB), :] * l_s[c, v] for c, v in units]
    e2 = [split2(x * o_s[c, pl.ds(v, group, stride=VB), :]) for x, (c, v) in zip(d, units)]
    d2 = [split2(x) for x in d]
    w = [spread2(x2) for x2 in time_parts(units, group, v_s)]
    ones = -ones_heads(group, count)
    both = [
        dots(
            jnp.concatenate([jnp.concatenate([a[0], b[0]], 1), jnp.concatenate([a[1], b[1]], 1)], 0),
            jnp.concatenate([w2[0], ones], 1),
            1,
            1,
        )
        for a, b, w2 in zip(d2, e2, w)
    ]
    dp = [b[:group] + b[group:] + dots(a[0], w2[1], 1, 1) for b, a, w2 in zip(both, d2, w)]
    probs = [p_s[c, v] for c, v in units]
    s2 = [split2(p * x) for p, x in zip(probs, dp)]
    p2 = [split2(p) for p in probs]
    k = [spread2(x2) for x2 in time_parts(units, group, k_s)]
    both = [dots(rows2(a), k2[0], 1, 0) for a, k2 in zip(s2, k)]
    dq = [b[:group] + b[group:] + dots(a[0], k2[1], 1, 0) for b, a, k2 in zip(both, s2, k)]
    q = time_parts(units, group, q_s)
    dk = [gather_heads(tn3(a, q2), group) for a, q2 in zip(s2, q)]
    dv = [gather_heads(tn3(a, x), group) for a, x in zip(p2, d2)]
    for (c, v), x, y, z in zip(units, dq, dk, dv):
        at = pl.ds(v, group, stride=VB)
        dq_s[c, at, :] = x
        dk_s[c, at, :] = y
        dv_s[c, at, :] = z


def store_halves(ref, x):
    rows = x.shape[0]
    ref[0, :rows, :] = x[:, :HALF]
    ref[1, :rows, :] = x[:, HALF:]


def load_halves(ref, rows):
    return jnp.concatenate([ref[0, :rows, :], ref[1, :rows, :]], 1)


def zero_tail(ref, rows):
    tail = ref.shape[1] - rows
    ref[:, rows:, :] = jnp.zeros((2, tail, HALF), F32)


def time_forward(x, w, vec, count, group, kept):
    q_s, k_s, v_s, o_s, p_s, l_s, z1_s, u_s, z2_s = kept
    rows = count * VB
    x2 = split2(x)
    store_halves(q_s, (mmw(x2, w["q"]) + vec[0:1]) * SCALE)
    store_halves(k_s, mmw(x2, w["k"]))
    store_halves(v_s, mmw(x2, w["v"]) + vec[1:2])
    for ref in (q_s, k_s, v_s):
        zero_tail(ref, rows)

    def some(i, carry):
        units = [(c, i * UNROLL + k) for k in range(UNROLL) for c in range(2)]
        time_attend(units, group, count, q_s, k_s, v_s, o_s, p_s, l_s)
        return carry

    lax.fori_loop(0, VB // UNROLL, some, 0)
    z1 = x + mmw(split2(load_halves(o_s, rows)), w["o"]) + vec[2:3]
    z1_s[...] = z1
    h, _, _ = norm_fwd(z1, vec[3:4], vec[4:5])
    u = mmw(split2(h), w["up"]) + jnp.concatenate([vec[5:6], vec[6:7]], 1)
    u_s[...] = u
    z2 = h + mmw(split2(u * gelu_cdf(u)), w["down"]) + vec[7:8]
    z2_s[...] = z2
    return norm_fwd(z2, vec[8:9], vec[9:10])[0]


def embed_block(pieces, emb, place):
    return mmw(split2(pieces), emb) + place


TIME_W = ("q", "k", "v", "o", "up", "down")


def time_fwd_kernel(first, count, group, *refs):
    if first:
        x_ref, emb_ref, place_ref = refs[:3]
        refs = refs[3:]
    else:
        x_ref = refs[0]
        refs = refs[1:]
    w = {name: refs[i][...] for i, name in enumerate(TIME_W)}
    vec_ref, y_ref = refs[6:8]
    rows = count * VB
    if first:
        place = jnp.broadcast_to(place_ref[...], (count, VB, D)).reshape(rows, D)
        x = embed_block(x_ref[...].reshape(rows, 16), emb_ref[...], place)
    else:
        x = x_ref[...].reshape(rows, D)
    y = time_forward(x, w, vec_ref[...], count, group, refs[8:])
    y_ref[...] = y.reshape(count, VB, D)


def whole(shape):
    return pl.BlockSpec(shape, lambda i: (0,) * len(shape))


def params_spec():
    return pltpu.CompilerParams(vmem_limit_bytes=VMEM_LIMIT)


def time_weight_specs():
    return [whole((D, D))] * 4 + [whole((D, FF)), whole((FF, D)), whole((24, D))]


def time_kept(count, group, nb):
    pad, rows = group * VB, count * VB
    shapes = [(2, pad, HALF)] * 4 + [(2, VB, group, 4 * group), (2, VB, group, HALF), (rows, D), (rows, FF), (rows, D)]
    specs = [pl.BlockSpec((None,) + s, lambda i, n=len(s): (i,) + (0,) * n) for s in shapes]
    return specs, [jax.ShapeDtypeStruct((nb,) + s, F32) for s in shapes]


def time_fwd(first, x, extra, weights, count):
    group = 64 if count > 32 else 32
    nv = x.shape[1]
    width = x.shape[2]
    specs = [pl.BlockSpec((count, VB, width), lambda i: (0, i, 0))]
    if first:
        specs += [whole((16, D)), whole((count, 1, D))]
    kept_specs, kept_shapes = time_kept(count, group, nv // VB)
    out = pl.pallas_call(
        functools.partial(time_fwd_kernel, first, count, group),
        grid=(nv // VB,),
        in_specs=specs + time_weight_specs(),
        out_specs=[pl.BlockSpec((count, VB, D), lambda i: (0, i, 0))] + kept_specs,
        out_shape=[jax.ShapeDtypeStruct((count, nv, D), F32)] + kept_shapes,
        compiler_params=params_spec(),
        name="time_fwd",
    )(x, *extra, *weights)
    return out[0], out[1:]


def time_bwd_kernel(first, count, group, *refs):
    if first:
        x_ref, emb_ref, place_ref = refs[:3]
        refs = refs[3:]
    else:
        x_ref = refs[0]
        refs = refs[1:]
    dy_ref = refs[0]
    q_s, k_s, v_s, o_s, p_s, l_s, z1_s, u_s, z2_s = refs[1:10]
    w = {name: refs[10 + i][...] for i, name in enumerate(TIME_W)}
    vec_ref = refs[16]
    outs = refs[17:]
    n_out = 9 if first else 8
    g = dict(zip(TIME_W + ("rows",), outs[:7]))
    tail = outs[7:n_out]
    do_s, dq_s, dk_s, dv_s = outs[n_out:]
    rows = count * VB
    step = pl.program_id(0)

    @pl.when(step == 0)
    def _():
        for ref in list(g.values()) + (list(tail) if first else []):
            ref[...] = jnp.zeros(ref.shape, F32)

    vec = vec_ref[...]
    if first:
        place = jnp.broadcast_to(place_ref[...], (count, VB, D)).reshape(rows, D)
        pieces = x_ref[...].reshape(rows, 16)
        x = embed_block(pieces, emb_ref[...], place)
    else:
        x = x_ref[...].reshape(rows, D)
    x2 = split2(x)
    mixed = load_halves(o_s, rows)
    h, unit1, inv1 = norm_fwd(z1_s[...], vec[3:4], vec[4:5])
    u = u_s[...]
    cdf = gelu_cdf(u)
    _, unit2, inv2 = norm_fwd(z2_s[...], vec[8:9], vec[9:10])
    dy = dy_ref[...].reshape(rows, D)
    g["rows"][8] += colsum(dy * unit2)
    g["rows"][9] += colsum(dy)
    dz2 = norm_bwd(dy, unit2, inv2, vec[8:9])
    g["rows"][7] += colsum(dz2)
    dz22 = split2(dz2)
    g["down"][...] += tn3(split2(u * cdf), dz22)
    du = mmwt(dz22, w["down"]) * gelu_slope(u, cdf)
    g["rows"][5] += colsum(du[:, :D])
    g["rows"][6] += colsum(du[:, D:])
    du2 = split2(du)
    g["up"][...] += tn3(split2(h), du2)
    dh = dz2 + mmwt(du2, w["up"])
    g["rows"][3] += colsum(dh * unit1)
    g["rows"][4] += colsum(dh)
    dz1 = norm_bwd(dh, unit1, inv1, vec[3:4])
    g["rows"][2] += colsum(dz1)
    dz12 = split2(dz1)
    g["o"][...] += tn3(split2(mixed), dz12)
    store_halves(do_s, mmwt(dz12, w["o"]))
    zero_tail(do_s, rows)

    def some(i, carry):
        units = [(c, i * UNROLL_BACK + k) for k in range(UNROLL_BACK) for c in range(2)]
        time_attend_back(units, group, count, q_s, k_s, v_s, o_s, p_s, l_s, do_s, dq_s, dk_s, dv_s)
        return carry

    lax.fori_loop(0, VB // UNROLL_BACK, some, 0)
    dq = load_halves(dq_s, rows) * SCALE
    g["rows"][0] += colsum(dq)
    dq2 = split2(dq)
    g["q"][...] += tn3(x2, dq2)
    dx = dz1 + mmwt(dq2, w["q"])
    dk2 = split2(load_halves(dk_s, rows))
    g["k"][...] += tn3(x2, dk2)
    dx = dx + mmwt(dk2, w["k"])
    dv = load_halves(dv_s, rows)
    g["rows"][1] += colsum(dv)
    dv2 = split2(dv)
    g["v"][...] += tn3(x2, dv2)
    dx = dx + mmwt(dv2, w["v"])
    if first:
        tail[0][...] += tn3(split2(pieces), split2(dx))
        tail[1][...] += dx
    else:
        tail[0][...] = dx.reshape(count, VB, D)


def time_bwd(first, x, extra, dy, kept, weights, count):
    group = 64 if count > 32 else 32
    nv = x.shape[1]
    width = x.shape[2]
    pad = group * VB
    block = pl.BlockSpec((count, VB, D), lambda i: (0, i, 0))
    specs = [pl.BlockSpec((count, VB, width), lambda i: (0, i, 0))]
    if first:
        specs += [whole((16, D)), whole((count, 1, D))]
    grad_shapes = [(D, D)] * 4 + [(D, FF), (FF, D), (10, 8, D)]
    if first:
        grad_shapes += [(16, D), (count * VB, D)]
    out_specs = [whole(s) for s in grad_shapes]
    out_shape = [jax.ShapeDtypeStruct(s, F32) for s in grad_shapes]
    if not first:
        out_specs.append(block)
        out_shape.append(jax.ShapeDtypeStruct((count, nv, D), F32))
    return pl.pallas_call(
        functools.partial(time_bwd_kernel, first, count, group),
        grid=(nv // VB,),
        in_specs=specs + [block] + time_kept(count, group, nv // VB)[0] + time_weight_specs(),
        out_specs=out_specs,
        out_shape=out_shape,
        scratch_shapes=[pltpu.VMEM((2, pad, HALF), F32)] * 4,
        compiler_params=params_spec(),
        name="time_bwd",
    )(x, *extra, dy, *kept, *weights)

SB_ROWS = 64


def head_rows():
    sub = lax.broadcasted_iota(jnp.int32, (8, D), 0)
    lane = lax.broadcasted_iota(jnp.int32, (8, D), 1)
    return jnp.where(sub == lane // 32, 1.0, 0.0).astype(F32)


def spread_rows(x):
    wide = jnp.broadcast_to(x[:, None, :], (RPAD, HEADS, D)) * head_rows()[None]
    return wide.reshape(RPAD * HEADS, D)


def gather_rows(x):
    return jnp.sum(x.reshape(RPAD, HEADS, D) * head_rows()[None], 1)


PACK = 24


def pack_rows(x, last=None):
    last = jnp.zeros((1, HALF), F32) if last is None else last
    return jnp.concatenate([x[:ROUT, :HALF], x[:ROUT, HALF:], last, jnp.zeros((PACK - 2 * ROUT - 1, HALF), F32)], 0)


def unpack_rows(x):
    x = jnp.concatenate([x[:ROUT], x[ROUT : 2 * ROUT]], 1)
    return jnp.concatenate([x, jnp.zeros((RPAD - ROUT, D), F32)], 0)


def unpack_block(ref, sb):
    return jnp.concatenate([unpack_rows(ref[s]) for s in range(sb)], 0)


def pack_block(ref, x, sb):
    for s in range(sb):
        ref[s] = pack_rows(x[s * RPAD : (s + 1) * RPAD])


def valid_lane(rows):
    return lax.broadcasted_iota(jnp.int32, (rows, HALF), 1) < ROUT * HEADS


def router_reduce(x, op):
    for shift in (8, 16, 32, 64):
        x = op(x, pltpu.roll(x, shift, 1))
    return x


def merge_rows(y, pairs, vec):
    wide = y.reshape(pairs, 2, SB_ROWS, D)
    wide = jnp.concatenate([wide[:, 0].reshape(pairs * SB_ROWS, D), wide[:, 1].reshape(pairs * SB_ROWS, D)], 1)
    gain = jnp.concatenate([vec[0:1], vec[1:2]], 1)
    bias = jnp.concatenate([vec[2:3], vec[3:4]], 1)
    return norm_fwd(wide, gain, bias) + (gain,)


RECV_W = ("so", "rk", "rv", "rq", "ro", "up", "down")


def recv_buffer(o2, w, vec):
    buf2 = split2(mmw(o2, w["so"]) + vec[12:13])
    kb = mmw(buf2, w["rk"])
    vb = mmw(buf2, w["rv"]) + vec[14:15]
    segs = range(kb.shape[0] // RPAD)
    k = [split2(spread_rows(kb[s * RPAD : (s + 1) * RPAD])) for s in segs]
    v = [split2(spread_rows(vb[s * RPAD : (s + 1) * RPAD])) for s in segs]
    return buf2, k, v


def recv_forward(send, o_rows, w, vec):
    sb = send.shape[0] // SB_ROWS
    send2 = split2(send)
    o2 = split2(o_rows)
    buf2, k, v = recv_buffer(o2, w, vec)
    q = (mmw(send2, w["rq"]) + vec[13:14]) * SCALE
    segs = range(sb)
    ok = valid_lane(SB_ROWS)
    scores = [jnp.where(ok, nt3(split2(q[s * SB_ROWS : (s + 1) * SB_ROWS]), k[s]), negative) for s in segs]
    probs = [jnp.exp(sc - router_reduce(sc, jnp.maximum)) for sc in scores]
    probs = [p / router_reduce(p, jnp.add) for p in probs]
    mixed = jnp.concatenate([nn3(split2(p), v2) for p, v2 in zip(probs, v)], 0)
    z3 = send + mmw(split2(mixed), w["ro"]) + vec[15:16]
    g, unit3, inv3 = norm_fwd(z3, vec[16:17], vec[17:18])
    u = mmw(split2(g), w["up"]) + jnp.concatenate([vec[18:19], vec[19:20]], 1)
    cdf = gelu_cdf(u)
    z4 = g + mmw(split2(u * cdf), w["down"]) + vec[20:21]
    y, unit4, inv4 = norm_fwd(z4, vec[21:22], vec[22:23])
    kept = (send2, o2, buf2, mixed, g, unit3, inv3, u, cdf, unit4, inv4, q, k, v, probs)
    return y, kept, (q, mixed, jnp.concatenate(probs, 0), z3, u, z4)


def recv_restore(send, o_rows, w, vec, saved):
    q, mixed, p, z3, u, z4 = saved
    o2 = split2(o_rows)
    buf2, k, v = recv_buffer(o2, w, vec)
    g, unit3, inv3 = norm_fwd(z3, vec[16:17], vec[17:18])
    y, unit4, inv4 = norm_fwd(z4, vec[21:22], vec[22:23])
    probs = [p[s * SB_ROWS : (s + 1) * SB_ROWS] for s in range(send.shape[0] // SB_ROWS)]
    return y, (split2(send), o2, buf2, mixed, g, unit3, inv3, u, gelu_cdf(u), unit4, inv4, q, k, v, probs)


KEPT_WIDTHS = (D, D, HALF, D, FF, D)


def kept_specs(sb):
    return [pl.BlockSpec((sb * SB_ROWS, k), lambda i: (i, 0)) for k in KEPT_WIDTHS]


RECV_G = RECV_W + ("rows",)


def recv_backward(dy, kept, w, vec, g):
    send2, o2, buf2, mixed, gg, unit3, inv3, u, cdf, unit4, inv4, q, k, v, probs = kept
    sb = dy.shape[0] // SB_ROWS
    rows = g["rows"]
    rows[9] += colsum(dy * unit4)
    rows[10] += colsum(dy)
    dz4 = norm_bwd(dy, unit4, inv4, vec[21:22])
    rows[8] += colsum(dz4)
    dz42 = split2(dz4)
    g["down"][...] += tn3(split2(u * cdf), dz42)
    du = mmwt(dz42, w["down"]) * gelu_slope(u, cdf)
    rows[6] += colsum(du[:, :D])
    rows[7] += colsum(du[:, D:])
    du2 = split2(du)
    g["up"][...] += tn3(split2(gg), du2)
    dg = dz4 + mmwt(du2, w["up"])
    rows[4] += colsum(dg * unit3)
    rows[5] += colsum(dg)
    dz3 = norm_bwd(dg, unit3, inv3, vec[16:17])
    rows[3] += colsum(dz3)
    dz32 = split2(dz3)
    g["ro"][...] += tn3(split2(mixed), dz32)
    do = mmwt(dz32, w["ro"])
    segs = range(sb)
    d = [split2(do[s * SB_ROWS : (s + 1) * SB_ROWS]) for s in segs]
    dp = [nt3(d2, v2) for d2, v2 in zip(d, v)]
    ds = [split2(p * (x - router_reduce(p * x, jnp.add))) for p, x in zip(probs, dp)]
    dq = jnp.concatenate([nn3(s2, k2) for s2, k2 in zip(ds, k)], 0) * SCALE
    q = [split2(q[s * SB_ROWS : (s + 1) * SB_ROWS]) for s in segs]
    dk = jnp.concatenate([gather_rows(tn3(s2, q2)) for s2, q2 in zip(ds, q)], 0)
    dv = jnp.concatenate([gather_rows(tn3(split2(p), d2)) for p, d2 in zip(probs, d)], 0)
    rows[1] += colsum(dq)
    dq2 = split2(dq)
    g["rq"][...] += tn3(send2, dq2)
    dsend = dz3 + mmwt(dq2, w["rq"])
    dk2 = split2(dk)
    dv2 = split2(dv)
    rows[2] += colsum(dv)
    g["rk"][...] += tn3(buf2, dk2)
    g["rv"][...] += tn3(buf2, dv2)
    dbuf = mmwt(dk2, w["rk"]) + mmwt(dv2, w["rv"])
    rows[0] += colsum(dbuf)
    dbuf2 = split2(dbuf)
    g["so"][...] += tn3(o2, dbuf2)
    return dsend, mmwt(dbuf2, w["so"])


def recv_weight_specs():
    return [whole((D, D))] * 5 + [whole((D, FF)), whole((FF, D)), whole((24, D))]


def seg_block(sb, rows=SB_ROWS, width=D):
    return pl.BlockSpec((sb, rows, width), lambda i: (i, 0, 0))


def pack_spec(sb):
    return seg_block(sb, PACK, HALF)


def recv_fwd_kernel(sb, send_ref, o_ref, *refs):
    w = {n: refs[i][...] for i, n in enumerate(RECV_W)}
    vec_ref, mvec_ref, mw_ref, out_ref = refs[7:11]
    y, _, saved = recv_forward(send_ref[...].reshape(sb * SB_ROWS, D), unpack_block(o_ref, sb), w, vec_ref[...])
    for ref, x in zip(refs[11:], saved):
        ref[...] = x
    mvec = mvec_ref[...]
    wide, _, _, _ = merge_rows(y, sb // 2, mvec)
    out_ref[...] = (mmw(split2(wide), mw_ref[...]) + mvec[4:5]).reshape(sb // 2, SB_ROWS, D)


def recv_fwd(send, o, weights, mvec, mw, sb):
    n = send.shape[0]
    return pl.pallas_call(
        functools.partial(recv_fwd_kernel, sb),
        grid=(n // sb,),
        in_specs=[seg_block(sb), pack_spec(sb)] + recv_weight_specs() + [whole((8, D)), whole((2 * D, D))],
        out_specs=[seg_block(sb // 2)] + kept_specs(sb),
        out_shape=[jax.ShapeDtypeStruct((n // 2, SB_ROWS, D), F32)]
        + [jax.ShapeDtypeStruct((n * SB_ROWS, k), F32) for k in KEPT_WIDTHS],
        compiler_params=params_spec(),
        name="recv_fwd",
    )(send, o, *weights, mvec, mw)


def recv_bwd_kernel(sb, send_ref, o_ref, dx_ref, *refs):
    saved = [ref[...] for ref in refs[:6]]
    refs = refs[6:]
    w = {n: refs[i][...] for i, n in enumerate(RECV_W)}
    vec_ref, mvec_ref, mw_ref, dsend_ref, do_ref = refs[7:12]
    g = dict(zip(RECV_G, refs[12:20]))
    dmw_ref, dmv_ref = refs[20:22]

    @pl.when(pl.program_id(0) == 0)
    def _():
        for ref in list(g.values()) + [dmw_ref, dmv_ref]:
            ref[...] = jnp.zeros(ref.shape, F32)

    vec = vec_ref[...]
    y, kept = recv_restore(send_ref[...].reshape(sb * SB_ROWS, D), unpack_block(o_ref, sb), w, vec, saved)
    pairs = sb // 2
    wide, unit, inv, gain = merge_rows(y, pairs, mvec_ref[...])
    dx = dx_ref[...].reshape(pairs * SB_ROWS, D)
    dmv_ref[4] += colsum(dx)
    dx2 = split2(dx)
    dmw_ref[...] += tn3(split2(wide), dx2)
    dn = mmwt(dx2, mw_ref[...])
    part = colsum(dn * unit)
    dmv_ref[0] += part[:, :D]
    dmv_ref[1] += part[:, D:]
    part = colsum(dn)
    dmv_ref[2] += part[:, :D]
    dmv_ref[3] += part[:, D:]
    dwide = norm_bwd(dn, unit, inv, gain)
    left = dwide[:, :D].reshape(pairs, 1, SB_ROWS, D)
    right = dwide[:, D:].reshape(pairs, 1, SB_ROWS, D)
    dy = jnp.concatenate([left, right], 1).reshape(sb * SB_ROWS, D)
    dsend, do = recv_backward(dy, kept, w, vec, g)
    dsend_ref[...] = dsend.reshape(sb, SB_ROWS, D)
    pack_block(do_ref, do, sb)


RECV_GRADS = [(D, D)] * 5 + [(D, FF), (FF, D), (11, 8, D)]


def recv_bwd(send, o, dx, kept, weights, mvec, mw, sb):
    n = send.shape[0]
    shapes = RECV_GRADS + [(2 * D, D), (5, 8, D)]
    return pl.pallas_call(
        functools.partial(recv_bwd_kernel, sb),
        grid=(n // sb,),
        in_specs=[seg_block(sb), pack_spec(sb), seg_block(sb // 2)]
        + kept_specs(sb)
        + recv_weight_specs()
        + [whole((8, D)), whole((2 * D, D))],
        out_specs=[seg_block(sb), pack_spec(sb)] + [whole(s) for s in shapes],
        out_shape=[jax.ShapeDtypeStruct((n, SB_ROWS, D), F32), jax.ShapeDtypeStruct(o.shape, F32)]
        + [jax.ShapeDtypeStruct(s, F32) for s in shapes],
        compiler_params=params_spec(),
        name="recv_bwd",
    )(send, o, dx, *kept, *weights, mvec, mw)


def tail_kernel(sb, send_ref, o_ref, tgt_ref, kept_ref, scale_ref, mean_ref, *refs):
    w = {n: refs[i][...] for i, n in enumerate(RECV_W)}
    vec_ref, head_ref, dsend_ref, do_ref = refs[7:11]
    g = dict(zip(RECV_G, refs[11:19]))
    dhead_ref = refs[19]

    @pl.when(pl.program_id(0) == 0)
    def _():
        for ref in list(g.values()) + [dhead_ref]:
            ref[...] = jnp.zeros(ref.shape, F32)

    vec = vec_ref[...]
    rows = sb * SB_ROWS
    y, kept, _ = recv_forward(
        send_ref[...].reshape(rows, D), unpack_block(o_ref, sb), w, vec
    )
    head = head_ref[...]
    y2 = split2(y)
    scale = jnp.broadcast_to(scale_ref[...][None], (sb, SB_ROWS, PPAD)).reshape(rows, PPAD)
    mean = jnp.broadcast_to(mean_ref[...][None], (sb, SB_ROWS, PPAD)).reshape(rows, PPAD)
    misfit = mmwt(y2, head) * scale + mean - tgt_ref[...].reshape(rows, PPAD)
    dpred = kept_ref[...].reshape(rows, PPAD) * misfit * scale
    dpred2 = split2(dpred)
    dhead_ref[...] += tn3(dpred2, y2)
    dy = mmw(dpred2, head)
    dsend, do = recv_backward(dy, kept, w, vec, g)
    dsend_ref[...] = dsend.reshape(sb, SB_ROWS, D)
    pack_block(do_ref, do, sb)


def tail(send, o, tgt, kept, scale, mean, weights, head, sb):
    n = send.shape[0]
    shapes = RECV_GRADS + [(PPAD, D)]
    return pl.pallas_call(
        functools.partial(tail_kernel, sb),
        grid=(n // sb,),
        in_specs=[seg_block(sb), pack_spec(sb), seg_block(sb, SB_ROWS, PPAD), seg_block(sb, SB_ROWS, PPAD)]
        + [whole((SB_ROWS, PPAD))] * 2
        + recv_weight_specs()
        + [whole((PPAD, D))],
        out_specs=[seg_block(sb), pack_spec(sb)] + [whole(s) for s in shapes],
        out_shape=[jax.ShapeDtypeStruct((n, SB_ROWS, D), F32), jax.ShapeDtypeStruct(o.shape, F32)]
        + [jax.ShapeDtypeStruct(s, F32) for s in shapes],
        compiler_params=params_spec(),
        name="tail",
    )(send, o, tgt, kept, scale, mean, *weights, head)


SEND_W = ("sq", "sk", "sv")


def send_project(dim2, r_rows, w, vec):
    r2 = split2(r_rows)
    sb = r_rows.shape[0] // RPAD
    k = mmw(dim2, w["sk"])
    v = mmw(dim2, w["sv"]) + vec[11:12]
    q = (mmw(r2, w["sq"]) + vec[10:11]) * SCALE
    k = [split2(k[s * SB_ROWS : (s + 1) * SB_ROWS]) for s in range(sb)]
    v = [split2(v[s * SB_ROWS : (s + 1) * SB_ROWS]) for s in range(sb)]
    q = [split2(spread_rows(q[s * RPAD : (s + 1) * RPAD])) for s in range(sb)]
    return r2, k, v, q


def send_fwd_kernel(sb, dim_ref, r_ref, here_ref, *refs):
    w = {n: refs[i][...] for i, n in enumerate(SEND_W)}
    vec_ref, o_ref = refs[3:]
    dim2 = split2(dim_ref[...].reshape(sb * SB_ROWS, D))
    _, k, v, q = send_project(dim2, r_ref[...].reshape(sb * RPAD, D), w, vec_ref[...])
    here = here_ref[...] > 0.5
    scores = [jnp.where(here, nt3(k2, q2), negative) for k2, q2 in zip(k, q)]
    tops = [jnp.max(sc, 0, keepdims=True) for sc in scores]
    probs = [jnp.where(here, jnp.exp(sc - top), 0.0) for sc, top in zip(scores, tops)]
    totals = [jnp.sum(p, 0, keepdims=True) for p in probs]
    safe = [jnp.where(t > 0.0, t, 1.0) for t in totals]
    mixed = [gather_rows(tn3(split2(p / t), v2)) for p, t, v2 in zip(probs, safe, v)]
    for s in range(sb):
        lse = jnp.where(totals[s] > 0.0, tops[s] + jnp.log(safe[s]), negative)
        o_ref[s] = pack_rows(mixed[s], lse)


def send_weight_specs():
    return [whole((D, D))] * 3 + [whole((24, D))]


def send_fwd(dim, routers, here, weights, sb, npad):
    n = dim.shape[0]
    return pl.pallas_call(
        functools.partial(send_fwd_kernel, sb),
        grid=(n // sb,),
        in_specs=[seg_block(sb), seg_block(sb, RPAD), whole((SB_ROWS, HALF))] + send_weight_specs(),
        out_specs=pack_spec(sb),
        out_shape=jax.ShapeDtypeStruct((npad, PACK, HALF), F32),
        compiler_params=params_spec(),
        name="send_fwd",
    )(dim, routers, here, *weights)


def send_bwd_kernel(sb, dim_ref, dpart_ref, r_ref, o_ref, do_ref, here_ref, *refs):
    w = {n: refs[i][...] for i, n in enumerate(SEND_W)}
    vec_ref, ddim_ref, dr_ref = refs[3:6]
    dsq_ref, dsk_ref, dsv_ref, rows = refs[6:10]

    @pl.when(pl.program_id(0) == 0)
    def _():
        for ref in (dsq_ref, dsk_ref, dsv_ref, rows):
            ref[...] = jnp.zeros(ref.shape, F32)

    dim2 = split2(dim_ref[...].reshape(sb * SB_ROWS, D))
    r2, k, v, q = send_project(dim2, r_ref[...].reshape(sb * RPAD, D), w, vec_ref[...])
    here = (here_ref[...] > 0.5) & valid_lane(SB_ROWS)
    segs = range(sb)
    scores = [nt3(k2, q2) for k2, q2 in zip(k, q)]
    probs = [jnp.where(here, jnp.exp(scores[s] - o_ref[s][2 * ROUT : 2 * ROUT + 1]), 0.0) for s in segs]
    dwide = [spread_rows(unpack_rows(do_ref[s])) for s in segs]
    owide = [
        jnp.broadcast_to(unpack_rows(o_ref[s])[:, None, :], (RPAD, HEADS, D)).reshape(RPAD * HEADS, D) for s in segs
    ]
    e = [split2(a * b) for a, b in zip(dwide, owide)]
    d = [split2(a) for a in dwide]
    one_row = jnp.ones((8, D), BF)
    means = [(dots(one_row, e2[0], 1, 1) + dots(one_row, e2[1], 1, 1))[0:1] for e2 in e]
    dp = [nt3(v2, d2) for v2, d2 in zip(v, d)]
    ds = [split2(p * (x - mean)) for p, x, mean in zip(probs, dp, means)]
    dk = jnp.concatenate([nn3(s2, q2) for s2, q2 in zip(ds, q)], 0)
    dv = jnp.concatenate([nn3(split2(p), d2) for p, d2 in zip(probs, d)], 0)
    dq = jnp.concatenate([gather_rows(tn3(s2, k2)) for s2, k2 in zip(ds, k)], 0) * SCALE
    dk2 = split2(dk)
    dv2 = split2(dv)
    rows[1] += colsum(dv)
    dsk_ref[...] += tn3(dim2, dk2)
    dsv_ref[...] += tn3(dim2, dv2)
    out = dpart_ref[...].reshape(sb * SB_ROWS, D) + mmwt(dk2, w["sk"]) + mmwt(dv2, w["sv"])
    ddim_ref[...] = out.reshape(sb, SB_ROWS, D)
    rows[0] += colsum(dq)
    dq2 = split2(dq)
    dsq_ref[...] += tn3(r2, dq2)
    dr_ref[...] = mmwt(dq2, w["sq"]).reshape(sb, RPAD, D)


def send_bwd(dim, dpart, routers, o, do, here, weights, sb):
    n = dim.shape[0]
    shapes = [(D, D)] * 3 + [(2, 8, D)]
    return pl.pallas_call(
        functools.partial(send_bwd_kernel, sb),
        grid=(n // sb,),
        in_specs=[seg_block(sb), seg_block(sb), seg_block(sb, RPAD), pack_spec(sb), pack_spec(sb), whole((SB_ROWS, HALF))]
        + send_weight_specs(),
        out_specs=[seg_block(sb), seg_block(sb, RPAD)] + [whole(s) for s in shapes],
        out_shape=[jax.ShapeDtypeStruct((n, SB_ROWS, D), F32), jax.ShapeDtypeStruct((n, RPAD, D), F32)]
        + [jax.ShapeDtypeStruct(s, F32) for s in shapes],
        compiler_params=params_spec(),
        name="send_bwd",
    )(dim, dpart, routers, o, do, here, *weights)

MESH = pl.DeviceIdType.MESH
ANY = pl.BlockSpec(memory_space=pl.ANY)
INVMEM = pl.BlockSpec(memory_space=pltpu.VMEM)


def grid_sizes():
    nf = lax.axis_size("fsdp")
    nx = 1
    while 2 * nx * nx < nf:
        nx *= 2
    return lax.axis_size("dp") // 2, nf // nx, nx


class Place:
    def __init__(self):
        self.ny, self.nz, self.nx = grid_sizes()
        dp, fs = lax.axis_index("dp"), lax.axis_index("fsdp")
        self.core, self.y = lax.rem(dp, 2), lax.div(dp, 2)
        self.x, self.z = lax.rem(fs, self.nx), lax.div(fs, self.nx)

    def at(self, y=None, core=None, z=None, x=None):
        y = self.y if y is None else y
        core = self.core if core is None else core
        z = self.z if z is None else z
        x = self.x if x is None else x
        return (y * 2 + core, z * self.nx + x)

    def other(self):
        return 1 - self.core

    def next_x(self, k):
        return lax.rem(self.x + k, self.nx)

    def next_y(self, k):
        return lax.rem(self.y + k, self.ny)

    def next_z(self, k):
        return lax.rem(self.z + k, self.nz)

    def neighbours(self):
        out = [self.at(core=self.other())]
        out += [self.at(x=self.next_x(k)) for k in range(1, self.nx)]
        out += [self.at(y=self.next_y(k)) for k in range(1, self.ny)]
        out += [self.at(z=self.next_z(k)) for k in range(1, self.nz)]
        return out


def greet(devices):
    barrier = pltpu.get_barrier_semaphore()
    for device in devices:
        pl.semaphore_signal(barrier, inc=1, device_id=device, device_id_type=MESH)
    pl.semaphore_wait(barrier, len(devices))


def remote(src, dst, send, recv, device):
    return pltpu.make_async_remote_copy(
        src_ref=src, dst_ref=dst, send_sem=send, recv_sem=recv, device_id=device, device_id_type=MESH
    )


def gather_kernel(n, *refs):
    shards, outs = refs[:n], refs[n : 2 * n]
    send, recv, local = refs[2 * n :]
    me = Place()
    y, c, z, x = me.y, me.core, me.z, me.x
    m = me.nx
    greet(me.neighbours())
    copies, slot = [], [0]

    def push(src, dst, device):
        copy = remote(src, dst, send.at[slot[0]], recv.at[slot[0]], device)
        slot[0] += 1
        copy.start()
        return copy

    own = [pltpu.make_async_copy(shards[j], outs[j].at[y, c, z, x], local.at[j]) for j in range(n)]
    for copy in own:
        copy.start()
    first = [
        push(shards[j], outs[j].at[y, c, z, x], me.at(z=me.next_z(k))) for j in range(n) for k in range(1, me.nz)
    ]
    for copy in own:
        copy.wait()
    for copy in first:
        copy.wait()
    base = slot[0]

    def rest(by_core):
        slot[0] = base
        shared, started = [], []
        sibling = me.at(core=1 - by_core)
        second = []
        for j in range(n):
            piece = outs[j].at[y, by_core, :, x]
            for k in range(1, m):
                peer = me.at(x=me.next_x(k)) if by_core == 0 else me.at(y=me.next_y(k))
                second.append(push(piece, piece, peer))
            shared.append(push(piece, piece, sibling))
        for copy in second:
            copy.wait()
        third = []
        for j in range(n):
            wide = outs[j].at[y, by_core] if by_core == 0 else outs[j].at[:, by_core, :, x]
            for k in range(1, m):
                peer = me.at(y=me.next_y(k)) if by_core == 0 else me.at(x=me.next_x(k))
                third.append(push(wide, wide, peer))
            for k in range(1, m):
                piece = outs[j].at[y, by_core, :, me.next_x(k)] if by_core == 0 else outs[j].at[me.next_y(k), by_core, :, x]
                shared.append(push(piece, piece, sibling))
        for copy in third:
            copy.wait()
        for j in range(n):
            for k in range(1, m):
                wide = outs[j].at[me.next_y(k), by_core] if by_core == 0 else outs[j].at[:, by_core, :, me.next_x(k)]
                shared.append(push(wide, wide, sibling))
        for copy in shared:
            copy.wait()

    for by_core in (0, 1):
        pl.when(c == by_core)(functools.partial(rest, by_core))


def gather_all(shards):
    ny, nz, nx = grid_sizes()
    n = len(shards)
    count = n * ((nz - 1) + (nx - 1) + 1 + (nx - 1) * 3)
    return pl.pallas_call(
        functools.partial(gather_kernel, n),
        in_specs=[ANY] * n,
        out_specs=[ANY] * n,
        out_shape=[jax.ShapeDtypeStruct((ny, 2, nz, nx) + s.shape, s.dtype) for s in shards],
        scratch_shapes=[pltpu.SemaphoreType.DMA((count,)), pltpu.SemaphoreType.DMA((count,)), pltpu.SemaphoreType.DMA((n,))],
        compiler_params=pltpu.CompilerParams(collective_id=0, has_side_effects=True, vmem_limit_bytes=16 << 20),
        name="gather_all",
    )(*shards)


def add_into(acc, at, terms, rows):
    total = acc[at]
    for ref, index in terms:
        total = total + ref[index]
    acc[at] = total


def scatter_kernel(n, *refs):
    grads, tile_ref = refs[:n], refs[n]
    outs, stat_ref = refs[n + 1 : 2 * n + 1], refs[2 * n + 1]
    acc, r1, r2, r3, r4 = (refs[2 * n + 2 + i * n : 2 * n + 2 + (i + 1) * n] for i in range(5))
    tc, tx, ty, tz, send, recv, local = refs[7 * n + 2 :]
    me = Place()
    y, c, z, x = me.y, me.core, me.z, me.x
    ny, nz, nx, m = me.ny, me.nz, me.nx, me.nx
    greet(me.neighbours())
    slot = [0]

    def push(src, dst, device):
        copy = remote(src, dst, send.at[slot[0]], recv.at[slot[0]], device)
        slot[0] += 1
        copy.start()
        return copy

    stage, own = [], []
    for j in range(n):
        stage.append([push(grads[j].at[:, me.other(), :, k], r1[j].at[:, k], me.at(core=me.other())) for k in range(nx)])
        mine = [
            pltpu.make_async_copy(grads[j].at[:, c, :, k], acc[j].at[:, k], local.at[j * nx + k]) for k in range(nx)
        ]
        for copy in mine:
            copy.start()
        own.append(mine)
    base = slot[0]

    def rest(by_core):
        slot[0] = base
        two, three, four = [], [], []
        for j in range(n):
            for copy in own[j] + stage[j]:
                copy.wait()

            def add1(i, carry):
                at = (lax.div(i, nx * nz), lax.rem(lax.div(i, nz), nx), lax.rem(i, nz))
                add_into(acc[j], at, [(r1[j], at)], None)
                return carry

            lax.fori_loop(0, ny * nx * nz, add1, 0)
            if by_core == 0:
                two.append([push(acc[j].at[:, me.next_x(k)], r2[j].at[k - 1], me.at(x=me.next_x(k))) for k in range(1, m)])
            else:
                two.append([push(acc[j].at[me.next_y(k)], r2[j].at[k - 1], me.at(y=me.next_y(k))) for k in range(1, m)])
        for j in range(n):
            for copy in two[j]:
                copy.wait()

            def add2(i, carry):
                a, b = lax.div(i, nz), lax.rem(i, nz)
                at = (a, x, b) if by_core == 0 else (y, a, b)
                add_into(acc[j], at, [(r2[j], (k, a, b)) for k in range(m - 1)], None)
                return carry

            lax.fori_loop(0, m * nz, add2, 0)
            if by_core == 0:
                three.append([push(acc[j].at[me.next_y(k), x], r3[j].at[k - 1], me.at(y=me.next_y(k))) for k in range(1, m)])
            else:
                three.append([push(acc[j].at[y, me.next_x(k)], r3[j].at[k - 1], me.at(x=me.next_x(k))) for k in range(1, m)])
        for j in range(n):
            for copy in three[j]:
                copy.wait()

            def add3(i, carry):
                add_into(acc[j], (y, x, i), [(r3[j], (k, i)) for k in range(m - 1)], None)
                return carry

            lax.fori_loop(0, nz, add3, 0)
            four.append(
                [push(acc[j].at[y, x, me.next_z(k)], r4[j].at[k - 1], me.at(z=me.next_z(k))) for k in range(1, nz)]
            )
        squares = jnp.zeros((8, HALF), F32)
        for j in range(n):
            for copy in four[j]:
                copy.wait()
            total = acc[j][y, x, z]
            for k in range(nz - 1):
                total = total + r4[j][k]
            outs[j][...] = total
            sq = colsum_any(total * total)
            squares = squares + sq[:, :HALF] + sq[:, HALF:]
        tc[c] = jnp.concatenate([squares, tile_ref[...]], 0)

    for by_core in (0, 1):
        pl.when(c == by_core)(functools.partial(rest, by_core))

    slot[0] = base + n * ((m - 1) * 2 + nz - 1)
    push(tc.at[c], tc.at[c], me.at(core=me.other())).wait()
    tx[x] = tc[0] + tc[1]
    for copy in [push(tx.at[x], tx.at[x], me.at(x=me.next_x(k))) for k in range(1, nx)]:
        copy.wait()
    ty[y] = functools.reduce(jnp.add, [tx[k] for k in range(nx)])
    for copy in [push(ty.at[y], ty.at[y], me.at(y=me.next_y(k))) for k in range(1, ny)]:
        copy.wait()
    tz[z] = functools.reduce(jnp.add, [ty[k] for k in range(ny)])
    for copy in [push(tz.at[z], tz.at[z], me.at(z=me.next_z(k))) for k in range(1, nz)]:
        copy.wait()
    stat_ref[...] = functools.reduce(jnp.add, [tz[k] for k in range(nz)])


def colsum_any(x):
    rows = x.shape[0]
    even = rows // 8 * 8
    out = colsum(x[:even]) if even else jnp.zeros((8, x.shape[1]), F32)
    if rows > even:
        out = out + jnp.pad(x[even:], ((0, 8 - rows + even), (0, 0)))
    return out


def scatter_sum(grads, tile):
    ny, nz, nx = grid_sizes()
    n = len(grads)
    shapes = [g.shape[-2:] for g in grads]
    count = n * nx + n * ((nx - 1) * 2 + nz - 1) + 1 + (nx - 1) + (ny - 1) + (nz - 1)

    def buffers(*lead):
        return [pltpu.VMEM(lead + s, F32) for s in shapes]

    return pl.pallas_call(
        functools.partial(scatter_kernel, n),
        in_specs=[ANY] * n + [INVMEM],
        out_specs=[INVMEM] * (n + 1),
        out_shape=[jax.ShapeDtypeStruct(s, F32) for s in shapes] + [jax.ShapeDtypeStruct((16, HALF), F32)],
        scratch_shapes=buffers(ny, nx, nz)
        + buffers(ny, nx, nz)
        + buffers(nx - 1, nx, nz)
        + buffers(nx - 1, nz)
        + buffers(nz - 1)
        + [pltpu.VMEM((k, 16, HALF), F32) for k in (2, nx, ny, nz)]
        + [pltpu.SemaphoreType.DMA((count,)), pltpu.SemaphoreType.DMA((count,)), pltpu.SemaphoreType.DMA((n * nx,))],
        compiler_params=pltpu.CompilerParams(collective_id=1, has_side_effects=True, vmem_limit_bytes=VMEM_LIMIT),
        name="scatter_sum",
    )(*grads, tile)


def group_kernel(stats, per, in_ref, out_ref, got, result, send, recv, local):
    nf = lax.axis_size("fsdp")
    dp, f = lax.axis_index("dp"), lax.axis_index("fsdp")
    peers = [lax.rem(f + k, nf) for k in range(1, nf)]
    greet([(dp, p) for p in peers])

    def part(ref, who):
        return ref.at[pl.ds(pl.multiple_of(who * per, per), per)]

    own = pltpu.make_async_copy(part(in_ref, f), got.at[f], local)
    own.start()
    copies = [
        remote(part(in_ref, p), got.at[f], send.at[k], recv.at[k], (dp, p)) for k, p in enumerate(peers)
    ]
    for copy in copies:
        copy.start()
    own.wait()
    for copy in copies:
        copy.wait()
    if stats:
        row = lax.broadcasted_iota(jnp.int32, (PACK, HALF), 0)
        lane = lax.broadcasted_iota(jnp.int32, (PACK, HALF), 1)
        router = jnp.where(row < ROUT, row, row - ROUT)
        pick = (lane // 8 == router) & (row < 2 * ROUT)
        src = lax.broadcasted_iota(jnp.int32, (HALF, D), 0)
        dst = lax.broadcasted_iota(jnp.int32, (HALF, D), 1)
        widen = jnp.where(src % 8 == dst // 32, 1.0, 0.0).astype(BF)

        def one(s, carry):
            lse = [got[d, s, 2 * ROUT : 2 * ROUT + 1, :] for d in range(nf)]
            top = functools.reduce(jnp.maximum, lse)
            total = top + jnp.log(functools.reduce(jnp.add, [jnp.exp(l - top) for l in lse]))
            out = jnp.where(row == 2 * ROUT, total, 0.0)
            share = jnp.concatenate([jnp.where(pick, jnp.exp(l - total), 0.0) for l in lse], 0)
            wide = mmw(split2(share), widen)
            for d in range(nf):
                w = wide[d * PACK : (d + 1) * PACK]
                w = jnp.where(row < ROUT, w[:, :HALF], w[:, HALF:])
                out = out + jnp.where(row < 2 * ROUT, w * got[d, s], 0.0)
            result[s] = out
            return carry

        lax.fori_loop(0, per, one, 0)
    else:
        result[...] = functools.reduce(jnp.add, [got[d] for d in range(nf)])
    own = pltpu.make_async_copy(result, part(out_ref, f), local)
    own.start()
    copies = [
        remote(result, part(out_ref, f), send.at[nf - 1 + k], recv.at[nf - 1 + k], (dp, p)) for k, p in enumerate(peers)
    ]
    for copy in copies:
        copy.start()
    own.wait()
    for copy in copies:
        copy.wait()


def group_combine(packed, stats, cid):
    nf = lax.axis_size("fsdp")
    per = packed.shape[0] // nf
    return pl.pallas_call(
        functools.partial(group_kernel, stats, per),
        in_specs=[INVMEM],
        out_specs=INVMEM,
        out_shape=jax.ShapeDtypeStruct(packed.shape, F32),
        scratch_shapes=[
            pltpu.VMEM((nf, per, PACK, HALF), F32),
            pltpu.VMEM((per, PACK, HALF), F32),
            pltpu.SemaphoreType.DMA((2 * nf - 2,)),
            pltpu.SemaphoreType.DMA((2 * nf - 2,)),
            pltpu.SemaphoreType.DMA,
        ],
        compiler_params=pltpu.CompilerParams(collective_id=cid, has_side_effects=True, vmem_limit_bytes=32 << 20),
        name="group_stats" if stats else "group_sum",
    )(packed)


def series_stats(series, observed):
    seen = observed.astype(F32)
    counted = jnp.maximum(jnp.sum(seen, -1, keepdims=True), 1.0)
    mean = jnp.sum(seen * series, -1, keepdims=True) / counted
    center = (series - mean) * seen
    scale = jnp.sqrt(jnp.sum(center * center, -1, keepdims=True) / counted + norm_eps)
    return center / scale, mean, scale


def adam_update(weight, first_moment, second_moment, gradient):
    first_new = beta_one * first_moment + (1.0 - beta_one) * gradient
    second_new = beta_two * second_moment + (1.0 - beta_two) * gradient * gradient
    corrected = (
        first_new
        / (1.0 - beta_one**step_count)
        / (jnp.sqrt(second_new / (1.0 - beta_two**step_count)) + adam_eps)
    )
    return (weight - learn_rate * (corrected + weight_decay * weight), first_new, second_new)


def segment_major(x, width):
    nv = x.shape[0]
    x = x.reshape(nv, -1, 12).transpose(1, 0, 2)
    return jnp.pad(x, ((0, 0), (0, 0), (0, width - 12)))


def pad_rows(x, rows):
    return jnp.pad(x, ((0, rows - x.shape[0]), (0, 0)))


def gradient_parts(series, observed, targets, target_mask, present, square, up, down, vectors, combine, nf):
    nv = series.shape[0]
    normed, mean, scale = series_stats(series, observed)
    pieces = segment_major(normed, 16)
    factor = 2.0 / (1 << 20)
    kept = segment_major(target_mask.astype(F32) * present[:, None] * factor, PPAD)
    tgt = segment_major(targets, PPAD)
    scale16 = jnp.broadcast_to(scale, (nv, PPAD))
    mean16 = jnp.broadcast_to(mean, (nv, PPAD))
    here = jnp.broadcast_to(present[:, None], (nv, HALF))

    emb = pad_rows(vectors[:12], 16).astype(BF)
    place = (vectors[12:13] + vectors[13:73])[:, None, :]
    layer_start = SEGLEN + 1 + SEG
    vecs = [pad_rows(vectors[layer_start + 23 * l : layer_start + 23 * l + 23], 24) for l in range(2)]
    merge_at = layer_start + 46
    mvec = pad_rows(vectors[merge_at : merge_at + 5], 8)
    mw = square[24:26].reshape(2 * D, D)
    head = pad_rows(vectors[merge_at + 5 : merge_at + 17], PPAD).astype(BF)
    router_at = merge_at + 17
    routers = []
    for l, n in ((0, SEG), (1, SEG // 2)):
        r = vectors[router_at + l * SEG * ROUT : router_at + l * SEG * ROUT + n * ROUT].reshape(n, ROUT, D)
        routers.append(jnp.pad(r, ((0, 0), (0, RPAD - ROUT), (0, 0))))
    time_w = [
        (*[square[12 * l + i] for i in (0, 1, 2, 3)], up[2 * l], down[2 * l], vecs[l]) for l in range(2)
    ]
    send_w = [(*[square[12 * l + i] for i in (4, 5, 6)], vecs[l]) for l in range(2)]
    recv_w = [
        (*[square[12 * l + i] for i in (7, 9, 10, 8, 11)], up[2 * l + 1], down[2 * l + 1], vecs[l]) for l in range(2)
    ]

    sb0, sb1, sf0, sf1, st = 12, 10, 20, 10, 10
    rf, rb = 20, 20
    dim0, kept0 = time_fwd(True, pieces, (emb, place), time_w[0], SEG)
    o0 = send_fwd(dim0, routers[0], here, send_w[0], sf0, -(-SEG // nf) * nf)
    o0 = combine(o0, True, 2)
    x1, *saved = recv_fwd(dim0, o0, recv_w[0], mvec, mw, rf)
    dim1, kept1 = time_fwd(False, x1, (), time_w[1], SEG // 2)
    o1 = send_fwd(dim1, routers[1], here, send_w[1], sf1, -(-SEG // 2 // nf) * nf)
    o1 = combine(o1, True, 3)
    out = tail(dim1, o1, tgt, kept, scale16, mean16, recv_w[1], head, st)
    ddim1, do1, grecv1, dhead = out[0], out[1], out[2:10], out[10]
    do1 = combine(do1, False, 4)
    out = send_bwd(dim1, ddim1, routers[1], o1, do1, here, send_w[1], sb1)
    ddim1, dr1, gsend1 = out[0], out[1], out[2:]
    out = time_bwd(False, x1, (), ddim1, kept1, time_w[1], SEG // 2)
    gtime1, dx1 = out[:7], out[7]
    out = recv_bwd(dim0, o0, dx1, saved, recv_w[0], mvec, mw, rb)
    ddim0, do0, grecv0, dmw, dmv = out[0], out[1], out[2:10], out[10], out[11]
    do0 = combine(do0, False, 5)
    out = send_bwd(dim0, ddim0, routers[0], o0, do0, here, send_w[0], sb0)
    ddim0, dr0, gsend0 = out[0], out[1], out[2:]
    out = time_bwd(True, pieces, (emb, place), ddim0, kept0, time_w[0], SEG)
    gtime0, demb, dplace = out[:7], out[7], out[8]

    mats, ups, downs, rows = [], [], [], []
    for gt, gs, gr in ((gtime0, gsend0, grecv0), (gtime1, gsend1, grecv1)):
        mats += [gt[0], gt[1], gt[2], gt[3], gs[0], gs[1], gs[2], gr[0], gr[3], gr[1], gr[2], gr[4]]
        ups += [gt[4], gr[5]]
        downs += [gt[5], gr[6]]
        rt, rs, rr = gt[6].sum(1), gs[3].sum(1), gr[7].sum(1)
        rows += [rt, rs, rr]
    mats += [dmw]
    dplace = dplace.reshape(SEG, VB, D).sum(1)
    vec = jnp.concatenate(
        [demb[:12], dplace.sum(0, keepdims=True), dplace]
        + rows
        + [dmv.sum(1), dhead[:12]]
        + [dr[:, :ROUT].reshape(-1, D) for dr in (dr0, dr1)],
        0,
    )
    return jnp.concatenate(mats, 0), jnp.concatenate(ups, 0), jnp.concatenate(downs, 0), vec


def on_device(series, observed, targets, target_mask, counts, matrices, feed_weights, vectors, matrices_first, matrices_second, feed_first, feed_second, vectors_first, vectors_second):
    local_vars = series.shape[1]
    nf = lax.axis_size("fsdp")
    devices = nf * lax.axis_size("dp")
    slot = lax.axis_index("fsdp") * local_vars + jnp.arange(local_vars, dtype=jnp.int32)
    present = (slot < counts[0]).astype(F32)
    own_rows = NVEC * D // devices
    vec_rows = -(-own_rows // D)

    def as_rows(x):
        return x.reshape(-1, D)

    def pad_flat(x):
        return jnp.pad(x, [(0, 0)] * (x.ndim - 1) + [(0, vec_rows * D - own_rows)])

    square, feed, vecs = gather_all(
        [as_rows(matrices.astype(BF)), as_rows(feed_weights.astype(BF)), as_rows(pad_flat(vectors.astype(BF)))]
    )
    square = square.reshape(NSQ, D, D)
    feed = feed.reshape(-1, D)
    up = feed[: 4 * FF].reshape(4, D, FF)
    down = feed[4 * FF :].reshape(4, FF, D)
    vecs = vecs.reshape(devices, -1)[:, :own_rows].reshape(NVEC, D).astype(F32)
    g_mat, g_up, g_down, g_vec = gradient_parts(
        series[0], observed[0], targets[0], target_mask[0], present, square, up, down, vecs, group_combine, nf
    )
    g_feed = jnp.concatenate([g_up.reshape(-1, D), g_down], 0)
    g_vec = pad_flat(g_vec.reshape(devices, own_rows))
    ny, nz, nx = grid_sizes()
    lead = (ny, 2, nz, nx)
    kept = target_mask[0].astype(F32) * present[:, None]
    tile = jnp.pad(jnp.sum(kept).reshape(1, 1), ((0, 7), (0, HALF - 1)))
    s_mat, s_feed, s_vec, sums = scatter_sum(
        [g_mat.reshape(lead + (-1, D)), g_feed.reshape(lead + (-1, D)), g_vec.reshape(lead + (-1, D))], tile
    )
    shards = (s_mat.reshape(-1), s_feed.reshape(-1), s_vec.reshape(-1)[:own_rows])
    upscale = (1 << 20) / jnp.maximum(jnp.sum(sums[8:]), 1.0)
    grad_norm = jnp.sqrt(jnp.sum(sums[:8])) * upscale
    factor = upscale * (clip_norm / jnp.maximum(grad_norm, clip_norm))
    new = (
        adam_update(matrices, matrices_first, matrices_second, shards[0] * factor)
        + adam_update(feed_weights, feed_first, feed_second, shards[1] * factor)
        + adam_update(vectors, vectors_first, vectors_second, shards[2] * factor)
    )
    return (grad_norm,) + new


def solution(mesh):
    both = P(("dp", "fsdp"))
    data = P("dp", "fsdp", None)
    return jax.shard_map(
        on_device,
        mesh=mesh,
        in_specs=(data,) * 4 + (P("dp"),) + (both,) * 9,
        out_specs=(P(),) + (both,) * 9,
        check_vma=False,
    )
```

```python
import functools
import jax
import jax.numpy as jnp
from jax import lax
from jax.experimental import pallas as pl
from jax.experimental.pallas import tpu as pltpu
from jax.sharding import PartitionSpec as P

D = 256
HEADS = 8
FF = 512
ROUT = 10
RPAD = 16
SEGLEN = 12
PRED = 12
PPAD = 16
SEG = 60
NSQ = 26
NVEC = 1036
HALF = 128
VB = 8
UNROLL = 8
UNROLL_BACK = 8

BF = jnp.bfloat16
F32 = jnp.float32
SCALE = (D // HEADS) ** (-0.5)
negative = -1e30
norm_eps = 1e-05
beta_one = 0.9
beta_two = 0.999
adam_eps = 1e-08
weight_decay = 0.01
learn_rate = 0.2
clip_norm = 0.01
step_count = 10.0
VMEM_LIMIT = 60 << 20


ANY = pl.BlockSpec(memory_space=pl.ANY)
INVMEM = pl.BlockSpec(memory_space=pltpu.VMEM)


def split2(x):
    hi = x.astype(BF)
    return hi, (x - hi.astype(F32)).astype(BF)


def dots(a, b, ca, cb):
    return lax.dot_general(a, b, (((ca,), (cb,)), ((), ())), preferred_element_type=F32)


def mmw(x2, w):
    return dots(x2[0], w, 1, 0) + dots(x2[1], w, 1, 0)


def mmwt(x2, w):
    return dots(x2[0], w, 1, 1) + dots(x2[1], w, 1, 1)


def rows2(a2):
    return jnp.concatenate([a2[0], a2[1]], 0)


def nn3(a2, b2):
    m = a2[0].shape[0]
    both = dots(rows2(a2), b2[0], 1, 0)
    return both[:m] + both[m:] + dots(a2[0], b2[1], 1, 0)


def nt3(a2, b2):
    m = a2[0].shape[0]
    both = dots(rows2(a2), b2[0], 1, 1)
    return both[:m] + both[m:] + dots(a2[0], b2[1], 1, 1)


def tn3(a2, b2):
    n = b2[0].shape[1]
    both = dots(a2[0], jnp.concatenate([b2[0], b2[1]], 1), 0, 0)
    return both[:, :n] + both[:, n:] + dots(a2[1], b2[0], 0, 0)


def norm_fwd(z, gain, bias):
    center = z - jnp.mean(z, -1, keepdims=True)
    inv = lax.rsqrt(jnp.mean(center * center, -1, keepdims=True) + norm_eps)
    unit = center * inv
    return unit * gain + bias, unit, inv


def norm_bwd(dy, unit, inv, gain):
    t = dy * gain
    return inv * (t - jnp.mean(t, -1, keepdims=True) - unit * jnp.mean(t * unit, -1, keepdims=True))


def colsum(x):
    return jnp.sum(x.reshape(x.shape[0] // 8, 8, x.shape[1]), 0)


def gelu_cdf(u):
    return 0.5 + 0.5 * lax.erf(u * 0.7071067811865476)


def gelu_slope(u, cdf):
    return cdf + u * (jnp.exp(-0.5 * u * u) * 0.3989422804014327)


def halves(x):
    return x[:, :HALF], x[:, HALF:]


def lane_head(rows):
    return lax.broadcasted_iota(jnp.int32, (rows, HALF), 1) // 32


def spread_heads(x, zero):
    head = lane_head(x.shape[0])
    return jnp.concatenate([jnp.where(head == h, x, zero) for h in range(4)], 0)


def gather_heads(x, group):
    head = lane_head(group)
    out = x[3 * group :]
    for h in range(3):
        out = jnp.where(head == h, x[h * group : (h + 1) * group], out)
    return out


def ones_heads(group, count):
    row = lax.broadcasted_iota(jnp.int32, (4 * group, HALF), 0)
    lane = lax.broadcasted_iota(jnp.int32, (4 * group, HALF), 1)
    return jnp.where((row // group == lane // 32) & (row % group < count), 1.0, 0.0).astype(BF)


def group_max(s, group, count):
    lane = lax.broadcasted_iota(jnp.int32, (s.shape[0], HALF), 1)
    outs = []
    for t in range(s.shape[1] // HALF):
        part = s[:, t * HALF : (t + 1) * HALF]
        top = None
        for g in range(HALF // group):
            here = (lane // group == g)
            best = jnp.max(jnp.where((lane // group == g) & (lane % group < count), part, negative), -1, keepdims=True)
            top = jnp.broadcast_to(best, part.shape) if top is None else jnp.where(here, best, top)
        outs.append(jnp.where(lane % group < count, part - top, negative))
    return jnp.concatenate(outs, 1)


def time_parts(units, group, ref):
    return [split2(ref[c, pl.ds(v, group, stride=VB), :]) for c, v in units]


def spread2(x2):
    zero = jnp.zeros((), BF)
    return spread_heads(x2[0], zero), spread_heads(x2[1], zero)


def time_attend(units, group, count, q_s, k_s, v_s, o_s, p_s, l_s):
    q = time_parts(units, group, q_s)
    k = [spread2(x2) for x2 in time_parts(units, group, k_s)]
    scores = [
        dots(jnp.concatenate(q2, 1), jnp.concatenate([k2[0], k2[0]], 1), 1, 1) + dots(q2[0], k2[1], 1, 1)
        for q2, k2 in zip(q, k)
    ]
    probs = [jnp.exp(group_max(s, group, count)) for s in scores]
    probs2 = [split2(p) for p in probs]
    w = [spread2(x2) for x2 in time_parts(units, group, v_s)]
    ones = ones_heads(group, count)
    both = [dots(rows2(p2), jnp.concatenate([w2[0], ones], 1), 1, 0) for p2, w2 in zip(probs2, w)]
    both = [b[:group] + b[group:] for b in both]
    inv = [1.0 / b[:, HALF:] for b in both]
    mixed = [(b[:, :HALF] + dots(p2[0], w2[1], 1, 0)) * i for b, p2, w2, i in zip(both, probs2, w, inv)]
    for (c, v), o, p, i in zip(units, mixed, probs, inv):
        o_s[c, pl.ds(v, group, stride=VB), :] = o
        p_s[c, v] = p
        l_s[c, v] = i


def time_attend_back(units, group, count, q_s, k_s, v_s, o_s, p_s, l_s, do_s, dq_s, dk_s, dv_s):
    d = [do_s[c, pl.ds(v, group, stride=VB), :] * l_s[c, v] for c, v in units]
    e2 = [split2(x * o_s[c, pl.ds(v, group, stride=VB), :]) for x, (c, v) in zip(d, units)]
    d2 = [split2(x) for x in d]
    w = [spread2(x2) for x2 in time_parts(units, group, v_s)]
    ones = -ones_heads(group, count)
    both = [
        dots(
            jnp.concatenate([jnp.concatenate([a[0], b[0]], 1), jnp.concatenate([a[1], b[1]], 1)], 0),
            jnp.concatenate([w2[0], ones], 1),
            1,
            1,
        )
        for a, b, w2 in zip(d2, e2, w)
    ]
    dp = [b[:group] + b[group:] + dots(a[0], w2[1], 1, 1) for b, a, w2 in zip(both, d2, w)]
    probs = [p_s[c, v] for c, v in units]
    s2 = [split2(p * x) for p, x in zip(probs, dp)]
    p2 = [split2(p) for p in probs]
    k = [spread2(x2) for x2 in time_parts(units, group, k_s)]
    both = [dots(rows2(a), k2[0], 1, 0) for a, k2 in zip(s2, k)]
    dq = [b[:group] + b[group:] + dots(a[0], k2[1], 1, 0) for b, a, k2 in zip(both, s2, k)]
    q = time_parts(units, group, q_s)
    dk = [gather_heads(tn3(a, q2), group) for a, q2 in zip(s2, q)]
    dv = [gather_heads(tn3(a, x), group) for a, x in zip(p2, d2)]
    for (c, v), x, y, z in zip(units, dq, dk, dv):
        at = pl.ds(v, group, stride=VB)
        dq_s[c, at, :] = x
        dk_s[c, at, :] = y
        dv_s[c, at, :] = z


def store_halves(ref, x):
    rows = x.shape[0]
    ref[0, :rows, :] = x[:, :HALF]
    ref[1, :rows, :] = x[:, HALF:]


def load_halves(ref, rows):
    return jnp.concatenate([ref[0, :rows, :], ref[1, :rows, :]], 1)


def zero_tail(ref, rows):
    tail = ref.shape[1] - rows
    ref[:, rows:, :] = jnp.zeros((2, tail, HALF), F32)


def time_forward(x, w, vec, count, group, kept):
    q_s, k_s, v_s, o_s, p_s, l_s, z1_s, u_s, z2_s = kept
    rows = count * VB
    x2 = split2(x)
    store_halves(q_s, (mmw(x2, w["q"]) + vec[0:1]) * SCALE)
    store_halves(k_s, mmw(x2, w["k"]))
    store_halves(v_s, mmw(x2, w["v"]) + vec[1:2])
    for ref in (q_s, k_s, v_s):
        zero_tail(ref, rows)

    def some(i, carry):
        units = [(c, i * UNROLL + k) for k in range(UNROLL) for c in range(2)]
        time_attend(units, group, count, q_s, k_s, v_s, o_s, p_s, l_s)
        return carry

    lax.fori_loop(0, VB // UNROLL, some, 0)
    z1 = x + mmw(split2(load_halves(o_s, rows)), w["o"]) + vec[2:3]
    z1_s[...] = z1
    h, _, _ = norm_fwd(z1, vec[3:4], vec[4:5])
    u = mmw(split2(h), w["up"]) + jnp.concatenate([vec[5:6], vec[6:7]], 1)
    u_s[...] = u
    z2 = h + mmw(split2(u * gelu_cdf(u)), w["down"]) + vec[7:8]
    z2_s[...] = z2
    return norm_fwd(z2, vec[8:9], vec[9:10])[0]


def embed_block(pieces, emb, place):
    return mmw(split2(pieces), emb) + place


TIME_W = ("q", "k", "v", "o", "up", "down")


def time_fwd_kernel(first, count, group, *refs):
    if first:
        x_ref, emb_ref, place_ref = refs[:3]
        refs = refs[3:]
    else:
        x_ref = refs[0]
        refs = refs[1:]
    w = {name: refs[i][...] for i, name in enumerate(TIME_W)}
    vec_ref, y_ref = refs[6:8]
    rows = count * VB
    if first:
        place = jnp.broadcast_to(place_ref[...], (count, VB, D)).reshape(rows, D)
        x = embed_block(x_ref[...].reshape(rows, 16), emb_ref[...], place)
    else:
        x = x_ref[...].reshape(rows, D)
    y = time_forward(x, w, vec_ref[...], count, group, refs[8:])
    y_ref[...] = y.reshape(count, VB, D)


def whole(shape):
    return pl.BlockSpec(shape, lambda i: (0,) * len(shape))


def params_spec():
    return pltpu.CompilerParams(vmem_limit_bytes=VMEM_LIMIT)


def pick(shape, index):
    return pl.BlockSpec((None,) + shape, lambda i: (index,) + (0,) * len(shape))


def weight_specs(squares, feed, layer):
    specs = [pick((D, D), k) for k in squares]
    if feed is not None:
        specs += [pick((D, FF), feed), pick((FF, D), 4 + feed)]
    return specs + [pick((24, D), layer)]


def weight_args(model, squares, feed):
    square, up, down, vecs = model
    return [square] * len(squares) + ([up, down] if feed is not None else []) + [vecs]


def flush(step, last, accs, mat_at, up_acc, down_acc, feed_at, up_rows, g_mat, g_feed, sems):
    @pl.when(step == last)
    def _():
        copies = []

        def add(src, dst):
            copies.append(pltpu.make_async_copy(src, dst, sems.at[len(copies)]))

        for acc, at in zip(accs, mat_at):
            add(acc, g_mat.at[pl.ds(at, acc.shape[0])] if len(acc.shape) == 3 else g_mat.at[at])
        if up_acc is not None:
            for k in range(D // up_rows):
                for half in range(2):
                    base = 2 * D * feed_at + (2 * k + half) * up_rows
                    add(up_acc.at[pl.ds(k * up_rows, up_rows), pl.ds(half * D, D)], g_feed.at[pl.ds(base, up_rows)])
            add(down_acc, g_feed.at[pl.ds(4 * FF + feed_at * FF, FF)])
        for copy in copies:
            copy.start()
        for copy in copies:
            copy.wait()


def pack_shapes():
    return [jax.ShapeDtypeStruct((NSQ, D, D), F32), jax.ShapeDtypeStruct((8 * FF, D), F32)]


def flush_count(mats, up_rows):
    return mats + (2 * D // up_rows + 1 if up_rows else 0)


def time_kept(count, group, nb):
    pad, rows = group * VB, count * VB
    shapes = [(2, pad, HALF)] * 4 + [(2, VB, group, 4 * group), (2, VB, group, HALF), (rows, D), (rows, FF), (rows, D)]
    specs = [pl.BlockSpec((None,) + s, lambda i, n=len(s): (i,) + (0,) * n) for s in shapes]
    return specs, [jax.ShapeDtypeStruct((nb,) + s, F32) for s in shapes]


def time_fwd(first, x, extra, model, layer, count):
    squares = [12 * layer + k for k in range(4)]
    group = 64 if count > 32 else 32
    nv = x.shape[1]
    width = x.shape[2]
    specs = [pl.BlockSpec((count, VB, width), lambda i: (0, i, 0))]
    if first:
        specs += [whole((16, D)), whole((count, 1, D))]
    kept_specs, kept_shapes = time_kept(count, group, nv // VB)
    out = pl.pallas_call(
        functools.partial(time_fwd_kernel, first, count, group),
        grid=(nv // VB,),
        in_specs=specs + weight_specs(squares, 2 * layer, layer),
        out_specs=[pl.BlockSpec((count, VB, D), lambda i: (0, i, 0))] + kept_specs,
        out_shape=[jax.ShapeDtypeStruct((count, nv, D), F32)] + kept_shapes,
        compiler_params=params_spec(),
        name="time_fwd",
    )(x, *extra, *weight_args(model, squares, 2 * layer))
    return out[0], out[1:]


def time_bwd_kernel(first, count, group, layer, up_rows, *refs):
    if first:
        x_ref, emb_ref, place_ref = refs[:3]
        refs = refs[3:]
    else:
        x_ref = refs[0]
        refs = refs[1:]
    dy_ref = refs[0]
    q_s, k_s, v_s, o_s, p_s, l_s, z1_s, u_s, z2_s = refs[1:10]
    w = {name: refs[10 + i][...] for i, name in enumerate(TIME_W)}
    vec_ref = refs[16]
    g_mat, g_feed = refs[19:21]
    outs = refs[21:]
    n_out = 3 if first else 2
    tail = outs[1:n_out]
    accs = outs[n_out : n_out + 6]
    sems = outs[n_out + 6]
    g = dict(zip(TIME_W + ("rows",), tuple(accs) + (outs[0],)))
    do_s, dq_s, dk_s, dv_s = outs[n_out + 7 :]
    rows = count * VB
    step = pl.program_id(0)

    @pl.when(step == 0)
    def _():
        for ref in list(g.values()) + (list(tail) if first else []):
            ref[...] = jnp.zeros(ref.shape, F32)

    vec = vec_ref[...]
    if first:
        place = jnp.broadcast_to(place_ref[...], (count, VB, D)).reshape(rows, D)
        pieces = x_ref[...].reshape(rows, 16)
        x = embed_block(pieces, emb_ref[...], place)
    else:
        x = x_ref[...].reshape(rows, D)
    x2 = split2(x)
    mixed = load_halves(o_s, rows)
    h, unit1, inv1 = norm_fwd(z1_s[...], vec[3:4], vec[4:5])
    u = u_s[...]
    cdf = gelu_cdf(u)
    _, unit2, inv2 = norm_fwd(z2_s[...], vec[8:9], vec[9:10])
    dy = dy_ref[...].reshape(rows, D)
    g["rows"][8] += colsum(dy * unit2)
    g["rows"][9] += colsum(dy)
    dz2 = norm_bwd(dy, unit2, inv2, vec[8:9])
    g["rows"][7] += colsum(dz2)
    dz22 = split2(dz2)
    g["down"][...] += tn3(split2(u * cdf), dz22)
    du = mmwt(dz22, w["down"]) * gelu_slope(u, cdf)
    g["rows"][5] += colsum(du[:, :D])
    g["rows"][6] += colsum(du[:, D:])
    du2 = split2(du)
    g["up"][...] += tn3(split2(h), du2)
    dh = dz2 + mmwt(du2, w["up"])
    g["rows"][3] += colsum(dh * unit1)
    g["rows"][4] += colsum(dh)
    dz1 = norm_bwd(dh, unit1, inv1, vec[3:4])
    g["rows"][2] += colsum(dz1)
    dz12 = split2(dz1)
    g["o"][...] += tn3(split2(mixed), dz12)
    store_halves(do_s, mmwt(dz12, w["o"]))
    zero_tail(do_s, rows)

    def some(i, carry):
        units = [(c, i * UNROLL_BACK + k) for k in range(UNROLL_BACK) for c in range(2)]
        time_attend_back(units, group, count, q_s, k_s, v_s, o_s, p_s, l_s, do_s, dq_s, dk_s, dv_s)
        return carry

    lax.fori_loop(0, VB // UNROLL_BACK, some, 0)
    dq = load_halves(dq_s, rows) * SCALE
    g["rows"][0] += colsum(dq)
    dq2 = split2(dq)
    g["q"][...] += tn3(x2, dq2)
    dx = dz1 + mmwt(dq2, w["q"])
    dk2 = split2(load_halves(dk_s, rows))
    g["k"][...] += tn3(x2, dk2)
    dx = dx + mmwt(dk2, w["k"])
    dv = load_halves(dv_s, rows)
    g["rows"][1] += colsum(dv)
    dv2 = split2(dv)
    g["v"][...] += tn3(x2, dv2)
    dx = dx + mmwt(dv2, w["v"])
    if first:
        tail[0][...] += tn3(split2(pieces), split2(dx))
        tail[1][...] += dx
    else:
        tail[0][...] = dx.reshape(count, VB, D)
    flush(
        step, pl.num_programs(0) - 1, accs[:4], [12 * layer + k for k in range(4)], accs[4], accs[5], 2 * layer, up_rows,
        g_mat, g_feed, sems,
    )


def time_bwd(first, x, extra, dy, kept, model, layer, count, packs, up_rows):
    group = 64 if count > 32 else 32
    nv = x.shape[1]
    width = x.shape[2]
    pad = group * VB
    squares = [12 * layer + k for k in range(4)]
    block = pl.BlockSpec((count, VB, D), lambda i: (0, i, 0))
    specs = [pl.BlockSpec((count, VB, width), lambda i: (0, i, 0))]
    if first:
        specs += [whole((16, D)), whole((count, 1, D))]
    specs += [block] + time_kept(count, group, nv // VB)[0] + weight_specs(squares, 2 * layer, layer)
    grad_shapes = [(10, 8, D)] + ([(16, D), (count * VB, D)] if first else [])
    out_specs = [ANY] * 2 + [whole(s) for s in grad_shapes]
    out_shape = pack_shapes() + [jax.ShapeDtypeStruct(s, F32) for s in grad_shapes]
    if not first:
        out_specs.append(block)
        out_shape.append(jax.ShapeDtypeStruct((count, nv, D), F32))
    return pl.pallas_call(
        functools.partial(time_bwd_kernel, first, count, group, layer, up_rows),
        grid=(nv // VB,),
        in_specs=specs + [ANY] * 2,
        out_specs=out_specs,
        out_shape=out_shape,
        input_output_aliases={len(specs): 0, len(specs) + 1: 1},
        scratch_shapes=[pltpu.VMEM((D, D), F32)] * 4
        + [pltpu.VMEM((D, FF), F32), pltpu.VMEM((FF, D), F32), pltpu.SemaphoreType.DMA((flush_count(4, up_rows),))]
        + [pltpu.VMEM((2, pad, HALF), F32)] * 4,
        compiler_params=params_spec(),
        name="time_bwd",
    )(x, *extra, dy, *kept, *weight_args(model, squares, 2 * layer), *packs)

SB_ROWS = 64


def head_rows():
    sub = lax.broadcasted_iota(jnp.int32, (8, D), 0)
    lane = lax.broadcasted_iota(jnp.int32, (8, D), 1)
    return jnp.where(sub == lane // 32, 1.0, 0.0).astype(F32)


def spread_rows(x):
    wide = jnp.broadcast_to(x[:, None, :], (RPAD, HEADS, D)) * head_rows()[None]
    return wide.reshape(RPAD * HEADS, D)


def gather_rows(x):
    return jnp.sum(x.reshape(RPAD, HEADS, D) * head_rows()[None], 1)


PACK = 24


def pack_rows(x, last=None):
    last = jnp.zeros((1, HALF), F32) if last is None else last
    return jnp.concatenate([x[:ROUT, :HALF], x[:ROUT, HALF:], last, jnp.zeros((PACK - 2 * ROUT - 1, HALF), F32)], 0)


def unpack_rows(x):
    x = jnp.concatenate([x[:ROUT], x[ROUT : 2 * ROUT]], 1)
    return jnp.concatenate([x, jnp.zeros((RPAD - ROUT, D), F32)], 0)


def unpack_block(ref, sb):
    return jnp.concatenate([unpack_rows(ref[s]) for s in range(sb)], 0)


def pack_block(ref, x, sb):
    for s in range(sb):
        ref[s] = pack_rows(x[s * RPAD : (s + 1) * RPAD])


def valid_lane(rows):
    return lax.broadcasted_iota(jnp.int32, (rows, HALF), 1) < ROUT * HEADS


def router_reduce(x, op):
    for shift in (8, 16, 32, 64):
        x = op(x, pltpu.roll(x, shift, 1))
    return x


def merge_rows(y, pairs, vec):
    wide = y.reshape(pairs, 2, SB_ROWS, D)
    wide = jnp.concatenate([wide[:, 0].reshape(pairs * SB_ROWS, D), wide[:, 1].reshape(pairs * SB_ROWS, D)], 1)
    gain = jnp.concatenate([vec[0:1], vec[1:2]], 1)
    bias = jnp.concatenate([vec[2:3], vec[3:4]], 1)
    return norm_fwd(wide, gain, bias) + (gain,)


RECV_W = ("so", "rk", "rv", "rq", "ro", "up", "down")


def recv_buffer(o2, w, vec):
    buf2 = split2(mmw(o2, w["so"]) + vec[12:13])
    kb = mmw(buf2, w["rk"])
    vb = mmw(buf2, w["rv"]) + vec[14:15]
    segs = range(kb.shape[0] // RPAD)
    k = [split2(spread_rows(kb[s * RPAD : (s + 1) * RPAD])) for s in segs]
    v = [split2(spread_rows(vb[s * RPAD : (s + 1) * RPAD])) for s in segs]
    return buf2, k, v


def recv_forward(send, o_rows, w, vec):
    sb = send.shape[0] // SB_ROWS
    send2 = split2(send)
    o2 = split2(o_rows)
    buf2, k, v = recv_buffer(o2, w, vec)
    q = (mmw(send2, w["rq"]) + vec[13:14]) * SCALE
    segs = range(sb)
    ok = valid_lane(SB_ROWS)
    scores = [jnp.where(ok, nt3(split2(q[s * SB_ROWS : (s + 1) * SB_ROWS]), k[s]), negative) for s in segs]
    probs = [jnp.exp(sc - router_reduce(sc, jnp.maximum)) for sc in scores]
    probs = [p / router_reduce(p, jnp.add) for p in probs]
    mixed = jnp.concatenate([nn3(split2(p), v2) for p, v2 in zip(probs, v)], 0)
    z3 = send + mmw(split2(mixed), w["ro"]) + vec[15:16]
    g, unit3, inv3 = norm_fwd(z3, vec[16:17], vec[17:18])
    u = mmw(split2(g), w["up"]) + jnp.concatenate([vec[18:19], vec[19:20]], 1)
    cdf = gelu_cdf(u)
    z4 = g + mmw(split2(u * cdf), w["down"]) + vec[20:21]
    y, unit4, inv4 = norm_fwd(z4, vec[21:22], vec[22:23])
    kept = (send2, o2, buf2, mixed, g, unit3, inv3, u, cdf, unit4, inv4, q, k, v, probs)
    return y, kept, (q, mixed, jnp.concatenate(probs, 0), z3, u, z4)


def recv_restore(send, o_rows, w, vec, saved):
    q, mixed, p, z3, u, z4 = saved
    o2 = split2(o_rows)
    buf2, k, v = recv_buffer(o2, w, vec)
    g, unit3, inv3 = norm_fwd(z3, vec[16:17], vec[17:18])
    y, unit4, inv4 = norm_fwd(z4, vec[21:22], vec[22:23])
    probs = [p[s * SB_ROWS : (s + 1) * SB_ROWS] for s in range(send.shape[0] // SB_ROWS)]
    return y, (split2(send), o2, buf2, mixed, g, unit3, inv3, u, gelu_cdf(u), unit4, inv4, q, k, v, probs)


KEPT_WIDTHS = (D, D, HALF, D, FF, D)


def kept_specs(sb):
    return [pl.BlockSpec((sb * SB_ROWS, k), lambda i: (i, 0)) for k in KEPT_WIDTHS]


RECV_G = RECV_W + ("rows",)


def recv_backward(dy, kept, w, vec, g):
    send2, o2, buf2, mixed, gg, unit3, inv3, u, cdf, unit4, inv4, q, k, v, probs = kept
    sb = dy.shape[0] // SB_ROWS
    rows = g["rows"]
    rows[9] += colsum(dy * unit4)
    rows[10] += colsum(dy)
    dz4 = norm_bwd(dy, unit4, inv4, vec[21:22])
    rows[8] += colsum(dz4)
    dz42 = split2(dz4)
    g["down"][...] += tn3(split2(u * cdf), dz42)
    du = mmwt(dz42, w["down"]) * gelu_slope(u, cdf)
    rows[6] += colsum(du[:, :D])
    rows[7] += colsum(du[:, D:])
    du2 = split2(du)
    g["up"][...] += tn3(split2(gg), du2)
    dg = dz4 + mmwt(du2, w["up"])
    rows[4] += colsum(dg * unit3)
    rows[5] += colsum(dg)
    dz3 = norm_bwd(dg, unit3, inv3, vec[16:17])
    rows[3] += colsum(dz3)
    dz32 = split2(dz3)
    g["ro"][...] += tn3(split2(mixed), dz32)
    do = mmwt(dz32, w["ro"])
    segs = range(sb)
    d = [split2(do[s * SB_ROWS : (s + 1) * SB_ROWS]) for s in segs]
    dp = [nt3(d2, v2) for d2, v2 in zip(d, v)]
    ds = [split2(p * (x - router_reduce(p * x, jnp.add))) for p, x in zip(probs, dp)]
    dq = jnp.concatenate([nn3(s2, k2) for s2, k2 in zip(ds, k)], 0) * SCALE
    q = [split2(q[s * SB_ROWS : (s + 1) * SB_ROWS]) for s in segs]
    dk = jnp.concatenate([gather_rows(tn3(s2, q2)) for s2, q2 in zip(ds, q)], 0)
    dv = jnp.concatenate([gather_rows(tn3(split2(p), d2)) for p, d2 in zip(probs, d)], 0)
    rows[1] += colsum(dq)
    dq2 = split2(dq)
    g["rq"][...] += tn3(send2, dq2)
    dsend = dz3 + mmwt(dq2, w["rq"])
    dk2 = split2(dk)
    dv2 = split2(dv)
    rows[2] += colsum(dv)
    g["rk"][...] += tn3(buf2, dk2)
    g["rv"][...] += tn3(buf2, dv2)
    dbuf = mmwt(dk2, w["rk"]) + mmwt(dv2, w["rv"])
    rows[0] += colsum(dbuf)
    dbuf2 = split2(dbuf)
    g["so"][...] += tn3(o2, dbuf2)
    return dsend, mmwt(dbuf2, w["so"])


def recv_squares(layer):
    return [12 * layer + k for k in (7, 9, 10, 8, 11)]


def seg_block(sb, rows=SB_ROWS, width=D):
    return pl.BlockSpec((sb, rows, width), lambda i: (i, 0, 0))


MERGE = pl.BlockSpec((2, D, D), lambda i: (12, 0, 0))


def pack_spec(sb):
    return seg_block(sb, PACK, HALF)


def recv_fwd_kernel(sb, send_ref, o_ref, *refs):
    w = {n: refs[i][...] for i, n in enumerate(RECV_W)}
    vec_ref, mvec_ref, mw_ref, out_ref = refs[7:11]
    y, _, saved = recv_forward(send_ref[...].reshape(sb * SB_ROWS, D), unpack_block(o_ref, sb), w, vec_ref[...])
    for ref, x in zip(refs[11:], saved):
        ref[...] = x
    mvec = mvec_ref[...]
    wide, _, _, _ = merge_rows(y, sb // 2, mvec)
    out_ref[...] = (mmw(split2(wide), mw_ref[...].reshape(2 * D, D)) + mvec[4:5]).reshape(sb // 2, SB_ROWS, D)


def recv_fwd(send, o, model, mvec, sb):
    squares = recv_squares(0)
    n = send.shape[0]
    return pl.pallas_call(
        functools.partial(recv_fwd_kernel, sb),
        grid=(n // sb,),
        in_specs=[seg_block(sb), pack_spec(sb)] + weight_specs(squares, 1, 0) + [whole((8, D)), MERGE],
        out_specs=[seg_block(sb // 2)] + kept_specs(sb),
        out_shape=[jax.ShapeDtypeStruct((n // 2, SB_ROWS, D), F32)]
        + [jax.ShapeDtypeStruct((n * SB_ROWS, k), F32) for k in KEPT_WIDTHS],
        compiler_params=params_spec(),
        name="recv_fwd",
    )(send, o, *weight_args(model, squares, 1), mvec, model[0])


def recv_bwd_kernel(sb, up_rows, send_ref, o_ref, dx_ref, *refs):
    saved = [ref[...] for ref in refs[:6]]
    refs = refs[6:]
    w = {n: refs[i][...] for i, n in enumerate(RECV_W)}
    vec_ref, mvec_ref, mw_ref = refs[7:10]
    g_mat, g_feed, dsend_ref, do_ref, rows_ref, dmv_ref = refs[12:18]
    accs, dmw_ref, sems = refs[18:25], refs[25], refs[26]
    g = dict(zip(RECV_G, tuple(accs) + (rows_ref,)))

    @pl.when(pl.program_id(0) == 0)
    def _():
        for ref in list(g.values()) + [dmw_ref, dmv_ref]:
            ref[...] = jnp.zeros(ref.shape, F32)

    vec = vec_ref[...]
    y, kept = recv_restore(send_ref[...].reshape(sb * SB_ROWS, D), unpack_block(o_ref, sb), w, vec, saved)
    pairs = sb // 2
    wide, unit, inv, gain = merge_rows(y, pairs, mvec_ref[...])
    dx = dx_ref[...].reshape(pairs * SB_ROWS, D)
    dmv_ref[4] += colsum(dx)
    dx2 = split2(dx)
    dmw_ref[...] += tn3(split2(wide), dx2).reshape(2, D, D)
    dn = mmwt(dx2, mw_ref[...].reshape(2 * D, D))
    part = colsum(dn * unit)
    dmv_ref[0] += part[:, :D]
    dmv_ref[1] += part[:, D:]
    part = colsum(dn)
    dmv_ref[2] += part[:, :D]
    dmv_ref[3] += part[:, D:]
    dwide = norm_bwd(dn, unit, inv, gain)
    left = dwide[:, :D].reshape(pairs, 1, SB_ROWS, D)
    right = dwide[:, D:].reshape(pairs, 1, SB_ROWS, D)
    dy = jnp.concatenate([left, right], 1).reshape(sb * SB_ROWS, D)
    dsend, do = recv_backward(dy, kept, w, vec, g)
    dsend_ref[...] = dsend.reshape(sb, SB_ROWS, D)
    pack_block(do_ref, do, sb)
    recv_flush(accs, [(dmw_ref, 24)], 0, up_rows, g_mat, g_feed, sems)


RECV_ACC = [pltpu.VMEM((D, D), F32)] * 5 + [pltpu.VMEM((D, FF), F32), pltpu.VMEM((FF, D), F32)]


def recv_flush(accs, more, layer, up_rows, g_mat, g_feed, sems):
    flush(
        pl.program_id(0), pl.num_programs(0) - 1, list(accs[:5]) + [m for m, _ in more],
        recv_squares(layer) + [at for _, at in more], accs[5], accs[6], 2 * layer + 1, up_rows, g_mat, g_feed, sems,
    )


def recv_bwd(send, o, dx, kept, model, mvec, sb, packs, up_rows):
    n = send.shape[0]
    squares = recv_squares(0)
    shapes = [(11, 8, D), (5, 8, D)]
    specs = [seg_block(sb), pack_spec(sb), seg_block(sb // 2)] + kept_specs(sb)
    specs += weight_specs(squares, 1, 0) + [whole((8, D)), MERGE]
    return pl.pallas_call(
        functools.partial(recv_bwd_kernel, sb, up_rows),
        grid=(n // sb,),
        in_specs=specs + [ANY] * 2,
        out_specs=[ANY] * 2 + [seg_block(sb), pack_spec(sb)] + [whole(s) for s in shapes],
        out_shape=pack_shapes()
        + [jax.ShapeDtypeStruct((n, SB_ROWS, D), F32), jax.ShapeDtypeStruct(o.shape, F32)]
        + [jax.ShapeDtypeStruct(s, F32) for s in shapes],
        input_output_aliases={len(specs): 0, len(specs) + 1: 1},
        scratch_shapes=RECV_ACC + [pltpu.VMEM((2, D, D), F32), pltpu.SemaphoreType.DMA((flush_count(6, up_rows),))],
        compiler_params=params_spec(),
        name="recv_bwd",
    )(send, o, dx, *kept, *weight_args(model, squares, 1), mvec, model[0], *packs)


def tail_kernel(sb, up_rows, send_ref, o_ref, tgt_ref, kept_ref, scale_ref, mean_ref, *refs):
    w = {n: refs[i][...] for i, n in enumerate(RECV_W)}
    vec_ref, head_ref, g_mat, g_feed, dsend_ref, do_ref, rows_ref, dhead_ref = refs[7:15]
    accs, sems = refs[15:22], refs[22]
    g = dict(zip(RECV_G, tuple(accs) + (rows_ref,)))

    @pl.when(pl.program_id(0) == 0)
    def _():
        for ref in list(g.values()) + [dhead_ref]:
            ref[...] = jnp.zeros(ref.shape, F32)

    vec = vec_ref[...]
    rows = sb * SB_ROWS
    y, kept, _ = recv_forward(
        send_ref[...].reshape(rows, D), unpack_block(o_ref, sb), w, vec
    )
    head = head_ref[...]
    y2 = split2(y)
    scale = jnp.broadcast_to(scale_ref[...][None], (sb, SB_ROWS, PPAD)).reshape(rows, PPAD)
    mean = jnp.broadcast_to(mean_ref[...][None], (sb, SB_ROWS, PPAD)).reshape(rows, PPAD)
    misfit = mmwt(y2, head) * scale + mean - tgt_ref[...].reshape(rows, PPAD)
    dpred = kept_ref[...].reshape(rows, PPAD) * misfit * scale
    dpred2 = split2(dpred)
    dhead_ref[...] += tn3(dpred2, y2)
    dy = mmw(dpred2, head)
    dsend, do = recv_backward(dy, kept, w, vec, g)
    dsend_ref[...] = dsend.reshape(sb, SB_ROWS, D)
    pack_block(do_ref, do, sb)
    recv_flush(accs, [], 1, up_rows, g_mat, g_feed, sems)


def tail(send, o, tgt, kept, scale, mean, model, head, sb, up_rows):
    n = send.shape[0]
    squares = recv_squares(1)
    shapes = [(11, 8, D), (PPAD, D)]
    return pl.pallas_call(
        functools.partial(tail_kernel, sb, up_rows),
        grid=(n // sb,),
        in_specs=[seg_block(sb), pack_spec(sb), seg_block(sb, SB_ROWS, PPAD), seg_block(sb, SB_ROWS, PPAD)]
        + [whole((SB_ROWS, PPAD))] * 2
        + weight_specs(squares, 3, 1)
        + [whole((PPAD, D))],
        out_specs=[ANY] * 2 + [seg_block(sb), pack_spec(sb)] + [whole(s) for s in shapes],
        out_shape=pack_shapes()
        + [jax.ShapeDtypeStruct((n, SB_ROWS, D), F32), jax.ShapeDtypeStruct(o.shape, F32)]
        + [jax.ShapeDtypeStruct(s, F32) for s in shapes],
        scratch_shapes=RECV_ACC + [pltpu.SemaphoreType.DMA((flush_count(5, up_rows),))],
        compiler_params=params_spec(),
        name="tail",
    )(send, o, tgt, kept, scale, mean, *weight_args(model, squares, 3), head)


SEND_W = ("sq", "sk", "sv")


def send_project(dim2, r_rows, w, vec):
    r2 = split2(r_rows)
    sb = r_rows.shape[0] // RPAD
    k = mmw(dim2, w["sk"])
    v = mmw(dim2, w["sv"]) + vec[11:12]
    q = (mmw(r2, w["sq"]) + vec[10:11]) * SCALE
    k = [split2(k[s * SB_ROWS : (s + 1) * SB_ROWS]) for s in range(sb)]
    v = [split2(v[s * SB_ROWS : (s + 1) * SB_ROWS]) for s in range(sb)]
    q = [split2(spread_rows(q[s * RPAD : (s + 1) * RPAD])) for s in range(sb)]
    return r2, k, v, q


def send_fwd_kernel(sb, dim_ref, r_ref, here_ref, *refs):
    w = {n: refs[i][...] for i, n in enumerate(SEND_W)}
    vec_ref, o_ref = refs[3:]
    dim2 = split2(dim_ref[...].reshape(sb * SB_ROWS, D))
    _, k, v, q = send_project(dim2, r_ref[...].reshape(sb * RPAD, D), w, vec_ref[...])
    here = here_ref[...] > 0.5
    scores = [jnp.where(here, nt3(k2, q2), negative) for k2, q2 in zip(k, q)]
    tops = [jnp.max(sc, 0, keepdims=True) for sc in scores]
    probs = [jnp.where(here, jnp.exp(sc - top), 0.0) for sc, top in zip(scores, tops)]
    totals = [jnp.sum(p, 0, keepdims=True) for p in probs]
    safe = [jnp.where(t > 0.0, t, 1.0) for t in totals]
    mixed = [gather_rows(tn3(split2(p / t), v2)) for p, t, v2 in zip(probs, safe, v)]
    for s in range(sb):
        lse = jnp.where(totals[s] > 0.0, tops[s] + jnp.log(safe[s]), negative)
        o_ref[s] = pack_rows(mixed[s], lse)


def send_squares(layer):
    return [12 * layer + k for k in (4, 5, 6)]


def send_fwd(dim, routers, here, model, layer, sb, npad):
    squares = send_squares(layer)
    n = dim.shape[0]
    return pl.pallas_call(
        functools.partial(send_fwd_kernel, sb),
        grid=(n // sb,),
        in_specs=[seg_block(sb), seg_block(sb, RPAD), whole((SB_ROWS, HALF))]
        + weight_specs(squares, None, layer),
        out_specs=pack_spec(sb),
        out_shape=jax.ShapeDtypeStruct((npad, PACK, HALF), F32),
        compiler_params=params_spec(),
        name="send_fwd",
    )(dim, routers, here, *weight_args(model, squares, None))


def send_bwd_kernel(sb, layer, dim_ref, dpart_ref, r_ref, o_ref, do_ref, here_ref, *refs):
    w = {n: refs[i][...] for i, n in enumerate(SEND_W)}
    vec_ref = refs[3]
    g_mat, ddim_ref, dr_ref, rows = refs[5:9]
    dsq_ref, dsk_ref, dsv_ref, sems = refs[9:13]

    @pl.when(pl.program_id(0) == 0)
    def _():
        for ref in (dsq_ref, dsk_ref, dsv_ref, rows):
            ref[...] = jnp.zeros(ref.shape, F32)

    dim2 = split2(dim_ref[...].reshape(sb * SB_ROWS, D))
    r2, k, v, q = send_project(dim2, r_ref[...].reshape(sb * RPAD, D), w, vec_ref[...])
    here = (here_ref[...] > 0.5) & valid_lane(SB_ROWS)
    segs = range(sb)
    scores = [nt3(k2, q2) for k2, q2 in zip(k, q)]
    probs = [jnp.where(here, jnp.exp(scores[s] - o_ref[s][2 * ROUT : 2 * ROUT + 1]), 0.0) for s in segs]
    dwide = [spread_rows(unpack_rows(do_ref[s])) for s in segs]
    owide = [
        jnp.broadcast_to(unpack_rows(o_ref[s])[:, None, :], (RPAD, HEADS, D)).reshape(RPAD * HEADS, D) for s in segs
    ]
    e = [split2(a * b) for a, b in zip(dwide, owide)]
    d = [split2(a) for a in dwide]
    one_row = jnp.ones((8, D), BF)
    means = [(dots(one_row, e2[0], 1, 1) + dots(one_row, e2[1], 1, 1))[0:1] for e2 in e]
    dp = [nt3(v2, d2) for v2, d2 in zip(v, d)]
    ds = [split2(p * (x - mean)) for p, x, mean in zip(probs, dp, means)]
    dk = jnp.concatenate([nn3(s2, q2) for s2, q2 in zip(ds, q)], 0)
    dv = jnp.concatenate([nn3(split2(p), d2) for p, d2 in zip(probs, d)], 0)
    dq = jnp.concatenate([gather_rows(tn3(s2, k2)) for s2, k2 in zip(ds, k)], 0) * SCALE
    dk2 = split2(dk)
    dv2 = split2(dv)
    rows[1] += colsum(dv)
    dsk_ref[...] += tn3(dim2, dk2)
    dsv_ref[...] += tn3(dim2, dv2)
    out = dpart_ref[...].reshape(sb * SB_ROWS, D) + mmwt(dk2, w["sk"]) + mmwt(dv2, w["sv"])
    ddim_ref[...] = out.reshape(sb, SB_ROWS, D)
    rows[0] += colsum(dq)
    dq2 = split2(dq)
    dsq_ref[...] += tn3(r2, dq2)
    dr_ref[...] = mmwt(dq2, w["sq"]).reshape(sb, RPAD, D)
    flush(
        pl.program_id(0), pl.num_programs(0) - 1, [dsq_ref, dsk_ref, dsv_ref], send_squares(layer), None, None, 0, 0,
        g_mat, None, sems,
    )


def send_bwd(dim, dpart, routers, o, do, here, model, layer, sb, g_mat):
    n = dim.shape[0]
    squares = send_squares(layer)
    specs = [seg_block(sb), seg_block(sb), seg_block(sb, RPAD), pack_spec(sb), pack_spec(sb), whole((SB_ROWS, HALF))]
    specs += weight_specs(squares, None, layer)
    return pl.pallas_call(
        functools.partial(send_bwd_kernel, sb, layer),
        grid=(n // sb,),
        in_specs=specs + [ANY],
        out_specs=[ANY, seg_block(sb), seg_block(sb, RPAD), whole((2, 8, D))],
        out_shape=pack_shapes()[:1]
        + [jax.ShapeDtypeStruct((n, SB_ROWS, D), F32), jax.ShapeDtypeStruct((n, RPAD, D), F32)]
        + [jax.ShapeDtypeStruct((2, 8, D), F32)],
        input_output_aliases={len(specs): 0},
        scratch_shapes=[pltpu.VMEM((D, D), F32)] * 3 + [pltpu.SemaphoreType.DMA((3,))],
        compiler_params=params_spec(),
        name="send_bwd",
    )(dim, dpart, routers, o, do, here, *weight_args(model, squares, None), g_mat)

MESH = pl.DeviceIdType.MESH


def grid_sizes():
    nf = lax.axis_size("fsdp")
    nx = 1
    while 2 * nx * nx < nf:
        nx *= 2
    return lax.axis_size("dp") // 2, nf // nx, nx


class Place:
    def __init__(self):
        self.ny, self.nz, self.nx = grid_sizes()
        dp, fs = lax.axis_index("dp"), lax.axis_index("fsdp")
        self.core, self.y = lax.rem(dp, 2), lax.div(dp, 2)
        self.x, self.z = lax.rem(fs, self.nx), lax.div(fs, self.nx)

    def at(self, y=None, core=None, z=None, x=None):
        y = self.y if y is None else y
        core = self.core if core is None else core
        z = self.z if z is None else z
        x = self.x if x is None else x
        return (y * 2 + core, z * self.nx + x)

    def other(self):
        return 1 - self.core

    def next_x(self, k):
        return lax.rem(self.x + k, self.nx)

    def next_y(self, k):
        return lax.rem(self.y + k, self.ny)

    def next_z(self, k):
        return lax.rem(self.z + k, self.nz)

    def neighbours(self):
        out = [self.at(core=self.other())]
        out += [self.at(x=self.next_x(k)) for k in range(1, self.nx)]
        out += [self.at(y=self.next_y(k)) for k in range(1, self.ny)]
        out += [self.at(z=self.next_z(k)) for k in range(1, self.nz)]
        return out


def greet(devices):
    barrier = pltpu.get_barrier_semaphore()
    for device in devices:
        pl.semaphore_signal(barrier, inc=1, device_id=device, device_id_type=MESH)
    pl.semaphore_wait(barrier, len(devices))


def remote(src, dst, send, recv, device):
    return pltpu.make_async_remote_copy(
        src_ref=src, dst_ref=dst, send_sem=send, recv_sem=recv, device_id=device, device_id_type=MESH
    )


def gather_kernel(n, *refs):
    shards, outs = refs[:n], refs[n : 2 * n]
    send, recv, local = refs[2 * n :]
    me = Place()
    y, c, z, x = me.y, me.core, me.z, me.x
    m = me.nx
    greet(me.neighbours())
    copies, slot = [], [0]

    def push(src, dst, device):
        copy = remote(src, dst, send.at[slot[0]], recv.at[slot[0]], device)
        slot[0] += 1
        copy.start()
        return copy

    own = [pltpu.make_async_copy(shards[j], outs[j].at[y, c, z, x], local.at[j]) for j in range(n)]
    for copy in own:
        copy.start()
    first = [
        push(shards[j], outs[j].at[y, c, z, x], me.at(z=me.next_z(k))) for j in range(n) for k in range(1, me.nz)
    ]
    for copy in own:
        copy.wait()
    for copy in first:
        copy.wait()
    base = slot[0]

    def rest(by_core):
        slot[0] = base
        shared, started = [], []
        sibling = me.at(core=1 - by_core)
        second = []
        for j in range(n):
            piece = outs[j].at[y, by_core, :, x]
            for k in range(1, m):
                peer = me.at(x=me.next_x(k)) if by_core == 0 else me.at(y=me.next_y(k))
                second.append(push(piece, piece, peer))
            shared.append(push(piece, piece, sibling))
        for copy in second:
            copy.wait()
        third = []
        for j in range(n):
            wide = outs[j].at[y, by_core] if by_core == 0 else outs[j].at[:, by_core, :, x]
            for k in range(1, m):
                peer = me.at(y=me.next_y(k)) if by_core == 0 else me.at(x=me.next_x(k))
                third.append(push(wide, wide, peer))
            for k in range(1, m):
                piece = outs[j].at[y, by_core, :, me.next_x(k)] if by_core == 0 else outs[j].at[me.next_y(k), by_core, :, x]
                shared.append(push(piece, piece, sibling))
        for copy in third:
            copy.wait()
        for j in range(n):
            for k in range(1, m):
                wide = outs[j].at[me.next_y(k), by_core] if by_core == 0 else outs[j].at[:, by_core, :, me.next_x(k)]
                shared.append(push(wide, wide, sibling))
        for copy in shared:
            copy.wait()

    for by_core in (0, 1):
        pl.when(c == by_core)(functools.partial(rest, by_core))


def gather_all(shards):
    ny, nz, nx = grid_sizes()
    n = len(shards)
    count = n * ((nz - 1) + (nx - 1) + 1 + (nx - 1) * 3)
    return pl.pallas_call(
        functools.partial(gather_kernel, n),
        in_specs=[ANY] * n,
        out_specs=[ANY] * n,
        out_shape=[jax.ShapeDtypeStruct((ny, 2, nz, nx) + s.shape, s.dtype) for s in shards],
        scratch_shapes=[pltpu.SemaphoreType.DMA((count,)), pltpu.SemaphoreType.DMA((count,)), pltpu.SemaphoreType.DMA((n,))],
        compiler_params=pltpu.CompilerParams(collective_id=0, has_side_effects=True, vmem_limit_bytes=16 << 20),
        name="gather_all",
    )(*shards)


def add_into(acc, at, terms, rows):
    total = acc[at]
    for ref, index in terms:
        total = total + ref[index]
    acc[at] = total


def scatter_kernel(n, *refs):
    grads, tile_ref = refs[:n], refs[n]
    outs, stat_ref = refs[n + 1 : 2 * n + 1], refs[2 * n + 1]
    acc, r1, r2, r3, r4 = (refs[2 * n + 2 + i * n : 2 * n + 2 + (i + 1) * n] for i in range(5))
    tc, tx, ty, tz, send, recv, local = refs[7 * n + 2 :]
    me = Place()
    y, c, z, x = me.y, me.core, me.z, me.x
    ny, nz, nx, m = me.ny, me.nz, me.nx, me.nx
    greet(me.neighbours())
    slot = [0]

    def push(src, dst, device):
        copy = remote(src, dst, send.at[slot[0]], recv.at[slot[0]], device)
        slot[0] += 1
        copy.start()
        return copy

    stage, own = [], []
    for j in range(n):
        stage.append([push(grads[j].at[:, me.other(), :, k], r1[j].at[:, k], me.at(core=me.other())) for k in range(nx)])
        mine = [
            pltpu.make_async_copy(grads[j].at[:, c, :, k], acc[j].at[:, k], local.at[j * nx + k]) for k in range(nx)
        ]
        for copy in mine:
            copy.start()
        own.append(mine)
    base = slot[0]

    def rest(by_core):
        slot[0] = base
        two, three, four = [], [], []
        for j in range(n):
            for copy in own[j] + stage[j]:
                copy.wait()

            def add1(i, carry):
                at = (lax.div(i, nx * nz), lax.rem(lax.div(i, nz), nx), lax.rem(i, nz))
                add_into(acc[j], at, [(r1[j], at)], None)
                return carry

            lax.fori_loop(0, ny * nx * nz, add1, 0)
            if by_core == 0:
                two.append([push(acc[j].at[:, me.next_x(k)], r2[j].at[k - 1], me.at(x=me.next_x(k))) for k in range(1, m)])
            else:
                two.append([push(acc[j].at[me.next_y(k)], r2[j].at[k - 1], me.at(y=me.next_y(k))) for k in range(1, m)])
        for j in range(n):
            for copy in two[j]:
                copy.wait()

            def add2(i, carry):
                a, b = lax.div(i, nz), lax.rem(i, nz)
                at = (a, x, b) if by_core == 0 else (y, a, b)
                add_into(acc[j], at, [(r2[j], (k, a, b)) for k in range(m - 1)], None)
                return carry

            lax.fori_loop(0, m * nz, add2, 0)
            if by_core == 0:
                three.append([push(acc[j].at[me.next_y(k), x], r3[j].at[k - 1], me.at(y=me.next_y(k))) for k in range(1, m)])
            else:
                three.append([push(acc[j].at[y, me.next_x(k)], r3[j].at[k - 1], me.at(x=me.next_x(k))) for k in range(1, m)])
        for j in range(n):
            for copy in three[j]:
                copy.wait()

            def add3(i, carry):
                add_into(acc[j], (y, x, i), [(r3[j], (k, i)) for k in range(m - 1)], None)
                return carry

            lax.fori_loop(0, nz, add3, 0)
            four.append(
                [push(acc[j].at[y, x, me.next_z(k)], r4[j].at[k - 1], me.at(z=me.next_z(k))) for k in range(1, nz)]
            )
        squares = jnp.zeros((8, HALF), F32)
        for j in range(n):
            for copy in four[j]:
                copy.wait()
            total = acc[j][y, x, z]
            for k in range(nz - 1):
                total = total + r4[j][k]
            outs[j][...] = total
            sq = colsum_any(total * total)
            squares = squares + sq[:, :HALF] + sq[:, HALF:]
        tc[c] = jnp.concatenate([squares, tile_ref[...]], 0)

    for by_core in (0, 1):
        pl.when(c == by_core)(functools.partial(rest, by_core))

    slot[0] = base + n * ((m - 1) * 2 + nz - 1)
    push(tc.at[c], tc.at[c], me.at(core=me.other())).wait()
    tx[x] = tc[0] + tc[1]
    for copy in [push(tx.at[x], tx.at[x], me.at(x=me.next_x(k))) for k in range(1, nx)]:
        copy.wait()
    ty[y] = functools.reduce(jnp.add, [tx[k] for k in range(nx)])
    for copy in [push(ty.at[y], ty.at[y], me.at(y=me.next_y(k))) for k in range(1, ny)]:
        copy.wait()
    tz[z] = functools.reduce(jnp.add, [ty[k] for k in range(ny)])
    for copy in [push(tz.at[z], tz.at[z], me.at(z=me.next_z(k))) for k in range(1, nz)]:
        copy.wait()
    stat_ref[...] = functools.reduce(jnp.add, [tz[k] for k in range(nz)])


def colsum_any(x):
    rows = x.shape[0]
    even = rows // 8 * 8
    out = colsum(x[:even]) if even else jnp.zeros((8, x.shape[1]), F32)
    if rows > even:
        out = out + jnp.pad(x[even:], ((0, 8 - rows + even), (0, 0)))
    return out


def scatter_sum(grads, tile):
    ny, nz, nx = grid_sizes()
    n = len(grads)
    shapes = [g.shape[-2:] for g in grads]
    count = n * nx + n * ((nx - 1) * 2 + nz - 1) + 1 + (nx - 1) + (ny - 1) + (nz - 1)

    def buffers(*lead):
        return [pltpu.VMEM(lead + s, F32) for s in shapes]

    return pl.pallas_call(
        functools.partial(scatter_kernel, n),
        in_specs=[ANY] * n + [INVMEM],
        out_specs=[INVMEM] * (n + 1),
        out_shape=[jax.ShapeDtypeStruct(s, F32) for s in shapes] + [jax.ShapeDtypeStruct((16, HALF), F32)],
        scratch_shapes=buffers(ny, nx, nz)
        + buffers(ny, nx, nz)
        + buffers(nx - 1, nx, nz)
        + buffers(nx - 1, nz)
        + buffers(nz - 1)
        + [pltpu.VMEM((k, 16, HALF), F32) for k in (2, nx, ny, nz)]
        + [pltpu.SemaphoreType.DMA((count,)), pltpu.SemaphoreType.DMA((count,)), pltpu.SemaphoreType.DMA((n * nx,))],
        compiler_params=pltpu.CompilerParams(collective_id=1, has_side_effects=True, vmem_limit_bytes=VMEM_LIMIT),
        name="scatter_sum",
    )(*grads, tile)


def group_kernel(stats, per, in_ref, out_ref, got, result, send, recv, local):
    nf = lax.axis_size("fsdp")
    dp, f = lax.axis_index("dp"), lax.axis_index("fsdp")
    peers = [lax.rem(f + k, nf) for k in range(1, nf)]
    greet([(dp, p) for p in peers])

    def part(ref, who):
        return ref.at[pl.ds(pl.multiple_of(who * per, per), per)]

    own = pltpu.make_async_copy(part(in_ref, f), got.at[f], local)
    own.start()
    copies = [
        remote(part(in_ref, p), got.at[f], send.at[k], recv.at[k], (dp, p)) for k, p in enumerate(peers)
    ]
    for copy in copies:
        copy.start()
    own.wait()
    for copy in copies:
        copy.wait()
    if stats:
        row = lax.broadcasted_iota(jnp.int32, (PACK, HALF), 0)
        lane = lax.broadcasted_iota(jnp.int32, (PACK, HALF), 1)
        router = jnp.where(row < ROUT, row, row - ROUT)
        pick = (lane // 8 == router) & (row < 2 * ROUT)
        src = lax.broadcasted_iota(jnp.int32, (HALF, D), 0)
        dst = lax.broadcasted_iota(jnp.int32, (HALF, D), 1)
        widen = jnp.where(src % 8 == dst // 32, 1.0, 0.0).astype(BF)

        def one(s, carry):
            lse = [got[d, s, 2 * ROUT : 2 * ROUT + 1, :] for d in range(nf)]
            top = functools.reduce(jnp.maximum, lse)
            total = top + jnp.log(functools.reduce(jnp.add, [jnp.exp(l - top) for l in lse]))
            out = jnp.where(row == 2 * ROUT, total, 0.0)
            share = jnp.concatenate([jnp.where(pick, jnp.exp(l - total), 0.0) for l in lse], 0)
            wide = mmw(split2(share), widen)
            for d in range(nf):
                w = wide[d * PACK : (d + 1) * PACK]
                w = jnp.where(row < ROUT, w[:, :HALF], w[:, HALF:])
                out = out + jnp.where(row < 2 * ROUT, w * got[d, s], 0.0)
            result[s] = out
            return carry

        lax.fori_loop(0, per, one, 0)
    else:
        result[...] = functools.reduce(jnp.add, [got[d] for d in range(nf)])
    own = pltpu.make_async_copy(result, part(out_ref, f), local)
    own.start()
    copies = [
        remote(result, part(out_ref, f), send.at[nf - 1 + k], recv.at[nf - 1 + k], (dp, p)) for k, p in enumerate(peers)
    ]
    for copy in copies:
        copy.start()
    own.wait()
    for copy in copies:
        copy.wait()


def group_combine(packed, stats, cid):
    nf = lax.axis_size("fsdp")
    per = packed.shape[0] // nf
    return pl.pallas_call(
        functools.partial(group_kernel, stats, per),
        in_specs=[INVMEM],
        out_specs=INVMEM,
        out_shape=jax.ShapeDtypeStruct(packed.shape, F32),
        scratch_shapes=[
            pltpu.VMEM((nf, per, PACK, HALF), F32),
            pltpu.VMEM((per, PACK, HALF), F32),
            pltpu.SemaphoreType.DMA((2 * nf - 2,)),
            pltpu.SemaphoreType.DMA((2 * nf - 2,)),
            pltpu.SemaphoreType.DMA,
        ],
        compiler_params=pltpu.CompilerParams(collective_id=cid, has_side_effects=True, vmem_limit_bytes=32 << 20),
        name="group_stats" if stats else "group_sum",
    )(packed)

LAYER_AT = SEGLEN + 1 + SEG
MERGE_AT = LAYER_AT + 46
HEAD_AT = MERGE_AT + 5
ROUTER_AT = HEAD_AT + PRED
VROWS = NVEC + 20


def own_size(devices):
    own = NVEC * D // devices
    return own, -(-own // D)


def prepare_kernel(nfeed, ser_ref, obs_ref, tgt_ref, mask_ref, count_ref, mat_ref, feed_ref, vec_ref, *outs):
    pieces, tgt, kept, scale_ref, mean_ref, here_ref, tile_ref, mat_o, feed_o, vec_o = outs
    for src, dst in ((mat_ref, mat_o), (feed_ref, feed_o), (vec_ref, vec_o)):
        rows = dst.shape[0]
        left, right = src[pl.ds(0, rows, stride=2), :], src[pl.ds(1, rows, stride=2), :]
        dst[...] = jnp.concatenate([left, right], 1).astype(BF)
    nv = ser_ref.shape[0]
    series, seen = ser_ref[...], obs_ref[...].astype(F32)
    counted = jnp.maximum(jnp.sum(seen, -1, keepdims=True), 1.0)
    mean = jnp.sum(seen * series, -1, keepdims=True) / counted
    center = (series - mean) * seen
    scale = jnp.sqrt(jnp.sum(center * center, -1, keepdims=True) / counted + norm_eps)
    slot = lax.axis_index("fsdp") * nv + lax.broadcasted_iota(jnp.int32, (nv, HALF), 0)
    here = jnp.where(slot < count_ref[0], 1.0, 0.0)
    here_ref[...] = here
    scale_ref[...] = jnp.broadcast_to(scale, (nv, PPAD))
    mean_ref[...] = jnp.broadcast_to(mean, (nv, PPAD))
    mask = mask_ref[...].astype(F32) * here[:, :1]
    tile_ref[...] = jnp.broadcast_to(jnp.sum(jnp.sum(mask, 0, keepdims=True), -1, keepdims=True), (8, HALF)) * (1.0 / (8 * HALF))
    lane = lax.broadcasted_iota(jnp.int32, (nv, PPAD), 1)

    def cut(x, dst):
        x = jnp.concatenate([x, jnp.zeros((nv, PPAD - 12), F32)], 1)
        for s in range(dst.shape[0]):
            dst[s] = jnp.where(lane < 12, x[:, 12 * s : 12 * s + PPAD], 0.0)

    cut(center / scale, pieces)
    cut(tgt_ref[...], tgt)
    cut(mask * (2.0 / (1 << 20)), kept)


def prepare(series, observed, targets, target_mask, counts, matrices, feed, vectors):
    nv = series.shape[0]
    shapes = [((SEG, nv, PPAD), F32), ((SEG // 2, nv, PPAD), F32), ((SEG // 2, nv, PPAD), F32), ((nv, PPAD), F32), ((nv, PPAD), F32)]
    shapes += [((nv, HALF), F32), ((8, HALF), F32)]
    shapes += [((x.shape[0] // 2, D), BF) for x in (matrices, feed, vectors)]
    return pl.pallas_call(
        functools.partial(prepare_kernel, 0),
        in_specs=[INVMEM] * 4 + [pl.BlockSpec(memory_space=pltpu.SMEM)] + [INVMEM] * 3,
        out_specs=[INVMEM] * len(shapes),
        out_shape=[jax.ShapeDtypeStruct(s, t) for s, t in shapes],
        compiler_params=pltpu.CompilerParams(vmem_limit_bytes=32 << 20),
        name="prepare",
    )(series, observed, targets, target_mask, counts, matrices, feed, vectors)


def unpack_kernel(devices, own, vec_ref, vecs, mvec, emb, place, head, r0, r1, flat):
    flat[...] = jnp.zeros(flat.shape, F32)
    rows = vec_ref.shape[1]
    lane = lax.broadcasted_iota(jnp.int32, (rows, D), 1)
    for d in range(devices):
        at, shift = divmod(own * d, D)
        block = vec_ref[d].astype(F32)
        if shift:
            block = pltpu.roll(block, shift, 1)
            flat[at + 1 : at + 1 + rows] += jnp.where(lane < shift, block, 0.0)
            block = jnp.where(lane >= shift, block, 0.0)
        flat[at : at + rows] += block

    def padded(at, count, total):
        return jnp.concatenate([flat[at : at + count], jnp.zeros((total - count, D), F32)], 0)

    for l in range(2):
        vecs[l] = padded(LAYER_AT + 23 * l, 23, 24)
    mvec[...] = padded(MERGE_AT, 5, 8)
    emb[...] = padded(0, SEGLEN, 16).astype(BF)
    head[...] = padded(HEAD_AT, PRED, PPAD).astype(BF)
    for s in range(SEG):
        place[s] = flat[SEGLEN + 1 + s : SEGLEN + 2 + s] + flat[SEGLEN : SEGLEN + 1]
        r0[s] = padded(ROUTER_AT + ROUT * s, ROUT, RPAD)
    for s in range(SEG // 2):
        r1[s] = padded(ROUTER_AT + ROUT * (SEG + s), ROUT, RPAD)


def unpack_vectors(gathered, own):
    devices, rows, _ = gathered.shape
    shapes = [((2, 24, D), F32), ((8, D), F32), ((16, D), BF), ((SEG, 1, D), F32), ((PPAD, D), BF)]
    shapes += [((SEG, RPAD, D), F32), ((SEG // 2, RPAD, D), F32)]
    return pl.pallas_call(
        functools.partial(unpack_kernel, devices, own),
        in_specs=[INVMEM],
        out_specs=[INVMEM] * len(shapes),
        out_shape=[jax.ShapeDtypeStruct(s, t) for s, t in shapes],
        scratch_shapes=[pltpu.VMEM((VROWS + 24, D), F32)],
        compiler_params=pltpu.CompilerParams(vmem_limit_bytes=32 << 20),
        name="unpack_vectors",
    )(gathered)


def assemble_kernel(devices, own, demb, dplace, *refs):
    (rt0, rs0, rr0, rt1, rs1, rr1, dmv, dhead, dr0, dr1), out, flat = refs[:10], refs[10], refs[11]
    flat[...] = jnp.zeros(flat.shape, F32)
    flat[0:SEGLEN] = demb[0:SEGLEN]
    place = jnp.sum(dplace[...].reshape(SEG, VB, D), 1)
    flat[SEGLEN : SEGLEN + 1] = jnp.sum(place, 0, keepdims=True)
    flat[SEGLEN + 1 : SEGLEN + 1 + SEG] = place
    at = LAYER_AT
    for ref in (rt0, rs0, rr0, rt1, rs1, rr1, dmv):
        count = ref.shape[0]
        flat[at : at + count] = jnp.sum(ref[...], 1)
        at += count
    flat[HEAD_AT : HEAD_AT + PRED] = dhead[0:PRED]
    for s in range(SEG):
        flat[ROUTER_AT + ROUT * s : ROUTER_AT + ROUT * (s + 1)] = dr0[s][:ROUT]
    for s in range(SEG // 2):
        flat[ROUTER_AT + ROUT * (SEG + s) : ROUTER_AT + ROUT * (SEG + s + 1)] = dr1[s][:ROUT]
    rows = out.shape[1]
    lane = lax.broadcasted_iota(jnp.int32, (rows, D), 1)
    inside = lax.broadcasted_iota(jnp.int32, (rows, D), 0) * D + lane < own
    for d in range(devices):
        at, shift = divmod(own * d, D)
        block = flat[at : at + rows]
        if shift:
            block = jnp.where(lane < D - shift, pltpu.roll(block, D - shift, 1), pltpu.roll(flat[at + 1 : at + 1 + rows], D - shift, 1))
        out[d] = jnp.where(inside, block, 0.0)


def assemble_vectors(parts, devices):
    own, rows = own_size(devices)
    return pl.pallas_call(
        functools.partial(assemble_kernel, devices, own),
        in_specs=[INVMEM] * len(parts),
        out_specs=INVMEM,
        out_shape=jax.ShapeDtypeStruct((devices, rows, D), F32),
        scratch_shapes=[pltpu.VMEM((VROWS + 24, D), F32)],
        compiler_params=pltpu.CompilerParams(vmem_limit_bytes=32 << 20),
        name="assemble_vectors",
    )(*parts)


def adam_update(weight, first_moment, second_moment, gradient):
    first_new = beta_one * first_moment + (1.0 - beta_one) * gradient
    second_new = beta_two * second_moment + (1.0 - beta_two) * gradient * gradient
    corrected = (
        first_new
        / (1.0 - beta_one**step_count)
        / (jnp.sqrt(second_new / (1.0 - beta_two**step_count)) + adam_eps)
    )
    return (weight - learn_rate * (corrected + weight_decay * weight), first_new, second_new)


def gradient_parts(ready, model, extras, up_rows, combine, nf, devices):
    pieces, tgt, kept, scale, mean, here = ready
    mvec, emb, place, head, routers0, routers1 = extras
    sb0, sb1, sf0, sf1, st = 12, 10, 20, 10, 10
    rf, rb = 20, 20
    half = SEG // 2
    dim0, kept0 = time_fwd(True, pieces, (emb, place), model, 0, SEG)
    o0 = send_fwd(dim0, routers0, here, model, 0, sf0, -(-SEG // nf) * nf)
    o0 = combine(o0, True, 2)
    x1, *saved = recv_fwd(dim0, o0, model, mvec, rf)
    dim1, kept1 = time_fwd(False, x1, (), model, 1, half)
    o1 = send_fwd(dim1, routers1, here, model, 1, sf1, -(-half // nf) * nf)
    o1 = combine(o1, True, 3)
    g_mat, g_feed, ddim1, do1, rr1, dhead = tail(dim1, o1, tgt, kept, scale, mean, model, head, st, up_rows)
    do1 = combine(do1, False, 4)
    g_mat, ddim1, dr1, rs1 = send_bwd(dim1, ddim1, routers1, o1, do1, here, model, 1, sb1, g_mat)
    g_mat, g_feed, rt1, dx1 = time_bwd(False, x1, (), ddim1, kept1, model, 1, half, (g_mat, g_feed), up_rows)
    g_mat, g_feed, ddim0, do0, rr0, dmv = recv_bwd(dim0, o0, dx1, saved, model, mvec, rb, (g_mat, g_feed), up_rows)
    do0 = combine(do0, False, 5)
    g_mat, ddim0, dr0, rs0 = send_bwd(dim0, ddim0, routers0, o0, do0, here, model, 0, sb0, g_mat)
    g_mat, g_feed, rt0, demb, dplace = time_bwd(
        True, pieces, (emb, place), ddim0, kept0, model, 0, SEG, (g_mat, g_feed), up_rows
    )
    g_vec = assemble_vectors((demb, dplace, rt0, rs0, rr0, rt1, rs1, rr1, dmv, dhead, dr0, dr1), devices)
    return g_mat, g_feed, g_vec


def on_device(series, observed, targets, target_mask, counts, matrices, feed_weights, vectors, matrices_first, matrices_second, feed_first, feed_second, vectors_first, vectors_second):
    nf = lax.axis_size("fsdp")
    nd = lax.axis_size("dp")
    devices = nf * nd
    own, vec_rows = own_size(devices)
    out = prepare(
        series[0],
        observed[0],
        targets[0],
        target_mask[0],
        counts,
        matrices.reshape(-1, HALF),
        feed_weights.reshape(-1, HALF),
        jnp.pad(vectors, (0, vec_rows * D - own)).reshape(-1, HALF),
    )
    ready, tile, shards = out[:6], out[6], out[7:]
    square, feed, vecs = gather_all(shards)
    square = square.reshape(NSQ, D, D)
    feed = feed.reshape(-1, D)
    up = feed[: 4 * FF].reshape(4, D, FF)
    down = feed.reshape(8, FF, D)
    vecs, *extras = unpack_vectors(vecs.reshape(devices, vec_rows, D), own)
    up_rows = feed_weights.shape[0] // FF
    g_mat, g_feed, g_vec = gradient_parts(ready, (square, up, down, vecs), extras, up_rows, group_combine, nf, devices)
    ny, nz, nx = grid_sizes()
    lead = (ny, 2, nz, nx)
    s_mat, s_feed, s_vec, sums = scatter_sum([g.reshape(lead + (-1, D)) for g in (g_mat, g_feed, g_vec)], tile)
    is_up = lax.axis_index("dp") * 2 < nd
    halves_of = s_feed.reshape(2, up_rows, D)
    s_feed = jnp.where(is_up, jnp.concatenate([halves_of[0], halves_of[1]], 1).reshape(-1), s_feed.reshape(-1))
    grads = (s_mat.reshape(-1), s_feed, s_vec.reshape(-1)[:own])
    upscale = (1 << 20) / jnp.maximum(jnp.sum(sums[8:]), 1.0)
    grad_norm = jnp.sqrt(jnp.sum(sums[:8])) * upscale
    factor = upscale * (clip_norm / jnp.maximum(grad_norm, clip_norm))
    new = (
        adam_update(matrices, matrices_first, matrices_second, grads[0] * factor)
        + adam_update(feed_weights, feed_first, feed_second, grads[1] * factor)
        + adam_update(vectors, vectors_first, vectors_second, grads[2] * factor)
    )
    return (grad_norm,) + new


def solution(mesh):
    both = P(("dp", "fsdp"))
    data = P("dp", "fsdp", None)
    return jax.shard_map(
        on_device,
        mesh=mesh,
        in_specs=(data,) * 4 + (P("dp"),) + (both,) * 9,
        out_specs=(P(),) + (both,) * 9,
        check_vma=False,
    )
```

```python
import functools
import jax
import jax.numpy as jnp
from jax import lax
from jax.experimental import pallas as pl
from jax.experimental.pallas import tpu as pltpu
from jax.sharding import PartitionSpec as P

D = 256
HEADS = 8
FF = 512
ROUT = 10
RPAD = 16
SEGLEN = 12
PRED = 12
PPAD = 16
SEG = 60
NSQ = 26
NVEC = 1036
HALF = 128
VB = 8
UNROLL = 8
UNROLL_BACK = 8

BF = jnp.bfloat16
F32 = jnp.float32
SCALE = (D // HEADS) ** (-0.5)
negative = -1e30
norm_eps = 1e-05
beta_one = 0.9
beta_two = 0.999
adam_eps = 1e-08
weight_decay = 0.01
learn_rate = 0.2
clip_norm = 0.01
step_count = 10.0
VMEM_LIMIT = 60 << 20


ANY = pl.BlockSpec(memory_space=pl.ANY)
INVMEM = pl.BlockSpec(memory_space=pltpu.VMEM)


def split2(x):
    hi = x.astype(BF)
    return hi, (x - hi.astype(F32)).astype(BF)


def dots(a, b, ca, cb):
    return lax.dot_general(a, b, (((ca,), (cb,)), ((), ())), preferred_element_type=F32)


def mmw(x2, w):
    return dots(x2[0], w, 1, 0) + dots(x2[1], w, 1, 0)


def mmwt(x2, w):
    return dots(x2[0], w, 1, 1) + dots(x2[1], w, 1, 1)


def rows2(a2):
    return jnp.concatenate([a2[0], a2[1]], 0)


def nn3(a2, b2):
    m = a2[0].shape[0]
    both = dots(rows2(a2), b2[0], 1, 0)
    return both[:m] + both[m:] + dots(a2[0], b2[1], 1, 0)


def nt3(a2, b2):
    m = a2[0].shape[0]
    both = dots(rows2(a2), b2[0], 1, 1)
    return both[:m] + both[m:] + dots(a2[0], b2[1], 1, 1)


def tn3(a2, b2):
    n = b2[0].shape[1]
    both = dots(a2[0], jnp.concatenate([b2[0], b2[1]], 1), 0, 0)
    return both[:, :n] + both[:, n:] + dots(a2[1], b2[0], 0, 0)


def norm_fwd(z, gain, bias):
    center = z - jnp.mean(z, -1, keepdims=True)
    inv = lax.rsqrt(jnp.mean(center * center, -1, keepdims=True) + norm_eps)
    unit = center * inv
    return unit * gain + bias, unit, inv


def norm_bwd(dy, unit, inv, gain):
    t = dy * gain
    return inv * (t - jnp.mean(t, -1, keepdims=True) - unit * jnp.mean(t * unit, -1, keepdims=True))


def colsum(x):
    return jnp.sum(x.reshape(x.shape[0] // 8, 8, x.shape[1]), 0)


def gelu_cdf(u):
    return 0.5 + 0.5 * lax.erf(u * 0.7071067811865476)


def gelu_slope(u, cdf):
    return cdf + u * (jnp.exp(-0.5 * u * u) * 0.3989422804014327)


def halves(x):
    return x[:, :HALF], x[:, HALF:]


def lane_head(rows):
    return lax.broadcasted_iota(jnp.int32, (rows, HALF), 1) // 32


def spread_heads(x, zero):
    head = lane_head(x.shape[0])
    return jnp.concatenate([jnp.where(head == h, x, zero) for h in range(4)], 0)


def gather_heads(x, group):
    head = lane_head(group)
    out = x[3 * group :]
    for h in range(3):
        out = jnp.where(head == h, x[h * group : (h + 1) * group], out)
    return out


def ones_heads(group, count):
    row = lax.broadcasted_iota(jnp.int32, (4 * group, HALF), 0)
    lane = lax.broadcasted_iota(jnp.int32, (4 * group, HALF), 1)
    return jnp.where((row // group == lane // 32) & (row % group < count), 1.0, 0.0).astype(BF)


def group_max(s, group, count):
    lane = lax.broadcasted_iota(jnp.int32, (s.shape[0], HALF), 1)
    outs = []
    for t in range(s.shape[1] // HALF):
        part = s[:, t * HALF : (t + 1) * HALF]
        top = None
        for g in range(HALF // group):
            here = (lane // group == g)
            best = jnp.max(jnp.where((lane // group == g) & (lane % group < count), part, negative), -1, keepdims=True)
            top = jnp.broadcast_to(best, part.shape) if top is None else jnp.where(here, best, top)
        outs.append(jnp.where(lane % group < count, part - top, negative))
    return jnp.concatenate(outs, 1)


def time_parts(units, group, ref):
    return [split2(ref[c, pl.ds(v, group, stride=VB), :]) for c, v in units]


def spread2(x2):
    zero = jnp.zeros((), BF)
    return spread_heads(x2[0], zero), spread_heads(x2[1], zero)


def time_attend(units, group, count, q_s, k_s, v_s, o_s, p_s, l_s):
    q = time_parts(units, group, q_s)
    k = [spread2(x2) for x2 in time_parts(units, group, k_s)]
    scores = [
        dots(jnp.concatenate(q2, 1), jnp.concatenate([k2[0], k2[0]], 1), 1, 1) + dots(q2[0], k2[1], 1, 1)
        for q2, k2 in zip(q, k)
    ]
    probs = [jnp.exp(group_max(s, group, count)) for s in scores]
    probs2 = [split2(p) for p in probs]
    w = [spread2(x2) for x2 in time_parts(units, group, v_s)]
    ones = ones_heads(group, count)
    both = [dots(rows2(p2), jnp.concatenate([w2[0], ones], 1), 1, 0) for p2, w2 in zip(probs2, w)]
    both = [b[:group] + b[group:] for b in both]
    inv = [1.0 / b[:, HALF:] for b in both]
    mixed = [(b[:, :HALF] + dots(p2[0], w2[1], 1, 0)) * i for b, p2, w2, i in zip(both, probs2, w, inv)]
    for (c, v), o, p, i in zip(units, mixed, probs, inv):
        o_s[c, pl.ds(v, group, stride=VB), :] = o
        p_s[c, v] = p
        l_s[c, v] = i


def time_attend_back(units, group, count, q_s, k_s, v_s, o_s, p_s, l_s, do_s, dq_s, dk_s, dv_s):
    d = [do_s[c, pl.ds(v, group, stride=VB), :] * l_s[c, v] for c, v in units]
    e2 = [split2(x * o_s[c, pl.ds(v, group, stride=VB), :]) for x, (c, v) in zip(d, units)]
    d2 = [split2(x) for x in d]
    w = [spread2(x2) for x2 in time_parts(units, group, v_s)]
    ones = -ones_heads(group, count)
    both = [
        dots(
            jnp.concatenate([jnp.concatenate([a[0], b[0]], 1), jnp.concatenate([a[1], b[1]], 1)], 0),
            jnp.concatenate([w2[0], ones], 1),
            1,
            1,
        )
        for a, b, w2 in zip(d2, e2, w)
    ]
    dp = [b[:group] + b[group:] + dots(a[0], w2[1], 1, 1) for b, a, w2 in zip(both, d2, w)]
    probs = [p_s[c, v] for c, v in units]
    s2 = [split2(p * x) for p, x in zip(probs, dp)]
    p2 = [split2(p) for p in probs]
    k = [spread2(x2) for x2 in time_parts(units, group, k_s)]
    both = [dots(rows2(a), k2[0], 1, 0) for a, k2 in zip(s2, k)]
    dq = [b[:group] + b[group:] + dots(a[0], k2[1], 1, 0) for b, a, k2 in zip(both, s2, k)]
    q = time_parts(units, group, q_s)
    dk = [gather_heads(tn3(a, q2), group) for a, q2 in zip(s2, q)]
    dv = [gather_heads(tn3(a, x), group) for a, x in zip(p2, d2)]
    for (c, v), x, y, z in zip(units, dq, dk, dv):
        at = pl.ds(v, group, stride=VB)
        dq_s[c, at, :] = x
        dk_s[c, at, :] = y
        dv_s[c, at, :] = z


def store_halves(ref, x):
    rows = x.shape[0]
    ref[0, :rows, :] = x[:, :HALF]
    ref[1, :rows, :] = x[:, HALF:]


def load_halves(ref, rows):
    return jnp.concatenate([ref[0, :rows, :], ref[1, :rows, :]], 1)


def zero_tail(ref, rows):
    tail = ref.shape[1] - rows
    ref[:, rows:, :] = jnp.zeros((2, tail, HALF), F32)


def time_forward(x, w, vec, count, group, kept):
    q_s, k_s, v_s, o_s, p_s, l_s, z1_s, u_s, z2_s = kept
    rows = count * VB
    x2 = split2(x)
    store_halves(q_s, (mmw(x2, w["q"]) + vec[0:1]) * SCALE)
    store_halves(k_s, mmw(x2, w["k"]))
    store_halves(v_s, mmw(x2, w["v"]) + vec[1:2])
    for ref in (q_s, k_s, v_s):
        zero_tail(ref, rows)

    def some(i, carry):
        units = [(c, i * UNROLL + k) for k in range(UNROLL) for c in range(2)]
        time_attend(units, group, count, q_s, k_s, v_s, o_s, p_s, l_s)
        return carry

    lax.fori_loop(0, VB // UNROLL, some, 0)
    z1 = x + mmw(split2(load_halves(o_s, rows)), w["o"]) + vec[2:3]
    z1_s[...] = z1
    h, _, _ = norm_fwd(z1, vec[3:4], vec[4:5])
    u = mmw(split2(h), w["up"]) + jnp.concatenate([vec[5:6], vec[6:7]], 1)
    u_s[...] = u
    z2 = h + mmw(split2(u * gelu_cdf(u)), w["down"]) + vec[7:8]
    z2_s[...] = z2
    return norm_fwd(z2, vec[8:9], vec[9:10])[0]


def embed_block(pieces, emb, place):
    return mmw(split2(pieces), emb) + place


TIME_W = ("q", "k", "v", "o", "up", "down")


def time_fwd_kernel(first, count, group, *refs):
    if first:
        x_ref, emb_ref, place_ref = refs[:3]
        refs = refs[3:]
    else:
        x_ref = refs[0]
        refs = refs[1:]
    w = {name: refs[i][...] for i, name in enumerate(TIME_W)}
    vec_ref, y_ref = refs[6:8]
    rows = count * VB
    if first:
        place = jnp.broadcast_to(place_ref[...], (count, VB, D)).reshape(rows, D)
        x = embed_block(x_ref[...].reshape(rows, 16), emb_ref[...], place)
    else:
        x = x_ref[...].reshape(rows, D)
    y = time_forward(x, w, vec_ref[...], count, group, refs[8:])
    y_ref[...] = y.reshape(count, VB, D)


def whole(shape):
    return pl.BlockSpec(shape, lambda i: (0,) * len(shape))


def params_spec():
    return pltpu.CompilerParams(vmem_limit_bytes=VMEM_LIMIT)


def pick(shape, index):
    return pl.BlockSpec((None,) + shape, lambda i: (index,) + (0,) * len(shape))


def weight_specs(squares, feed, layer):
    specs = [pick((D, D), k) for k in squares]
    if feed is not None:
        specs += [pick((D, FF), feed), pick((FF, D), 4 + feed)]
    return specs + [pick((24, D), layer)]


def weight_args(model, squares, feed):
    square, up, down, vecs = model
    return [square] * len(squares) + ([up, down] if feed is not None else []) + [vecs]


def flush(step, last, accs, mat_at, up_acc, down_acc, feed_at, up_rows, g_mat, g_feed, sems):
    @pl.when(step == last)
    def _():
        copies = []

        def add(src, dst):
            copies.append(pltpu.make_async_copy(src, dst, sems.at[len(copies)]))

        for acc, at in zip(accs, mat_at):
            add(acc, g_mat.at[pl.ds(at, acc.shape[0])] if len(acc.shape) == 3 else g_mat.at[at])
        if up_acc is not None:
            for k in range(D // up_rows):
                for half in range(2):
                    base = 2 * D * feed_at + (2 * k + half) * up_rows
                    add(up_acc.at[pl.ds(k * up_rows, up_rows), pl.ds(half * D, D)], g_feed.at[pl.ds(base, up_rows)])
            add(down_acc, g_feed.at[pl.ds(4 * FF + feed_at * FF, FF)])
        for copy in copies:
            copy.start()
        for copy in copies:
            copy.wait()


def pack_shapes():
    return [jax.ShapeDtypeStruct((NSQ, D, D), F32), jax.ShapeDtypeStruct((8 * FF, D), F32)]


def flush_count(mats, up_rows):
    return mats + (2 * D // up_rows + 1 if up_rows else 0)


def time_kept(count, group, nb):
    pad, rows = group * VB, count * VB
    shapes = [(2, pad, HALF)] * 4 + [(2, VB, group, 4 * group), (2, VB, group, HALF), (rows, D), (rows, FF), (rows, D)]
    specs = [pl.BlockSpec((None,) + s, lambda i, n=len(s): (i,) + (0,) * n) for s in shapes]
    return specs, [jax.ShapeDtypeStruct((nb,) + s, F32) for s in shapes]


def time_fwd(first, x, extra, model, layer, count):
    squares = [12 * layer + k for k in range(4)]
    group = 64 if count > 32 else 32
    nv = x.shape[1]
    width = x.shape[2]
    specs = [pl.BlockSpec((count, VB, width), lambda i: (0, i, 0))]
    if first:
        specs += [whole((16, D)), whole((count, 1, D))]
    kept_specs, kept_shapes = time_kept(count, group, nv // VB)
    out = pl.pallas_call(
        functools.partial(time_fwd_kernel, first, count, group),
        grid=(nv // VB,),
        in_specs=specs + weight_specs(squares, 2 * layer, layer),
        out_specs=[pl.BlockSpec((count, VB, D), lambda i: (0, i, 0))] + kept_specs,
        out_shape=[jax.ShapeDtypeStruct((count, nv, D), F32)] + kept_shapes,
        compiler_params=params_spec(),
        name="time_fwd",
    )(x, *extra, *weight_args(model, squares, 2 * layer))
    return out[0], out[1:]


def time_bwd_kernel(first, count, group, layer, up_rows, *refs):
    if first:
        x_ref, emb_ref, place_ref = refs[:3]
        refs = refs[3:]
    else:
        x_ref = refs[0]
        refs = refs[1:]
    dy_ref = refs[0]
    q_s, k_s, v_s, o_s, p_s, l_s, z1_s, u_s, z2_s = refs[1:10]
    w = {name: refs[10 + i][...] for i, name in enumerate(TIME_W)}
    vec_ref = refs[16]
    g_mat, g_feed = refs[19:21]
    outs = refs[21:]
    n_out = 3 if first else 2
    tail = outs[1:n_out]
    accs = outs[n_out : n_out + 6]
    sems = outs[n_out + 6]
    g = dict(zip(TIME_W + ("rows",), tuple(accs) + (outs[0],)))
    do_s, dq_s, dk_s, dv_s = outs[n_out + 7 :]
    rows = count * VB
    step = pl.program_id(0)

    @pl.when(step == 0)
    def _():
        for ref in list(g.values()) + (list(tail) if first else []):
            ref[...] = jnp.zeros(ref.shape, F32)

    vec = vec_ref[...]
    if first:
        place = jnp.broadcast_to(place_ref[...], (count, VB, D)).reshape(rows, D)
        pieces = x_ref[...].reshape(rows, 16)
        x = embed_block(pieces, emb_ref[...], place)
    else:
        x = x_ref[...].reshape(rows, D)
    x2 = split2(x)
    mixed = load_halves(o_s, rows)
    h, unit1, inv1 = norm_fwd(z1_s[...], vec[3:4], vec[4:5])
    u = u_s[...]
    cdf = gelu_cdf(u)
    _, unit2, inv2 = norm_fwd(z2_s[...], vec[8:9], vec[9:10])
    dy = dy_ref[...].reshape(rows, D)
    g["rows"][8] += colsum(dy * unit2)
    g["rows"][9] += colsum(dy)
    dz2 = norm_bwd(dy, unit2, inv2, vec[8:9])
    g["rows"][7] += colsum(dz2)
    dz22 = split2(dz2)
    g["down"][...] += tn3(split2(u * cdf), dz22)
    du = mmwt(dz22, w["down"]) * gelu_slope(u, cdf)
    g["rows"][5] += colsum(du[:, :D])
    g["rows"][6] += colsum(du[:, D:])
    du2 = split2(du)
    g["up"][...] += tn3(split2(h), du2)
    dh = dz2 + mmwt(du2, w["up"])
    g["rows"][3] += colsum(dh * unit1)
    g["rows"][4] += colsum(dh)
    dz1 = norm_bwd(dh, unit1, inv1, vec[3:4])
    g["rows"][2] += colsum(dz1)
    dz12 = split2(dz1)
    g["o"][...] += tn3(split2(mixed), dz12)
    store_halves(do_s, mmwt(dz12, w["o"]))
    zero_tail(do_s, rows)

    def some(i, carry):
        units = [(c, i * UNROLL_BACK + k) for k in range(UNROLL_BACK) for c in range(2)]
        time_attend_back(units, group, count, q_s, k_s, v_s, o_s, p_s, l_s, do_s, dq_s, dk_s, dv_s)
        return carry

    lax.fori_loop(0, VB // UNROLL_BACK, some, 0)
    dq = load_halves(dq_s, rows) * SCALE
    g["rows"][0] += colsum(dq)
    dq2 = split2(dq)
    g["q"][...] += tn3(x2, dq2)
    dx = dz1 + mmwt(dq2, w["q"])
    dk2 = split2(load_halves(dk_s, rows))
    g["k"][...] += tn3(x2, dk2)
    dx = dx + mmwt(dk2, w["k"])
    dv = load_halves(dv_s, rows)
    g["rows"][1] += colsum(dv)
    dv2 = split2(dv)
    g["v"][...] += tn3(x2, dv2)
    dx = dx + mmwt(dv2, w["v"])
    if first:
        tail[0][...] += tn3(split2(pieces), split2(dx))
        tail[1][...] += dx
    else:
        tail[0][...] = dx.reshape(count, VB, D)
    flush(
        step, pl.num_programs(0) - 1, accs[:4], [12 * layer + k for k in range(4)], accs[4], accs[5], 2 * layer, up_rows,
        g_mat, g_feed, sems,
    )


def time_bwd(first, x, extra, dy, kept, model, layer, count, packs, up_rows):
    group = 64 if count > 32 else 32
    nv = x.shape[1]
    width = x.shape[2]
    pad = group * VB
    squares = [12 * layer + k for k in range(4)]
    block = pl.BlockSpec((count, VB, D), lambda i: (0, i, 0))
    specs = [pl.BlockSpec((count, VB, width), lambda i: (0, i, 0))]
    if first:
        specs += [whole((16, D)), whole((count, 1, D))]
    specs += [block] + time_kept(count, group, nv // VB)[0] + weight_specs(squares, 2 * layer, layer)
    grad_shapes = [(10, 8, D)] + ([(16, D), (count * VB, D)] if first else [])
    out_specs = [ANY] * 2 + [whole(s) for s in grad_shapes]
    out_shape = pack_shapes() + [jax.ShapeDtypeStruct(s, F32) for s in grad_shapes]
    if not first:
        out_specs.append(block)
        out_shape.append(jax.ShapeDtypeStruct((count, nv, D), F32))
    return pl.pallas_call(
        functools.partial(time_bwd_kernel, first, count, group, layer, up_rows),
        grid=(nv // VB,),
        in_specs=specs + [ANY] * 2,
        out_specs=out_specs,
        out_shape=out_shape,
        input_output_aliases={len(specs): 0, len(specs) + 1: 1},
        scratch_shapes=[pltpu.VMEM((D, D), F32)] * 4
        + [pltpu.VMEM((D, FF), F32), pltpu.VMEM((FF, D), F32), pltpu.SemaphoreType.DMA((flush_count(4, up_rows),))]
        + [pltpu.VMEM((2, pad, HALF), F32)] * 4,
        compiler_params=params_spec(),
        name="time_bwd",
    )(x, *extra, dy, *kept, *weight_args(model, squares, 2 * layer), *packs)

SB_ROWS = 64


def head_rows():
    sub = lax.broadcasted_iota(jnp.int32, (8, D), 0)
    lane = lax.broadcasted_iota(jnp.int32, (8, D), 1)
    return jnp.where(sub == lane // 32, 1.0, 0.0).astype(F32)


def spread_rows(x):
    wide = jnp.broadcast_to(x[:, None, :], (RPAD, HEADS, D)) * head_rows()[None]
    return wide.reshape(RPAD * HEADS, D)


def gather_rows(x):
    return jnp.sum(x.reshape(RPAD, HEADS, D) * head_rows()[None], 1)


PACK = 24


def pack_rows(x, last=None):
    last = jnp.zeros((1, HALF), F32) if last is None else last
    return jnp.concatenate([x[:ROUT, :HALF], x[:ROUT, HALF:], last, jnp.zeros((PACK - 2 * ROUT - 1, HALF), F32)], 0)


def unpack_rows(x):
    x = jnp.concatenate([x[:ROUT], x[ROUT : 2 * ROUT]], 1)
    return jnp.concatenate([x, jnp.zeros((RPAD - ROUT, D), F32)], 0)


def unpack_block(ref, sb):
    return jnp.concatenate([unpack_rows(ref[s]) for s in range(sb)], 0)


def pack_block(ref, x, sb):
    for s in range(sb):
        ref[s] = pack_rows(x[s * RPAD : (s + 1) * RPAD])


def valid_lane(rows):
    return lax.broadcasted_iota(jnp.int32, (rows, HALF), 1) < ROUT * HEADS


def router_reduce(x, op):
    for shift in (8, 16, 32, 64):
        x = op(x, pltpu.roll(x, shift, 1))
    return x


def merge_rows(y, pairs, vec):
    wide = y.reshape(pairs, 2, SB_ROWS, D)
    wide = jnp.concatenate([wide[:, 0].reshape(pairs * SB_ROWS, D), wide[:, 1].reshape(pairs * SB_ROWS, D)], 1)
    gain = jnp.concatenate([vec[0:1], vec[1:2]], 1)
    bias = jnp.concatenate([vec[2:3], vec[3:4]], 1)
    return norm_fwd(wide, gain, bias) + (gain,)


RECV_W = ("so", "rk", "rv", "rq", "ro", "up", "down")


def recv_buffer(o2, w, vec):
    buf2 = split2(mmw(o2, w["so"]) + vec[12:13])
    kb = mmw(buf2, w["rk"])
    vb = mmw(buf2, w["rv"]) + vec[14:15]
    segs = range(kb.shape[0] // RPAD)
    k = [split2(spread_rows(kb[s * RPAD : (s + 1) * RPAD])) for s in segs]
    v = [split2(spread_rows(vb[s * RPAD : (s + 1) * RPAD])) for s in segs]
    return buf2, k, v


def recv_forward(send, o_rows, w, vec):
    sb = send.shape[0] // SB_ROWS
    send2 = split2(send)
    o2 = split2(o_rows)
    buf2, k, v = recv_buffer(o2, w, vec)
    q = (mmw(send2, w["rq"]) + vec[13:14]) * SCALE
    segs = range(sb)
    ok = valid_lane(SB_ROWS)
    scores = [jnp.where(ok, nt3(split2(q[s * SB_ROWS : (s + 1) * SB_ROWS]), k[s]), negative) for s in segs]
    probs = [jnp.exp(sc - router_reduce(sc, jnp.maximum)) for sc in scores]
    probs = [p / router_reduce(p, jnp.add) for p in probs]
    mixed = jnp.concatenate([nn3(split2(p), v2) for p, v2 in zip(probs, v)], 0)
    z3 = send + mmw(split2(mixed), w["ro"]) + vec[15:16]
    g, unit3, inv3 = norm_fwd(z3, vec[16:17], vec[17:18])
    u = mmw(split2(g), w["up"]) + jnp.concatenate([vec[18:19], vec[19:20]], 1)
    cdf = gelu_cdf(u)
    z4 = g + mmw(split2(u * cdf), w["down"]) + vec[20:21]
    y, unit4, inv4 = norm_fwd(z4, vec[21:22], vec[22:23])
    kept = (send2, o2, buf2, mixed, g, unit3, inv3, u, cdf, unit4, inv4, q, k, v, probs)
    return y, kept, (q, mixed, jnp.concatenate(probs, 0), z3, u, z4)


def recv_restore(send, o_rows, w, vec, saved):
    q, mixed, p, z3, u, z4 = saved
    o2 = split2(o_rows)
    buf2, k, v = recv_buffer(o2, w, vec)
    g, unit3, inv3 = norm_fwd(z3, vec[16:17], vec[17:18])
    y, unit4, inv4 = norm_fwd(z4, vec[21:22], vec[22:23])
    probs = [p[s * SB_ROWS : (s + 1) * SB_ROWS] for s in range(send.shape[0] // SB_ROWS)]
    return y, (split2(send), o2, buf2, mixed, g, unit3, inv3, u, gelu_cdf(u), unit4, inv4, q, k, v, probs)


KEPT_WIDTHS = (D, D, HALF, D, FF, D)


def kept_specs(sb):
    return [pl.BlockSpec((sb * SB_ROWS, k), lambda i: (i, 0)) for k in KEPT_WIDTHS]


RECV_G = RECV_W + ("rows",)


def recv_backward(dy, kept, w, vec, g):
    send2, o2, buf2, mixed, gg, unit3, inv3, u, cdf, unit4, inv4, q, k, v, probs = kept
    sb = dy.shape[0] // SB_ROWS
    rows = g["rows"]
    rows[9] += colsum(dy * unit4)
    rows[10] += colsum(dy)
    dz4 = norm_bwd(dy, unit4, inv4, vec[21:22])
    rows[8] += colsum(dz4)
    dz42 = split2(dz4)
    g["down"][...] += tn3(split2(u * cdf), dz42)
    du = mmwt(dz42, w["down"]) * gelu_slope(u, cdf)
    rows[6] += colsum(du[:, :D])
    rows[7] += colsum(du[:, D:])
    du2 = split2(du)
    g["up"][...] += tn3(split2(gg), du2)
    dg = dz4 + mmwt(du2, w["up"])
    rows[4] += colsum(dg * unit3)
    rows[5] += colsum(dg)
    dz3 = norm_bwd(dg, unit3, inv3, vec[16:17])
    rows[3] += colsum(dz3)
    dz32 = split2(dz3)
    g["ro"][...] += tn3(split2(mixed), dz32)
    do = mmwt(dz32, w["ro"])
    segs = range(sb)
    d = [split2(do[s * SB_ROWS : (s + 1) * SB_ROWS]) for s in segs]
    dp = [nt3(d2, v2) for d2, v2 in zip(d, v)]
    ds = [split2(p * (x - router_reduce(p * x, jnp.add))) for p, x in zip(probs, dp)]
    dq = jnp.concatenate([nn3(s2, k2) for s2, k2 in zip(ds, k)], 0) * SCALE
    q = [split2(q[s * SB_ROWS : (s + 1) * SB_ROWS]) for s in segs]
    dk = jnp.concatenate([gather_rows(tn3(s2, q2)) for s2, q2 in zip(ds, q)], 0)
    dv = jnp.concatenate([gather_rows(tn3(split2(p), d2)) for p, d2 in zip(probs, d)], 0)
    rows[1] += colsum(dq)
    dq2 = split2(dq)
    g["rq"][...] += tn3(send2, dq2)
    dsend = dz3 + mmwt(dq2, w["rq"])
    dk2 = split2(dk)
    dv2 = split2(dv)
    rows[2] += colsum(dv)
    g["rk"][...] += tn3(buf2, dk2)
    g["rv"][...] += tn3(buf2, dv2)
    dbuf = mmwt(dk2, w["rk"]) + mmwt(dv2, w["rv"])
    rows[0] += colsum(dbuf)
    dbuf2 = split2(dbuf)
    g["so"][...] += tn3(o2, dbuf2)
    return dsend, mmwt(dbuf2, w["so"])


def recv_squares(layer):
    return [12 * layer + k for k in (7, 9, 10, 8, 11)]


def seg_block(sb, rows=SB_ROWS, width=D):
    return pl.BlockSpec((sb, rows, width), lambda i: (i, 0, 0))


MERGE = pl.BlockSpec((2, D, D), lambda i: (12, 0, 0))


def pack_spec(sb):
    return seg_block(sb, PACK, HALF)


def recv_fwd_kernel(sb, send_ref, o_ref, *refs):
    w = {n: refs[i][...] for i, n in enumerate(RECV_W)}
    vec_ref, mvec_ref, mw_ref, out_ref = refs[7:11]
    y, _, saved = recv_forward(send_ref[...].reshape(sb * SB_ROWS, D), unpack_block(o_ref, sb), w, vec_ref[...])
    for ref, x in zip(refs[11:], saved):
        ref[...] = x
    mvec = mvec_ref[...]
    wide, _, _, _ = merge_rows(y, sb // 2, mvec)
    out_ref[...] = (mmw(split2(wide), mw_ref[...].reshape(2 * D, D)) + mvec[4:5]).reshape(sb // 2, SB_ROWS, D)


def recv_fwd(send, o, model, mvec, sb):
    squares = recv_squares(0)
    n = send.shape[0]
    return pl.pallas_call(
        functools.partial(recv_fwd_kernel, sb),
        grid=(n // sb,),
        in_specs=[seg_block(sb), pack_spec(sb)] + weight_specs(squares, 1, 0) + [whole((8, D)), MERGE],
        out_specs=[seg_block(sb // 2)] + kept_specs(sb),
        out_shape=[jax.ShapeDtypeStruct((n // 2, SB_ROWS, D), F32)]
        + [jax.ShapeDtypeStruct((n * SB_ROWS, k), F32) for k in KEPT_WIDTHS],
        compiler_params=params_spec(),
        name="recv_fwd",
    )(send, o, *weight_args(model, squares, 1), mvec, model[0])


def recv_bwd_kernel(sb, up_rows, send_ref, o_ref, dx_ref, *refs):
    saved = [ref[...] for ref in refs[:6]]
    refs = refs[6:]
    w = {n: refs[i][...] for i, n in enumerate(RECV_W)}
    vec_ref, mvec_ref, mw_ref = refs[7:10]
    g_mat, g_feed, dsend_ref, do_ref, rows_ref, dmv_ref = refs[12:18]
    accs, dmw_ref, sems = refs[18:25], refs[25], refs[26]
    g = dict(zip(RECV_G, tuple(accs) + (rows_ref,)))

    @pl.when(pl.program_id(0) == 0)
    def _():
        for ref in list(g.values()) + [dmw_ref, dmv_ref]:
            ref[...] = jnp.zeros(ref.shape, F32)

    vec = vec_ref[...]
    y, kept = recv_restore(send_ref[...].reshape(sb * SB_ROWS, D), unpack_block(o_ref, sb), w, vec, saved)
    pairs = sb // 2
    wide, unit, inv, gain = merge_rows(y, pairs, mvec_ref[...])
    dx = dx_ref[...].reshape(pairs * SB_ROWS, D)
    dmv_ref[4] += colsum(dx)
    dx2 = split2(dx)
    dmw_ref[...] += tn3(split2(wide), dx2).reshape(2, D, D)
    dn = mmwt(dx2, mw_ref[...].reshape(2 * D, D))
    part = colsum(dn * unit)
    dmv_ref[0] += part[:, :D]
    dmv_ref[1] += part[:, D:]
    part = colsum(dn)
    dmv_ref[2] += part[:, :D]
    dmv_ref[3] += part[:, D:]
    dwide = norm_bwd(dn, unit, inv, gain)
    left = dwide[:, :D].reshape(pairs, 1, SB_ROWS, D)
    right = dwide[:, D:].reshape(pairs, 1, SB_ROWS, D)
    dy = jnp.concatenate([left, right], 1).reshape(sb * SB_ROWS, D)
    dsend, do = recv_backward(dy, kept, w, vec, g)
    dsend_ref[...] = dsend.reshape(sb, SB_ROWS, D)
    pack_block(do_ref, do, sb)
    recv_flush(accs, [(dmw_ref, 24)], 0, up_rows, g_mat, g_feed, sems)


RECV_ACC = [pltpu.VMEM((D, D), F32)] * 5 + [pltpu.VMEM((D, FF), F32), pltpu.VMEM((FF, D), F32)]


def recv_flush(accs, more, layer, up_rows, g_mat, g_feed, sems):
    flush(
        pl.program_id(0), pl.num_programs(0) - 1, list(accs[:5]) + [m for m, _ in more],
        recv_squares(layer) + [at for _, at in more], accs[5], accs[6], 2 * layer + 1, up_rows, g_mat, g_feed, sems,
    )


def recv_bwd(send, o, dx, kept, model, mvec, sb, packs, up_rows):
    n = send.shape[0]
    squares = recv_squares(0)
    shapes = [(11, 8, D), (5, 8, D)]
    specs = [seg_block(sb), pack_spec(sb), seg_block(sb // 2)] + kept_specs(sb)
    specs += weight_specs(squares, 1, 0) + [whole((8, D)), MERGE]
    return pl.pallas_call(
        functools.partial(recv_bwd_kernel, sb, up_rows),
        grid=(n // sb,),
        in_specs=specs + [ANY] * 2,
        out_specs=[ANY] * 2 + [seg_block(sb), pack_spec(sb)] + [whole(s) for s in shapes],
        out_shape=pack_shapes()
        + [jax.ShapeDtypeStruct((n, SB_ROWS, D), F32), jax.ShapeDtypeStruct(o.shape, F32)]
        + [jax.ShapeDtypeStruct(s, F32) for s in shapes],
        input_output_aliases={len(specs): 0, len(specs) + 1: 1},
        scratch_shapes=RECV_ACC + [pltpu.VMEM((2, D, D), F32), pltpu.SemaphoreType.DMA((flush_count(6, up_rows),))],
        compiler_params=params_spec(),
        name="recv_bwd",
    )(send, o, dx, *kept, *weight_args(model, squares, 1), mvec, model[0], *packs)


def tail_kernel(sb, up_rows, send_ref, o_ref, tgt_ref, kept_ref, scale_ref, mean_ref, *refs):
    w = {n: refs[i][...] for i, n in enumerate(RECV_W)}
    vec_ref, head_ref, g_mat, g_feed, dsend_ref, do_ref, rows_ref, dhead_ref = refs[7:15]
    accs, sems = refs[15:22], refs[22]
    g = dict(zip(RECV_G, tuple(accs) + (rows_ref,)))

    @pl.when(pl.program_id(0) == 0)
    def _():
        for ref in list(g.values()) + [dhead_ref]:
            ref[...] = jnp.zeros(ref.shape, F32)

    vec = vec_ref[...]
    rows = sb * SB_ROWS
    y, kept, _ = recv_forward(
        send_ref[...].reshape(rows, D), unpack_block(o_ref, sb), w, vec
    )
    head = head_ref[...]
    y2 = split2(y)
    scale = jnp.broadcast_to(scale_ref[...][None], (sb, SB_ROWS, PPAD)).reshape(rows, PPAD)
    mean = jnp.broadcast_to(mean_ref[...][None], (sb, SB_ROWS, PPAD)).reshape(rows, PPAD)
    misfit = mmwt(y2, head) * scale + mean - tgt_ref[...].reshape(rows, PPAD)
    dpred = kept_ref[...].reshape(rows, PPAD) * misfit * scale
    dpred2 = split2(dpred)
    dhead_ref[...] += tn3(dpred2, y2)
    dy = mmw(dpred2, head)
    dsend, do = recv_backward(dy, kept, w, vec, g)
    dsend_ref[...] = dsend.reshape(sb, SB_ROWS, D)
    pack_block(do_ref, do, sb)
    recv_flush(accs, [], 1, up_rows, g_mat, g_feed, sems)


def tail(send, o, tgt, kept, scale, mean, model, head, sb, up_rows):
    n = send.shape[0]
    squares = recv_squares(1)
    shapes = [(11, 8, D), (PPAD, D)]
    return pl.pallas_call(
        functools.partial(tail_kernel, sb, up_rows),
        grid=(n // sb,),
        in_specs=[seg_block(sb), pack_spec(sb), seg_block(sb, SB_ROWS, PPAD), seg_block(sb, SB_ROWS, PPAD)]
        + [whole((SB_ROWS, PPAD))] * 2
        + weight_specs(squares, 3, 1)
        + [whole((PPAD, D))],
        out_specs=[ANY] * 2 + [seg_block(sb), pack_spec(sb)] + [whole(s) for s in shapes],
        out_shape=pack_shapes()
        + [jax.ShapeDtypeStruct((n, SB_ROWS, D), F32), jax.ShapeDtypeStruct(o.shape, F32)]
        + [jax.ShapeDtypeStruct(s, F32) for s in shapes],
        scratch_shapes=RECV_ACC + [pltpu.SemaphoreType.DMA((flush_count(5, up_rows),))],
        compiler_params=params_spec(),
        name="tail",
    )(send, o, tgt, kept, scale, mean, *weight_args(model, squares, 3), head)


SEND_W = ("sq", "sk", "sv")


def send_project(dim2, r_rows, w, vec):
    r2 = split2(r_rows)
    sb = r_rows.shape[0] // RPAD
    k = mmw(dim2, w["sk"])
    v = mmw(dim2, w["sv"]) + vec[11:12]
    q = (mmw(r2, w["sq"]) + vec[10:11]) * SCALE
    k = [split2(k[s * SB_ROWS : (s + 1) * SB_ROWS]) for s in range(sb)]
    v = [split2(v[s * SB_ROWS : (s + 1) * SB_ROWS]) for s in range(sb)]
    q = [split2(spread_rows(q[s * RPAD : (s + 1) * RPAD])) for s in range(sb)]
    return r2, k, v, q


def send_fwd_kernel(sb, dim_ref, r_ref, here_ref, *refs):
    w = {n: refs[i][...] for i, n in enumerate(SEND_W)}
    vec_ref, o_ref = refs[3:]
    dim2 = split2(dim_ref[...].reshape(sb * SB_ROWS, D))
    _, k, v, q = send_project(dim2, r_ref[...].reshape(sb * RPAD, D), w, vec_ref[...])
    here = here_ref[...] > 0.5
    scores = [jnp.where(here, nt3(k2, q2), negative) for k2, q2 in zip(k, q)]
    tops = [jnp.max(sc, 0, keepdims=True) for sc in scores]
    probs = [jnp.where(here, jnp.exp(sc - top), 0.0) for sc, top in zip(scores, tops)]
    totals = [jnp.sum(p, 0, keepdims=True) for p in probs]
    safe = [jnp.where(t > 0.0, t, 1.0) for t in totals]
    mixed = [gather_rows(tn3(split2(p / t), v2)) for p, t, v2 in zip(probs, safe, v)]
    for s in range(sb):
        lse = jnp.where(totals[s] > 0.0, tops[s] + jnp.log(safe[s]), negative)
        o_ref[s] = pack_rows(mixed[s], lse)


def send_squares(layer):
    return [12 * layer + k for k in (4, 5, 6)]


def send_fwd(dim, routers, here, model, layer, sb, npad):
    squares = send_squares(layer)
    n = dim.shape[0]
    return pl.pallas_call(
        functools.partial(send_fwd_kernel, sb),
        grid=(n // sb,),
        in_specs=[seg_block(sb), seg_block(sb, RPAD), whole((SB_ROWS, HALF))]
        + weight_specs(squares, None, layer),
        out_specs=pack_spec(sb),
        out_shape=jax.ShapeDtypeStruct((npad, PACK, HALF), F32),
        compiler_params=params_spec(),
        name="send_fwd",
    )(dim, routers, here, *weight_args(model, squares, None))


def send_bwd_kernel(sb, layer, dim_ref, dpart_ref, r_ref, o_ref, do_ref, here_ref, *refs):
    w = {n: refs[i][...] for i, n in enumerate(SEND_W)}
    vec_ref = refs[3]
    g_mat, ddim_ref, dr_ref, rows = refs[5:9]
    dsq_ref, dsk_ref, dsv_ref, sems = refs[9:13]

    @pl.when(pl.program_id(0) == 0)
    def _():
        for ref in (dsq_ref, dsk_ref, dsv_ref, rows):
            ref[...] = jnp.zeros(ref.shape, F32)

    dim2 = split2(dim_ref[...].reshape(sb * SB_ROWS, D))
    r2, k, v, q = send_project(dim2, r_ref[...].reshape(sb * RPAD, D), w, vec_ref[...])
    here = (here_ref[...] > 0.5) & valid_lane(SB_ROWS)
    segs = range(sb)
    scores = [nt3(k2, q2) for k2, q2 in zip(k, q)]
    probs = [jnp.where(here, jnp.exp(scores[s] - o_ref[s][2 * ROUT : 2 * ROUT + 1]), 0.0) for s in segs]
    dwide = [spread_rows(unpack_rows(do_ref[s])) for s in segs]
    owide = [
        jnp.broadcast_to(unpack_rows(o_ref[s])[:, None, :], (RPAD, HEADS, D)).reshape(RPAD * HEADS, D) for s in segs
    ]
    e = [split2(a * b) for a, b in zip(dwide, owide)]
    d = [split2(a) for a in dwide]
    one_row = jnp.ones((8, D), BF)
    means = [(dots(one_row, e2[0], 1, 1) + dots(one_row, e2[1], 1, 1))[0:1] for e2 in e]
    dp = [nt3(v2, d2) for v2, d2 in zip(v, d)]
    ds = [split2(p * (x - mean)) for p, x, mean in zip(probs, dp, means)]
    dk = jnp.concatenate([nn3(s2, q2) for s2, q2 in zip(ds, q)], 0)
    dv = jnp.concatenate([nn3(split2(p), d2) for p, d2 in zip(probs, d)], 0)
    dq = jnp.concatenate([gather_rows(tn3(s2, k2)) for s2, k2 in zip(ds, k)], 0) * SCALE
    dk2 = split2(dk)
    dv2 = split2(dv)
    rows[1] += colsum(dv)
    dsk_ref[...] += tn3(dim2, dk2)
    dsv_ref[...] += tn3(dim2, dv2)
    out = dpart_ref[...].reshape(sb * SB_ROWS, D) + mmwt(dk2, w["sk"]) + mmwt(dv2, w["sv"])
    ddim_ref[...] = out.reshape(sb, SB_ROWS, D)
    rows[0] += colsum(dq)
    dq2 = split2(dq)
    dsq_ref[...] += tn3(r2, dq2)
    dr_ref[...] = mmwt(dq2, w["sq"]).reshape(sb, RPAD, D)
    flush(
        pl.program_id(0), pl.num_programs(0) - 1, [dsq_ref, dsk_ref, dsv_ref], send_squares(layer), None, None, 0, 0,
        g_mat, None, sems,
    )


def send_bwd(dim, dpart, routers, o, do, here, model, layer, sb, g_mat):
    n = dim.shape[0]
    squares = send_squares(layer)
    specs = [seg_block(sb), seg_block(sb), seg_block(sb, RPAD), pack_spec(sb), pack_spec(sb), whole((SB_ROWS, HALF))]
    specs += weight_specs(squares, None, layer)
    return pl.pallas_call(
        functools.partial(send_bwd_kernel, sb, layer),
        grid=(n // sb,),
        in_specs=specs + [ANY],
        out_specs=[ANY, seg_block(sb), seg_block(sb, RPAD), whole((2, 8, D))],
        out_shape=pack_shapes()[:1]
        + [jax.ShapeDtypeStruct((n, SB_ROWS, D), F32), jax.ShapeDtypeStruct((n, RPAD, D), F32)]
        + [jax.ShapeDtypeStruct((2, 8, D), F32)],
        input_output_aliases={len(specs): 0},
        scratch_shapes=[pltpu.VMEM((D, D), F32)] * 3 + [pltpu.SemaphoreType.DMA((3,))],
        compiler_params=params_spec(),
        name="send_bwd",
    )(dim, dpart, routers, o, do, here, *weight_args(model, squares, None), g_mat)

MESH = pl.DeviceIdType.MESH


def grid_sizes():
    nf = lax.axis_size("fsdp")
    nx = 1
    while 2 * nx * nx < nf:
        nx *= 2
    return lax.axis_size("dp") // 2, nf // nx, nx


class Place:
    def __init__(self):
        self.ny, self.nz, self.nx = grid_sizes()
        dp, fs = lax.axis_index("dp"), lax.axis_index("fsdp")
        self.core, self.y = lax.rem(dp, 2), lax.div(dp, 2)
        self.x, self.z = lax.rem(fs, self.nx), lax.div(fs, self.nx)

    def at(self, y=None, core=None, z=None, x=None):
        y = self.y if y is None else y
        core = self.core if core is None else core
        z = self.z if z is None else z
        x = self.x if x is None else x
        return (y * 2 + core, z * self.nx + x)

    def other(self):
        return 1 - self.core

    def next_x(self, k):
        return lax.rem(self.x + k, self.nx)

    def next_y(self, k):
        return lax.rem(self.y + k, self.ny)

    def next_z(self, k):
        return lax.rem(self.z + k, self.nz)

    def neighbours(self):
        out = [self.at(core=self.other())]
        out += [self.at(x=self.next_x(k)) for k in range(1, self.nx)]
        out += [self.at(y=self.next_y(k)) for k in range(1, self.ny)]
        out += [self.at(z=self.next_z(k)) for k in range(1, self.nz)]
        return out


def greet(devices):
    barrier = pltpu.get_barrier_semaphore()
    for device in devices:
        pl.semaphore_signal(barrier, inc=1, device_id=device, device_id_type=MESH)
    pl.semaphore_wait(barrier, len(devices))


def remote(src, dst, send, recv, device):
    return pltpu.make_async_remote_copy(
        src_ref=src, dst_ref=dst, send_sem=send, recv_sem=recv, device_id=device, device_id_type=MESH
    )


def gather_kernel(n, *refs):
    shards, outs = refs[:n], refs[n : 2 * n]
    send, recv, local = refs[2 * n :]
    me = Place()
    y, c, z, x = me.y, me.core, me.z, me.x
    m = me.nx
    greet(me.neighbours())
    slot = [0]

    def push(src, dst, device):
        copy = remote(src, dst, send.at[slot[0]], recv.at[slot[0]], device)
        slot[0] += 1
        copy.start()
        return copy

    def finish(copies):
        for copy in copies:
            copy.wait()

    own = [pltpu.make_async_copy(shards[j], outs[j].at[y, c, z, x], local.at[j]) for j in range(n)]
    for copy in own:
        copy.start()

    def along_z(j):
        return [push(shards[j], outs[j].at[y, c, z, x], me.at(z=me.next_z(k))) for k in range(1, me.nz)]

    first = along_z(0)
    finish(own)
    base = slot[0]

    def rest(by_core):
        slot[0] = base
        sibling = me.at(core=1 - by_core)
        shared = []

        def second(j):
            piece = outs[j].at[y, by_core, :, x]
            out = []
            for k in range(1, m):
                out.append(push(piece, piece, me.at(x=me.next_x(k)) if by_core == 0 else me.at(y=me.next_y(k))))
            shared.append(push(piece, piece, sibling))
            return out

        def third(j):
            wide = outs[j].at[y, by_core] if by_core == 0 else outs[j].at[:, by_core, :, x]
            out = []
            for k in range(1, m):
                out.append(push(wide, wide, me.at(y=me.next_y(k)) if by_core == 0 else me.at(x=me.next_x(k))))
            for k in range(1, m):
                piece = outs[j].at[y, by_core, :, me.next_x(k)] if by_core == 0 else outs[j].at[me.next_y(k), by_core, :, x]
                shared.append(push(piece, piece, sibling))
            return out

        def fourth(j):
            for k in range(1, m):
                wide = outs[j].at[me.next_y(k), by_core] if by_core == 0 else outs[j].at[:, by_core, :, me.next_x(k)]
                shared.append(push(wide, wide, sibling))

        one, two, three = {0: first}, {}, {}
        for t in range(n + 2):
            if t < n:
                finish(one[t])
                if t + 1 < n:
                    one[t + 1] = along_z(t + 1)
            if 0 < t <= n:
                finish(two[t - 1])
            if t < n:
                two[t] = second(t)
            if t > 1:
                finish(three[t - 2])
            if 0 < t <= n:
                three[t - 1] = third(t - 1)
            if t > 1:
                fourth(t - 2)
        finish(shared)

    for by_core in (0, 1):
        pl.when(c == by_core)(functools.partial(rest, by_core))


def gather_all(shards):
    ny, nz, nx = grid_sizes()
    n = len(shards)
    count = n * ((nz - 1) + (nx - 1) + 1 + (nx - 1) * 3)
    return pl.pallas_call(
        functools.partial(gather_kernel, n),
        in_specs=[ANY] * n,
        out_specs=[ANY] * n,
        out_shape=[jax.ShapeDtypeStruct((ny, 2, nz, nx) + s.shape, s.dtype) for s in shards],
        scratch_shapes=[pltpu.SemaphoreType.DMA((count,)), pltpu.SemaphoreType.DMA((count,)), pltpu.SemaphoreType.DMA((n,))],
        compiler_params=pltpu.CompilerParams(collective_id=0, has_side_effects=True, vmem_limit_bytes=16 << 20),
        name="gather_all",
    )(*shards)


def row_chunks(rows):
    count = max(1, rows // 40)
    if rows % 8:
        count = 1
    cuts = [rows // 8 * k // count * 8 for k in range(count)] + [rows]
    return [(a, b - a) for a, b in zip(cuts, cuts[1:])]


def scatter_kernel(shapes, *refs):
    n = len(shapes)
    chunks = [(j, a, b) for j, s in enumerate(shapes) for a, b in row_chunks(s[0])]
    total = len(chunks)
    grads, tile_ref = refs[:n], refs[n]
    outs, stat_ref = refs[n + 1 : 2 * n + 1], refs[2 * n + 1]
    bufs = refs[2 * n + 2 :]
    acc, r1, r2, r3, r4 = (bufs[i * total : (i + 1) * total] for i in range(5))
    tp, tz, send, recv, local = bufs[5 * total :]
    me = Place()
    y, c, z, x = me.y, me.core, me.z, me.x
    ny, nz, nx, m = me.ny, me.nz, me.nx, me.nx
    plane = plane_peers(me)
    greet([p for p, _ in plane] + [me.at(z=me.next_z(k)) for k in range(1, nz)])
    slot = [0]

    def push(src, dst, device):
        copy = remote(src, dst, send.at[slot[0]], recv.at[slot[0]], device)
        slot[0] += 1
        copy.start()
        return copy

    def finish(copies):
        for copy in copies:
            copy.wait()

    def rest(by_core):
        slot[0] = 0
        sibling = me.at(core=1 - by_core)

        def one(i):
            j, a, b = chunks[i]
            out = []
            for k in range(nx):
                out.append(push(grads[j].at[:, 1 - by_core, :, k, pl.ds(a, b)], r1[i].at[:, k], sibling))
                copy = pltpu.make_async_copy(grads[j].at[:, by_core, :, k, pl.ds(a, b)], acc[i].at[:, k], local.at[i * nx + k])
                copy.start()
                out.append(copy)
            return out

        def add1(i):
            def body(k, carry):
                at = (lax.div(k, nx * nz), lax.rem(lax.div(k, nz), nx), lax.rem(k, nz))
                acc[i][at] = acc[i][at] + r1[i][at]
                return carry

            lax.fori_loop(0, ny * nx * nz, body, 0)

        def two(i):
            if by_core == 0:
                return [push(acc[i].at[:, me.next_x(k)], r2[i].at[k - 1], me.at(x=me.next_x(k))) for k in range(1, m)]
            return [push(acc[i].at[me.next_y(k)], r2[i].at[k - 1], me.at(y=me.next_y(k))) for k in range(1, m)]

        def add2(i):
            def body(k, carry):
                a, b = lax.div(k, nz), lax.rem(k, nz)
                at = (a, x, b) if by_core == 0 else (y, a, b)
                value = acc[i][at]
                for q in range(m - 1):
                    value = value + r2[i][q, a, b]
                acc[i][at] = value
                return carry

            lax.fori_loop(0, m * nz, body, 0)

        def three(i):
            if by_core == 0:
                return [push(acc[i].at[me.next_y(k), x], r3[i].at[k - 1], me.at(y=me.next_y(k))) for k in range(1, m)]
            return [push(acc[i].at[y, me.next_x(k)], r3[i].at[k - 1], me.at(x=me.next_x(k))) for k in range(1, m)]

        def add3(i):
            def body(k, carry):
                value = acc[i][y, x, k]
                for q in range(m - 1):
                    value = value + r3[i][q, k]
                acc[i][y, x, k] = value
                return carry

            lax.fori_loop(0, nz, body, 0)

        def four(i):
            return [push(acc[i].at[y, x, me.next_z(k)], r4[i].at[k - 1], me.at(z=me.next_z(k))) for k in range(1, nz)]

        def end(i):
            j, a, b = chunks[i]
            value = acc[i][y, x, z]
            for k in range(nz - 1):
                value = value + r4[i][k]
            outs[j][a : a + b] = value
            sq = colsum_any(value * value)
            return sq[:, :HALF] + sq[:, HALF:]

        squares = jnp.zeros((8, HALF), F32)
        ahead = 3
        p1, p2, p3, p4 = {i: one(i) for i in range(min(ahead, total))}, {}, {}, {}
        for t in range(total + 3):
            if t < total:
                finish(p1[t])
                if t + ahead < total:
                    p1[t + ahead] = one(t + ahead)
                add1(t)
                p2[t] = two(t)
            if 0 <= t - 1 < total:
                finish(p2[t - 1])
                add2(t - 1)
                p3[t - 1] = three(t - 1)
            if 0 <= t - 2 < total:
                finish(p3[t - 2])
                add3(t - 2)
                p4[t - 2] = four(t - 2)
            if 0 <= t - 3 < total:
                finish(p4[t - 3])
                squares = squares + end(t - 3)
        tp[(y * 2 + by_core) * nx + x] = jnp.concatenate([squares, tile_ref[...]], 0)

    for by_core in (0, 1):
        pl.when(c == by_core)(functools.partial(rest, by_core))

    slot[0] = total * (nx + 2 * (m - 1) + nz - 1)
    mine = tp.at[(y * 2 + c) * nx + x]
    finish([push(mine, mine, p) for p, _ in plane])
    tz[z] = functools.reduce(jnp.add, [tp[k] for k in range(2 * ny * nx)])
    finish([push(tz.at[z], tz.at[z], me.at(z=me.next_z(k))) for k in range(1, nz)])
    stat_ref[...] = functools.reduce(jnp.add, [tz[k] for k in range(nz)])


def plane_peers(me):
    out = []
    for k in range(1, 2 * me.ny * me.nx):
        dc, dy, dx = k % 2, k // 2 % me.ny, k // (2 * me.ny)
        out.append((me.at(core=lax.rem(me.core + dc, 2), y=lax.rem(me.y + dy, me.ny), x=lax.rem(me.x + dx, me.nx)), k))
    return out


def colsum_any(x):
    rows = x.shape[0]
    even = rows // 8 * 8
    out = colsum(x[:even]) if even else jnp.zeros((8, x.shape[1]), F32)
    if rows > even:
        out = out + jnp.pad(x[even:], ((0, 8 - rows + even), (0, 0)))
    return out


def scatter_sum(grads, tile):
    ny, nz, nx = grid_sizes()
    n = len(grads)
    shapes = [g.shape[-2:] for g in grads]
    pieces = [(b, s[1]) for s in shapes for _, b in row_chunks(s[0])]
    total = len(pieces)
    count = total * (nx + (nx - 1) * 2 + nz - 1) + 2 * ny * nx - 1 + nz - 1

    def buffers(*lead):
        return [pltpu.VMEM(lead + s, F32) for s in pieces]

    return pl.pallas_call(
        functools.partial(scatter_kernel, shapes),
        in_specs=[ANY] * n + [INVMEM],
        out_specs=[INVMEM] * (n + 1),
        out_shape=[jax.ShapeDtypeStruct(s, F32) for s in shapes] + [jax.ShapeDtypeStruct((16, HALF), F32)],
        scratch_shapes=buffers(ny, nx, nz)
        + buffers(ny, nx, nz)
        + buffers(nx - 1, nx, nz)
        + buffers(nx - 1, nz)
        + buffers(nz - 1)
        + [pltpu.VMEM((2 * ny * nx, 16, HALF), F32), pltpu.VMEM((nz, 16, HALF), F32)]
        + [pltpu.SemaphoreType.DMA((count,)), pltpu.SemaphoreType.DMA((count,)), pltpu.SemaphoreType.DMA((total * nx,))],
        compiler_params=pltpu.CompilerParams(collective_id=1, has_side_effects=True, vmem_limit_bytes=VMEM_LIMIT),
        name="scatter_sum",
    )(*grads, tile)


def group_kernel(stats, per, in_ref, out_ref, got, result, send, recv, local):
    nf = lax.axis_size("fsdp")
    dp, f = lax.axis_index("dp"), lax.axis_index("fsdp")
    peers = [lax.rem(f + k, nf) for k in range(1, nf)]
    greet([(dp, p) for p in peers])

    def part(ref, who):
        return ref.at[pl.ds(pl.multiple_of(who * per, per), per)]

    own = pltpu.make_async_copy(part(in_ref, f), got.at[f], local)
    own.start()
    copies = [
        remote(part(in_ref, p), got.at[f], send.at[k], recv.at[k], (dp, p)) for k, p in enumerate(peers)
    ]
    for copy in copies:
        copy.start()
    own.wait()
    for copy in copies:
        copy.wait()
    if stats:
        row = lax.broadcasted_iota(jnp.int32, (PACK, HALF), 0)
        lane = lax.broadcasted_iota(jnp.int32, (PACK, HALF), 1)
        router = jnp.where(row < ROUT, row, row - ROUT)
        pick = (lane // 8 == router) & (row < 2 * ROUT)
        src = lax.broadcasted_iota(jnp.int32, (HALF, D), 0)
        dst = lax.broadcasted_iota(jnp.int32, (HALF, D), 1)
        widen = jnp.where(src % 8 == dst // 32, 1.0, 0.0).astype(BF)

        def one(s, carry):
            lse = [got[d, s, 2 * ROUT : 2 * ROUT + 1, :] for d in range(nf)]
            top = functools.reduce(jnp.maximum, lse)
            total = top + jnp.log(functools.reduce(jnp.add, [jnp.exp(l - top) for l in lse]))
            out = jnp.where(row == 2 * ROUT, total, 0.0)
            share = jnp.concatenate([jnp.where(pick, jnp.exp(l - total), 0.0) for l in lse], 0)
            wide = mmw(split2(share), widen)
            for d in range(nf):
                w = wide[d * PACK : (d + 1) * PACK]
                w = jnp.where(row < ROUT, w[:, :HALF], w[:, HALF:])
                out = out + jnp.where(row < 2 * ROUT, w * got[d, s], 0.0)
            result[s] = out
            return carry

        lax.fori_loop(0, per, one, 0)
    else:
        result[...] = functools.reduce(jnp.add, [got[d] for d in range(nf)])
    own = pltpu.make_async_copy(result, part(out_ref, f), local)
    own.start()
    copies = [
        remote(result, part(out_ref, f), send.at[nf - 1 + k], recv.at[nf - 1 + k], (dp, p)) for k, p in enumerate(peers)
    ]
    for copy in copies:
        copy.start()
    own.wait()
    for copy in copies:
        copy.wait()


def group_combine(packed, stats, cid):
    nf = lax.axis_size("fsdp")
    per = packed.shape[0] // nf
    return pl.pallas_call(
        functools.partial(group_kernel, stats, per),
        in_specs=[ANY],
        out_specs=ANY,
        out_shape=jax.ShapeDtypeStruct(packed.shape, F32),
        scratch_shapes=[
            pltpu.VMEM((nf, per, PACK, HALF), F32),
            pltpu.VMEM((per, PACK, HALF), F32),
            pltpu.SemaphoreType.DMA((2 * nf - 2,)),
            pltpu.SemaphoreType.DMA((2 * nf - 2,)),
            pltpu.SemaphoreType.DMA,
        ],
        compiler_params=pltpu.CompilerParams(collective_id=cid, has_side_effects=True, vmem_limit_bytes=32 << 20),
        name="group_stats" if stats else "group_sum",
    )(packed)

LAYER_AT = SEGLEN + 1 + SEG
MERGE_AT = LAYER_AT + 46
HEAD_AT = MERGE_AT + 5
ROUTER_AT = HEAD_AT + PRED
VROWS = NVEC + 20


def own_size(devices):
    own = NVEC * D // devices
    return own, -(-own // D)


def prepare_kernel(nfeed, ser_ref, obs_ref, tgt_ref, mask_ref, count_ref, mat_ref, feed_ref, vec_ref, *outs):
    pieces, tgt, kept, scale_ref, mean_ref, here_ref, tile_ref, mat_o, feed_o, vec_o = outs
    for src, dst in ((mat_ref, mat_o), (feed_ref, feed_o), (vec_ref, vec_o)):
        rows = dst.shape[0]
        left, right = src[pl.ds(0, rows, stride=2), :], src[pl.ds(1, rows, stride=2), :]
        dst[...] = jnp.concatenate([left, right], 1).astype(BF)
    nv = ser_ref.shape[0]
    series, seen = ser_ref[...], obs_ref[...].astype(F32)
    counted = jnp.maximum(jnp.sum(seen, -1, keepdims=True), 1.0)
    mean = jnp.sum(seen * series, -1, keepdims=True) / counted
    center = (series - mean) * seen
    scale = jnp.sqrt(jnp.sum(center * center, -1, keepdims=True) / counted + norm_eps)
    slot = lax.axis_index("fsdp") * nv + lax.broadcasted_iota(jnp.int32, (nv, HALF), 0)
    here = jnp.where(slot < count_ref[0], 1.0, 0.0)
    here_ref[...] = here
    scale_ref[...] = jnp.broadcast_to(scale, (nv, PPAD))
    mean_ref[...] = jnp.broadcast_to(mean, (nv, PPAD))
    mask = mask_ref[...].astype(F32) * here[:, :1]
    tile_ref[...] = jnp.broadcast_to(jnp.sum(jnp.sum(mask, 0, keepdims=True), -1, keepdims=True), (8, HALF)) * (1.0 / (8 * HALF))
    lane = lax.broadcasted_iota(jnp.int32, (nv, PPAD), 1)

    def cut(x, dst):
        x = jnp.concatenate([x, jnp.zeros((nv, PPAD - 12), F32)], 1)
        for s in range(dst.shape[0]):
            dst[s] = jnp.where(lane < 12, x[:, 12 * s : 12 * s + PPAD], 0.0)

    cut(center / scale, pieces)
    cut(tgt_ref[...], tgt)
    cut(mask * (2.0 / (1 << 20)), kept)


def prepare(series, observed, targets, target_mask, counts, matrices, feed, vectors):
    nv = series.shape[0]
    shapes = [((SEG, nv, PPAD), F32), ((SEG // 2, nv, PPAD), F32), ((SEG // 2, nv, PPAD), F32), ((nv, PPAD), F32), ((nv, PPAD), F32)]
    shapes += [((nv, HALF), F32), ((8, HALF), F32)]
    shapes += [((x.shape[0] // 2, D), BF) for x in (matrices, feed, vectors)]
    return pl.pallas_call(
        functools.partial(prepare_kernel, 0),
        grid=(1,),
        in_specs=[whole(x.shape) for x in (series, observed, targets, target_mask)]
        + [pl.BlockSpec(memory_space=pltpu.SMEM)]
        + [whole(x.shape) for x in (matrices, feed, vectors)],
        out_specs=[whole(s) for s, _ in shapes],
        out_shape=[jax.ShapeDtypeStruct(s, t) for s, t in shapes],
        compiler_params=pltpu.CompilerParams(vmem_limit_bytes=32 << 20),
        name="prepare",
    )(series, observed, targets, target_mask, counts, matrices, feed, vectors)


def unpack_kernel(devices, own, vec_ref, vecs, mvec, emb, place, head, r0, r1, flat):
    flat[...] = jnp.zeros(flat.shape, F32)
    rows = vec_ref.shape[1]
    lane = lax.broadcasted_iota(jnp.int32, (rows, D), 1)
    for d in range(devices):
        at, shift = divmod(own * d, D)
        block = vec_ref[d].astype(F32)
        if shift:
            block = pltpu.roll(block, shift, 1)
            flat[at + 1 : at + 1 + rows] += jnp.where(lane < shift, block, 0.0)
            block = jnp.where(lane >= shift, block, 0.0)
        flat[at : at + rows] += block

    def padded(at, count, total):
        return jnp.concatenate([flat[at : at + count], jnp.zeros((total - count, D), F32)], 0)

    for l in range(2):
        vecs[l] = padded(LAYER_AT + 23 * l, 23, 24)
    mvec[...] = padded(MERGE_AT, 5, 8)
    emb[...] = padded(0, SEGLEN, 16).astype(BF)
    head[...] = padded(HEAD_AT, PRED, PPAD).astype(BF)
    for s in range(SEG):
        place[s] = flat[SEGLEN + 1 + s : SEGLEN + 2 + s] + flat[SEGLEN : SEGLEN + 1]
        r0[s] = padded(ROUTER_AT + ROUT * s, ROUT, RPAD)
    for s in range(SEG // 2):
        r1[s] = padded(ROUTER_AT + ROUT * (SEG + s), ROUT, RPAD)


def unpack_vectors(gathered, own):
    devices, rows, _ = gathered.shape
    shapes = [((2, 24, D), F32), ((8, D), F32), ((16, D), BF), ((SEG, 1, D), F32), ((PPAD, D), BF)]
    shapes += [((SEG, RPAD, D), F32), ((SEG // 2, RPAD, D), F32)]
    return pl.pallas_call(
        functools.partial(unpack_kernel, devices, own),
        grid=(1,),
        in_specs=[whole(gathered.shape)],
        out_specs=[whole(s) for s, _ in shapes],
        out_shape=[jax.ShapeDtypeStruct(s, t) for s, t in shapes],
        scratch_shapes=[pltpu.VMEM((VROWS + 24, D), F32)],
        compiler_params=pltpu.CompilerParams(vmem_limit_bytes=32 << 20),
        name="unpack_vectors",
    )(gathered)


def assemble_kernel(devices, own, demb, dplace, *refs):
    (rt0, rs0, rr0, rt1, rs1, rr1, dmv, dhead, dr0, dr1), out, flat = refs[:10], refs[10], refs[11]
    flat[...] = jnp.zeros(flat.shape, F32)
    flat[0:SEGLEN] = demb[0:SEGLEN]
    place = jnp.sum(dplace[...].reshape(SEG, VB, D), 1)
    flat[SEGLEN : SEGLEN + 1] = jnp.sum(place, 0, keepdims=True)
    flat[SEGLEN + 1 : SEGLEN + 1 + SEG] = place
    at = LAYER_AT
    for ref in (rt0, rs0, rr0, rt1, rs1, rr1, dmv):
        count = ref.shape[0]
        flat[at : at + count] = jnp.sum(ref[...], 1)
        at += count
    flat[HEAD_AT : HEAD_AT + PRED] = dhead[0:PRED]
    for s in range(SEG):
        flat[ROUTER_AT + ROUT * s : ROUTER_AT + ROUT * (s + 1)] = dr0[s][:ROUT]
    for s in range(SEG // 2):
        flat[ROUTER_AT + ROUT * (SEG + s) : ROUTER_AT + ROUT * (SEG + s + 1)] = dr1[s][:ROUT]
    rows = out.shape[1]
    lane = lax.broadcasted_iota(jnp.int32, (rows, D), 1)
    inside = lax.broadcasted_iota(jnp.int32, (rows, D), 0) * D + lane < own
    for d in range(devices):
        at, shift = divmod(own * d, D)
        block = flat[at : at + rows]
        if shift:
            block = jnp.where(lane < D - shift, pltpu.roll(block, D - shift, 1), pltpu.roll(flat[at + 1 : at + 1 + rows], D - shift, 1))
        out[d] = jnp.where(inside, block, 0.0)


def assemble_vectors(parts, devices):
    own, rows = own_size(devices)
    return pl.pallas_call(
        functools.partial(assemble_kernel, devices, own),
        grid=(1,),
        in_specs=[whole(p.shape) for p in parts],
        out_specs=whole((devices, rows, D)),
        out_shape=jax.ShapeDtypeStruct((devices, rows, D), F32),
        scratch_shapes=[pltpu.VMEM((VROWS + 24, D), F32)],
        compiler_params=pltpu.CompilerParams(vmem_limit_bytes=32 << 20),
        name="assemble_vectors",
    )(*parts)


def adam_update(weight, first_moment, second_moment, gradient):
    first_new = beta_one * first_moment + (1.0 - beta_one) * gradient
    second_new = beta_two * second_moment + (1.0 - beta_two) * gradient * gradient
    corrected = (
        first_new
        / (1.0 - beta_one**step_count)
        / (jnp.sqrt(second_new / (1.0 - beta_two**step_count)) + adam_eps)
    )
    return (weight - learn_rate * (corrected + weight_decay * weight), first_new, second_new)


def gradient_parts(ready, model, extras, up_rows, combine, nf, devices):
    pieces, tgt, kept, scale, mean, here = ready
    mvec, emb, place, head, routers0, routers1 = extras
    sb0, sb1, sf0, sf1, st = 12, 10, 20, 10, 10
    rf, rb = 20, 20
    half = SEG // 2
    dim0, kept0 = time_fwd(True, pieces, (emb, place), model, 0, SEG)
    o0 = send_fwd(dim0, routers0, here, model, 0, sf0, -(-SEG // nf) * nf)
    o0 = combine(o0, True, 2)
    x1, *saved = recv_fwd(dim0, o0, model, mvec, rf)
    dim1, kept1 = time_fwd(False, x1, (), model, 1, half)
    o1 = send_fwd(dim1, routers1, here, model, 1, sf1, -(-half // nf) * nf)
    o1 = combine(o1, True, 3)
    g_mat, g_feed, ddim1, do1, rr1, dhead = tail(dim1, o1, tgt, kept, scale, mean, model, head, st, up_rows)
    do1 = combine(do1, False, 4)
    g_mat, ddim1, dr1, rs1 = send_bwd(dim1, ddim1, routers1, o1, do1, here, model, 1, sb1, g_mat)
    g_mat, g_feed, rt1, dx1 = time_bwd(False, x1, (), ddim1, kept1, model, 1, half, (g_mat, g_feed), up_rows)
    g_mat, g_feed, ddim0, do0, rr0, dmv = recv_bwd(dim0, o0, dx1, saved, model, mvec, rb, (g_mat, g_feed), up_rows)
    do0 = combine(do0, False, 5)
    g_mat, ddim0, dr0, rs0 = send_bwd(dim0, ddim0, routers0, o0, do0, here, model, 0, sb0, g_mat)
    g_mat, g_feed, rt0, demb, dplace = time_bwd(
        True, pieces, (emb, place), ddim0, kept0, model, 0, SEG, (g_mat, g_feed), up_rows
    )
    g_vec = assemble_vectors((demb, dplace, rt0, rs0, rr0, rt1, rs1, rr1, dmv, dhead, dr0, dr1), devices)
    return g_mat, g_feed, g_vec


def on_device(series, observed, targets, target_mask, counts, matrices, feed_weights, vectors, matrices_first, matrices_second, feed_first, feed_second, vectors_first, vectors_second):
    nf = lax.axis_size("fsdp")
    nd = lax.axis_size("dp")
    devices = nf * nd
    own, vec_rows = own_size(devices)
    out = prepare(
        series[0],
        observed[0],
        targets[0],
        target_mask[0],
        counts,
        matrices.reshape(-1, HALF),
        feed_weights.reshape(-1, HALF),
        jnp.pad(vectors, (0, vec_rows * D - own)).reshape(-1, HALF),
    )
    ready, tile, shards = out[:6], out[6], out[7:]
    square, feed, vecs = gather_all(shards)
    square = square.reshape(NSQ, D, D)
    feed = feed.reshape(-1, D)
    up = feed[: 4 * FF].reshape(4, D, FF)
    down = feed.reshape(8, FF, D)
    vecs, *extras = unpack_vectors(vecs.reshape(devices, vec_rows, D), own)
    up_rows = feed_weights.shape[0] // FF
    g_mat, g_feed, g_vec = gradient_parts(ready, (square, up, down, vecs), extras, up_rows, group_combine, nf, devices)
    ny, nz, nx = grid_sizes()
    lead = (ny, 2, nz, nx)
    s_mat, s_feed, s_vec, sums = scatter_sum([g.reshape(lead + (-1, D)) for g in (g_mat, g_feed, g_vec)], tile)
    is_up = lax.axis_index("dp") * 2 < nd
    halves_of = s_feed.reshape(2, up_rows, D)
    s_feed = jnp.where(is_up, jnp.concatenate([halves_of[0], halves_of[1]], 1).reshape(-1), s_feed.reshape(-1))
    grads = (s_mat.reshape(-1), s_feed, s_vec.reshape(-1)[:own])
    upscale = (1 << 20) / jnp.maximum(jnp.sum(sums[8:]), 1.0)
    grad_norm = jnp.sqrt(jnp.sum(sums[:8])) * upscale
    factor = upscale * (clip_norm / jnp.maximum(grad_norm, clip_norm))
    new = (
        adam_update(matrices, matrices_first, matrices_second, grads[0] * factor)
        + adam_update(feed_weights, feed_first, feed_second, grads[1] * factor)
        + adam_update(vectors, vectors_first, vectors_second, grads[2] * factor)
    )
    return (grad_norm,) + new


def solution(mesh):
    both = P(("dp", "fsdp"))
    data = P("dp", "fsdp", None)
    return jax.shard_map(
        on_device,
        mesh=mesh,
        in_specs=(data,) * 4 + (P("dp"),) + (both,) * 9,
        out_specs=(P(),) + (both,) * 9,
        check_vma=False,
    )
```

```python
import functools
import jax
import jax.numpy as jnp
from jax import lax
from jax.experimental import pallas as pl
from jax.experimental.pallas import tpu as pltpu
from jax.sharding import PartitionSpec as P

D = 256
HEADS = 8
FF = 512
ROUT = 10
RPAD = 16
SEGLEN = 12
PRED = 12
PPAD = 16
SEG = 60
NSQ = 26
NVEC = 1036
HALF = 128
VB = 8
UNROLL = 8
UNROLL_BACK = 8

BF = jnp.bfloat16
F32 = jnp.float32
SCALE = (D // HEADS) ** (-0.5)
negative = -1e30
norm_eps = 1e-05
beta_one = 0.9
beta_two = 0.999
adam_eps = 1e-08
weight_decay = 0.01
learn_rate = 0.2
clip_norm = 0.01
step_count = 10.0
VMEM_LIMIT = 60 << 20


ANY = pl.BlockSpec(memory_space=pl.ANY)
INVMEM = pl.BlockSpec(memory_space=pltpu.VMEM)


def split2(x):
    hi = x.astype(BF)
    return hi, (x - hi.astype(F32)).astype(BF)


def dots(a, b, ca, cb):
    return lax.dot_general(a, b, (((ca,), (cb,)), ((), ())), preferred_element_type=F32)


def mmw(x2, w):
    return dots(x2[0], w, 1, 0) + dots(x2[1], w, 1, 0)


def mmwt(x2, w):
    return dots(x2[0], w, 1, 1) + dots(x2[1], w, 1, 1)


def rows2(a2):
    return jnp.concatenate([a2[0], a2[1]], 0)


def nn3(a2, b2):
    m = a2[0].shape[0]
    both = dots(rows2(a2), b2[0], 1, 0)
    return both[:m] + both[m:] + dots(a2[0], b2[1], 1, 0)


def nt3(a2, b2):
    m = a2[0].shape[0]
    both = dots(rows2(a2), b2[0], 1, 1)
    return both[:m] + both[m:] + dots(a2[0], b2[1], 1, 1)


def tn3(a2, b2):
    n = b2[0].shape[1]
    both = dots(a2[0], jnp.concatenate([b2[0], b2[1]], 1), 0, 0)
    return both[:, :n] + both[:, n:] + dots(a2[1], b2[0], 0, 0)


def norm_fwd(z, gain, bias):
    center = z - jnp.mean(z, -1, keepdims=True)
    inv = lax.rsqrt(jnp.mean(center * center, -1, keepdims=True) + norm_eps)
    unit = center * inv
    return unit * gain + bias, unit, inv


def norm_bwd(dy, unit, inv, gain):
    t = dy * gain
    return inv * (t - jnp.mean(t, -1, keepdims=True) - unit * jnp.mean(t * unit, -1, keepdims=True))


def colsum(x):
    return jnp.sum(x.reshape(x.shape[0] // 8, 8, x.shape[1]), 0)


def gelu_cdf(u):
    return 0.5 + 0.5 * lax.erf(u * 0.7071067811865476)


def gelu_slope(u, cdf):
    return cdf + u * (jnp.exp(-0.5 * u * u) * 0.3989422804014327)


def halves(x):
    return x[:, :HALF], x[:, HALF:]


def lane_head(rows):
    return lax.broadcasted_iota(jnp.int32, (rows, HALF), 1) // 32


def spread_heads(x, zero):
    head = lane_head(x.shape[0])
    return jnp.concatenate([jnp.where(head == h, x, zero) for h in range(4)], 0)


def gather_heads(x, group):
    head = lane_head(group)
    out = x[3 * group :]
    for h in range(3):
        out = jnp.where(head == h, x[h * group : (h + 1) * group], out)
    return out


def ones_heads(group, count):
    row = lax.broadcasted_iota(jnp.int32, (4 * group, HALF), 0)
    lane = lax.broadcasted_iota(jnp.int32, (4 * group, HALF), 1)
    return jnp.where((row // group == lane // 32) & (row % group < count), 1.0, 0.0).astype(BF)


def group_max(s, group, count):
    lane = lax.broadcasted_iota(jnp.int32, (s.shape[0], HALF), 1)
    outs = []
    for t in range(s.shape[1] // HALF):
        part = s[:, t * HALF : (t + 1) * HALF]
        top = None
        for g in range(HALF // group):
            here = (lane // group == g)
            best = jnp.max(jnp.where((lane // group == g) & (lane % group < count), part, negative), -1, keepdims=True)
            top = jnp.broadcast_to(best, part.shape) if top is None else jnp.where(here, best, top)
        outs.append(jnp.where(lane % group < count, part - top, negative))
    return jnp.concatenate(outs, 1)


def time_parts(units, group, ref):
    return [split2(ref[c, pl.ds(v, group, stride=VB), :]) for c, v in units]


def spread2(x2):
    zero = jnp.zeros((), BF)
    return spread_heads(x2[0], zero), spread_heads(x2[1], zero)


def time_attend(units, group, count, q_s, k_s, v_s, o_s, p_s, l_s):
    q = time_parts(units, group, q_s)
    k = [spread2(x2) for x2 in time_parts(units, group, k_s)]
    scores = [
        dots(jnp.concatenate(q2, 1), jnp.concatenate([k2[0], k2[0]], 1), 1, 1) + dots(q2[0], k2[1], 1, 1)
        for q2, k2 in zip(q, k)
    ]
    probs = [jnp.exp(group_max(s, group, count)) for s in scores]
    probs2 = [split2(p) for p in probs]
    w = [spread2(x2) for x2 in time_parts(units, group, v_s)]
    ones = ones_heads(group, count)
    both = [dots(rows2(p2), jnp.concatenate([w2[0], ones], 1), 1, 0) for p2, w2 in zip(probs2, w)]
    both = [b[:group] + b[group:] for b in both]
    inv = [1.0 / b[:, HALF:] for b in both]
    mixed = [(b[:, :HALF] + dots(p2[0], w2[1], 1, 0)) * i for b, p2, w2, i in zip(both, probs2, w, inv)]
    for (c, v), o, p, i in zip(units, mixed, probs, inv):
        o_s[c, pl.ds(v, group, stride=VB), :] = o
        p_s[c, v] = p
        l_s[c, v] = i


def time_attend_back(units, group, count, q_s, k_s, v_s, o_s, p_s, l_s, do_s, dq_s, dk_s, dv_s):
    d = [do_s[c, pl.ds(v, group, stride=VB), :] * l_s[c, v] for c, v in units]
    e2 = [split2(x * o_s[c, pl.ds(v, group, stride=VB), :]) for x, (c, v) in zip(d, units)]
    d2 = [split2(x) for x in d]
    w = [spread2(x2) for x2 in time_parts(units, group, v_s)]
    ones = -ones_heads(group, count)
    both = [
        dots(
            jnp.concatenate([jnp.concatenate([a[0], b[0]], 1), jnp.concatenate([a[1], b[1]], 1)], 0),
            jnp.concatenate([w2[0], ones], 1),
            1,
            1,
        )
        for a, b, w2 in zip(d2, e2, w)
    ]
    dp = [b[:group] + b[group:] + dots(a[0], w2[1], 1, 1) for b, a, w2 in zip(both, d2, w)]
    probs = [p_s[c, v] for c, v in units]
    s2 = [split2(p * x) for p, x in zip(probs, dp)]
    p2 = [split2(p) for p in probs]
    k = [spread2(x2) for x2 in time_parts(units, group, k_s)]
    both = [dots(rows2(a), k2[0], 1, 0) for a, k2 in zip(s2, k)]
    dq = [b[:group] + b[group:] + dots(a[0], k2[1], 1, 0) for b, a, k2 in zip(both, s2, k)]
    q = time_parts(units, group, q_s)
    dk = [gather_heads(tn3(a, q2), group) for a, q2 in zip(s2, q)]
    dv = [gather_heads(tn3(a, x), group) for a, x in zip(p2, d2)]
    for (c, v), x, y, z in zip(units, dq, dk, dv):
        at = pl.ds(v, group, stride=VB)
        dq_s[c, at, :] = x
        dk_s[c, at, :] = y
        dv_s[c, at, :] = z


def store_halves(ref, x):
    rows = x.shape[0]
    ref[0, :rows, :] = x[:, :HALF]
    ref[1, :rows, :] = x[:, HALF:]


def load_halves(ref, rows):
    return jnp.concatenate([ref[0, :rows, :], ref[1, :rows, :]], 1)


def zero_tail(ref, rows):
    tail = ref.shape[1] - rows
    ref[:, rows:, :] = jnp.zeros((2, tail, HALF), F32)


def time_forward(x, w, vec, count, group, kept):
    q_s, k_s, v_s, o_s, p_s, l_s, z1_s, u_s, z2_s = kept
    rows = count * VB
    x2 = split2(x)
    store_halves(q_s, (mmw(x2, w["q"]) + vec[0:1]) * SCALE)
    store_halves(k_s, mmw(x2, w["k"]))
    store_halves(v_s, mmw(x2, w["v"]) + vec[1:2])
    for ref in (q_s, k_s, v_s):
        zero_tail(ref, rows)

    def some(i, carry):
        units = [(c, i * UNROLL + k) for k in range(UNROLL) for c in range(2)]
        time_attend(units, group, count, q_s, k_s, v_s, o_s, p_s, l_s)
        return carry

    lax.fori_loop(0, VB // UNROLL, some, 0)
    z1 = x + mmw(split2(load_halves(o_s, rows)), w["o"]) + vec[2:3]
    z1_s[...] = z1
    h, _, _ = norm_fwd(z1, vec[3:4], vec[4:5])
    u = mmw(split2(h), w["up"]) + jnp.concatenate([vec[5:6], vec[6:7]], 1)
    u_s[...] = u
    z2 = h + mmw(split2(u * gelu_cdf(u)), w["down"]) + vec[7:8]
    z2_s[...] = z2
    return norm_fwd(z2, vec[8:9], vec[9:10])[0]


def embed_block(pieces, emb, place):
    return mmw(split2(pieces), emb) + place


TIME_W = ("q", "k", "v", "o", "up", "down")


def time_fwd_kernel(first, count, group, *refs):
    if first:
        x_ref, emb_ref, place_ref = refs[:3]
        refs = refs[3:]
    else:
        x_ref = refs[0]
        refs = refs[1:]
    w = {name: refs[i][...] for i, name in enumerate(TIME_W)}
    vec_ref, y_ref = refs[6:8]
    rows = count * VB
    if first:
        place = jnp.broadcast_to(place_ref[...], (count, VB, D)).reshape(rows, D)
        x = embed_block(x_ref[...].reshape(rows, 16), emb_ref[...], place)
    else:
        x = x_ref[...].reshape(rows, D)
    y = time_forward(x, w, vec_ref[...], count, group, refs[8:])
    y_ref[...] = y.reshape(count, VB, D)


def whole(shape):
    return pl.BlockSpec(shape, lambda i: (0,) * len(shape))


def params_spec():
    return pltpu.CompilerParams(vmem_limit_bytes=VMEM_LIMIT)


def pick(shape, index):
    return pl.BlockSpec((None,) + shape, lambda i: (index,) + (0,) * len(shape))


def weight_specs(squares, feed, layer):
    specs = [pick((D, D), k) for k in squares]
    if feed is not None:
        specs += [pick((D, FF), feed), pick((FF, D), 4 + feed)]
    return specs + [pick((24, D), layer)]


def weight_args(model, squares, feed):
    square, up, down, vecs = model
    return [square] * len(squares) + ([up, down] if feed is not None else []) + [vecs]


def flush(step, last, accs, mat_at, feeds, up_rows, g_mat, g_feed, sems):
    @pl.when(step == last)
    def _():
        copies = []

        def add(src, dst):
            copies.append(pltpu.make_async_copy(src, dst, sems.at[len(copies)]))

        for acc, at in zip(accs, mat_at):
            add(acc, g_mat.at[pl.ds(at, acc.shape[0])] if len(acc.shape) == 3 else g_mat.at[at])
        for up_acc, down_acc, feed_at in feeds:
            for k in range(D // up_rows):
                for half in range(2):
                    base = 2 * D * feed_at + (2 * k + half) * up_rows
                    add(up_acc.at[pl.ds(k * up_rows, up_rows), pl.ds(half * D, D)], g_feed.at[pl.ds(base, up_rows)])
            add(down_acc, g_feed.at[pl.ds(4 * FF + feed_at * FF, FF)])
        for copy in copies:
            copy.start()
        for copy in copies:
            copy.wait()


def pack_shapes():
    return [jax.ShapeDtypeStruct((NSQ, D, D), F32), jax.ShapeDtypeStruct((8 * FF, D), F32)]


def flush_count(mats, feeds, up_rows):
    return mats + feeds * (2 * D // up_rows + 1 if up_rows else 0)


def time_kept(count, group, nb):
    pad, rows = group * VB, count * VB
    shapes = [(2, pad, HALF)] * 4 + [(2, VB, group, 4 * group), (2, VB, group, HALF), (rows, D), (rows, FF), (rows, D)]
    specs = [pl.BlockSpec((None,) + s, lambda i, n=len(s): (i,) + (0,) * n) for s in shapes]
    return specs, [jax.ShapeDtypeStruct((nb,) + s, F32) for s in shapes]


def time_fwd(first, x, extra, model, layer, count):
    squares = [12 * layer + k for k in range(4)]
    group = 64 if count > 32 else 32
    nv = x.shape[1]
    width = x.shape[2]
    specs = [pl.BlockSpec((count, VB, width), lambda i: (0, i, 0))]
    if first:
        specs += [whole((16, D)), whole((count, 1, D))]
    kept_specs, kept_shapes = time_kept(count, group, nv // VB)
    out = pl.pallas_call(
        functools.partial(time_fwd_kernel, first, count, group),
        grid=(nv // VB,),
        in_specs=specs + weight_specs(squares, 2 * layer, layer),
        out_specs=[pl.BlockSpec((count, VB, D), lambda i: (0, i, 0))] + kept_specs,
        out_shape=[jax.ShapeDtypeStruct((count, nv, D), F32)] + kept_shapes,
        compiler_params=params_spec(),
        name="time_fwd",
    )(x, *extra, *weight_args(model, squares, 2 * layer))
    return out[0], out[1:]


def time_bwd_kernel(first, count, group, layer, up_rows, *refs):
    if first:
        x_ref, emb_ref, place_ref = refs[:3]
        refs = refs[3:]
    else:
        x_ref = refs[0]
        refs = refs[1:]
    dy_ref = refs[0]
    q_s, k_s, v_s, o_s, p_s, l_s, z1_s, u_s, z2_s = refs[1:10]
    w = {name: refs[10 + i][...] for i, name in enumerate(TIME_W)}
    vec_ref = refs[16]
    later = refs[17:21]
    g_mat, g_feed = refs[23:25]
    outs = refs[25:]
    n_out = 3 if first else 2
    tail = outs[1:n_out]
    accs = outs[n_out : n_out + 6]
    sems = outs[n_out + 6]
    g = dict(zip(TIME_W + ("rows",), tuple(accs) + (outs[0],)))
    do_s, dq_s, dk_s, dv_s = outs[n_out + 7 :]
    rows = count * VB
    step = pl.program_id(0)

    @pl.when(step == 0)
    def _():
        for ref in list(g.values()) + (list(tail) if first else []):
            ref[...] = jnp.zeros(ref.shape, F32)

    vec = vec_ref[...]
    if first:
        place = jnp.broadcast_to(place_ref[...], (count, VB, D)).reshape(rows, D)
        pieces = x_ref[...].reshape(rows, 16)
        x = embed_block(pieces, emb_ref[...], place)
    else:
        x = x_ref[...].reshape(rows, D)
    x2 = split2(x)
    mixed = load_halves(o_s, rows)
    h, unit1, inv1 = norm_fwd(z1_s[...], vec[3:4], vec[4:5])
    u = u_s[...]
    cdf = gelu_cdf(u)
    _, unit2, inv2 = norm_fwd(z2_s[...], vec[8:9], vec[9:10])
    dy = dy_ref[...].reshape(rows, D)
    g["rows"][8] += colsum(dy * unit2)
    g["rows"][9] += colsum(dy)
    dz2 = norm_bwd(dy, unit2, inv2, vec[8:9])
    g["rows"][7] += colsum(dz2)
    dz22 = split2(dz2)
    g["down"][...] += tn3(split2(u * cdf), dz22)
    du = mmwt(dz22, w["down"]) * gelu_slope(u, cdf)
    g["rows"][5] += colsum(du[:, :D])
    g["rows"][6] += colsum(du[:, D:])
    du2 = split2(du)
    g["up"][...] += tn3(split2(h), du2)
    dh = dz2 + mmwt(du2, w["up"])
    g["rows"][3] += colsum(dh * unit1)
    g["rows"][4] += colsum(dh)
    dz1 = norm_bwd(dh, unit1, inv1, vec[3:4])
    g["rows"][2] += colsum(dz1)
    dz12 = split2(dz1)
    g["o"][...] += tn3(split2(mixed), dz12)
    store_halves(do_s, mmwt(dz12, w["o"]))
    zero_tail(do_s, rows)

    def some(i, carry):
        units = [(c, i * UNROLL_BACK + k) for k in range(UNROLL_BACK) for c in range(2)]
        time_attend_back(units, group, count, q_s, k_s, v_s, o_s, p_s, l_s, do_s, dq_s, dk_s, dv_s)
        return carry

    lax.fori_loop(0, VB // UNROLL_BACK, some, 0)
    dq = load_halves(dq_s, rows) * SCALE
    g["rows"][0] += colsum(dq)
    dq2 = split2(dq)
    g["q"][...] += tn3(x2, dq2)
    dx = dz1 + mmwt(dq2, w["q"])
    dk2 = split2(load_halves(dk_s, rows))
    g["k"][...] += tn3(x2, dk2)
    dx = dx + mmwt(dk2, w["k"])
    dv = load_halves(dv_s, rows)
    g["rows"][1] += colsum(dv)
    dv2 = split2(dv)
    g["v"][...] += tn3(x2, dv2)
    dx = dx + mmwt(dv2, w["v"])
    if first:
        tail[0][...] += tn3(split2(pieces), split2(dx))
        tail[1][...] += dx
    else:
        tail[0][...] = dx.reshape(count, VB, D)
    flush(
        step, pl.num_programs(0) - 1, list(accs[:4]) + list(later[:2]), [12 * layer + k for k in (0, 1, 2, 3, 8, 11)],
        [(accs[4], accs[5], 2 * layer), (later[2], later[3], 2 * layer + 1)], up_rows, g_mat, g_feed, sems,
    )


def time_bwd(first, x, extra, dy, kept, model, layer, count, later, packs, up_rows):
    group = 64 if count > 32 else 32
    nv = x.shape[1]
    width = x.shape[2]
    pad = group * VB
    squares = [12 * layer + k for k in range(4)]
    block = pl.BlockSpec((count, VB, D), lambda i: (0, i, 0))
    specs = [pl.BlockSpec((count, VB, width), lambda i: (0, i, 0))]
    if first:
        specs += [whole((16, D)), whole((count, 1, D))]
    specs += [block] + time_kept(count, group, nv // VB)[0] + weight_specs(squares, 2 * layer, layer) + [ANY] * 4
    grad_shapes = [(10, 8, D)] + ([(16, D), (count * VB, D)] if first else [])
    out_specs = [ANY] * 2 + [whole(s) for s in grad_shapes]
    out_shape = pack_shapes() + [jax.ShapeDtypeStruct(s, F32) for s in grad_shapes]
    if not first:
        out_specs.append(block)
        out_shape.append(jax.ShapeDtypeStruct((count, nv, D), F32))
    return pl.pallas_call(
        functools.partial(time_bwd_kernel, first, count, group, layer, up_rows),
        grid=(nv // VB,),
        in_specs=specs + [ANY] * 2,
        out_specs=out_specs,
        out_shape=out_shape,
        input_output_aliases={len(specs): 0, len(specs) + 1: 1},
        scratch_shapes=[pltpu.VMEM((D, D), F32)] * 4
        + [pltpu.VMEM((D, FF), F32), pltpu.VMEM((FF, D), F32), pltpu.SemaphoreType.DMA((flush_count(6, 2, up_rows),))]
        + [pltpu.VMEM((2, pad, HALF), F32)] * 4,
        compiler_params=params_spec(),
        name="time_bwd",
    )(x, *extra, dy, *kept, *weight_args(model, squares, 2 * layer), *later, *packs)

SB_ROWS = 64


def head_rows():
    sub = lax.broadcasted_iota(jnp.int32, (8, D), 0)
    lane = lax.broadcasted_iota(jnp.int32, (8, D), 1)
    return jnp.where(sub == lane // 32, 1.0, 0.0).astype(F32)


def spread_rows(x):
    wide = jnp.broadcast_to(x[:, None, :], (RPAD, HEADS, D)) * head_rows()[None]
    return wide.reshape(RPAD * HEADS, D)


def gather_rows(x):
    return jnp.sum(x.reshape(RPAD, HEADS, D) * head_rows()[None], 1)


PACK = 24


def pack_rows(x, last=None):
    last = jnp.zeros((1, HALF), F32) if last is None else last
    return jnp.concatenate([x[:ROUT, :HALF], x[:ROUT, HALF:], last, jnp.zeros((PACK - 2 * ROUT - 1, HALF), F32)], 0)


def unpack_rows(x):
    x = jnp.concatenate([x[:ROUT], x[ROUT : 2 * ROUT]], 1)
    return jnp.concatenate([x, jnp.zeros((RPAD - ROUT, D), F32)], 0)


def unpack_block(ref, sb):
    return jnp.concatenate([unpack_rows(ref[s]) for s in range(sb)], 0)


def pack_block(ref, x, sb):
    for s in range(sb):
        ref[s] = pack_rows(x[s * RPAD : (s + 1) * RPAD])


def valid_lane(rows):
    return lax.broadcasted_iota(jnp.int32, (rows, HALF), 1) < ROUT * HEADS


def router_reduce(x, op):
    for shift in (8, 16, 32, 64):
        x = op(x, pltpu.roll(x, shift, 1))
    return x


def merge_rows(y, pairs, vec):
    wide = y.reshape(pairs, 2, SB_ROWS, D)
    wide = jnp.concatenate([wide[:, 0].reshape(pairs * SB_ROWS, D), wide[:, 1].reshape(pairs * SB_ROWS, D)], 1)
    gain = jnp.concatenate([vec[0:1], vec[1:2]], 1)
    bias = jnp.concatenate([vec[2:3], vec[3:4]], 1)
    return norm_fwd(wide, gain, bias) + (gain,)


RECV_W = ("so", "rk", "rv", "rq", "ro", "up", "down")


def recv_buffer(o2, w, vec):
    buf2 = split2(mmw(o2, w["so"]) + vec[12:13])
    kb = mmw(buf2, w["rk"])
    vb = mmw(buf2, w["rv"]) + vec[14:15]
    segs = range(kb.shape[0] // RPAD)
    k = [split2(spread_rows(kb[s * RPAD : (s + 1) * RPAD])) for s in segs]
    v = [split2(spread_rows(vb[s * RPAD : (s + 1) * RPAD])) for s in segs]
    return buf2, k, v


def recv_forward(send, o_rows, w, vec):
    sb = send.shape[0] // SB_ROWS
    send2 = split2(send)
    o2 = split2(o_rows)
    buf2, k, v = recv_buffer(o2, w, vec)
    q = (mmw(send2, w["rq"]) + vec[13:14]) * SCALE
    segs = range(sb)
    ok = valid_lane(SB_ROWS)
    scores = [jnp.where(ok, nt3(split2(q[s * SB_ROWS : (s + 1) * SB_ROWS]), k[s]), negative) for s in segs]
    probs = [jnp.exp(sc - router_reduce(sc, jnp.maximum)) for sc in scores]
    probs = [p / router_reduce(p, jnp.add) for p in probs]
    mixed = jnp.concatenate([nn3(split2(p), v2) for p, v2 in zip(probs, v)], 0)
    z3 = send + mmw(split2(mixed), w["ro"]) + vec[15:16]
    g, unit3, inv3 = norm_fwd(z3, vec[16:17], vec[17:18])
    u = mmw(split2(g), w["up"]) + jnp.concatenate([vec[18:19], vec[19:20]], 1)
    cdf = gelu_cdf(u)
    z4 = g + mmw(split2(u * cdf), w["down"]) + vec[20:21]
    y, unit4, inv4 = norm_fwd(z4, vec[21:22], vec[22:23])
    kept = (send2, o2, buf2, mixed, g, unit3, inv3, u, cdf, unit4, inv4, q, k, v, probs)
    return y, kept, (q, mixed, jnp.concatenate(probs, 0), z3, u, z4)


def recv_restore(send, o_rows, w, vec, saved):
    q, mixed, p, z3, u, z4 = saved
    o2 = split2(o_rows)
    buf2, k, v = recv_buffer(o2, w, vec)
    g, unit3, inv3 = norm_fwd(z3, vec[16:17], vec[17:18])
    y, unit4, inv4 = norm_fwd(z4, vec[21:22], vec[22:23])
    probs = [p[s * SB_ROWS : (s + 1) * SB_ROWS] for s in range(send.shape[0] // SB_ROWS)]
    return y, (split2(send), o2, buf2, mixed, g, unit3, inv3, u, gelu_cdf(u), unit4, inv4, q, k, v, probs)


KEPT_WIDTHS = (D, D, HALF, D, FF, D)


def kept_specs(sb):
    return [pl.BlockSpec((sb * SB_ROWS, k), lambda i: (i, 0)) for k in KEPT_WIDTHS]


RECV_G = ("so", "rk", "rv", "rows")
LATER_WIDTHS = (D, D, FF, D)


def row_specs(sb, widths):
    return [pl.BlockSpec((sb * SB_ROWS, k), lambda i: (i, 0)) for k in widths]


def row_shapes(n, widths):
    return [jax.ShapeDtypeStruct((n * SB_ROWS, k), F32) for k in widths]


def put(refs, values):
    for ref, value in zip(refs, values):
        ref[...] = value


def recv_backward(dy, kept, w, vec, g):
    send2, o2, buf2, mixed, gg, unit3, inv3, u, cdf, unit4, inv4, q, k, v, probs = kept
    sb = dy.shape[0] // SB_ROWS
    rows = g["rows"]
    rows[9] += colsum(dy * unit4)
    rows[10] += colsum(dy)
    dz4 = norm_bwd(dy, unit4, inv4, vec[21:22])
    rows[8] += colsum(dz4)
    dz42 = split2(dz4)
    du = mmwt(dz42, w["down"]) * gelu_slope(u, cdf)
    rows[6] += colsum(du[:, :D])
    rows[7] += colsum(du[:, D:])
    du2 = split2(du)
    dg = dz4 + mmwt(du2, w["up"])
    rows[4] += colsum(dg * unit3)
    rows[5] += colsum(dg)
    dz3 = norm_bwd(dg, unit3, inv3, vec[16:17])
    rows[3] += colsum(dz3)
    dz32 = split2(dz3)
    do = mmwt(dz32, w["ro"])
    segs = range(sb)
    d = [split2(do[s * SB_ROWS : (s + 1) * SB_ROWS]) for s in segs]
    dp = [nt3(d2, v2) for d2, v2 in zip(d, v)]
    ds = [split2(p * (x - router_reduce(p * x, jnp.add))) for p, x in zip(probs, dp)]
    dq = jnp.concatenate([nn3(s2, k2) for s2, k2 in zip(ds, k)], 0) * SCALE
    q = [split2(q[s * SB_ROWS : (s + 1) * SB_ROWS]) for s in segs]
    dk = jnp.concatenate([gather_rows(tn3(s2, q2)) for s2, q2 in zip(ds, q)], 0)
    dv = jnp.concatenate([gather_rows(tn3(split2(p), d2)) for p, d2 in zip(probs, d)], 0)
    rows[1] += colsum(dq)
    dq2 = split2(dq)
    dsend = dz3 + mmwt(dq2, w["rq"])
    dk2 = split2(dk)
    dv2 = split2(dv)
    rows[2] += colsum(dv)
    g["rk"][...] += tn3(buf2, dk2)
    g["rv"][...] += tn3(buf2, dv2)
    dbuf = mmwt(dk2, w["rk"]) + mmwt(dv2, w["rv"])
    rows[0] += colsum(dbuf)
    dbuf2 = split2(dbuf)
    g["so"][...] += tn3(o2, dbuf2)
    return dsend, mmwt(dbuf2, w["so"]), (dq, dz3, du, dz4)


def recv_squares(layer):
    return [12 * layer + k for k in (7, 9, 10, 8, 11)]


def seg_block(sb, rows=SB_ROWS, width=D):
    return pl.BlockSpec((sb, rows, width), lambda i: (i, 0, 0))


MERGE = pl.BlockSpec((2, D, D), lambda i: (12, 0, 0))


def pack_spec(sb):
    return seg_block(sb, PACK, HALF)


def recv_fwd_kernel(sb, send_ref, o_ref, *refs):
    w = {n: refs[i][...] for i, n in enumerate(RECV_W)}
    vec_ref, mvec_ref, mw_ref, out_ref = refs[7:11]
    y, _, saved = recv_forward(send_ref[...].reshape(sb * SB_ROWS, D), unpack_block(o_ref, sb), w, vec_ref[...])
    for ref, x in zip(refs[11:], saved):
        ref[...] = x
    mvec = mvec_ref[...]
    wide, _, _, _ = merge_rows(y, sb // 2, mvec)
    out_ref[...] = (mmw(split2(wide), mw_ref[...].reshape(2 * D, D)) + mvec[4:5]).reshape(sb // 2, SB_ROWS, D)


def recv_fwd(send, o, model, mvec, sb):
    squares = recv_squares(0)
    n = send.shape[0]
    return pl.pallas_call(
        functools.partial(recv_fwd_kernel, sb),
        grid=(n // sb,),
        in_specs=[seg_block(sb), pack_spec(sb)] + weight_specs(squares, 1, 0) + [whole((8, D)), MERGE],
        out_specs=[seg_block(sb // 2)] + kept_specs(sb),
        out_shape=[jax.ShapeDtypeStruct((n // 2, SB_ROWS, D), F32)]
        + [jax.ShapeDtypeStruct((n * SB_ROWS, k), F32) for k in KEPT_WIDTHS],
        compiler_params=params_spec(),
        name="recv_fwd",
    )(send, o, *weight_args(model, squares, 1), mvec, model[0])


def recv_bwd_kernel(sb, send_ref, o_ref, dx_ref, *refs):
    saved = [ref[...] for ref in refs[:6]]
    refs = refs[6:]
    w = {n: refs[i][...] for i, n in enumerate(RECV_W)}
    vec_ref, mvec_ref, mw_ref = refs[7:10]
    g_mat, dsend_ref, do_ref, rows_ref, dmv_ref = refs[11:16]
    later, accs, dmw_ref, sems = refs[16:20], refs[20:23], refs[23], refs[24]
    g = dict(zip(RECV_G, tuple(accs) + (rows_ref,)))

    @pl.when(pl.program_id(0) == 0)
    def _():
        for ref in list(g.values()) + [dmw_ref, dmv_ref]:
            ref[...] = jnp.zeros(ref.shape, F32)

    vec = vec_ref[...]
    y, kept = recv_restore(send_ref[...].reshape(sb * SB_ROWS, D), unpack_block(o_ref, sb), w, vec, saved)
    pairs = sb // 2
    wide, unit, inv, gain = merge_rows(y, pairs, mvec_ref[...])
    dx = dx_ref[...].reshape(pairs * SB_ROWS, D)
    dmv_ref[4] += colsum(dx)
    dx2 = split2(dx)
    dmw_ref[...] += tn3(split2(wide), dx2).reshape(2, D, D)
    dn = mmwt(dx2, mw_ref[...].reshape(2 * D, D))
    part = colsum(dn * unit)
    dmv_ref[0] += part[:, :D]
    dmv_ref[1] += part[:, D:]
    part = colsum(dn)
    dmv_ref[2] += part[:, :D]
    dmv_ref[3] += part[:, D:]
    dwide = norm_bwd(dn, unit, inv, gain)
    left = dwide[:, :D].reshape(pairs, 1, SB_ROWS, D)
    right = dwide[:, D:].reshape(pairs, 1, SB_ROWS, D)
    dy = jnp.concatenate([left, right], 1).reshape(sb * SB_ROWS, D)
    dsend, do, grads = recv_backward(dy, kept, w, vec, g)
    put(later, grads)
    dsend_ref[...] = dsend.reshape(sb, SB_ROWS, D)
    pack_block(do_ref, do, sb)
    recv_flush(accs, [(dmw_ref, 24)], 0, g_mat, sems)


RECV_ACC = [pltpu.VMEM((D, D), F32)] * 3


def recv_flush(accs, more, layer, g_mat, sems):
    flush(
        pl.program_id(0), pl.num_programs(0) - 1, list(accs) + [m for m, _ in more],
        recv_squares(layer)[:3] + [at for _, at in more], [], 0, g_mat, None, sems,
    )


def recv_bwd(send, o, dx, kept, model, mvec, sb, g_mat):
    n = send.shape[0]
    squares = recv_squares(0)
    shapes = [(11, 8, D), (5, 8, D)]
    specs = [seg_block(sb), pack_spec(sb), seg_block(sb // 2)] + kept_specs(sb)
    specs += weight_specs(squares, 1, 0) + [whole((8, D)), MERGE]
    return pl.pallas_call(
        functools.partial(recv_bwd_kernel, sb),
        grid=(n // sb,),
        in_specs=specs + [ANY],
        out_specs=[ANY, seg_block(sb), pack_spec(sb)] + [whole(s) for s in shapes] + row_specs(sb, LATER_WIDTHS),
        out_shape=pack_shapes()[:1]
        + [jax.ShapeDtypeStruct((n, SB_ROWS, D), F32), jax.ShapeDtypeStruct(o.shape, F32)]
        + [jax.ShapeDtypeStruct(s, F32) for s in shapes]
        + row_shapes(n, LATER_WIDTHS),
        input_output_aliases={len(specs): 0},
        scratch_shapes=RECV_ACC + [pltpu.VMEM((2, D, D), F32), pltpu.SemaphoreType.DMA((4,))],
        compiler_params=params_spec(),
        name="recv_bwd",
    )(send, o, dx, *kept, *weight_args(model, squares, 1), mvec, model[0], g_mat)


def tail_kernel(sb, send_ref, o_ref, tgt_ref, kept_ref, scale_ref, mean_ref, *refs):
    w = {n: refs[i][...] for i, n in enumerate(RECV_W)}
    vec_ref, head_ref, g_mat, g_feed, dsend_ref, do_ref, rows_ref, dhead_ref = refs[7:15]
    saved, later, accs, sems = refs[15:18], refs[18:22], refs[22:25], refs[25]
    g = dict(zip(RECV_G, tuple(accs) + (rows_ref,)))

    @pl.when(pl.program_id(0) == 0)
    def _():
        for ref in list(g.values()) + [dhead_ref]:
            ref[...] = jnp.zeros(ref.shape, F32)

    vec = vec_ref[...]
    rows = sb * SB_ROWS
    y, kept, (_, mixed, _, z3, u, _) = recv_forward(
        send_ref[...].reshape(rows, D), unpack_block(o_ref, sb), w, vec
    )
    head = head_ref[...]
    y2 = split2(y)
    scale = jnp.broadcast_to(scale_ref[...][None], (sb, SB_ROWS, PPAD)).reshape(rows, PPAD)
    mean = jnp.broadcast_to(mean_ref[...][None], (sb, SB_ROWS, PPAD)).reshape(rows, PPAD)
    misfit = mmwt(y2, head) * scale + mean - tgt_ref[...].reshape(rows, PPAD)
    put(saved, (mixed, z3, u))
    dpred = kept_ref[...].reshape(rows, PPAD) * misfit * scale
    dpred2 = split2(dpred)
    dhead_ref[...] += tn3(dpred2, y2)
    dy = mmw(dpred2, head)
    dsend, do, grads = recv_backward(dy, kept, w, vec, g)
    put(later, grads)
    dsend_ref[...] = dsend.reshape(sb, SB_ROWS, D)
    pack_block(do_ref, do, sb)
    recv_flush(accs, [], 1, g_mat, sems)


def tail(send, o, tgt, kept, scale, mean, model, head, sb):
    n = send.shape[0]
    squares = recv_squares(1)
    shapes = [(11, 8, D), (PPAD, D)]
    return pl.pallas_call(
        functools.partial(tail_kernel, sb),
        grid=(n // sb,),
        in_specs=[seg_block(sb), pack_spec(sb), seg_block(sb, SB_ROWS, PPAD), seg_block(sb, SB_ROWS, PPAD)]
        + [whole((SB_ROWS, PPAD))] * 2
        + weight_specs(squares, 3, 1)
        + [whole((PPAD, D))],
        out_specs=[ANY] * 2 + [seg_block(sb), pack_spec(sb)] + [whole(s) for s in shapes]
        + row_specs(sb, (D, D, FF) + LATER_WIDTHS),
        out_shape=pack_shapes()
        + [jax.ShapeDtypeStruct((n, SB_ROWS, D), F32), jax.ShapeDtypeStruct(o.shape, F32)]
        + [jax.ShapeDtypeStruct(s, F32) for s in shapes]
        + row_shapes(n, (D, D, FF) + LATER_WIDTHS),
        scratch_shapes=RECV_ACC + [pltpu.SemaphoreType.DMA((3,))],
        compiler_params=params_spec(),
        name="tail",
    )(send, o, tgt, kept, scale, mean, *weight_args(model, squares, 3), head)


SEND_W = ("sq", "sk", "sv")


def send_project(dim2, r_rows, w, vec):
    r2 = split2(r_rows)
    sb = r_rows.shape[0] // RPAD
    k = mmw(dim2, w["sk"])
    v = mmw(dim2, w["sv"]) + vec[11:12]
    q = (mmw(r2, w["sq"]) + vec[10:11]) * SCALE
    k = [split2(k[s * SB_ROWS : (s + 1) * SB_ROWS]) for s in range(sb)]
    v = [split2(v[s * SB_ROWS : (s + 1) * SB_ROWS]) for s in range(sb)]
    q = [split2(spread_rows(q[s * RPAD : (s + 1) * RPAD])) for s in range(sb)]
    return r2, k, v, q


def send_fwd_kernel(sb, dim_ref, r_ref, here_ref, *refs):
    w = {n: refs[i][...] for i, n in enumerate(SEND_W)}
    vec_ref, o_ref = refs[3:]
    dim2 = split2(dim_ref[...].reshape(sb * SB_ROWS, D))
    _, k, v, q = send_project(dim2, r_ref[...].reshape(sb * RPAD, D), w, vec_ref[...])
    here = here_ref[...] > 0.5
    scores = [jnp.where(here, nt3(k2, q2), negative) for k2, q2 in zip(k, q)]
    tops = [jnp.max(sc, 0, keepdims=True) for sc in scores]
    probs = [jnp.where(here, jnp.exp(sc - top), 0.0) for sc, top in zip(scores, tops)]
    totals = [jnp.sum(p, 0, keepdims=True) for p in probs]
    safe = [jnp.where(t > 0.0, t, 1.0) for t in totals]
    mixed = [gather_rows(tn3(split2(p / t), v2)) for p, t, v2 in zip(probs, safe, v)]
    for s in range(sb):
        lse = jnp.where(totals[s] > 0.0, tops[s] + jnp.log(safe[s]), negative)
        o_ref[s] = pack_rows(mixed[s], lse)


def send_squares(layer):
    return [12 * layer + k for k in (4, 5, 6)]


def send_fwd(dim, routers, here, model, layer, sb, npad):
    squares = send_squares(layer)
    n = dim.shape[0]
    return pl.pallas_call(
        functools.partial(send_fwd_kernel, sb),
        grid=(n // sb,),
        in_specs=[seg_block(sb), seg_block(sb, RPAD), whole((SB_ROWS, HALF))]
        + weight_specs(squares, None, layer),
        out_specs=pack_spec(sb),
        out_shape=jax.ShapeDtypeStruct((npad, PACK, HALF), F32),
        compiler_params=params_spec(),
        name="send_fwd",
    )(dim, routers, here, *weight_args(model, squares, None))


def send_bwd_kernel(sb, layer, dim_ref, dpart_ref, r_ref, o_ref, do_ref, here_ref, *refs):
    w = {n: refs[i][...] for i, n in enumerate(SEND_W)}
    vec_ref = refs[3]
    g_mat, ddim_ref, dr_ref, rows = refs[5:9]
    dsq_ref, dsk_ref, dsv_ref, sems = refs[9:13]

    @pl.when(pl.program_id(0) == 0)
    def _():
        for ref in (dsq_ref, dsk_ref, dsv_ref, rows):
            ref[...] = jnp.zeros(ref.shape, F32)

    dim2 = split2(dim_ref[...].reshape(sb * SB_ROWS, D))
    r2, k, v, q = send_project(dim2, r_ref[...].reshape(sb * RPAD, D), w, vec_ref[...])
    here = (here_ref[...] > 0.5) & valid_lane(SB_ROWS)
    segs = range(sb)
    scores = [nt3(k2, q2) for k2, q2 in zip(k, q)]
    probs = [jnp.where(here, jnp.exp(scores[s] - o_ref[s][2 * ROUT : 2 * ROUT + 1]), 0.0) for s in segs]
    dwide = [spread_rows(unpack_rows(do_ref[s])) for s in segs]
    owide = [
        jnp.broadcast_to(unpack_rows(o_ref[s])[:, None, :], (RPAD, HEADS, D)).reshape(RPAD * HEADS, D) for s in segs
    ]
    e = [split2(a * b) for a, b in zip(dwide, owide)]
    d = [split2(a) for a in dwide]
    one_row = jnp.ones((8, D), BF)
    means = [(dots(one_row, e2[0], 1, 1) + dots(one_row, e2[1], 1, 1))[0:1] for e2 in e]
    dp = [nt3(v2, d2) for v2, d2 in zip(v, d)]
    ds = [split2(p * (x - mean)) for p, x, mean in zip(probs, dp, means)]
    dk = jnp.concatenate([nn3(s2, q2) for s2, q2 in zip(ds, q)], 0)
    dv = jnp.concatenate([nn3(split2(p), d2) for p, d2 in zip(probs, d)], 0)
    dq = jnp.concatenate([gather_rows(tn3(s2, k2)) for s2, k2 in zip(ds, k)], 0) * SCALE
    dk2 = split2(dk)
    dv2 = split2(dv)
    rows[1] += colsum(dv)
    dsk_ref[...] += tn3(dim2, dk2)
    dsv_ref[...] += tn3(dim2, dv2)
    out = dpart_ref[...].reshape(sb * SB_ROWS, D) + mmwt(dk2, w["sk"]) + mmwt(dv2, w["sv"])
    ddim_ref[...] = out.reshape(sb, SB_ROWS, D)
    rows[0] += colsum(dq)
    dq2 = split2(dq)
    dsq_ref[...] += tn3(r2, dq2)
    dr_ref[...] = mmwt(dq2, w["sq"]).reshape(sb, RPAD, D)
    flush(
        pl.program_id(0), pl.num_programs(0) - 1, [dsq_ref, dsk_ref, dsv_ref], send_squares(layer), [], 0, g_mat, None,
        sems,
    )


def send_bwd(dim, dpart, routers, o, do, here, model, layer, sb, g_mat):
    n = dim.shape[0]
    squares = send_squares(layer)
    specs = [seg_block(sb), seg_block(sb), seg_block(sb, RPAD), pack_spec(sb), pack_spec(sb), whole((SB_ROWS, HALF))]
    specs += weight_specs(squares, None, layer)
    return pl.pallas_call(
        functools.partial(send_bwd_kernel, sb, layer),
        grid=(n // sb,),
        in_specs=specs + [ANY],
        out_specs=[ANY, seg_block(sb), seg_block(sb, RPAD), whole((2, 8, D))],
        out_shape=pack_shapes()[:1]
        + [jax.ShapeDtypeStruct((n, SB_ROWS, D), F32), jax.ShapeDtypeStruct((n, RPAD, D), F32)]
        + [jax.ShapeDtypeStruct((2, 8, D), F32)],
        input_output_aliases={len(specs): 0},
        scratch_shapes=[pltpu.VMEM((D, D), F32)] * 3 + [pltpu.SemaphoreType.DMA((3,))],
        compiler_params=params_spec(),
        name="send_bwd",
    )(dim, dpart, routers, o, do, here, *weight_args(model, squares, None), g_mat)

MESH = pl.DeviceIdType.MESH


def grid_sizes():
    nf = lax.axis_size("fsdp")
    nx = 1
    while 2 * nx * nx < nf:
        nx *= 2
    return lax.axis_size("dp") // 2, nf // nx, nx


class Place:
    def __init__(self):
        self.ny, self.nz, self.nx = grid_sizes()
        dp, fs = lax.axis_index("dp"), lax.axis_index("fsdp")
        self.core, self.y = lax.rem(dp, 2), lax.div(dp, 2)
        self.x, self.z = lax.rem(fs, self.nx), lax.div(fs, self.nx)

    def at(self, y=None, core=None, z=None, x=None):
        y = self.y if y is None else y
        core = self.core if core is None else core
        z = self.z if z is None else z
        x = self.x if x is None else x
        return (y * 2 + core, z * self.nx + x)

    def other(self):
        return 1 - self.core

    def next_x(self, k):
        return lax.rem(self.x + k, self.nx)

    def next_y(self, k):
        return lax.rem(self.y + k, self.ny)

    def next_z(self, k):
        return lax.rem(self.z + k, self.nz)

    def neighbours(self):
        out = [self.at(core=self.other())]
        out += [self.at(x=self.next_x(k)) for k in range(1, self.nx)]
        out += [self.at(y=self.next_y(k)) for k in range(1, self.ny)]
        out += [self.at(z=self.next_z(k)) for k in range(1, self.nz)]
        return out


def greet(devices):
    barrier = pltpu.get_barrier_semaphore()
    for device in devices:
        pl.semaphore_signal(barrier, inc=1, device_id=device, device_id_type=MESH)
    pl.semaphore_wait(barrier, len(devices))


def remote(src, dst, send, recv, device):
    return pltpu.make_async_remote_copy(
        src_ref=src, dst_ref=dst, send_sem=send, recv_sem=recv, device_id=device, device_id_type=MESH
    )


def gather_kernel(n, *refs):
    shards, outs = refs[:n], refs[n : 2 * n]
    send, recv, local = refs[2 * n :]
    me = Place()
    y, c, z, x = me.y, me.core, me.z, me.x
    m = me.nx
    greet(me.neighbours())
    slot = [0]

    def push(src, dst, device):
        copy = remote(src, dst, send.at[slot[0]], recv.at[slot[0]], device)
        slot[0] += 1
        copy.start()
        return copy

    def finish(copies):
        for copy in copies:
            copy.wait()

    own = [pltpu.make_async_copy(shards[j], outs[j].at[y, c, z, x], local.at[j]) for j in range(n)]
    for copy in own:
        copy.start()

    def along_z(j):
        return [push(shards[j], outs[j].at[y, c, z, x], me.at(z=me.next_z(k))) for k in range(1, me.nz)]

    first = along_z(0)
    finish(own)
    base = slot[0]

    def rest(by_core):
        slot[0] = base
        sibling = me.at(core=1 - by_core)
        shared = []

        def second(j):
            piece = outs[j].at[y, by_core, :, x]
            out = []
            for k in range(1, m):
                out.append(push(piece, piece, me.at(x=me.next_x(k)) if by_core == 0 else me.at(y=me.next_y(k))))
            shared.append(push(piece, piece, sibling))
            return out

        def third(j):
            wide = outs[j].at[y, by_core] if by_core == 0 else outs[j].at[:, by_core, :, x]
            out = []
            for k in range(1, m):
                out.append(push(wide, wide, me.at(y=me.next_y(k)) if by_core == 0 else me.at(x=me.next_x(k))))
            for k in range(1, m):
                piece = outs[j].at[y, by_core, :, me.next_x(k)] if by_core == 0 else outs[j].at[me.next_y(k), by_core, :, x]
                shared.append(push(piece, piece, sibling))
            return out

        def fourth(j):
            for k in range(1, m):
                wide = outs[j].at[me.next_y(k), by_core] if by_core == 0 else outs[j].at[:, by_core, :, me.next_x(k)]
                shared.append(push(wide, wide, sibling))

        one, two, three = {0: first}, {}, {}
        for t in range(n + 2):
            if t < n:
                finish(one[t])
                if t + 1 < n:
                    one[t + 1] = along_z(t + 1)
            if 0 < t <= n:
                finish(two[t - 1])
            if t < n:
                two[t] = second(t)
            if t > 1:
                finish(three[t - 2])
            if 0 < t <= n:
                three[t - 1] = third(t - 1)
            if t > 1:
                fourth(t - 2)
        finish(shared)

    for by_core in (0, 1):
        pl.when(c == by_core)(functools.partial(rest, by_core))


def gather_all(shards):
    ny, nz, nx = grid_sizes()
    n = len(shards)
    count = n * ((nz - 1) + (nx - 1) + 1 + (nx - 1) * 3)
    return pl.pallas_call(
        functools.partial(gather_kernel, n),
        in_specs=[ANY] * n,
        out_specs=[ANY] * n,
        out_shape=[jax.ShapeDtypeStruct((ny, 2, nz, nx) + s.shape, s.dtype) for s in shards],
        scratch_shapes=[pltpu.SemaphoreType.DMA((count,)), pltpu.SemaphoreType.DMA((count,)), pltpu.SemaphoreType.DMA((n,))],
        compiler_params=pltpu.CompilerParams(collective_id=0, has_side_effects=True, vmem_limit_bytes=VMEM_LIMIT),
        name="gather_all",
    )(*shards)


def row_chunks(rows):
    count = max(1, rows // 40)
    if rows % 8:
        count = 1
    cuts = [rows // 8 * k // count * 8 for k in range(count)] + [rows]
    return [(a, b - a) for a, b in zip(cuts, cuts[1:])]


def scatter_kernel(shapes, *refs):
    n = len(shapes)
    chunks = [(j, a, b) for j, s in enumerate(shapes) for a, b in row_chunks(s[0])]
    total = len(chunks)
    grads, tile_ref = refs[:n], refs[n]
    outs, stat_ref = refs[n + 1 : 2 * n + 1], refs[2 * n + 1]
    bufs = refs[2 * n + 2 :]
    acc, r1, r2, r3, r4 = (bufs[i * total : (i + 1) * total] for i in range(5))
    tp, tz, send, recv, local = bufs[5 * total :]
    me = Place()
    y, c, z, x = me.y, me.core, me.z, me.x
    ny, nz, nx, m = me.ny, me.nz, me.nx, me.nx
    plane = plane_peers(me)
    greet([p for p, _ in plane] + [me.at(z=me.next_z(k)) for k in range(1, nz)])
    slot = [0]

    def push(src, dst, device):
        copy = remote(src, dst, send.at[slot[0]], recv.at[slot[0]], device)
        slot[0] += 1
        copy.start()
        return copy

    def finish(copies):
        for copy in copies:
            copy.wait()

    def rest(by_core):
        slot[0] = 0
        sibling = me.at(core=1 - by_core)

        def one(i):
            j, a, b = chunks[i]
            out = []
            for k in range(nx):
                out.append(push(grads[j].at[:, 1 - by_core, :, k, pl.ds(a, b)], r1[i].at[:, k], sibling))
                copy = pltpu.make_async_copy(grads[j].at[:, by_core, :, k, pl.ds(a, b)], acc[i].at[:, k], local.at[i * nx + k])
                copy.start()
                out.append(copy)
            return out

        def add1(i):
            def body(k, carry):
                at = (lax.div(k, nx * nz), lax.rem(lax.div(k, nz), nx), lax.rem(k, nz))
                acc[i][at] = acc[i][at] + r1[i][at]
                return carry

            lax.fori_loop(0, ny * nx * nz, body, 0)

        def two(i):
            if by_core == 0:
                return [push(acc[i].at[:, me.next_x(k)], r2[i].at[k - 1], me.at(x=me.next_x(k))) for k in range(1, m)]
            return [push(acc[i].at[me.next_y(k)], r2[i].at[k - 1], me.at(y=me.next_y(k))) for k in range(1, m)]

        def add2(i):
            def body(k, carry):
                a, b = lax.div(k, nz), lax.rem(k, nz)
                at = (a, x, b) if by_core == 0 else (y, a, b)
                value = acc[i][at]
                for q in range(m - 1):
                    value = value + r2[i][q, a, b]
                acc[i][at] = value
                return carry

            lax.fori_loop(0, m * nz, body, 0)

        def three(i):
            if by_core == 0:
                return [push(acc[i].at[me.next_y(k), x], r3[i].at[k - 1], me.at(y=me.next_y(k))) for k in range(1, m)]
            return [push(acc[i].at[y, me.next_x(k)], r3[i].at[k - 1], me.at(x=me.next_x(k))) for k in range(1, m)]

        def add3(i):
            def body(k, carry):
                value = acc[i][y, x, k]
                for q in range(m - 1):
                    value = value + r3[i][q, k]
                acc[i][y, x, k] = value
                return carry

            lax.fori_loop(0, nz, body, 0)

        def four(i):
            return [push(acc[i].at[y, x, me.next_z(k)], r4[i].at[k - 1], me.at(z=me.next_z(k))) for k in range(1, nz)]

        def end(i):
            j, a, b = chunks[i]
            value = acc[i][y, x, z]
            for k in range(nz - 1):
                value = value + r4[i][k]
            outs[j][a : a + b] = value
            sq = colsum_any(value * value)
            return sq[:, :HALF] + sq[:, HALF:]

        squares = jnp.zeros((8, HALF), F32)
        ahead = 3
        p1, p2, p3, p4 = {i: one(i) for i in range(min(ahead, total))}, {}, {}, {}
        for t in range(total + 3):
            if t < total:
                finish(p1[t])
                if t + ahead < total:
                    p1[t + ahead] = one(t + ahead)
                add1(t)
                p2[t] = two(t)
            if 0 <= t - 1 < total:
                finish(p2[t - 1])
                add2(t - 1)
                p3[t - 1] = three(t - 1)
            if 0 <= t - 2 < total:
                finish(p3[t - 2])
                add3(t - 2)
                p4[t - 2] = four(t - 2)
            if 0 <= t - 3 < total:
                finish(p4[t - 3])
                squares = squares + end(t - 3)
        tp[(y * 2 + by_core) * nx + x] = jnp.concatenate([squares, tile_ref[...]], 0)

    for by_core in (0, 1):
        pl.when(c == by_core)(functools.partial(rest, by_core))

    slot[0] = total * (nx + 2 * (m - 1) + nz - 1)
    mine = tp.at[(y * 2 + c) * nx + x]
    finish([push(mine, mine, p) for p, _ in plane])
    tz[z] = functools.reduce(jnp.add, [tp[k] for k in range(2 * ny * nx)])
    finish([push(tz.at[z], tz.at[z], me.at(z=me.next_z(k))) for k in range(1, nz)])
    stat_ref[...] = functools.reduce(jnp.add, [tz[k] for k in range(nz)])


def plane_peers(me):
    out = []
    for k in range(1, 2 * me.ny * me.nx):
        dc, dy, dx = k % 2, k // 2 % me.ny, k // (2 * me.ny)
        out.append((me.at(core=lax.rem(me.core + dc, 2), y=lax.rem(me.y + dy, me.ny), x=lax.rem(me.x + dx, me.nx)), k))
    return out


def colsum_any(x):
    rows = x.shape[0]
    even = rows // 8 * 8
    out = colsum(x[:even]) if even else jnp.zeros((8, x.shape[1]), F32)
    if rows > even:
        out = out + jnp.pad(x[even:], ((0, 8 - rows + even), (0, 0)))
    return out


def scatter_sum(grads, tile):
    ny, nz, nx = grid_sizes()
    n = len(grads)
    shapes = [g.shape[-2:] for g in grads]
    pieces = [(b, s[1]) for s in shapes for _, b in row_chunks(s[0])]
    total = len(pieces)
    count = total * (nx + (nx - 1) * 2 + nz - 1) + 2 * ny * nx - 1 + nz - 1

    def buffers(*lead):
        return [pltpu.VMEM(lead + s, F32) for s in pieces]

    return pl.pallas_call(
        functools.partial(scatter_kernel, shapes),
        in_specs=[ANY] * n + [INVMEM],
        out_specs=[INVMEM] * (n + 1),
        out_shape=[jax.ShapeDtypeStruct(s, F32) for s in shapes] + [jax.ShapeDtypeStruct((16, HALF), F32)],
        scratch_shapes=buffers(ny, nx, nz)
        + buffers(ny, nx, nz)
        + buffers(nx - 1, nx, nz)
        + buffers(nx - 1, nz)
        + buffers(nz - 1)
        + [pltpu.VMEM((2 * ny * nx, 16, HALF), F32), pltpu.VMEM((nz, 16, HALF), F32)]
        + [pltpu.SemaphoreType.DMA((count,)), pltpu.SemaphoreType.DMA((count,)), pltpu.SemaphoreType.DMA((total * nx,))],
        compiler_params=pltpu.CompilerParams(collective_id=1, has_side_effects=True, vmem_limit_bytes=VMEM_LIMIT),
        name="scatter_sum",
    )(*grads, tile)


def group_part(ref, who, per):
    return ref.at[pl.ds(pl.multiple_of(who * per, per), per)]


def group_out(per, in_ref, got, send, recv, local):
    nf = lax.axis_size("fsdp")
    dp, f = lax.axis_index("dp"), lax.axis_index("fsdp")
    copies = [pltpu.make_async_copy(group_part(in_ref, f, per), got.at[f], local)]
    for k in range(1, nf):
        p = lax.rem(f + k, nf)
        copies.append(remote(group_part(in_ref, p, per), got.at[f], send.at[k - 1], recv.at[k - 1], (dp, p)))
    return copies


def group_back(per, result, out_ref, send, recv, local):
    nf = lax.axis_size("fsdp")
    dp, f = lax.axis_index("dp"), lax.axis_index("fsdp")
    copies = [pltpu.make_async_copy(result, group_part(out_ref, f, per), local)]
    for k in range(1, nf):
        p = lax.rem(f + k, nf)
        copies.append(remote(result, group_part(out_ref, f, per), send.at[nf - 2 + k], recv.at[nf - 2 + k], (dp, p)))
    return copies


def greet_group():
    nf = lax.axis_size("fsdp")
    dp, f = lax.axis_index("dp"), lax.axis_index("fsdp")
    greet([(dp, lax.rem(f + k, nf)) for k in range(1, nf)])


def start_all(copies):
    for copy in copies:
        copy.start()


def wait_all(copies):
    for copy in copies:
        copy.wait()


def stats_kernel(per, in_ref, out_ref, got, result, send, recv, local):
    nf = lax.axis_size("fsdp")
    greet_group()
    copies = group_out(per, in_ref, got, send, recv, local)
    start_all(copies)
    wait_all(copies)
    row = lax.broadcasted_iota(jnp.int32, (PACK, HALF), 0)
    lane = lax.broadcasted_iota(jnp.int32, (PACK, HALF), 1)
    router = jnp.where(row < ROUT, row, row - ROUT)
    chosen = (lane // 8 == router) & (row < 2 * ROUT)
    src = lax.broadcasted_iota(jnp.int32, (HALF, D), 0)
    dst = lax.broadcasted_iota(jnp.int32, (HALF, D), 1)
    widen = jnp.where(src % 8 == dst // 32, 1.0, 0.0).astype(BF)

    def one(s, carry):
        lse = [got[d, s, 2 * ROUT : 2 * ROUT + 1, :] for d in range(nf)]
        top = functools.reduce(jnp.maximum, lse)
        total = top + jnp.log(functools.reduce(jnp.add, [jnp.exp(l - top) for l in lse]))
        out = jnp.where(row == 2 * ROUT, total, 0.0)
        share = jnp.concatenate([jnp.where(chosen, jnp.exp(l - total), 0.0) for l in lse], 0)
        wide = mmw(split2(share), widen)
        for d in range(nf):
            w = wide[d * PACK : (d + 1) * PACK]
            w = jnp.where(row < ROUT, w[:, :HALF], w[:, HALF:])
            out = out + jnp.where(row < 2 * ROUT, w * got[d, s], 0.0)
        result[s] = out
        return carry

    lax.fori_loop(0, per, one, 0)
    copies = group_back(per, result, out_ref, send, recv, local)
    start_all(copies)
    wait_all(copies)


def sum_kernel(per, turn, in_ref, x_ref, mixed_ref, z_ref, u_ref, dq_ref, dz3_ref, du_ref, dz4_ref, vec_ref, *refs):
    out_ref, rq, ro, up, down, got, result, send, recv, local = refs
    step = pl.program_id(0)

    @pl.when(step == 0)
    def _():
        greet_group()
        start_all(group_out(per, in_ref, got, send, recv, local))
        for ref in (rq, ro, up, down):
            ref[...] = jnp.zeros(ref.shape, F32)

    @pl.when(step == turn)
    def _():
        wait_all(group_out(per, in_ref, got, send, recv, local))
        result[...] = functools.reduce(jnp.add, [got[d] for d in range(lax.axis_size("fsdp"))])
        start_all(group_back(per, result, out_ref, send, recv, local))

    rq[...] += tn3(split2(x_ref[...]), split2(dq_ref[...]))
    ro[...] += tn3(split2(mixed_ref[...]), split2(dz3_ref[...]))
    g, _, _ = norm_fwd(z_ref[...], vec_ref[16:17], vec_ref[17:18])
    up[...] += tn3(split2(g), split2(du_ref[...]))
    u = u_ref[...]
    down[...] += tn3(split2(u * gelu_cdf(u)), split2(dz4_ref[...]))

    @pl.when(step == pl.num_programs(0) - 1)
    def _():
        wait_all(group_back(per, result, out_ref, send, recv, local))


def group_scratch(per, nf):
    return [
        pltpu.VMEM((nf, per, PACK, HALF), F32),
        pltpu.VMEM((per, PACK, HALF), F32),
        pltpu.SemaphoreType.DMA((2 * nf - 2,)),
        pltpu.SemaphoreType.DMA((2 * nf - 2,)),
        pltpu.SemaphoreType.DMA,
    ]


def group_params(cid):
    return pltpu.CompilerParams(collective_id=cid, has_side_effects=True, vmem_limit_bytes=VMEM_LIMIT)


def group_stats(packed, cid):
    nf = lax.axis_size("fsdp")
    per = packed.shape[0] // nf
    return pl.pallas_call(
        functools.partial(stats_kernel, per),
        in_specs=[ANY],
        out_specs=ANY,
        out_shape=jax.ShapeDtypeStruct(packed.shape, F32),
        scratch_shapes=group_scratch(per, nf),
        compiler_params=group_params(cid),
        name="group_stats",
    )(packed)


def group_sum(packed, work, vecs, layer, cid):
    nf = lax.axis_size("fsdp")
    per = packed.shape[0] // nf
    rows = 480
    steps = work[0].shape[0] // rows
    shapes = [(D, D), (D, D), (D, FF), (FF, D)]
    return pl.pallas_call(
        functools.partial(sum_kernel, per, steps - steps // 4),
        grid=(steps,),
        in_specs=[ANY] + [pl.BlockSpec((rows, w.shape[1]), lambda i: (i, 0)) for w in work] + [pick((24, D), layer)],
        out_specs=[ANY] + [whole(s) for s in shapes],
        out_shape=[jax.ShapeDtypeStruct(packed.shape, F32)] + [jax.ShapeDtypeStruct(s, F32) for s in shapes],
        scratch_shapes=group_scratch(per, nf),
        compiler_params=group_params(cid),
        name="group_sum",
    )(packed, *work, vecs)

LAYER_AT = SEGLEN + 1 + SEG
MERGE_AT = LAYER_AT + 46
HEAD_AT = MERGE_AT + 5
ROUTER_AT = HEAD_AT + PRED
VROWS = NVEC + 20


def own_size(devices):
    own = NVEC * D // devices
    return own, -(-own // D)


def prepare_kernel(nfeed, ser_ref, obs_ref, tgt_ref, mask_ref, count_ref, mat_ref, feed_ref, vec_ref, *outs):
    pieces, tgt, kept, scale_ref, mean_ref, here_ref, tile_ref, mat_o, feed_o, vec_o = outs
    for src, dst in ((mat_ref, mat_o), (feed_ref, feed_o), (vec_ref, vec_o)):
        rows = dst.shape[0]
        left, right = src[pl.ds(0, rows, stride=2), :], src[pl.ds(1, rows, stride=2), :]
        dst[...] = jnp.concatenate([left, right], 1).astype(BF)
    nv = ser_ref.shape[0]
    series, seen = ser_ref[...], obs_ref[...].astype(F32)
    counted = jnp.maximum(jnp.sum(seen, -1, keepdims=True), 1.0)
    mean = jnp.sum(seen * series, -1, keepdims=True) / counted
    center = (series - mean) * seen
    scale = jnp.sqrt(jnp.sum(center * center, -1, keepdims=True) / counted + norm_eps)
    slot = lax.axis_index("fsdp") * nv + lax.broadcasted_iota(jnp.int32, (nv, HALF), 0)
    here = jnp.where(slot < count_ref[0], 1.0, 0.0)
    here_ref[...] = here
    scale_ref[...] = jnp.broadcast_to(scale, (nv, PPAD))
    mean_ref[...] = jnp.broadcast_to(mean, (nv, PPAD))
    mask = mask_ref[...].astype(F32) * here[:, :1]
    tile_ref[...] = jnp.broadcast_to(jnp.sum(jnp.sum(mask, 0, keepdims=True), -1, keepdims=True), (8, HALF)) * (1.0 / (8 * HALF))
    lane = lax.broadcasted_iota(jnp.int32, (nv, PPAD), 1)

    def cut(x, dst):
        x = jnp.concatenate([x, jnp.zeros((nv, PPAD - 12), F32)], 1)
        for s in range(dst.shape[0]):
            dst[s] = jnp.where(lane < 12, x[:, 12 * s : 12 * s + PPAD], 0.0)

    cut(center / scale, pieces)
    cut(tgt_ref[...], tgt)
    cut(mask * (2.0 / (1 << 20)), kept)


def prepare(series, observed, targets, target_mask, counts, matrices, feed, vectors):
    nv = series.shape[0]
    shapes = [((SEG, nv, PPAD), F32), ((SEG // 2, nv, PPAD), F32), ((SEG // 2, nv, PPAD), F32), ((nv, PPAD), F32), ((nv, PPAD), F32)]
    shapes += [((nv, HALF), F32), ((8, HALF), F32)]
    shapes += [((x.shape[0] // 2, D), BF) for x in (matrices, feed, vectors)]
    return pl.pallas_call(
        functools.partial(prepare_kernel, 0),
        grid=(1,),
        in_specs=[whole(x.shape) for x in (series, observed, targets, target_mask)]
        + [pl.BlockSpec(memory_space=pltpu.SMEM)]
        + [whole(x.shape) for x in (matrices, feed, vectors)],
        out_specs=[whole(s) for s, _ in shapes],
        out_shape=[jax.ShapeDtypeStruct(s, t) for s, t in shapes],
        compiler_params=pltpu.CompilerParams(vmem_limit_bytes=VMEM_LIMIT),
        name="prepare",
    )(series, observed, targets, target_mask, counts, matrices, feed, vectors)


def unpack_kernel(devices, own, vec_ref, vecs, mvec, emb, place, head, r0, r1, flat):
    flat[...] = jnp.zeros(flat.shape, F32)
    rows = vec_ref.shape[1]
    lane = lax.broadcasted_iota(jnp.int32, (rows, D), 1)
    for d in range(devices):
        at, shift = divmod(own * d, D)
        block = vec_ref[d].astype(F32)
        if shift:
            block = pltpu.roll(block, shift, 1)
            flat[at + 1 : at + 1 + rows] += jnp.where(lane < shift, block, 0.0)
            block = jnp.where(lane >= shift, block, 0.0)
        flat[at : at + rows] += block

    def padded(at, count, total):
        return jnp.concatenate([flat[at : at + count], jnp.zeros((total - count, D), F32)], 0)

    for l in range(2):
        vecs[l] = padded(LAYER_AT + 23 * l, 23, 24)
    mvec[...] = padded(MERGE_AT, 5, 8)
    emb[...] = padded(0, SEGLEN, 16).astype(BF)
    head[...] = padded(HEAD_AT, PRED, PPAD).astype(BF)
    for s in range(SEG):
        place[s] = flat[SEGLEN + 1 + s : SEGLEN + 2 + s] + flat[SEGLEN : SEGLEN + 1]
        r0[s] = padded(ROUTER_AT + ROUT * s, ROUT, RPAD)
    for s in range(SEG // 2):
        r1[s] = padded(ROUTER_AT + ROUT * (SEG + s), ROUT, RPAD)


def unpack_vectors(gathered, own):
    devices, rows, _ = gathered.shape
    shapes = [((2, 24, D), F32), ((8, D), F32), ((16, D), BF), ((SEG, 1, D), F32), ((PPAD, D), BF)]
    shapes += [((SEG, RPAD, D), F32), ((SEG // 2, RPAD, D), F32)]
    return pl.pallas_call(
        functools.partial(unpack_kernel, devices, own),
        grid=(1,),
        in_specs=[whole(gathered.shape)],
        out_specs=[whole(s) for s, _ in shapes],
        out_shape=[jax.ShapeDtypeStruct(s, t) for s, t in shapes],
        scratch_shapes=[pltpu.VMEM((VROWS + 24, D), F32)],
        compiler_params=pltpu.CompilerParams(vmem_limit_bytes=VMEM_LIMIT),
        name="unpack_vectors",
    )(gathered)


def assemble_kernel(devices, own, demb, dplace, *refs):
    (rt0, rs0, rr0, rt1, rs1, rr1, dmv, dhead, dr0, dr1), out, flat = refs[:10], refs[10], refs[11]
    flat[...] = jnp.zeros(flat.shape, F32)
    flat[0:SEGLEN] = demb[0:SEGLEN]
    place = jnp.sum(dplace[...].reshape(SEG, VB, D), 1)
    flat[SEGLEN : SEGLEN + 1] = jnp.sum(place, 0, keepdims=True)
    flat[SEGLEN + 1 : SEGLEN + 1 + SEG] = place
    at = LAYER_AT
    for ref in (rt0, rs0, rr0, rt1, rs1, rr1, dmv):
        count = ref.shape[0]
        flat[at : at + count] = jnp.sum(ref[...], 1)
        at += count
    flat[HEAD_AT : HEAD_AT + PRED] = dhead[0:PRED]
    for s in range(SEG):
        flat[ROUTER_AT + ROUT * s : ROUTER_AT + ROUT * (s + 1)] = dr0[s][:ROUT]
    for s in range(SEG // 2):
        flat[ROUTER_AT + ROUT * (SEG + s) : ROUTER_AT + ROUT * (SEG + s + 1)] = dr1[s][:ROUT]
    rows = out.shape[1]
    lane = lax.broadcasted_iota(jnp.int32, (rows, D), 1)
    inside = lax.broadcasted_iota(jnp.int32, (rows, D), 0) * D + lane < own
    for d in range(devices):
        at, shift = divmod(own * d, D)
        block = flat[at : at + rows]
        if shift:
            block = jnp.where(lane < D - shift, pltpu.roll(block, D - shift, 1), pltpu.roll(flat[at + 1 : at + 1 + rows], D - shift, 1))
        out[d] = jnp.where(inside, block, 0.0)


def assemble_vectors(parts, devices):
    own, rows = own_size(devices)
    return pl.pallas_call(
        functools.partial(assemble_kernel, devices, own),
        grid=(1,),
        in_specs=[whole(p.shape) for p in parts],
        out_specs=whole((devices, rows, D)),
        out_shape=jax.ShapeDtypeStruct((devices, rows, D), F32),
        scratch_shapes=[pltpu.VMEM((VROWS + 24, D), F32)],
        compiler_params=pltpu.CompilerParams(vmem_limit_bytes=VMEM_LIMIT),
        name="assemble_vectors",
    )(*parts)


def adam_update(weight, first_moment, second_moment, gradient):
    first_new = beta_one * first_moment + (1.0 - beta_one) * gradient
    second_new = beta_two * second_moment + (1.0 - beta_two) * gradient * gradient
    corrected = (
        first_new
        / (1.0 - beta_one**step_count)
        / (jnp.sqrt(second_new / (1.0 - beta_two**step_count)) + adam_eps)
    )
    return (weight - learn_rate * (corrected + weight_decay * weight), first_new, second_new)


def gradient_parts(ready, model, extras, up_rows, group_stats, group_sum, nf, devices):
    pieces, tgt, kept, scale, mean, here = ready
    mvec, emb, place, head, routers0, routers1 = extras
    sb0, sb1, sf0, sf1, st = 12, 10, 20, 10, 10
    rf, rb = 20, 20
    half = SEG // 2
    dim0, kept0 = time_fwd(True, pieces, (emb, place), model, 0, SEG)
    o0 = send_fwd(dim0, routers0, here, model, 0, sf0, -(-SEG // nf) * nf)
    o0 = group_stats(o0, 2)
    x1, *saved = recv_fwd(dim0, o0, model, mvec, rf)
    dim1, kept1 = time_fwd(False, x1, (), model, 1, half)
    o1 = send_fwd(dim1, routers1, here, model, 1, sf1, -(-half // nf) * nf)
    o1 = group_stats(o1, 3)
    vecs = model[3]
    g_mat, g_feed, ddim1, do1, rr1, dhead, *work = tail(dim1, o1, tgt, kept, scale, mean, model, head, st)
    do1, *later = group_sum(do1, [dim1.reshape(-1, D)] + work, vecs, 1, 4)
    g_mat, ddim1, dr1, rs1 = send_bwd(dim1, ddim1, routers1, o1, do1, here, model, 1, sb1, g_mat)
    g_mat, g_feed, rt1, dx1 = time_bwd(
        False, x1, (), ddim1, kept1, model, 1, half, later, (g_mat, g_feed), up_rows
    )
    g_mat, ddim0, do0, rr0, dmv, *work = recv_bwd(dim0, o0, dx1, saved, model, mvec, rb, g_mat)
    work = [dim0.reshape(-1, D), saved[1], saved[3], saved[4]] + work
    do0, *later = group_sum(do0, work, vecs, 0, 5)
    g_mat, ddim0, dr0, rs0 = send_bwd(dim0, ddim0, routers0, o0, do0, here, model, 0, sb0, g_mat)
    g_mat, g_feed, rt0, demb, dplace = time_bwd(
        True, pieces, (emb, place), ddim0, kept0, model, 0, SEG, later, (g_mat, g_feed), up_rows
    )
    g_vec = assemble_vectors((demb, dplace, rt0, rs0, rr0, rt1, rs1, rr1, dmv, dhead, dr0, dr1), devices)
    return g_mat, g_feed, g_vec


def on_device(series, observed, targets, target_mask, counts, matrices, feed_weights, vectors, matrices_first, matrices_second, feed_first, feed_second, vectors_first, vectors_second):
    nf = lax.axis_size("fsdp")
    nd = lax.axis_size("dp")
    devices = nf * nd
    own, vec_rows = own_size(devices)
    out = prepare(
        series[0],
        observed[0],
        targets[0],
        target_mask[0],
        counts,
        matrices.reshape(-1, HALF),
        feed_weights.reshape(-1, HALF),
        jnp.pad(vectors, (0, vec_rows * D - own)).reshape(-1, HALF),
    )
    ready, tile, shards = out[:6], out[6], out[7:]
    square, feed, vecs = gather_all(shards)
    square = square.reshape(NSQ, D, D)
    feed = feed.reshape(-1, D)
    up = feed[: 4 * FF].reshape(4, D, FF)
    down = feed.reshape(8, FF, D)
    vecs, *extras = unpack_vectors(vecs.reshape(devices, vec_rows, D), own)
    up_rows = feed_weights.shape[0] // FF
    g_mat, g_feed, g_vec = gradient_parts(ready, (square, up, down, vecs), extras, up_rows, group_stats, group_sum, nf, devices)
    ny, nz, nx = grid_sizes()
    lead = (ny, 2, nz, nx)
    s_mat, s_feed, s_vec, sums = scatter_sum([g.reshape(lead + (-1, D)) for g in (g_mat, g_feed, g_vec)], tile)
    is_up = lax.axis_index("dp") * 2 < nd
    halves_of = s_feed.reshape(2, up_rows, D)
    s_feed = jnp.where(is_up, jnp.concatenate([halves_of[0], halves_of[1]], 1).reshape(-1), s_feed.reshape(-1))
    grads = (s_mat.reshape(-1), s_feed, s_vec.reshape(-1)[:own])
    upscale = (1 << 20) / jnp.maximum(jnp.sum(sums[8:]), 1.0)
    grad_norm = jnp.sqrt(jnp.sum(sums[:8])) * upscale
    factor = upscale * (clip_norm / jnp.maximum(grad_norm, clip_norm))
    new = (
        adam_update(matrices, matrices_first, matrices_second, grads[0] * factor)
        + adam_update(feed_weights, feed_first, feed_second, grads[1] * factor)
        + adam_update(vectors, vectors_first, vectors_second, grads[2] * factor)
    )
    return (grad_norm,) + new


def solution(mesh):
    both = P(("dp", "fsdp"))
    data = P("dp", "fsdp", None)
    return jax.shard_map(
        on_device,
        mesh=mesh,
        in_specs=(data,) * 4 + (P("dp"),) + (both,) * 9,
        out_specs=(P(),) + (both,) * 9,
        check_vma=False,
    )
```

```python
import functools
import jax
import jax.numpy as jnp
from jax import lax
from jax.experimental import pallas as pl
from jax.experimental.pallas import tpu as pltpu
from jax.sharding import PartitionSpec as P

D = 256
HEADS = 8
FF = 512
ROUT = 10
RPAD = 16
SEGLEN = 12
PRED = 12
PPAD = 16
SEG = 60
NSQ = 26
NVEC = 1036
HALF = 128
VB = 8
UNROLL = 8
UNROLL_BACK = 8

BF = jnp.bfloat16
F32 = jnp.float32
SCALE = (D // HEADS) ** (-0.5)
negative = -1e30
norm_eps = 1e-05
beta_one = 0.9
beta_two = 0.999
adam_eps = 1e-08
weight_decay = 0.01
learn_rate = 0.2
clip_norm = 0.01
step_count = 10.0
VMEM_LIMIT = 60 << 20


ANY = pl.BlockSpec(memory_space=pl.ANY)
INVMEM = pl.BlockSpec(memory_space=pltpu.VMEM)


def split2(x):
    hi = x.astype(BF)
    return hi, (x - hi.astype(F32)).astype(BF)


def dots(a, b, ca, cb):
    return lax.dot_general(a, b, (((ca,), (cb,)), ((), ())), preferred_element_type=F32)


def mmw(x2, w):
    return dots(x2[0], w, 1, 0) + dots(x2[1], w, 1, 0)


def mmwt(x2, w):
    return dots(x2[0], w, 1, 1) + dots(x2[1], w, 1, 1)


def rows2(a2):
    return jnp.concatenate([a2[0], a2[1]], 0)


def nn3(a2, b2):
    m = a2[0].shape[0]
    both = dots(rows2(a2), b2[0], 1, 0)
    return both[:m] + both[m:] + dots(a2[0], b2[1], 1, 0)


def nt3(a2, b2):
    m = a2[0].shape[0]
    both = dots(rows2(a2), b2[0], 1, 1)
    return both[:m] + both[m:] + dots(a2[0], b2[1], 1, 1)


def tn3(a2, b2):
    n = b2[0].shape[1]
    both = dots(a2[0], jnp.concatenate([b2[0], b2[1]], 1), 0, 0)
    return both[:, :n] + both[:, n:] + dots(a2[1], b2[0], 0, 0)


def tn3_short(a2, b2):
    return dots(jnp.concatenate([a2[0], a2[0], a2[1]], 0), jnp.concatenate([b2[0], b2[1], b2[0]], 0), 0, 0)


def nn3_short(a2, b2):
    return dots(jnp.concatenate([a2[0], a2[0], a2[1]], 1), jnp.concatenate([b2[0], b2[1], b2[0]], 0), 1, 0)


def corner(r, m, n):
    return r[:m, :n] + r[m:, :n] + r[:m, n:]


def nn3_narrow(a2, b2):
    r = dots(rows2(a2), jnp.concatenate([b2[0], b2[1]], 1), 1, 0)
    return corner(r, a2[0].shape[0], b2[0].shape[1])


def nt3_narrow(a2, b2):
    return corner(dots(rows2(a2), rows2(b2), 1, 1), a2[0].shape[0], b2[0].shape[0])


def norm_fwd(z, gain, bias):
    center = z - jnp.mean(z, -1, keepdims=True)
    inv = lax.rsqrt(jnp.mean(center * center, -1, keepdims=True) + norm_eps)
    unit = center * inv
    return unit * gain + bias, unit, inv


def norm_bwd(dy, unit, inv, gain):
    t = dy * gain
    return inv * (t - jnp.mean(t, -1, keepdims=True) - unit * jnp.mean(t * unit, -1, keepdims=True))


def colsum(x):
    return jnp.sum(x.reshape(x.shape[0] // 8, 8, x.shape[1]), 0)


def gelu_cdf(u):
    return 0.5 + 0.5 * lax.erf(u * 0.7071067811865476)


def gelu_slope(u, cdf):
    return cdf + u * (jnp.exp(-0.5 * u * u) * 0.3989422804014327)


def halves(x):
    return x[:, :HALF], x[:, HALF:]


def lane_head(rows):
    return lax.broadcasted_iota(jnp.int32, (rows, HALF), 1) // 32


def spread_heads(x, zero):
    head = lane_head(x.shape[0])
    return jnp.concatenate([jnp.where(head == h, x, zero) for h in range(4)], 0)


def gather_heads(x, group):
    head = lane_head(group)
    out = x[3 * group :]
    for h in range(3):
        out = jnp.where(head == h, x[h * group : (h + 1) * group], out)
    return out


def ones_heads(group, count):
    row = lax.broadcasted_iota(jnp.int32, (4 * group, HALF), 0)
    lane = lax.broadcasted_iota(jnp.int32, (4 * group, HALF), 1)
    return jnp.where((row // group == lane // 32) & (row % group < count), 1.0, 0.0).astype(BF)


def group_max(s, group, count):
    lane = lax.broadcasted_iota(jnp.int32, (s.shape[0], HALF), 1)
    outs = []
    for t in range(s.shape[1] // HALF):
        part = s[:, t * HALF : (t + 1) * HALF]
        top = None
        for g in range(HALF // group):
            here = (lane // group == g)
            best = jnp.max(jnp.where((lane // group == g) & (lane % group < count), part, negative), -1, keepdims=True)
            top = jnp.broadcast_to(best, part.shape) if top is None else jnp.where(here, best, top)
        outs.append(jnp.where(lane % group < count, part - top, negative))
    return jnp.concatenate(outs, 1)


def time_parts(units, group, ref):
    return [split2(ref[c, pl.ds(v, group, stride=VB), :]) for c, v in units]


def spread2(x2):
    zero = jnp.zeros((), BF)
    return spread_heads(x2[0], zero), spread_heads(x2[1], zero)


def time_attend(units, group, count, q_s, k_s, v_s, o_s, p_s, l_s):
    q = time_parts(units, group, q_s)
    k = [spread2(x2) for x2 in time_parts(units, group, k_s)]
    scores = [
        dots(jnp.concatenate(q2, 1), jnp.concatenate([k2[0], k2[0]], 1), 1, 1) + dots(q2[0], k2[1], 1, 1)
        for q2, k2 in zip(q, k)
    ]
    probs = [jnp.exp(group_max(s, group, count)) for s in scores]
    probs2 = [split2(p) for p in probs]
    w = [spread2(x2) for x2 in time_parts(units, group, v_s)]
    ones = ones_heads(group, count)
    both = [dots(rows2(p2), jnp.concatenate([w2[0], ones], 1), 1, 0) for p2, w2 in zip(probs2, w)]
    both = [b[:group] + b[group:] for b in both]
    inv = [1.0 / b[:, HALF:] for b in both]
    mixed = [(b[:, :HALF] + dots(p2[0], w2[1], 1, 0)) * i for b, p2, w2, i in zip(both, probs2, w, inv)]
    for (c, v), o, p, i in zip(units, mixed, probs, inv):
        o_s[c, pl.ds(v, group, stride=VB), :] = o
        p_s[c, v] = p
        l_s[c, v] = i


def time_attend_back(units, group, count, q_s, k_s, v_s, o_s, p_s, l_s, do_s, dq_s, dk_s, dv_s):
    d = [do_s[c, pl.ds(v, group, stride=VB), :] * l_s[c, v] for c, v in units]
    e2 = [split2(x * o_s[c, pl.ds(v, group, stride=VB), :]) for x, (c, v) in zip(d, units)]
    d2 = [split2(x) for x in d]
    w = [spread2(x2) for x2 in time_parts(units, group, v_s)]
    ones = -ones_heads(group, count)
    both = [
        dots(
            jnp.concatenate([jnp.concatenate([a[0], b[0]], 1), jnp.concatenate([a[1], b[1]], 1)], 0),
            jnp.concatenate([w2[0], ones], 1),
            1,
            1,
        )
        for a, b, w2 in zip(d2, e2, w)
    ]
    dp = [b[:group] + b[group:] + dots(a[0], w2[1], 1, 1) for b, a, w2 in zip(both, d2, w)]
    probs = [p_s[c, v] for c, v in units]
    s2 = [split2(p * x) for p, x in zip(probs, dp)]
    p2 = [split2(p) for p in probs]
    k = [spread2(x2) for x2 in time_parts(units, group, k_s)]
    dq = [nn3_narrow(a, k2) for a, k2 in zip(s2, k)]
    q = time_parts(units, group, q_s)
    dk = [gather_heads(tn3_short(a, q2), group) for a, q2 in zip(s2, q)]
    dv = [gather_heads(tn3_short(a, x), group) for a, x in zip(p2, d2)]
    for (c, v), x, y, z in zip(units, dq, dk, dv):
        at = pl.ds(v, group, stride=VB)
        dq_s[c, at, :] = x
        dk_s[c, at, :] = y
        dv_s[c, at, :] = z


def store_halves(ref, x):
    rows = x.shape[0]
    ref[0, :rows, :] = x[:, :HALF]
    ref[1, :rows, :] = x[:, HALF:]


def load_halves(ref, rows):
    return jnp.concatenate([ref[0, :rows, :], ref[1, :rows, :]], 1)


def zero_tail(ref, rows):
    tail = ref.shape[1] - rows
    ref[:, rows:, :] = jnp.zeros((2, tail, HALF), F32)


def time_forward(x, w, vec, count, group, kept):
    q_s, k_s, v_s, o_s, p_s, l_s, z1_s, u_s, z2_s = kept
    rows = count * VB
    x2 = split2(x)
    store_halves(q_s, (mmw(x2, w["q"]) + vec[0:1]) * SCALE)
    store_halves(k_s, mmw(x2, w["k"]))
    store_halves(v_s, mmw(x2, w["v"]) + vec[1:2])
    for ref in (q_s, k_s, v_s):
        zero_tail(ref, rows)

    def some(i, carry):
        units = [(c, i * UNROLL + k) for k in range(UNROLL) for c in range(2)]
        time_attend(units, group, count, q_s, k_s, v_s, o_s, p_s, l_s)
        return carry

    lax.fori_loop(0, VB // UNROLL, some, 0)
    z1 = x + mmw(split2(load_halves(o_s, rows)), w["o"]) + vec[2:3]
    z1_s[...] = z1
    h, _, _ = norm_fwd(z1, vec[3:4], vec[4:5])
    u = mmw(split2(h), w["up"]) + jnp.concatenate([vec[5:6], vec[6:7]], 1)
    u_s[...] = u
    z2 = h + mmw(split2(u * gelu_cdf(u)), w["down"]) + vec[7:8]
    z2_s[...] = z2
    return norm_fwd(z2, vec[8:9], vec[9:10])[0]


def embed_block(pieces, emb, place):
    return mmw(split2(pieces), emb) + place


TIME_W = ("q", "k", "v", "o", "up", "down")


def time_fwd_kernel(first, count, group, *refs):
    if first:
        x_ref, emb_ref, place_ref = refs[:3]
        refs = refs[3:]
    else:
        x_ref = refs[0]
        refs = refs[1:]
    w = {name: refs[i][...] for i, name in enumerate(TIME_W)}
    vec_ref, y_ref = refs[6:8]
    rows = count * VB
    if first:
        place = jnp.broadcast_to(place_ref[...], (count, VB, D)).reshape(rows, D)
        x = embed_block(x_ref[...].reshape(rows, 16), emb_ref[...], place)
    else:
        x = x_ref[...].reshape(rows, D)
    y = time_forward(x, w, vec_ref[...], count, group, refs[8:])
    y_ref[...] = y.reshape(count, VB, D)


def whole(shape):
    return pl.BlockSpec(shape, lambda i: (0,) * len(shape))


def params_spec():
    return pltpu.CompilerParams(vmem_limit_bytes=VMEM_LIMIT)


def pick(shape, index):
    return pl.BlockSpec((None,) + shape, lambda i: (index,) + (0,) * len(shape))


def weight_specs(squares, feed, layer):
    specs = [pick((D, D), k) for k in squares]
    if feed is not None:
        specs += [pick((D, FF), feed), pick((FF, D), 4 + feed)]
    return specs + [pick((24, D), layer)]


def weight_args(model, squares, feed):
    square, up, down, vecs = model
    return [square] * len(squares) + ([up, down] if feed is not None else []) + [vecs]


def flush(step, last, accs, mat_at, feeds, up_rows, g_mat, g_feed, sems):
    @pl.when(step == last)
    def _():
        copies = []

        def add(src, dst):
            copies.append(pltpu.make_async_copy(src, dst, sems.at[len(copies)]))

        for acc, at in zip(accs, mat_at):
            add(acc, g_mat.at[pl.ds(at, acc.shape[0])] if len(acc.shape) == 3 else g_mat.at[at])
        for up_acc, down_acc, feed_at in feeds:
            for k in range(D // up_rows):
                for half in range(2):
                    base = 2 * D * feed_at + (2 * k + half) * up_rows
                    add(up_acc.at[pl.ds(k * up_rows, up_rows), pl.ds(half * D, D)], g_feed.at[pl.ds(base, up_rows)])
            add(down_acc, g_feed.at[pl.ds(4 * FF + feed_at * FF, FF)])
        for copy in copies:
            copy.start()
        for copy in copies:
            copy.wait()


def pack_shapes():
    return [jax.ShapeDtypeStruct((NSQ, D, D), F32), jax.ShapeDtypeStruct((8 * FF, D), F32)]


def flush_count(mats, feeds, up_rows):
    return mats + feeds * (2 * D // up_rows + 1 if up_rows else 0)


def time_kept(count, group, nb):
    pad, rows = group * VB, count * VB
    shapes = [(2, pad, HALF)] * 4 + [(2, VB, group, 4 * group), (2, VB, group, HALF), (rows, D), (rows, FF), (rows, D)]
    specs = [pl.BlockSpec((None,) + s, lambda i, n=len(s): (i,) + (0,) * n) for s in shapes]
    return specs, [jax.ShapeDtypeStruct((nb,) + s, F32) for s in shapes]


def time_fwd(first, x, extra, model, layer, count):
    squares = [12 * layer + k for k in range(4)]
    group = 64 if count > 32 else 32
    nv = x.shape[1]
    width = x.shape[2]
    specs = [pl.BlockSpec((count, VB, width), lambda i: (0, i, 0))]
    if first:
        specs += [whole((16, D)), whole((count, 1, D))]
    kept_specs, kept_shapes = time_kept(count, group, nv // VB)
    out = pl.pallas_call(
        functools.partial(time_fwd_kernel, first, count, group),
        grid=(nv // VB,),
        in_specs=specs + weight_specs(squares, 2 * layer, layer),
        out_specs=[pl.BlockSpec((count, VB, D), lambda i: (0, i, 0))] + kept_specs,
        out_shape=[jax.ShapeDtypeStruct((count, nv, D), F32)] + kept_shapes,
        compiler_params=params_spec(),
        name="time_fwd",
    )(x, *extra, *weight_args(model, squares, 2 * layer))
    return out[0], out[1:]


def time_bwd_kernel(first, count, group, layer, up_rows, *refs):
    if first:
        x_ref, emb_ref, place_ref = refs[:3]
        refs = refs[3:]
    else:
        x_ref = refs[0]
        refs = refs[1:]
    dy_ref = refs[0]
    q_s, k_s, v_s, o_s, p_s, l_s, z1_s, u_s, z2_s = refs[1:10]
    w = {name: refs[10 + i][...] for i, name in enumerate(TIME_W)}
    vec_ref = refs[16]
    later = refs[17:21]
    g_mat, g_feed = refs[23:25]
    outs = refs[25:]
    n_out = 3 if first else 2
    tail = outs[1:n_out]
    accs = outs[n_out : n_out + 6]
    sems = outs[n_out + 6]
    g = dict(zip(TIME_W + ("rows",), tuple(accs) + (outs[0],)))
    do_s, dq_s, dk_s, dv_s = outs[n_out + 7 :]
    rows = count * VB
    step = pl.program_id(0)

    @pl.when(step == 0)
    def _():
        for ref in list(g.values()) + (list(tail) if first else []):
            ref[...] = jnp.zeros(ref.shape, F32)

    vec = vec_ref[...]
    if first:
        place = jnp.broadcast_to(place_ref[...], (count, VB, D)).reshape(rows, D)
        pieces = x_ref[...].reshape(rows, 16)
        x = embed_block(pieces, emb_ref[...], place)
    else:
        x = x_ref[...].reshape(rows, D)
    x2 = split2(x)
    mixed = load_halves(o_s, rows)
    h, unit1, inv1 = norm_fwd(z1_s[...], vec[3:4], vec[4:5])
    u = u_s[...]
    cdf = gelu_cdf(u)
    _, unit2, inv2 = norm_fwd(z2_s[...], vec[8:9], vec[9:10])
    dy = dy_ref[...].reshape(rows, D)
    g["rows"][8] += colsum(dy * unit2)
    g["rows"][9] += colsum(dy)
    dz2 = norm_bwd(dy, unit2, inv2, vec[8:9])
    g["rows"][7] += colsum(dz2)
    dz22 = split2(dz2)
    g["down"][...] += tn3(split2(u * cdf), dz22)
    du = mmwt(dz22, w["down"]) * gelu_slope(u, cdf)
    g["rows"][5] += colsum(du[:, :D])
    g["rows"][6] += colsum(du[:, D:])
    du2 = split2(du)
    g["up"][...] += tn3(split2(h), du2)
    dh = dz2 + mmwt(du2, w["up"])
    g["rows"][3] += colsum(dh * unit1)
    g["rows"][4] += colsum(dh)
    dz1 = norm_bwd(dh, unit1, inv1, vec[3:4])
    g["rows"][2] += colsum(dz1)
    dz12 = split2(dz1)
    g["o"][...] += tn3(split2(mixed), dz12)
    store_halves(do_s, mmwt(dz12, w["o"]))
    zero_tail(do_s, rows)

    def some(i, carry):
        units = [(c, i * UNROLL_BACK + k) for k in range(UNROLL_BACK) for c in range(2)]
        time_attend_back(units, group, count, q_s, k_s, v_s, o_s, p_s, l_s, do_s, dq_s, dk_s, dv_s)
        return carry

    lax.fori_loop(0, VB // UNROLL_BACK, some, 0)
    dq = load_halves(dq_s, rows) * SCALE
    g["rows"][0] += colsum(dq)
    dq2 = split2(dq)
    g["q"][...] += tn3(x2, dq2)
    dx = dz1 + mmwt(dq2, w["q"])
    dk2 = split2(load_halves(dk_s, rows))
    g["k"][...] += tn3(x2, dk2)
    dx = dx + mmwt(dk2, w["k"])
    dv = load_halves(dv_s, rows)
    g["rows"][1] += colsum(dv)
    dv2 = split2(dv)
    g["v"][...] += tn3(x2, dv2)
    dx = dx + mmwt(dv2, w["v"])
    if first:
        tail[0][...] += tn3(split2(pieces), split2(dx))
        tail[1][...] += dx
    else:
        tail[0][...] = dx.reshape(count, VB, D)
    flush(
        step, pl.num_programs(0) - 1, list(accs[:4]) + list(later[:2]), [12 * layer + k for k in (0, 1, 2, 3, 8, 11)],
        [(accs[4], accs[5], 2 * layer), (later[2], later[3], 2 * layer + 1)], up_rows, g_mat, g_feed, sems,
    )


def time_bwd(first, x, extra, dy, kept, model, layer, count, later, packs, up_rows):
    group = 64 if count > 32 else 32
    nv = x.shape[1]
    width = x.shape[2]
    pad = group * VB
    squares = [12 * layer + k for k in range(4)]
    block = pl.BlockSpec((count, VB, D), lambda i: (0, i, 0))
    specs = [pl.BlockSpec((count, VB, width), lambda i: (0, i, 0))]
    if first:
        specs += [whole((16, D)), whole((count, 1, D))]
    specs += [block] + time_kept(count, group, nv // VB)[0] + weight_specs(squares, 2 * layer, layer)
    specs += [whole((D, D)), whole((D, D)), whole((D, FF)), whole((FF, D))]
    grad_shapes = [(10, 8, D)] + ([(16, D), (count * VB, D)] if first else [])
    out_specs = [ANY] * 2 + [whole(s) for s in grad_shapes]
    out_shape = pack_shapes() + [jax.ShapeDtypeStruct(s, F32) for s in grad_shapes]
    if not first:
        out_specs.append(block)
        out_shape.append(jax.ShapeDtypeStruct((count, nv, D), F32))
    return pl.pallas_call(
        functools.partial(time_bwd_kernel, first, count, group, layer, up_rows),
        grid=(nv // VB,),
        in_specs=specs + [ANY] * 2,
        out_specs=out_specs,
        out_shape=out_shape,
        input_output_aliases={len(specs): 0, len(specs) + 1: 1},
        scratch_shapes=[pltpu.VMEM((D, D), F32)] * 4
        + [pltpu.VMEM((D, FF), F32), pltpu.VMEM((FF, D), F32), pltpu.SemaphoreType.DMA((flush_count(6, 2, up_rows),))]
        + [pltpu.VMEM((2, pad, HALF), F32)] * 4,
        compiler_params=params_spec(),
        name="time_bwd",
    )(x, *extra, dy, *kept, *weight_args(model, squares, 2 * layer), *later, *packs)

SB_ROWS = 64


def head_rows():
    sub = lax.broadcasted_iota(jnp.int32, (8, D), 0)
    lane = lax.broadcasted_iota(jnp.int32, (8, D), 1)
    return jnp.where(sub == lane // 32, 1.0, 0.0).astype(F32)


def spread_rows(x):
    wide = jnp.broadcast_to(x[:, None, :], (RPAD, HEADS, D)) * head_rows()[None]
    return wide.reshape(RPAD * HEADS, D)


def gather_rows(x):
    return jnp.sum(x.reshape(RPAD, HEADS, D) * head_rows()[None], 1)


PACK = 24


def pack_rows(x, last=None):
    last = jnp.zeros((1, HALF), F32) if last is None else last
    return jnp.concatenate([x[:ROUT, :HALF], x[:ROUT, HALF:], last, jnp.zeros((PACK - 2 * ROUT - 1, HALF), F32)], 0)


def unpack_rows(x):
    x = jnp.concatenate([x[:ROUT], x[ROUT : 2 * ROUT]], 1)
    return jnp.concatenate([x, jnp.zeros((RPAD - ROUT, D), F32)], 0)


def unpack_block(ref, sb):
    return jnp.concatenate([unpack_rows(ref[s]) for s in range(sb)], 0)


def pack_block(ref, x, sb):
    for s in range(sb):
        ref[s] = pack_rows(x[s * RPAD : (s + 1) * RPAD])


def valid_lane(rows):
    return lax.broadcasted_iota(jnp.int32, (rows, HALF), 1) < ROUT * HEADS


def router_reduce(x, op):
    for shift in (8, 16, 32, 64):
        x = op(x, pltpu.roll(x, shift, 1))
    return x


def merge_rows(y, pairs, vec):
    wide = y.reshape(pairs, 2, SB_ROWS, D)
    wide = jnp.concatenate([wide[:, 0].reshape(pairs * SB_ROWS, D), wide[:, 1].reshape(pairs * SB_ROWS, D)], 1)
    gain = jnp.concatenate([vec[0:1], vec[1:2]], 1)
    bias = jnp.concatenate([vec[2:3], vec[3:4]], 1)
    return norm_fwd(wide, gain, bias) + (gain,)


RECV_W = ("so", "rk", "rv", "rq", "ro", "up", "down")


def recv_buffer(o2, w, vec):
    buf2 = split2(mmw(o2, w["so"]) + vec[12:13])
    kb = mmw(buf2, w["rk"])
    vb = mmw(buf2, w["rv"]) + vec[14:15]
    segs = range(kb.shape[0] // RPAD)
    k = [split2(spread_rows(kb[s * RPAD : (s + 1) * RPAD])) for s in segs]
    v = [split2(spread_rows(vb[s * RPAD : (s + 1) * RPAD])) for s in segs]
    return buf2, k, v


def recv_forward(send, o_rows, w, vec):
    sb = send.shape[0] // SB_ROWS
    send2 = split2(send)
    o2 = split2(o_rows)
    buf2, k, v = recv_buffer(o2, w, vec)
    q = (mmw(send2, w["rq"]) + vec[13:14]) * SCALE
    segs = range(sb)
    ok = valid_lane(SB_ROWS)
    scores = [jnp.where(ok, nt3_narrow(split2(q[s * SB_ROWS : (s + 1) * SB_ROWS]), k[s]), negative) for s in segs]
    probs = [jnp.exp(sc - router_reduce(sc, jnp.maximum)) for sc in scores]
    probs = [p / router_reduce(p, jnp.add) for p in probs]
    mixed = jnp.concatenate([nn3_short(split2(p), v2) for p, v2 in zip(probs, v)], 0)
    z3 = send + mmw(split2(mixed), w["ro"]) + vec[15:16]
    g, unit3, inv3 = norm_fwd(z3, vec[16:17], vec[17:18])
    u = mmw(split2(g), w["up"]) + jnp.concatenate([vec[18:19], vec[19:20]], 1)
    cdf = gelu_cdf(u)
    z4 = g + mmw(split2(u * cdf), w["down"]) + vec[20:21]
    y, unit4, inv4 = norm_fwd(z4, vec[21:22], vec[22:23])
    kept = (send2, o2, buf2, mixed, g, unit3, inv3, u, cdf, unit4, inv4, q, k, v, probs)
    return y, kept, (q, mixed, jnp.concatenate(probs, 0), z3, u, z4)


def recv_restore(send, o_rows, w, vec, saved):
    q, mixed, p, z3, u, z4 = saved
    o2 = split2(o_rows)
    buf2, k, v = recv_buffer(o2, w, vec)
    g, unit3, inv3 = norm_fwd(z3, vec[16:17], vec[17:18])
    y, unit4, inv4 = norm_fwd(z4, vec[21:22], vec[22:23])
    probs = [p[s * SB_ROWS : (s + 1) * SB_ROWS] for s in range(send.shape[0] // SB_ROWS)]
    return y, (split2(send), o2, buf2, mixed, g, unit3, inv3, u, gelu_cdf(u), unit4, inv4, q, k, v, probs)


KEPT_WIDTHS = (D, D, HALF, D, FF, D)


def kept_specs(sb):
    return [pl.BlockSpec((sb * SB_ROWS, k), lambda i: (i, 0)) for k in KEPT_WIDTHS]


RECV_G = ("so", "rk", "rv", "rows")
LATER_WIDTHS = (D, D, FF, D)


def row_specs(sb, widths):
    return [pl.BlockSpec((sb * SB_ROWS, k), lambda i: (i, 0)) for k in widths]


def row_shapes(n, widths):
    return [jax.ShapeDtypeStruct((n * SB_ROWS, k), F32) for k in widths]


def put(refs, values):
    for ref, value in zip(refs, values):
        ref[...] = value


def recv_backward(dy, kept, w, vec, g):
    send2, o2, buf2, mixed, gg, unit3, inv3, u, cdf, unit4, inv4, q, k, v, probs = kept
    sb = dy.shape[0] // SB_ROWS
    rows = g["rows"]
    rows[9] += colsum(dy * unit4)
    rows[10] += colsum(dy)
    dz4 = norm_bwd(dy, unit4, inv4, vec[21:22])
    rows[8] += colsum(dz4)
    dz42 = split2(dz4)
    du = mmwt(dz42, w["down"]) * gelu_slope(u, cdf)
    rows[6] += colsum(du[:, :D])
    rows[7] += colsum(du[:, D:])
    du2 = split2(du)
    dg = dz4 + mmwt(du2, w["up"])
    rows[4] += colsum(dg * unit3)
    rows[5] += colsum(dg)
    dz3 = norm_bwd(dg, unit3, inv3, vec[16:17])
    rows[3] += colsum(dz3)
    dz32 = split2(dz3)
    do = mmwt(dz32, w["ro"])
    segs = range(sb)
    d = [split2(do[s * SB_ROWS : (s + 1) * SB_ROWS]) for s in segs]
    dp = [nt3_narrow(d2, v2) for d2, v2 in zip(d, v)]
    ds = [split2(p * (x - router_reduce(p * x, jnp.add))) for p, x in zip(probs, dp)]
    dq = jnp.concatenate([nn3_short(s2, k2) for s2, k2 in zip(ds, k)], 0) * SCALE
    q = [split2(q[s * SB_ROWS : (s + 1) * SB_ROWS]) for s in segs]
    dk = jnp.concatenate([gather_rows(tn3_short(s2, q2)) for s2, q2 in zip(ds, q)], 0)
    dv = jnp.concatenate([gather_rows(tn3_short(split2(p), d2)) for p, d2 in zip(probs, d)], 0)
    rows[1] += colsum(dq)
    dq2 = split2(dq)
    dsend = dz3 + mmwt(dq2, w["rq"])
    dk2 = split2(dk)
    dv2 = split2(dv)
    rows[2] += colsum(dv)
    g["rk"][...] += tn3(buf2, dk2)
    g["rv"][...] += tn3(buf2, dv2)
    dbuf = mmwt(dk2, w["rk"]) + mmwt(dv2, w["rv"])
    rows[0] += colsum(dbuf)
    dbuf2 = split2(dbuf)
    g["so"][...] += tn3(o2, dbuf2)
    return dsend, mmwt(dbuf2, w["so"]), (dq, dz3, du, dz4)


def recv_squares(layer):
    return [12 * layer + k for k in (7, 9, 10, 8, 11)]


def seg_block(sb, rows=SB_ROWS, width=D):
    return pl.BlockSpec((sb, rows, width), lambda i: (i, 0, 0))


MERGE = pl.BlockSpec((2, D, D), lambda i: (12, 0, 0))


def pack_spec(sb):
    return seg_block(sb, PACK, HALF)


def recv_fwd_kernel(sb, send_ref, o_ref, *refs):
    w = {n: refs[i][...] for i, n in enumerate(RECV_W)}
    vec_ref, mvec_ref, mw_ref, out_ref = refs[7:11]
    y, _, saved = recv_forward(send_ref[...].reshape(sb * SB_ROWS, D), unpack_block(o_ref, sb), w, vec_ref[...])
    for ref, x in zip(refs[11:], saved):
        ref[...] = x
    mvec = mvec_ref[...]
    wide, _, _, _ = merge_rows(y, sb // 2, mvec)
    out_ref[...] = (mmw(split2(wide), mw_ref[...].reshape(2 * D, D)) + mvec[4:5]).reshape(sb // 2, SB_ROWS, D)


def recv_fwd(send, o, model, mvec, sb):
    squares = recv_squares(0)
    n = send.shape[0]
    return pl.pallas_call(
        functools.partial(recv_fwd_kernel, sb),
        grid=(n // sb,),
        in_specs=[seg_block(sb), pack_spec(sb)] + weight_specs(squares, 1, 0) + [whole((8, D)), MERGE],
        out_specs=[seg_block(sb // 2)] + kept_specs(sb),
        out_shape=[jax.ShapeDtypeStruct((n // 2, SB_ROWS, D), F32)]
        + [jax.ShapeDtypeStruct((n * SB_ROWS, k), F32) for k in KEPT_WIDTHS],
        compiler_params=params_spec(),
        name="recv_fwd",
    )(send, o, *weight_args(model, squares, 1), mvec, model[0])


def recv_bwd_kernel(sb, send_ref, o_ref, dx_ref, *refs):
    saved = [ref[...] for ref in refs[:6]]
    refs = refs[6:]
    w = {n: refs[i][...] for i, n in enumerate(RECV_W)}
    vec_ref, mvec_ref, mw_ref = refs[7:10]
    g_mat, dsend_ref, do_ref, rows_ref, dmv_ref = refs[11:16]
    later, accs, dmw_ref, sems = refs[16:20], refs[20:23], refs[23], refs[24]
    g = dict(zip(RECV_G, tuple(accs) + (rows_ref,)))

    @pl.when(pl.program_id(0) == 0)
    def _():
        for ref in list(g.values()) + [dmw_ref, dmv_ref]:
            ref[...] = jnp.zeros(ref.shape, F32)

    vec = vec_ref[...]
    y, kept = recv_restore(send_ref[...].reshape(sb * SB_ROWS, D), unpack_block(o_ref, sb), w, vec, saved)
    pairs = sb // 2
    wide, unit, inv, gain = merge_rows(y, pairs, mvec_ref[...])
    dx = dx_ref[...].reshape(pairs * SB_ROWS, D)
    dmv_ref[4] += colsum(dx)
    dx2 = split2(dx)
    dmw_ref[...] += tn3(split2(wide), dx2).reshape(2, D, D)
    dn = mmwt(dx2, mw_ref[...].reshape(2 * D, D))
    part = colsum(dn * unit)
    dmv_ref[0] += part[:, :D]
    dmv_ref[1] += part[:, D:]
    part = colsum(dn)
    dmv_ref[2] += part[:, :D]
    dmv_ref[3] += part[:, D:]
    dwide = norm_bwd(dn, unit, inv, gain)
    left = dwide[:, :D].reshape(pairs, 1, SB_ROWS, D)
    right = dwide[:, D:].reshape(pairs, 1, SB_ROWS, D)
    dy = jnp.concatenate([left, right], 1).reshape(sb * SB_ROWS, D)
    dsend, do, grads = recv_backward(dy, kept, w, vec, g)
    put(later, grads)
    dsend_ref[...] = dsend.reshape(sb, SB_ROWS, D)
    pack_block(do_ref, do, sb)
    recv_flush(accs, [(dmw_ref, 24)], 0, g_mat, sems)


RECV_ACC = [pltpu.VMEM((D, D), F32)] * 3


def recv_flush(accs, more, layer, g_mat, sems):
    flush(
        pl.program_id(0), pl.num_programs(0) - 1, list(accs) + [m for m, _ in more],
        recv_squares(layer)[:3] + [at for _, at in more], [], 0, g_mat, None, sems,
    )


def recv_bwd(send, o, dx, kept, model, mvec, sb, g_mat):
    n = send.shape[0]
    squares = recv_squares(0)
    shapes = [(11, 8, D), (5, 8, D)]
    specs = [seg_block(sb), pack_spec(sb), seg_block(sb // 2)] + kept_specs(sb)
    specs += weight_specs(squares, 1, 0) + [whole((8, D)), MERGE]
    return pl.pallas_call(
        functools.partial(recv_bwd_kernel, sb),
        grid=(n // sb,),
        in_specs=specs + [ANY],
        out_specs=[ANY, seg_block(sb), pack_spec(sb)] + [whole(s) for s in shapes] + row_specs(sb, LATER_WIDTHS),
        out_shape=pack_shapes()[:1]
        + [jax.ShapeDtypeStruct((n, SB_ROWS, D), F32), jax.ShapeDtypeStruct(o.shape, F32)]
        + [jax.ShapeDtypeStruct(s, F32) for s in shapes]
        + row_shapes(n, LATER_WIDTHS),
        input_output_aliases={len(specs): 0},
        scratch_shapes=RECV_ACC + [pltpu.VMEM((2, D, D), F32), pltpu.SemaphoreType.DMA((4,))],
        compiler_params=params_spec(),
        name="recv_bwd",
    )(send, o, dx, *kept, *weight_args(model, squares, 1), mvec, model[0], g_mat)


def tail_kernel(sb, send_ref, o_ref, tgt_ref, kept_ref, scale_ref, mean_ref, *refs):
    w = {n: refs[i][...] for i, n in enumerate(RECV_W)}
    vec_ref, head_ref, g_mat, g_feed, dsend_ref, do_ref, rows_ref, dhead_ref = refs[7:15]
    saved, later, accs, sems = refs[15:18], refs[18:22], refs[22:25], refs[25]
    g = dict(zip(RECV_G, tuple(accs) + (rows_ref,)))

    @pl.when(pl.program_id(0) == 0)
    def _():
        for ref in list(g.values()) + [dhead_ref]:
            ref[...] = jnp.zeros(ref.shape, F32)

    vec = vec_ref[...]
    rows = sb * SB_ROWS
    y, kept, (_, mixed, _, z3, u, _) = recv_forward(
        send_ref[...].reshape(rows, D), unpack_block(o_ref, sb), w, vec
    )
    head = head_ref[...]
    y2 = split2(y)
    scale = jnp.broadcast_to(scale_ref[...][None], (sb, SB_ROWS, PPAD)).reshape(rows, PPAD)
    mean = jnp.broadcast_to(mean_ref[...][None], (sb, SB_ROWS, PPAD)).reshape(rows, PPAD)
    misfit = mmwt(y2, head) * scale + mean - tgt_ref[...].reshape(rows, PPAD)
    put(saved, (mixed, z3, u))
    dpred = kept_ref[...].reshape(rows, PPAD) * misfit * scale
    dpred2 = split2(dpred)
    dhead_ref[...] += tn3(dpred2, y2)
    dy = mmw(dpred2, head)
    dsend, do, grads = recv_backward(dy, kept, w, vec, g)
    put(later, grads)
    dsend_ref[...] = dsend.reshape(sb, SB_ROWS, D)
    pack_block(do_ref, do, sb)
    recv_flush(accs, [], 1, g_mat, sems)


def tail(send, o, tgt, kept, scale, mean, model, head, sb):
    n = send.shape[0]
    squares = recv_squares(1)
    shapes = [(11, 8, D), (PPAD, D)]
    return pl.pallas_call(
        functools.partial(tail_kernel, sb),
        grid=(n // sb,),
        in_specs=[seg_block(sb), pack_spec(sb), seg_block(sb, SB_ROWS, PPAD), seg_block(sb, SB_ROWS, PPAD)]
        + [whole((SB_ROWS, PPAD))] * 2
        + weight_specs(squares, 3, 1)
        + [whole((PPAD, D))],
        out_specs=[ANY] * 2 + [seg_block(sb), pack_spec(sb)] + [whole(s) for s in shapes]
        + row_specs(sb, (D, D, FF) + LATER_WIDTHS),
        out_shape=pack_shapes()
        + [jax.ShapeDtypeStruct((n, SB_ROWS, D), F32), jax.ShapeDtypeStruct(o.shape, F32)]
        + [jax.ShapeDtypeStruct(s, F32) for s in shapes]
        + row_shapes(n, (D, D, FF) + LATER_WIDTHS),
        scratch_shapes=RECV_ACC + [pltpu.SemaphoreType.DMA((3,))],
        compiler_params=params_spec(),
        name="tail",
    )(send, o, tgt, kept, scale, mean, *weight_args(model, squares, 3), head)


SEND_W = ("sq", "sk", "sv")


def send_project(dim2, r_rows, w, vec):
    r2 = split2(r_rows)
    sb = r_rows.shape[0] // RPAD
    k = mmw(dim2, w["sk"])
    v = mmw(dim2, w["sv"]) + vec[11:12]
    q = (mmw(r2, w["sq"]) + vec[10:11]) * SCALE
    k = [split2(k[s * SB_ROWS : (s + 1) * SB_ROWS]) for s in range(sb)]
    v = [split2(v[s * SB_ROWS : (s + 1) * SB_ROWS]) for s in range(sb)]
    q = [split2(spread_rows(q[s * RPAD : (s + 1) * RPAD])) for s in range(sb)]
    return r2, k, v, q


def send_fwd_kernel(sb, dim_ref, r_ref, here_ref, *refs):
    w = {n: refs[i][...] for i, n in enumerate(SEND_W)}
    vec_ref, o_ref = refs[3:]
    dim2 = split2(dim_ref[...].reshape(sb * SB_ROWS, D))
    _, k, v, q = send_project(dim2, r_ref[...].reshape(sb * RPAD, D), w, vec_ref[...])
    here = here_ref[...] > 0.5
    scores = [jnp.where(here, nt3_narrow(k2, q2), negative) for k2, q2 in zip(k, q)]
    tops = [jnp.max(sc, 0, keepdims=True) for sc in scores]
    probs = [jnp.where(here, jnp.exp(sc - top), 0.0) for sc, top in zip(scores, tops)]
    totals = [jnp.sum(p, 0, keepdims=True) for p in probs]
    safe = [jnp.where(t > 0.0, t, 1.0) for t in totals]
    mixed = [gather_rows(tn3_short(split2(p / t), v2)) for p, t, v2 in zip(probs, safe, v)]
    for s in range(sb):
        lse = jnp.where(totals[s] > 0.0, tops[s] + jnp.log(safe[s]), negative)
        o_ref[s] = pack_rows(mixed[s], lse)


def send_squares(layer):
    return [12 * layer + k for k in (4, 5, 6)]


def send_fwd(dim, routers, here, model, layer, sb, npad):
    squares = send_squares(layer)
    n = dim.shape[0]
    return pl.pallas_call(
        functools.partial(send_fwd_kernel, sb),
        grid=(n // sb,),
        in_specs=[seg_block(sb), seg_block(sb, RPAD), whole((SB_ROWS, HALF))]
        + weight_specs(squares, None, layer),
        out_specs=pack_spec(sb),
        out_shape=jax.ShapeDtypeStruct((npad, PACK, HALF), F32),
        compiler_params=params_spec(),
        name="send_fwd",
    )(dim, routers, here, *weight_args(model, squares, None))


def send_bwd_kernel(sb, layer, dim_ref, dpart_ref, r_ref, o_ref, do_ref, here_ref, *refs):
    w = {n: refs[i][...] for i, n in enumerate(SEND_W)}
    vec_ref = refs[3]
    g_mat, ddim_ref, dr_ref, rows = refs[5:9]
    dsq_ref, dsk_ref, dsv_ref, sems = refs[9:13]

    @pl.when(pl.program_id(0) == 0)
    def _():
        for ref in (dsq_ref, dsk_ref, dsv_ref, rows):
            ref[...] = jnp.zeros(ref.shape, F32)

    dim2 = split2(dim_ref[...].reshape(sb * SB_ROWS, D))
    r2, k, v, q = send_project(dim2, r_ref[...].reshape(sb * RPAD, D), w, vec_ref[...])
    here = (here_ref[...] > 0.5) & valid_lane(SB_ROWS)
    segs = range(sb)
    scores = [nt3_narrow(k2, q2) for k2, q2 in zip(k, q)]
    probs = [jnp.where(here, jnp.exp(scores[s] - o_ref[s][2 * ROUT : 2 * ROUT + 1]), 0.0) for s in segs]
    dwide = [spread_rows(unpack_rows(do_ref[s])) for s in segs]
    owide = [
        jnp.broadcast_to(unpack_rows(o_ref[s])[:, None, :], (RPAD, HEADS, D)).reshape(RPAD * HEADS, D) for s in segs
    ]
    e = [split2(a * b) for a, b in zip(dwide, owide)]
    d = [split2(a) for a in dwide]
    one_row = jnp.ones((8, D), BF)
    means = [(dots(one_row, e2[0], 1, 1) + dots(one_row, e2[1], 1, 1))[0:1] for e2 in e]
    dp = [nt3_narrow(v2, d2) for v2, d2 in zip(v, d)]
    ds = [split2(p * (x - mean)) for p, x, mean in zip(probs, dp, means)]
    dk = jnp.concatenate([nn3_short(s2, q2) for s2, q2 in zip(ds, q)], 0)
    dv = jnp.concatenate([nn3_short(split2(p), d2) for p, d2 in zip(probs, d)], 0)
    dq = jnp.concatenate([gather_rows(tn3_short(s2, k2)) for s2, k2 in zip(ds, k)], 0) * SCALE
    dk2 = split2(dk)
    dv2 = split2(dv)
    rows[1] += colsum(dv)
    dsk_ref[...] += tn3(dim2, dk2)
    dsv_ref[...] += tn3(dim2, dv2)
    out = dpart_ref[...].reshape(sb * SB_ROWS, D) + mmwt(dk2, w["sk"]) + mmwt(dv2, w["sv"])
    ddim_ref[...] = out.reshape(sb, SB_ROWS, D)
    rows[0] += colsum(dq)
    dq2 = split2(dq)
    dsq_ref[...] += tn3(r2, dq2)
    dr_ref[...] = mmwt(dq2, w["sq"]).reshape(sb, RPAD, D)
    flush(
        pl.program_id(0), pl.num_programs(0) - 1, [dsq_ref, dsk_ref, dsv_ref], send_squares(layer), [], 0, g_mat, None,
        sems,
    )


def send_bwd(dim, dpart, routers, o, do, here, model, layer, sb, g_mat):
    n = dim.shape[0]
    squares = send_squares(layer)
    specs = [seg_block(sb), seg_block(sb), seg_block(sb, RPAD), pack_spec(sb), pack_spec(sb), whole((SB_ROWS, HALF))]
    specs += weight_specs(squares, None, layer)
    return pl.pallas_call(
        functools.partial(send_bwd_kernel, sb, layer),
        grid=(n // sb,),
        in_specs=specs + [ANY],
        out_specs=[ANY, seg_block(sb), seg_block(sb, RPAD), whole((2, 8, D))],
        out_shape=pack_shapes()[:1]
        + [jax.ShapeDtypeStruct((n, SB_ROWS, D), F32), jax.ShapeDtypeStruct((n, RPAD, D), F32)]
        + [jax.ShapeDtypeStruct((2, 8, D), F32)],
        input_output_aliases={len(specs): 0},
        scratch_shapes=[pltpu.VMEM((D, D), F32)] * 3 + [pltpu.SemaphoreType.DMA((3,))],
        compiler_params=params_spec(),
        name="send_bwd",
    )(dim, dpart, routers, o, do, here, *weight_args(model, squares, None), g_mat)

MESH = pl.DeviceIdType.MESH


def grid_sizes():
    nf = lax.axis_size("fsdp")
    nx = 1
    while 2 * nx * nx < nf:
        nx *= 2
    return lax.axis_size("dp") // 2, nf // nx, nx


class Place:
    def __init__(self):
        self.ny, self.nz, self.nx = grid_sizes()
        dp, fs = lax.axis_index("dp"), lax.axis_index("fsdp")
        self.core, self.y = lax.rem(dp, 2), lax.div(dp, 2)
        self.x, self.z = lax.rem(fs, self.nx), lax.div(fs, self.nx)

    def at(self, y=None, core=None, z=None, x=None):
        y = self.y if y is None else y
        core = self.core if core is None else core
        z = self.z if z is None else z
        x = self.x if x is None else x
        return (y * 2 + core, z * self.nx + x)

    def other(self):
        return 1 - self.core

    def next_x(self, k):
        return lax.rem(self.x + k, self.nx)

    def next_y(self, k):
        return lax.rem(self.y + k, self.ny)

    def next_z(self, k):
        return lax.rem(self.z + k, self.nz)

    def neighbours(self):
        out = [self.at(core=self.other())]
        out += [self.at(x=self.next_x(k)) for k in range(1, self.nx)]
        out += [self.at(y=self.next_y(k)) for k in range(1, self.ny)]
        out += [self.at(z=self.next_z(k)) for k in range(1, self.nz)]
        return out


def greet(devices):
    barrier = pltpu.get_barrier_semaphore()
    for device in devices:
        pl.semaphore_signal(barrier, inc=1, device_id=device, device_id_type=MESH)
    pl.semaphore_wait(barrier, len(devices))


def remote(src, dst, send, recv, device):
    return pltpu.make_async_remote_copy(
        src_ref=src, dst_ref=dst, send_sem=send, recv_sem=recv, device_id=device, device_id_type=MESH
    )


def gather_kernel(n, *refs):
    shards, outs = refs[:n], refs[n : 2 * n]
    send, recv, local = refs[2 * n :]
    me = Place()
    y, c, z, x = me.y, me.core, me.z, me.x
    m = me.nx
    greet(me.neighbours())
    slot = [0]

    def push(src, dst, device):
        copy = remote(src, dst, send.at[slot[0]], recv.at[slot[0]], device)
        slot[0] += 1
        copy.start()
        return copy

    def finish(copies):
        for copy in copies:
            copy.wait()

    own = [pltpu.make_async_copy(shards[j], outs[j].at[y, c, z, x], local.at[j]) for j in range(n)]
    for copy in own:
        copy.start()

    def along_z(j):
        return [push(shards[j], outs[j].at[y, c, z, x], me.at(z=me.next_z(k))) for k in range(1, me.nz)]

    first = along_z(0)
    finish(own)
    base = slot[0]

    def rest(by_core):
        slot[0] = base
        sibling = me.at(core=1 - by_core)
        shared = []

        def second(j):
            piece = outs[j].at[y, by_core, :, x]
            out = []
            for k in range(1, m):
                out.append(push(piece, piece, me.at(x=me.next_x(k)) if by_core == 0 else me.at(y=me.next_y(k))))
            shared.append(push(piece, piece, sibling))
            return out

        def third(j):
            wide = outs[j].at[y, by_core] if by_core == 0 else outs[j].at[:, by_core, :, x]
            out = []
            for k in range(1, m):
                out.append(push(wide, wide, me.at(y=me.next_y(k)) if by_core == 0 else me.at(x=me.next_x(k))))
            for k in range(1, m):
                piece = outs[j].at[y, by_core, :, me.next_x(k)] if by_core == 0 else outs[j].at[me.next_y(k), by_core, :, x]
                shared.append(push(piece, piece, sibling))
            return out

        def fourth(j):
            for k in range(1, m):
                wide = outs[j].at[me.next_y(k), by_core] if by_core == 0 else outs[j].at[:, by_core, :, me.next_x(k)]
                shared.append(push(wide, wide, sibling))

        one, two, three = {0: first}, {}, {}
        for t in range(n + 2):
            if t < n:
                finish(one[t])
                if t + 1 < n:
                    one[t + 1] = along_z(t + 1)
            if 0 < t <= n:
                finish(two[t - 1])
            if t < n:
                two[t] = second(t)
            if t > 1:
                finish(three[t - 2])
            if 0 < t <= n:
                three[t - 1] = third(t - 1)
            if t > 1:
                fourth(t - 2)
        finish(shared)

    for by_core in (0, 1):
        pl.when(c == by_core)(functools.partial(rest, by_core))


def gather_all(shards):
    ny, nz, nx = grid_sizes()
    n = len(shards)
    count = n * ((nz - 1) + (nx - 1) + 1 + (nx - 1) * 3)
    return pl.pallas_call(
        functools.partial(gather_kernel, n),
        in_specs=[ANY] * n,
        out_specs=[ANY] * n,
        out_shape=[jax.ShapeDtypeStruct((ny, 2, nz, nx) + s.shape, s.dtype) for s in shards],
        scratch_shapes=[pltpu.SemaphoreType.DMA((count,)), pltpu.SemaphoreType.DMA((count,)), pltpu.SemaphoreType.DMA((n,))],
        compiler_params=pltpu.CompilerParams(collective_id=0, has_side_effects=True, vmem_limit_bytes=VMEM_LIMIT),
        name="gather_all",
    )(*shards)


def row_chunks(rows):
    count = max(1, rows // 40)
    if rows % 8:
        count = 1
    cuts = [rows // 8 * k // count * 8 for k in range(count)] + [rows]
    return [(a, b - a) for a, b in zip(cuts, cuts[1:])]


def scatter_kernel(shapes, *refs):
    n = len(shapes)
    chunks = [(j, a, b) for j, s in enumerate(shapes) for a, b in row_chunks(s[0])]
    total = len(chunks)
    grads, tile_ref = refs[:n], refs[n]
    outs, stat_ref = refs[n + 1 : 2 * n + 1], refs[2 * n + 1]
    bufs = refs[2 * n + 2 :]
    acc, r1, r2, r3, r4 = (bufs[i * total : (i + 1) * total] for i in range(5))
    tp, tz, send, recv, local = bufs[5 * total :]
    me = Place()
    y, c, z, x = me.y, me.core, me.z, me.x
    ny, nz, nx, m = me.ny, me.nz, me.nx, me.nx
    plane = plane_peers(me)
    greet([p for p, _ in plane] + [me.at(z=me.next_z(k)) for k in range(1, nz)])
    slot = [0]

    def push(src, dst, device):
        copy = remote(src, dst, send.at[slot[0]], recv.at[slot[0]], device)
        slot[0] += 1
        copy.start()
        return copy

    def finish(copies):
        for copy in copies:
            copy.wait()

    def rest(by_core):
        slot[0] = 0
        sibling = me.at(core=1 - by_core)

        def one(i):
            j, a, b = chunks[i]
            out = []
            for k in range(nx):
                out.append(push(grads[j].at[:, 1 - by_core, :, k, pl.ds(a, b)], r1[i].at[:, k], sibling))
                copy = pltpu.make_async_copy(grads[j].at[:, by_core, :, k, pl.ds(a, b)], acc[i].at[:, k], local.at[i * nx + k])
                copy.start()
                out.append(copy)
            return out

        def add1(i):
            def body(k, carry):
                at = (lax.div(k, nx * nz), lax.rem(lax.div(k, nz), nx), lax.rem(k, nz))
                acc[i][at] = acc[i][at] + r1[i][at]
                return carry

            lax.fori_loop(0, ny * nx * nz, body, 0)

        def two(i):
            if by_core == 0:
                return [push(acc[i].at[:, me.next_x(k)], r2[i].at[k - 1], me.at(x=me.next_x(k))) for k in range(1, m)]
            return [push(acc[i].at[me.next_y(k)], r2[i].at[k - 1], me.at(y=me.next_y(k))) for k in range(1, m)]

        def add2(i):
            def body(k, carry):
                a, b = lax.div(k, nz), lax.rem(k, nz)
                at = (a, x, b) if by_core == 0 else (y, a, b)
                value = acc[i][at]
                for q in range(m - 1):
                    value = value + r2[i][q, a, b]
                acc[i][at] = value
                return carry

            lax.fori_loop(0, m * nz, body, 0)

        def three(i):
            if by_core == 0:
                return [push(acc[i].at[me.next_y(k), x], r3[i].at[k - 1], me.at(y=me.next_y(k))) for k in range(1, m)]
            return [push(acc[i].at[y, me.next_x(k)], r3[i].at[k - 1], me.at(x=me.next_x(k))) for k in range(1, m)]

        def add3(i):
            def body(k, carry):
                value = acc[i][y, x, k]
                for q in range(m - 1):
                    value = value + r3[i][q, k]
                acc[i][y, x, k] = value
                return carry

            lax.fori_loop(0, nz, body, 0)

        def four(i):
            return [push(acc[i].at[y, x, me.next_z(k)], r4[i].at[k - 1], me.at(z=me.next_z(k))) for k in range(1, nz)]

        def end(i):
            j, a, b = chunks[i]
            value = acc[i][y, x, z]
            for k in range(nz - 1):
                value = value + r4[i][k]
            outs[j][a : a + b] = value
            sq = colsum_any(value * value)
            return sq[:, :HALF] + sq[:, HALF:]

        squares = jnp.zeros((8, HALF), F32)
        ahead = 3
        p1, p2, p3, p4 = {i: one(i) for i in range(min(ahead, total))}, {}, {}, {}
        for t in range(total + 3):
            if t < total:
                finish(p1[t])
                if t + ahead < total:
                    p1[t + ahead] = one(t + ahead)
                add1(t)
                p2[t] = two(t)
            if 0 <= t - 1 < total:
                finish(p2[t - 1])
                add2(t - 1)
                p3[t - 1] = three(t - 1)
            if 0 <= t - 2 < total:
                finish(p3[t - 2])
                add3(t - 2)
                p4[t - 2] = four(t - 2)
            if 0 <= t - 3 < total:
                finish(p4[t - 3])
                squares = squares + end(t - 3)
        tp[(y * 2 + by_core) * nx + x] = jnp.concatenate([squares, tile_ref[...]], 0)

    for by_core in (0, 1):
        pl.when(c == by_core)(functools.partial(rest, by_core))

    slot[0] = total * (nx + 2 * (m - 1) + nz - 1)
    mine = tp.at[(y * 2 + c) * nx + x]
    finish([push(mine, mine, p) for p, _ in plane])
    tz[z] = functools.reduce(jnp.add, [tp[k] for k in range(2 * ny * nx)])
    finish([push(tz.at[z], tz.at[z], me.at(z=me.next_z(k))) for k in range(1, nz)])
    stat_ref[...] = functools.reduce(jnp.add, [tz[k] for k in range(nz)])


def plane_peers(me):
    out = []
    for k in range(1, 2 * me.ny * me.nx):
        dc, dy, dx = k % 2, k // 2 % me.ny, k // (2 * me.ny)
        out.append((me.at(core=lax.rem(me.core + dc, 2), y=lax.rem(me.y + dy, me.ny), x=lax.rem(me.x + dx, me.nx)), k))
    return out


def colsum_any(x):
    rows = x.shape[0]
    even = rows // 8 * 8
    out = colsum(x[:even]) if even else jnp.zeros((8, x.shape[1]), F32)
    if rows > even:
        out = out + jnp.pad(x[even:], ((0, 8 - rows + even), (0, 0)))
    return out


def scatter_sum(grads, tile):
    ny, nz, nx = grid_sizes()
    n = len(grads)
    shapes = [g.shape[-2:] for g in grads]
    pieces = [(b, s[1]) for s in shapes for _, b in row_chunks(s[0])]
    total = len(pieces)
    count = total * (nx + (nx - 1) * 2 + nz - 1) + 2 * ny * nx - 1 + nz - 1

    def buffers(*lead):
        return [pltpu.VMEM(lead + s, F32) for s in pieces]

    return pl.pallas_call(
        functools.partial(scatter_kernel, shapes),
        in_specs=[ANY] * n + [INVMEM],
        out_specs=[INVMEM] * (n + 1),
        out_shape=[jax.ShapeDtypeStruct(s, F32) for s in shapes] + [jax.ShapeDtypeStruct((16, HALF), F32)],
        scratch_shapes=buffers(ny, nx, nz)
        + buffers(ny, nx, nz)
        + buffers(nx - 1, nx, nz)
        + buffers(nx - 1, nz)
        + buffers(nz - 1)
        + [pltpu.VMEM((2 * ny * nx, 16, HALF), F32), pltpu.VMEM((nz, 16, HALF), F32)]
        + [pltpu.SemaphoreType.DMA((count,)), pltpu.SemaphoreType.DMA((count,)), pltpu.SemaphoreType.DMA((total * nx,))],
        compiler_params=pltpu.CompilerParams(collective_id=1, has_side_effects=True, vmem_limit_bytes=VMEM_LIMIT),
        name="scatter_sum",
    )(*grads, tile)


def group_part(ref, who, per):
    return ref.at[pl.ds(pl.multiple_of(who * per, per), per)]


def group_out(per, in_ref, got, send, recv, local):
    nf = lax.axis_size("fsdp")
    dp, f = lax.axis_index("dp"), lax.axis_index("fsdp")
    copies = [pltpu.make_async_copy(group_part(in_ref, f, per), got.at[f], local)]
    for k in range(1, nf):
        p = lax.rem(f + k, nf)
        copies.append(remote(group_part(in_ref, p, per), got.at[f], send.at[k - 1], recv.at[k - 1], (dp, p)))
    return copies


def group_back(per, result, out_ref, send, recv, local):
    nf = lax.axis_size("fsdp")
    dp, f = lax.axis_index("dp"), lax.axis_index("fsdp")
    copies = [pltpu.make_async_copy(result, group_part(out_ref, f, per), local)]
    for k in range(1, nf):
        p = lax.rem(f + k, nf)
        copies.append(remote(result, group_part(out_ref, f, per), send.at[nf - 2 + k], recv.at[nf - 2 + k], (dp, p)))
    return copies


def greet_group():
    nf = lax.axis_size("fsdp")
    dp, f = lax.axis_index("dp"), lax.axis_index("fsdp")
    greet([(dp, lax.rem(f + k, nf)) for k in range(1, nf)])


def start_all(copies):
    for copy in copies:
        copy.start()


def wait_all(copies):
    for copy in copies:
        copy.wait()


def stats_kernel(per, in_ref, out_ref, got, result, send, recv, local):
    nf = lax.axis_size("fsdp")
    greet_group()
    copies = group_out(per, in_ref, got, send, recv, local)
    start_all(copies)
    wait_all(copies)
    row = lax.broadcasted_iota(jnp.int32, (PACK, HALF), 0)
    lane = lax.broadcasted_iota(jnp.int32, (PACK, HALF), 1)
    router = jnp.where(row < ROUT, row, row - ROUT)
    chosen = (lane // 8 == router) & (row < 2 * ROUT)
    src = lax.broadcasted_iota(jnp.int32, (HALF, D), 0)
    dst = lax.broadcasted_iota(jnp.int32, (HALF, D), 1)
    widen = jnp.where(src % 8 == dst // 32, 1.0, 0.0).astype(BF)

    def one(s, carry):
        lse = [got[d, s, 2 * ROUT : 2 * ROUT + 1, :] for d in range(nf)]
        top = functools.reduce(jnp.maximum, lse)
        total = top + jnp.log(functools.reduce(jnp.add, [jnp.exp(l - top) for l in lse]))
        out = jnp.where(row == 2 * ROUT, total, 0.0)
        share = jnp.concatenate([jnp.where(chosen, jnp.exp(l - total), 0.0) for l in lse], 0)
        wide = mmw(split2(share), widen)
        for d in range(nf):
            w = wide[d * PACK : (d + 1) * PACK]
            w = jnp.where(row < ROUT, w[:, :HALF], w[:, HALF:])
            out = out + jnp.where(row < 2 * ROUT, w * got[d, s], 0.0)
        result[s] = out
        return carry

    lax.fori_loop(0, per, one, 0)
    copies = group_back(per, result, out_ref, send, recv, local)
    start_all(copies)
    wait_all(copies)


def sum_kernel(per, turn, in_ref, x_ref, mixed_ref, z_ref, u_ref, dq_ref, dz3_ref, du_ref, dz4_ref, vec_ref, *refs):
    out_ref, rq, ro, up, down, got, result, send, recv, local = refs
    step = pl.program_id(0)

    @pl.when(step == 0)
    def _():
        greet_group()
        start_all(group_out(per, in_ref, got, send, recv, local))
        for ref in (rq, ro, up, down):
            ref[...] = jnp.zeros(ref.shape, F32)

    @pl.when(step == turn)
    def _():
        wait_all(group_out(per, in_ref, got, send, recv, local))
        result[...] = functools.reduce(jnp.add, [got[d] for d in range(lax.axis_size("fsdp"))])
        start_all(group_back(per, result, out_ref, send, recv, local))

    rq[...] += tn3(split2(x_ref[...]), split2(dq_ref[...]))
    ro[...] += tn3(split2(mixed_ref[...]), split2(dz3_ref[...]))
    g, _, _ = norm_fwd(z_ref[...], vec_ref[16:17], vec_ref[17:18])
    up[...] += tn3(split2(g), split2(du_ref[...]))
    u = u_ref[...]
    down[...] += tn3(split2(u * gelu_cdf(u)), split2(dz4_ref[...]))

    @pl.when(step == pl.num_programs(0) - 1)
    def _():
        wait_all(group_back(per, result, out_ref, send, recv, local))


def group_scratch(per, nf):
    return [
        pltpu.VMEM((nf, per, PACK, HALF), F32),
        pltpu.VMEM((per, PACK, HALF), F32),
        pltpu.SemaphoreType.DMA((2 * nf - 2,)),
        pltpu.SemaphoreType.DMA((2 * nf - 2,)),
        pltpu.SemaphoreType.DMA,
    ]


def group_params(cid):
    return pltpu.CompilerParams(collective_id=cid, has_side_effects=True, vmem_limit_bytes=VMEM_LIMIT)


def group_stats(packed, cid):
    nf = lax.axis_size("fsdp")
    per = packed.shape[0] // nf
    return pl.pallas_call(
        functools.partial(stats_kernel, per),
        in_specs=[ANY],
        out_specs=ANY,
        out_shape=jax.ShapeDtypeStruct(packed.shape, F32),
        scratch_shapes=group_scratch(per, nf),
        compiler_params=group_params(cid),
        name="group_stats",
    )(packed)


def group_sum(packed, work, vecs, layer, cid):
    nf = lax.axis_size("fsdp")
    per = packed.shape[0] // nf
    rows = 480
    steps = work[0].shape[0] // rows
    shapes = [(D, D), (D, D), (D, FF), (FF, D)]
    return pl.pallas_call(
        functools.partial(sum_kernel, per, steps - steps // 4),
        grid=(steps,),
        in_specs=[ANY] + [pl.BlockSpec((rows, w.shape[1]), lambda i: (i, 0)) for w in work] + [pick((24, D), layer)],
        out_specs=[ANY] + [whole(s) for s in shapes],
        out_shape=[jax.ShapeDtypeStruct(packed.shape, F32)] + [jax.ShapeDtypeStruct(s, F32) for s in shapes],
        scratch_shapes=group_scratch(per, nf),
        compiler_params=group_params(cid),
        name="group_sum",
    )(packed, *work, vecs)

LAYER_AT = SEGLEN + 1 + SEG
MERGE_AT = LAYER_AT + 46
HEAD_AT = MERGE_AT + 5
ROUTER_AT = HEAD_AT + PRED
VROWS = NVEC + 20


def own_size(devices):
    own = NVEC * D // devices
    return own, -(-own // D)


def prepare_kernel(nfeed, ser_ref, obs_ref, tgt_ref, mask_ref, count_ref, mat_ref, feed_ref, vec_ref, *outs):
    pieces, tgt, kept, scale_ref, mean_ref, here_ref, tile_ref, mat_o, feed_o, vec_o = outs
    for src, dst in ((mat_ref, mat_o), (feed_ref, feed_o), (vec_ref, vec_o)):
        rows = dst.shape[0]
        left, right = src[pl.ds(0, rows, stride=2), :], src[pl.ds(1, rows, stride=2), :]
        dst[...] = jnp.concatenate([left, right], 1).astype(BF)
    nv = ser_ref.shape[0]
    series, seen = ser_ref[...], obs_ref[...].astype(F32)
    counted = jnp.maximum(jnp.sum(seen, -1, keepdims=True), 1.0)
    mean = jnp.sum(seen * series, -1, keepdims=True) / counted
    center = (series - mean) * seen
    scale = jnp.sqrt(jnp.sum(center * center, -1, keepdims=True) / counted + norm_eps)
    slot = lax.axis_index("fsdp") * nv + lax.broadcasted_iota(jnp.int32, (nv, HALF), 0)
    here = jnp.where(slot < count_ref[0], 1.0, 0.0)
    here_ref[...] = here
    scale_ref[...] = jnp.broadcast_to(scale, (nv, PPAD))
    mean_ref[...] = jnp.broadcast_to(mean, (nv, PPAD))
    mask = mask_ref[...].astype(F32) * here[:, :1]
    tile_ref[...] = jnp.broadcast_to(jnp.sum(jnp.sum(mask, 0, keepdims=True), -1, keepdims=True), (8, HALF)) * (1.0 / (8 * HALF))
    lane = lax.broadcasted_iota(jnp.int32, (nv, PPAD), 1)

    def cut(x, dst):
        x = jnp.concatenate([x, jnp.zeros((nv, PPAD - 12), F32)], 1)
        for s in range(dst.shape[0]):
            dst[s] = jnp.where(lane < 12, x[:, 12 * s : 12 * s + PPAD], 0.0)

    cut(center / scale, pieces)
    cut(tgt_ref[...], tgt)
    cut(mask * (2.0 / (1 << 20)), kept)


def prepare(series, observed, targets, target_mask, counts, matrices, feed, vectors):
    nv = series.shape[0]
    shapes = [((SEG, nv, PPAD), F32), ((SEG // 2, nv, PPAD), F32), ((SEG // 2, nv, PPAD), F32), ((nv, PPAD), F32), ((nv, PPAD), F32)]
    shapes += [((nv, HALF), F32), ((8, HALF), F32)]
    shapes += [((x.shape[0] // 2, D), BF) for x in (matrices, feed, vectors)]
    return pl.pallas_call(
        functools.partial(prepare_kernel, 0),
        grid=(1,),
        in_specs=[whole(x.shape) for x in (series, observed, targets, target_mask)]
        + [pl.BlockSpec(memory_space=pltpu.SMEM)]
        + [whole(x.shape) for x in (matrices, feed, vectors)],
        out_specs=[whole(s) for s, _ in shapes],
        out_shape=[jax.ShapeDtypeStruct(s, t) for s, t in shapes],
        compiler_params=pltpu.CompilerParams(vmem_limit_bytes=VMEM_LIMIT),
        name="prepare",
    )(series, observed, targets, target_mask, counts, matrices, feed, vectors)


def unpack_kernel(devices, own, vec_ref, vecs, mvec, emb, place, head, r0, r1, flat):
    flat[...] = jnp.zeros(flat.shape, F32)
    rows = vec_ref.shape[1]
    lane = lax.broadcasted_iota(jnp.int32, (rows, D), 1)
    for d in range(devices):
        at, shift = divmod(own * d, D)
        block = vec_ref[d].astype(F32)
        if shift:
            block = pltpu.roll(block, shift, 1)
            flat[at + 1 : at + 1 + rows] += jnp.where(lane < shift, block, 0.0)
            block = jnp.where(lane >= shift, block, 0.0)
        flat[at : at + rows] += block

    def padded(at, count, total):
        return jnp.concatenate([flat[at : at + count], jnp.zeros((total - count, D), F32)], 0)

    for l in range(2):
        vecs[l] = padded(LAYER_AT + 23 * l, 23, 24)
    mvec[...] = padded(MERGE_AT, 5, 8)
    emb[...] = padded(0, SEGLEN, 16).astype(BF)
    head[...] = padded(HEAD_AT, PRED, PPAD).astype(BF)
    for s in range(SEG):
        place[s] = flat[SEGLEN + 1 + s : SEGLEN + 2 + s] + flat[SEGLEN : SEGLEN + 1]
        r0[s] = padded(ROUTER_AT + ROUT * s, ROUT, RPAD)
    for s in range(SEG // 2):
        r1[s] = padded(ROUTER_AT + ROUT * (SEG + s), ROUT, RPAD)


def unpack_vectors(gathered, own):
    devices, rows, _ = gathered.shape
    shapes = [((2, 24, D), F32), ((8, D), F32), ((16, D), BF), ((SEG, 1, D), F32), ((PPAD, D), BF)]
    shapes += [((SEG, RPAD, D), F32), ((SEG // 2, RPAD, D), F32)]
    return pl.pallas_call(
        functools.partial(unpack_kernel, devices, own),
        grid=(1,),
        in_specs=[whole(gathered.shape)],
        out_specs=[whole(s) for s, _ in shapes],
        out_shape=[jax.ShapeDtypeStruct(s, t) for s, t in shapes],
        scratch_shapes=[pltpu.VMEM((VROWS + 24, D), F32)],
        compiler_params=pltpu.CompilerParams(vmem_limit_bytes=VMEM_LIMIT),
        name="unpack_vectors",
    )(gathered)


def assemble_kernel(devices, own, demb, dplace, *refs):
    (rt0, rs0, rr0, rt1, rs1, rr1, dmv, dhead, dr0, dr1), out, flat = refs[:10], refs[10], refs[11]
    flat[...] = jnp.zeros(flat.shape, F32)
    flat[0:SEGLEN] = demb[0:SEGLEN]
    place = jnp.sum(dplace[...].reshape(SEG, VB, D), 1)
    flat[SEGLEN : SEGLEN + 1] = jnp.sum(place, 0, keepdims=True)
    flat[SEGLEN + 1 : SEGLEN + 1 + SEG] = place
    at = LAYER_AT
    for ref in (rt0, rs0, rr0, rt1, rs1, rr1, dmv):
        count = ref.shape[0]
        flat[at : at + count] = jnp.sum(ref[...], 1)
        at += count
    flat[HEAD_AT : HEAD_AT + PRED] = dhead[0:PRED]
    for s in range(SEG):
        flat[ROUTER_AT + ROUT * s : ROUTER_AT + ROUT * (s + 1)] = dr0[s][:ROUT]
    for s in range(SEG // 2):
        flat[ROUTER_AT + ROUT * (SEG + s) : ROUTER_AT + ROUT * (SEG + s + 1)] = dr1[s][:ROUT]
    rows = out.shape[1]
    lane = lax.broadcasted_iota(jnp.int32, (rows, D), 1)
    inside = lax.broadcasted_iota(jnp.int32, (rows, D), 0) * D + lane < own
    for d in range(devices):
        at, shift = divmod(own * d, D)
        block = flat[at : at + rows]
        if shift:
            block = jnp.where(lane < D - shift, pltpu.roll(block, D - shift, 1), pltpu.roll(flat[at + 1 : at + 1 + rows], D - shift, 1))
        out[d] = jnp.where(inside, block, 0.0)


def assemble_vectors(parts, devices):
    own, rows = own_size(devices)
    return pl.pallas_call(
        functools.partial(assemble_kernel, devices, own),
        grid=(1,),
        in_specs=[whole(p.shape) for p in parts],
        out_specs=whole((devices, rows, D)),
        out_shape=jax.ShapeDtypeStruct((devices, rows, D), F32),
        scratch_shapes=[pltpu.VMEM((VROWS + 24, D), F32)],
        compiler_params=pltpu.CompilerParams(vmem_limit_bytes=VMEM_LIMIT),
        name="assemble_vectors",
    )(*parts)


def adam_update(weight, first_moment, second_moment, gradient):
    first_new = beta_one * first_moment + (1.0 - beta_one) * gradient
    second_new = beta_two * second_moment + (1.0 - beta_two) * gradient * gradient
    corrected = (
        first_new
        / (1.0 - beta_one**step_count)
        / (jnp.sqrt(second_new / (1.0 - beta_two**step_count)) + adam_eps)
    )
    return (weight - learn_rate * (corrected + weight_decay * weight), first_new, second_new)


def gradient_parts(ready, model, extras, up_rows, group_stats, group_sum, nf, devices):
    pieces, tgt, kept, scale, mean, here = ready
    mvec, emb, place, head, routers0, routers1 = extras
    sb0, sb1, sf0, sf1, st = 12, 10, 20, 10, 10
    rf, rb = 20, 20
    half = SEG // 2
    dim0, kept0 = time_fwd(True, pieces, (emb, place), model, 0, SEG)
    o0 = send_fwd(dim0, routers0, here, model, 0, sf0, -(-SEG // nf) * nf)
    o0 = group_stats(o0, 2)
    x1, *saved = recv_fwd(dim0, o0, model, mvec, rf)
    dim1, kept1 = time_fwd(False, x1, (), model, 1, half)
    o1 = send_fwd(dim1, routers1, here, model, 1, sf1, -(-half // nf) * nf)
    o1 = group_stats(o1, 3)
    vecs = model[3]
    g_mat, g_feed, ddim1, do1, rr1, dhead, *work = tail(dim1, o1, tgt, kept, scale, mean, model, head, st)
    do1, *later = group_sum(do1, [dim1.reshape(-1, D)] + work, vecs, 1, 4)
    g_mat, ddim1, dr1, rs1 = send_bwd(dim1, ddim1, routers1, o1, do1, here, model, 1, sb1, g_mat)
    g_mat, g_feed, rt1, dx1 = time_bwd(
        False, x1, (), ddim1, kept1, model, 1, half, later, (g_mat, g_feed), up_rows
    )
    g_mat, ddim0, do0, rr0, dmv, *work = recv_bwd(dim0, o0, dx1, saved, model, mvec, rb, g_mat)
    work = [dim0.reshape(-1, D), saved[1], saved[3], saved[4]] + work
    do0, *later = group_sum(do0, work, vecs, 0, 5)
    g_mat, ddim0, dr0, rs0 = send_bwd(dim0, ddim0, routers0, o0, do0, here, model, 0, sb0, g_mat)
    g_mat, g_feed, rt0, demb, dplace = time_bwd(
        True, pieces, (emb, place), ddim0, kept0, model, 0, SEG, later, (g_mat, g_feed), up_rows
    )
    g_vec = assemble_vectors((demb, dplace, rt0, rs0, rr0, rt1, rs1, rr1, dmv, dhead, dr0, dr1), devices)
    return g_mat, g_feed, g_vec


def on_device(series, observed, targets, target_mask, counts, matrices, feed_weights, vectors, matrices_first, matrices_second, feed_first, feed_second, vectors_first, vectors_second):
    nf = lax.axis_size("fsdp")
    nd = lax.axis_size("dp")
    devices = nf * nd
    own, vec_rows = own_size(devices)
    out = prepare(
        series[0],
        observed[0],
        targets[0],
        target_mask[0],
        counts,
        matrices.reshape(-1, HALF),
        feed_weights.reshape(-1, HALF),
        jnp.pad(vectors, (0, vec_rows * D - own)).reshape(-1, HALF),
    )
    ready, tile, shards = out[:6], out[6], out[7:]
    square, feed, vecs = gather_all(shards)
    square = square.reshape(NSQ, D, D)
    feed = feed.reshape(-1, D)
    up = feed[: 4 * FF].reshape(4, D, FF)
    down = feed.reshape(8, FF, D)
    vecs, *extras = unpack_vectors(vecs.reshape(devices, vec_rows, D), own)
    up_rows = feed_weights.shape[0] // FF
    g_mat, g_feed, g_vec = gradient_parts(ready, (square, up, down, vecs), extras, up_rows, group_stats, group_sum, nf, devices)
    ny, nz, nx = grid_sizes()
    lead = (ny, 2, nz, nx)
    s_mat, s_feed, s_vec, sums = scatter_sum([g.reshape(lead + (-1, D)) for g in (g_mat, g_feed, g_vec)], tile)
    is_up = lax.axis_index("dp") * 2 < nd
    halves_of = s_feed.reshape(2, up_rows, D)
    s_feed = jnp.where(is_up, jnp.concatenate([halves_of[0], halves_of[1]], 1).reshape(-1), s_feed.reshape(-1))
    grads = (s_mat.reshape(-1), s_feed, s_vec.reshape(-1)[:own])
    upscale = (1 << 20) / jnp.maximum(jnp.sum(sums[8:]), 1.0)
    grad_norm = jnp.sqrt(jnp.sum(sums[:8])) * upscale
    factor = upscale * (clip_norm / jnp.maximum(grad_norm, clip_norm))
    new = (
        adam_update(matrices, matrices_first, matrices_second, grads[0] * factor)
        + adam_update(feed_weights, feed_first, feed_second, grads[1] * factor)
        + adam_update(vectors, vectors_first, vectors_second, grads[2] * factor)
    )
    return (grad_norm,) + new


def solution(mesh):
    both = P(("dp", "fsdp"))
    data = P("dp", "fsdp", None)
    return jax.shard_map(
        on_device,
        mesh=mesh,
        in_specs=(data,) * 4 + (P("dp"),) + (both,) * 9,
        out_specs=(P(),) + (both,) * 9,
        check_vma=False,
    )
```

```python
import functools
import jax
import jax.numpy as jnp
from jax import lax
from jax.experimental import pallas as pl
from jax.experimental.pallas import tpu as pltpu
from jax.sharding import PartitionSpec as P

D = 256
HEADS = 8
FF = 512
ROUT = 10
RPAD = 16
SEGLEN = 12
PRED = 12
PPAD = 16
SEG = 60
NSQ = 26
NVEC = 1036
HALF = 128
VB = 8
UNROLL = 8
UNROLL_BACK = 8

BF = jnp.bfloat16
F32 = jnp.float32
SCALE = (D // HEADS) ** (-0.5)
negative = -1e30
norm_eps = 1e-05
beta_one = 0.9
beta_two = 0.999
adam_eps = 1e-08
weight_decay = 0.01
learn_rate = 0.2
clip_norm = 0.01
step_count = 10.0
VMEM_LIMIT = 60 << 20


ANY = pl.BlockSpec(memory_space=pl.ANY)
INVMEM = pl.BlockSpec(memory_space=pltpu.VMEM)


def split2(x):
    hi = x.astype(BF)
    return hi, (x - hi.astype(F32)).astype(BF)


def dots(a, b, ca, cb):
    return lax.dot_general(a, b, (((ca,), (cb,)), ((), ())), preferred_element_type=F32)


def mmw(x2, w):
    return dots(x2[0], w, 1, 0) + dots(x2[1], w, 1, 0)


def mmwt(x2, w):
    return dots(x2[0], w, 1, 1) + dots(x2[1], w, 1, 1)


def rows2(a2):
    return jnp.concatenate([a2[0], a2[1]], 0)


def nn3(a2, b2):
    m = a2[0].shape[0]
    both = dots(rows2(a2), b2[0], 1, 0)
    return both[:m] + both[m:] + dots(a2[0], b2[1], 1, 0)


def nt3(a2, b2):
    m = a2[0].shape[0]
    both = dots(rows2(a2), b2[0], 1, 1)
    return both[:m] + both[m:] + dots(a2[0], b2[1], 1, 1)


def tn3(a2, b2):
    n = b2[0].shape[1]
    both = dots(a2[0], jnp.concatenate([b2[0], b2[1]], 1), 0, 0)
    return both[:, :n] + both[:, n:] + dots(a2[1], b2[0], 0, 0)


def tn3_short(a2, b2):
    return dots(jnp.concatenate([a2[0], a2[0], a2[1]], 0), jnp.concatenate([b2[0], b2[1], b2[0]], 0), 0, 0)


def nn3_short(a2, b2):
    return dots(jnp.concatenate([a2[0], a2[0], a2[1]], 1), jnp.concatenate([b2[0], b2[1], b2[0]], 0), 1, 0)


def corner(r, m, n):
    return r[:m, :n] + r[m:, :n] + r[:m, n:]


def nn3_narrow(a2, b2):
    r = dots(rows2(a2), jnp.concatenate([b2[0], b2[1]], 1), 1, 0)
    return corner(r, a2[0].shape[0], b2[0].shape[1])


def nt3_narrow(a2, b2):
    return corner(dots(rows2(a2), rows2(b2), 1, 1), a2[0].shape[0], b2[0].shape[0])


def norm_fwd(z, gain, bias):
    center = z - jnp.mean(z, -1, keepdims=True)
    inv = lax.rsqrt(jnp.mean(center * center, -1, keepdims=True) + norm_eps)
    unit = center * inv
    return unit * gain + bias, unit, inv


def norm_bwd(dy, unit, inv, gain):
    t = dy * gain
    return inv * (t - jnp.mean(t, -1, keepdims=True) - unit * jnp.mean(t * unit, -1, keepdims=True))


def colsum(x):
    return jnp.sum(x.reshape(x.shape[0] // 8, 8, x.shape[1]), 0)


def gelu_cdf(u):
    return 0.5 + 0.5 * lax.erf(u * 0.7071067811865476)


def gelu_slope(u, cdf):
    return cdf + u * (jnp.exp(-0.5 * u * u) * 0.3989422804014327)


def halves(x):
    return x[:, :HALF], x[:, HALF:]


def lane_head(rows):
    return lax.broadcasted_iota(jnp.int32, (rows, HALF), 1) // 32


def spread_heads(x, zero):
    head = lane_head(x.shape[0])
    return jnp.concatenate([jnp.where(head == h, x, zero) for h in range(4)], 0)


def gather_heads(x, group):
    head = lane_head(group)
    out = x[3 * group :]
    for h in range(3):
        out = jnp.where(head == h, x[h * group : (h + 1) * group], out)
    return out


def ones_heads(group, count):
    row = lax.broadcasted_iota(jnp.int32, (4 * group, HALF), 0)
    lane = lax.broadcasted_iota(jnp.int32, (4 * group, HALF), 1)
    return jnp.where((row // group == lane // 32) & (row % group < count), 1.0, 0.0).astype(BF)


def group_max(s, group, count):
    lane = lax.broadcasted_iota(jnp.int32, (s.shape[0], HALF), 1)
    outs = []
    for t in range(s.shape[1] // HALF):
        part = s[:, t * HALF : (t + 1) * HALF]
        top = None
        for g in range(HALF // group):
            here = (lane // group == g)
            best = jnp.max(jnp.where((lane // group == g) & (lane % group < count), part, negative), -1, keepdims=True)
            top = jnp.broadcast_to(best, part.shape) if top is None else jnp.where(here, best, top)
        outs.append(jnp.where(lane % group < count, part - top, negative))
    return jnp.concatenate(outs, 1)


def time_parts(units, group, ref):
    return [split2(ref[c, pl.ds(v, group, stride=VB), :]) for c, v in units]


def spread2(x2):
    zero = jnp.zeros((), BF)
    return spread_heads(x2[0], zero), spread_heads(x2[1], zero)


def time_attend(units, group, count, q_s, k_s, v_s, o_s, p_s, l_s):
    q = time_parts(units, group, q_s)
    k = [spread2(x2) for x2 in time_parts(units, group, k_s)]
    scores = [
        dots(jnp.concatenate(q2, 1), jnp.concatenate([k2[0], k2[0]], 1), 1, 1) + dots(q2[0], k2[1], 1, 1)
        for q2, k2 in zip(q, k)
    ]
    probs = [jnp.exp(group_max(s, group, count)) for s in scores]
    probs2 = [split2(p) for p in probs]
    w = [spread2(x2) for x2 in time_parts(units, group, v_s)]
    ones = ones_heads(group, count)
    both = [dots(rows2(p2), jnp.concatenate([w2[0], ones], 1), 1, 0) for p2, w2 in zip(probs2, w)]
    both = [b[:group] + b[group:] for b in both]
    inv = [1.0 / b[:, HALF:] for b in both]
    mixed = [(b[:, :HALF] + dots(p2[0], w2[1], 1, 0)) * i for b, p2, w2, i in zip(both, probs2, w, inv)]
    for (c, v), o, p, i in zip(units, mixed, probs, inv):
        o_s[c, pl.ds(v, group, stride=VB), :] = o
        p_s[c, v] = p
        l_s[c, v] = i


def time_attend_back(units, group, count, q_s, k_s, v_s, o_s, p_s, l_s, do_s, dq_s, dk_s, dv_s):
    d = [do_s[c, pl.ds(v, group, stride=VB), :] * l_s[c, v] for c, v in units]
    e2 = [split2(x * o_s[c, pl.ds(v, group, stride=VB), :]) for x, (c, v) in zip(d, units)]
    d2 = [split2(x) for x in d]
    w = [spread2(x2) for x2 in time_parts(units, group, v_s)]
    ones = -ones_heads(group, count)
    both = [
        dots(
            jnp.concatenate([jnp.concatenate([a[0], b[0]], 1), jnp.concatenate([a[1], b[1]], 1)], 0),
            jnp.concatenate([w2[0], ones], 1),
            1,
            1,
        )
        for a, b, w2 in zip(d2, e2, w)
    ]
    dp = [b[:group] + b[group:] + dots(a[0], w2[1], 1, 1) for b, a, w2 in zip(both, d2, w)]
    probs = [p_s[c, v] for c, v in units]
    s2 = [split2(p * x) for p, x in zip(probs, dp)]
    p2 = [split2(p) for p in probs]
    k = [spread2(x2) for x2 in time_parts(units, group, k_s)]
    dq = [nn3_narrow(a, k2) for a, k2 in zip(s2, k)]
    q = time_parts(units, group, q_s)
    dk = [gather_heads(tn3_short(a, q2), group) for a, q2 in zip(s2, q)]
    dv = [gather_heads(tn3_short(a, x), group) for a, x in zip(p2, d2)]
    for (c, v), x, y, z in zip(units, dq, dk, dv):
        at = pl.ds(v, group, stride=VB)
        dq_s[c, at, :] = x
        dk_s[c, at, :] = y
        dv_s[c, at, :] = z


def store_halves(ref, x):
    rows = x.shape[0]
    ref[0, :rows, :] = x[:, :HALF]
    ref[1, :rows, :] = x[:, HALF:]


def load_halves(ref, rows):
    return jnp.concatenate([ref[0, :rows, :], ref[1, :rows, :]], 1)


def zero_tail(ref, rows):
    tail = ref.shape[1] - rows
    ref[:, rows:, :] = jnp.zeros((2, tail, HALF), F32)


def time_forward(x, w, vec, count, group, kept):
    q_s, k_s, v_s, o_s, p_s, l_s, z1_s, u_s, z2_s = kept
    rows = count * VB
    x2 = split2(x)
    store_halves(q_s, (mmw(x2, w["q"]) + vec[0:1]) * SCALE)
    store_halves(k_s, mmw(x2, w["k"]))
    store_halves(v_s, mmw(x2, w["v"]) + vec[1:2])
    for ref in (q_s, k_s, v_s):
        zero_tail(ref, rows)

    def some(i, carry):
        units = [(c, i * UNROLL + k) for k in range(UNROLL) for c in range(2)]
        time_attend(units, group, count, q_s, k_s, v_s, o_s, p_s, l_s)
        return carry

    lax.fori_loop(0, VB // UNROLL, some, 0)
    z1 = x + mmw(split2(load_halves(o_s, rows)), w["o"]) + vec[2:3]
    z1_s[...] = z1
    h, _, _ = norm_fwd(z1, vec[3:4], vec[4:5])
    u = mmw(split2(h), w["up"]) + jnp.concatenate([vec[5:6], vec[6:7]], 1)
    u_s[...] = u
    z2 = h + mmw(split2(u * gelu_cdf(u)), w["down"]) + vec[7:8]
    z2_s[...] = z2
    return norm_fwd(z2, vec[8:9], vec[9:10])[0]


def embed_block(pieces, emb, place):
    return mmw(split2(pieces), emb) + place


TIME_W = ("q", "k", "v", "o", "up", "down")


def time_fwd_kernel(first, count, group, *refs):
    if first:
        x_ref, emb_ref, place_ref = refs[:3]
        refs = refs[3:]
    else:
        x_ref = refs[0]
        refs = refs[1:]
    w = {name: refs[i][...] for i, name in enumerate(TIME_W)}
    vec_ref, y_ref = refs[6:8]
    rows = count * VB
    if first:
        place = jnp.broadcast_to(place_ref[...], (count, VB, D)).reshape(rows, D)
        x = embed_block(x_ref[...].reshape(rows, 16), emb_ref[...], place)
    else:
        x = x_ref[...].reshape(rows, D)
    y = time_forward(x, w, vec_ref[...], count, group, refs[8:])
    y_ref[...] = y.reshape(count, VB, D)


def whole(shape):
    return pl.BlockSpec(shape, lambda i: (0,) * len(shape))


def params_spec():
    return pltpu.CompilerParams(vmem_limit_bytes=VMEM_LIMIT)


def pick(shape, index):
    return pl.BlockSpec((None,) + shape, lambda i: (index,) + (0,) * len(shape))


def weight_specs(squares, feed, layer):
    specs = [pick((D, D), k) for k in squares]
    if feed is not None:
        specs += [pick((D, FF), feed), pick((FF, D), 4 + feed)]
    return specs + [pick((24, D), layer)]


def weight_args(model, squares, feed):
    square, up, down, vecs = model
    return [square] * len(squares) + ([up, down] if feed is not None else []) + [vecs]


def flush(step, last, accs, mat_at, feeds, up_rows, g_mat, g_feed, sems):
    @pl.when(step == last)
    def _():
        copies = []

        def add(src, dst):
            copies.append(pltpu.make_async_copy(src, dst, sems.at[len(copies)]))

        for acc, at in zip(accs, mat_at):
            add(acc, g_mat.at[pl.ds(at, acc.shape[0])] if len(acc.shape) == 3 else g_mat.at[at])
        for up_acc, down_acc, feed_at in feeds:
            for k in range(D // up_rows):
                for half in range(2):
                    base = 2 * D * feed_at + (2 * k + half) * up_rows
                    add(up_acc.at[pl.ds(k * up_rows, up_rows), pl.ds(half * D, D)], g_feed.at[pl.ds(base, up_rows)])
            add(down_acc, g_feed.at[pl.ds(4 * FF + feed_at * FF, FF)])
        for copy in copies:
            copy.start()
        for copy in copies:
            copy.wait()


def pack_shapes():
    return [jax.ShapeDtypeStruct((NSQ, D, D), F32), jax.ShapeDtypeStruct((8 * FF, D), F32)]


def flush_count(mats, feeds, up_rows):
    return mats + feeds * (2 * D // up_rows + 1 if up_rows else 0)


def time_kept(count, group, nb):
    pad, rows = group * VB, count * VB
    shapes = [(2, pad, HALF)] * 4 + [(2, VB, group, 4 * group), (2, VB, group, HALF), (rows, D), (rows, FF), (rows, D)]
    specs = [pl.BlockSpec((None,) + s, lambda i, n=len(s): (i,) + (0,) * n) for s in shapes]
    return specs, [jax.ShapeDtypeStruct((nb,) + s, F32) for s in shapes]


def time_fwd(first, x, extra, model, layer, count):
    squares = [12 * layer + k for k in range(4)]
    group = 64 if count > 32 else 32
    nv = x.shape[1]
    width = x.shape[2]
    specs = [pl.BlockSpec((count, VB, width), lambda i: (0, i, 0))]
    if first:
        specs += [whole((16, D)), whole((count, 1, D))]
    kept_specs, kept_shapes = time_kept(count, group, nv // VB)
    out = pl.pallas_call(
        functools.partial(time_fwd_kernel, first, count, group),
        grid=(nv // VB,),
        in_specs=specs + weight_specs(squares, 2 * layer, layer),
        out_specs=[pl.BlockSpec((count, VB, D), lambda i: (0, i, 0))] + kept_specs,
        out_shape=[jax.ShapeDtypeStruct((count, nv, D), F32)] + kept_shapes,
        compiler_params=params_spec(),
        name="time_fwd",
    )(x, *extra, *weight_args(model, squares, 2 * layer))
    return out[0], out[1:]


def time_bwd_kernel(first, count, group, layer, up_rows, *refs):
    if first:
        x_ref, emb_ref, place_ref = refs[:3]
        refs = refs[3:]
    else:
        x_ref = refs[0]
        refs = refs[1:]
    dy_ref = refs[0]
    q_s, k_s, v_s, o_s, p_s, l_s, z1_s, u_s, z2_s = refs[1:10]
    w = {name: refs[10 + i][...] for i, name in enumerate(TIME_W)}
    vec_ref = refs[16]
    later = refs[17:21]
    g_mat, g_feed = refs[23:25]
    outs = refs[25:]
    n_out = 3 if first else 2
    tail = outs[1:n_out]
    accs = outs[n_out : n_out + 6]
    sems = outs[n_out + 6]
    g = dict(zip(TIME_W + ("rows",), tuple(accs) + (outs[0],)))
    do_s, dq_s, dk_s, dv_s = outs[n_out + 7 :]
    rows = count * VB
    step = pl.program_id(0)

    @pl.when(step == 0)
    def _():
        for ref in list(g.values()) + (list(tail) if first else []):
            ref[...] = jnp.zeros(ref.shape, F32)

    vec = vec_ref[...]
    if first:
        place = jnp.broadcast_to(place_ref[...], (count, VB, D)).reshape(rows, D)
        pieces = x_ref[...].reshape(rows, 16)
        x = embed_block(pieces, emb_ref[...], place)
    else:
        x = x_ref[...].reshape(rows, D)
    x2 = split2(x)
    mixed = load_halves(o_s, rows)
    h, unit1, inv1 = norm_fwd(z1_s[...], vec[3:4], vec[4:5])
    u = u_s[...]
    cdf = gelu_cdf(u)
    _, unit2, inv2 = norm_fwd(z2_s[...], vec[8:9], vec[9:10])
    dy = dy_ref[...].reshape(rows, D)
    g["rows"][8] += colsum(dy * unit2)
    g["rows"][9] += colsum(dy)
    dz2 = norm_bwd(dy, unit2, inv2, vec[8:9])
    g["rows"][7] += colsum(dz2)
    dz22 = split2(dz2)
    g["down"][...] += tn3(split2(u * cdf), dz22)
    du = mmwt(dz22, w["down"]) * gelu_slope(u, cdf)
    g["rows"][5] += colsum(du[:, :D])
    g["rows"][6] += colsum(du[:, D:])
    du2 = split2(du)
    g["up"][...] += tn3(split2(h), du2)
    dh = dz2 + mmwt(du2, w["up"])
    g["rows"][3] += colsum(dh * unit1)
    g["rows"][4] += colsum(dh)
    dz1 = norm_bwd(dh, unit1, inv1, vec[3:4])
    g["rows"][2] += colsum(dz1)
    dz12 = split2(dz1)
    g["o"][...] += tn3(split2(mixed), dz12)
    store_halves(do_s, mmwt(dz12, w["o"]))
    zero_tail(do_s, rows)

    def some(i, carry):
        units = [(c, i * UNROLL_BACK + k) for k in range(UNROLL_BACK) for c in range(2)]
        time_attend_back(units, group, count, q_s, k_s, v_s, o_s, p_s, l_s, do_s, dq_s, dk_s, dv_s)
        return carry

    lax.fori_loop(0, VB // UNROLL_BACK, some, 0)
    dq = load_halves(dq_s, rows) * SCALE
    g["rows"][0] += colsum(dq)
    dq2 = split2(dq)
    g["q"][...] += tn3(x2, dq2)
    dx = dz1 + mmwt(dq2, w["q"])
    dk2 = split2(load_halves(dk_s, rows))
    g["k"][...] += tn3(x2, dk2)
    dx = dx + mmwt(dk2, w["k"])
    dv = load_halves(dv_s, rows)
    g["rows"][1] += colsum(dv)
    dv2 = split2(dv)
    g["v"][...] += tn3(x2, dv2)
    dx = dx + mmwt(dv2, w["v"])
    if first:
        tail[0][...] += tn3(split2(pieces), split2(dx))
        tail[1][...] += dx
    else:
        tail[0][...] = dx.reshape(count, VB, D)
    flush(
        step, pl.num_programs(0) - 1, list(accs[:4]) + list(later[:2]), [12 * layer + k for k in (0, 1, 2, 3, 8, 11)],
        [(accs[4], accs[5], 2 * layer), (later[2], later[3], 2 * layer + 1)], up_rows, g_mat, g_feed, sems,
    )


def time_bwd(first, x, extra, dy, kept, model, layer, count, later, packs, up_rows):
    group = 64 if count > 32 else 32
    nv = x.shape[1]
    width = x.shape[2]
    pad = group * VB
    squares = [12 * layer + k for k in range(4)]
    block = pl.BlockSpec((count, VB, D), lambda i: (0, i, 0))
    specs = [pl.BlockSpec((count, VB, width), lambda i: (0, i, 0))]
    if first:
        specs += [whole((16, D)), whole((count, 1, D))]
    specs += [block] + time_kept(count, group, nv // VB)[0] + weight_specs(squares, 2 * layer, layer)
    specs += [whole((D, D)), whole((D, D)), whole((D, FF)), whole((FF, D))]
    grad_shapes = [(10, 8, D)] + ([(16, D), (count * VB, D)] if first else [])
    out_specs = [ANY] * 2 + [whole(s) for s in grad_shapes]
    out_shape = pack_shapes() + [jax.ShapeDtypeStruct(s, F32) for s in grad_shapes]
    if not first:
        out_specs.append(block)
        out_shape.append(jax.ShapeDtypeStruct((count, nv, D), F32))
    return pl.pallas_call(
        functools.partial(time_bwd_kernel, first, count, group, layer, up_rows),
        grid=(nv // VB,),
        in_specs=specs + [ANY] * 2,
        out_specs=out_specs,
        out_shape=out_shape,
        input_output_aliases={len(specs): 0, len(specs) + 1: 1},
        scratch_shapes=[pltpu.VMEM((D, D), F32)] * 4
        + [pltpu.VMEM((D, FF), F32), pltpu.VMEM((FF, D), F32), pltpu.SemaphoreType.DMA((flush_count(6, 2, up_rows),))]
        + [pltpu.VMEM((2, pad, HALF), F32)] * 4,
        compiler_params=params_spec(),
        name="time_bwd",
    )(x, *extra, dy, *kept, *weight_args(model, squares, 2 * layer), *later, *packs)

SB_ROWS = 64


def head_rows():
    sub = lax.broadcasted_iota(jnp.int32, (8, D), 0)
    lane = lax.broadcasted_iota(jnp.int32, (8, D), 1)
    return jnp.where(sub == lane // 32, 1.0, 0.0).astype(F32)


def spread_rows(x):
    wide = jnp.broadcast_to(x[:, None, :], (RPAD, HEADS, D)) * head_rows()[None]
    return wide.reshape(RPAD * HEADS, D)


def gather_rows(x):
    return jnp.sum(x.reshape(RPAD, HEADS, D) * head_rows()[None], 1)


PACK = 24


def pack_rows(x, last=None):
    last = jnp.zeros((1, HALF), F32) if last is None else last
    return jnp.concatenate([x[:ROUT, :HALF], x[:ROUT, HALF:], last, jnp.zeros((PACK - 2 * ROUT - 1, HALF), F32)], 0)


def unpack_rows(x):
    x = jnp.concatenate([x[:ROUT], x[ROUT : 2 * ROUT]], 1)
    return jnp.concatenate([x, jnp.zeros((RPAD - ROUT, D), F32)], 0)


def unpack_block(ref, sb):
    return jnp.concatenate([unpack_rows(ref[s]) for s in range(sb)], 0)


TALL = 2 * ROUT


def tall_spec(sb):
    return pl.BlockSpec((sb * TALL, HALF), lambda i: (i, 0))


def tall_rows(n, parts):
    return -(-n * TALL // (8 * parts)) * 8 * parts


def pack_block(ref, x, sb):
    for s in range(sb):
        rows = x[s * RPAD : s * RPAD + ROUT]
        ref[s * TALL : (s + 1) * TALL] = jnp.concatenate([rows[:, :HALF], rows[:, HALF:]], 0)


def valid_lane(rows):
    return lax.broadcasted_iota(jnp.int32, (rows, HALF), 1) < ROUT * HEADS


def router_reduce(x, op):
    for shift in (8, 16, 32, 64):
        x = op(x, pltpu.roll(x, shift, 1))
    return x


def merge_rows(y, pairs, vec):
    wide = y.reshape(pairs, 2, SB_ROWS, D)
    wide = jnp.concatenate([wide[:, 0].reshape(pairs * SB_ROWS, D), wide[:, 1].reshape(pairs * SB_ROWS, D)], 1)
    gain = jnp.concatenate([vec[0:1], vec[1:2]], 1)
    bias = jnp.concatenate([vec[2:3], vec[3:4]], 1)
    return norm_fwd(wide, gain, bias) + (gain,)


RECV_W = ("so", "rk", "rv", "rq", "ro", "up", "down")


def recv_buffer(o2, w, vec):
    buf2 = split2(mmw(o2, w["so"]) + vec[12:13])
    kb = mmw(buf2, w["rk"])
    vb = mmw(buf2, w["rv"]) + vec[14:15]
    segs = range(kb.shape[0] // RPAD)
    k = [split2(spread_rows(kb[s * RPAD : (s + 1) * RPAD])) for s in segs]
    v = [split2(spread_rows(vb[s * RPAD : (s + 1) * RPAD])) for s in segs]
    return buf2, k, v


def recv_forward(send, o_rows, w, vec):
    sb = send.shape[0] // SB_ROWS
    send2 = split2(send)
    o2 = split2(o_rows)
    buf2, k, v = recv_buffer(o2, w, vec)
    q = (mmw(send2, w["rq"]) + vec[13:14]) * SCALE
    segs = range(sb)
    ok = valid_lane(SB_ROWS)
    scores = [jnp.where(ok, nt3_narrow(split2(q[s * SB_ROWS : (s + 1) * SB_ROWS]), k[s]), negative) for s in segs]
    probs = [jnp.exp(sc - router_reduce(sc, jnp.maximum)) for sc in scores]
    probs = [p / router_reduce(p, jnp.add) for p in probs]
    mixed = jnp.concatenate([nn3_short(split2(p), v2) for p, v2 in zip(probs, v)], 0)
    z3 = send + mmw(split2(mixed), w["ro"]) + vec[15:16]
    g, unit3, inv3 = norm_fwd(z3, vec[16:17], vec[17:18])
    u = mmw(split2(g), w["up"]) + jnp.concatenate([vec[18:19], vec[19:20]], 1)
    cdf = gelu_cdf(u)
    z4 = g + mmw(split2(u * cdf), w["down"]) + vec[20:21]
    y, unit4, inv4 = norm_fwd(z4, vec[21:22], vec[22:23])
    kept = (send2, o2, buf2, mixed, g, unit3, inv3, u, cdf, unit4, inv4, q, k, v, probs)
    return y, kept, (q, mixed, jnp.concatenate(probs, 0), z3, u, z4)


def recv_restore(send, o_rows, w, vec, saved):
    q, mixed, p, z3, u, z4 = saved
    o2 = split2(o_rows)
    buf2, k, v = recv_buffer(o2, w, vec)
    g, unit3, inv3 = norm_fwd(z3, vec[16:17], vec[17:18])
    y, unit4, inv4 = norm_fwd(z4, vec[21:22], vec[22:23])
    probs = [p[s * SB_ROWS : (s + 1) * SB_ROWS] for s in range(send.shape[0] // SB_ROWS)]
    return y, (split2(send), o2, buf2, mixed, g, unit3, inv3, u, gelu_cdf(u), unit4, inv4, q, k, v, probs)


KEPT_WIDTHS = (D, D, HALF, D, FF, D)


def kept_specs(sb):
    return [pl.BlockSpec((sb * SB_ROWS, k), lambda i: (i, 0)) for k in KEPT_WIDTHS]


RECV_G = ("so", "rk", "rv", "rows")
LATER_WIDTHS = (D, D, FF, D)


def row_specs(sb, widths):
    return [pl.BlockSpec((sb * SB_ROWS, k), lambda i: (i, 0)) for k in widths]


def row_shapes(n, widths):
    return [jax.ShapeDtypeStruct((n * SB_ROWS, k), F32) for k in widths]


def put(refs, values):
    for ref, value in zip(refs, values):
        ref[...] = value


def recv_backward(dy, kept, w, vec, g):
    send2, o2, buf2, mixed, gg, unit3, inv3, u, cdf, unit4, inv4, q, k, v, probs = kept
    sb = dy.shape[0] // SB_ROWS
    rows = g["rows"]
    rows[9] += colsum(dy * unit4)
    rows[10] += colsum(dy)
    dz4 = norm_bwd(dy, unit4, inv4, vec[21:22])
    rows[8] += colsum(dz4)
    dz42 = split2(dz4)
    du = mmwt(dz42, w["down"]) * gelu_slope(u, cdf)
    rows[6] += colsum(du[:, :D])
    rows[7] += colsum(du[:, D:])
    du2 = split2(du)
    dg = dz4 + mmwt(du2, w["up"])
    rows[4] += colsum(dg * unit3)
    rows[5] += colsum(dg)
    dz3 = norm_bwd(dg, unit3, inv3, vec[16:17])
    rows[3] += colsum(dz3)
    dz32 = split2(dz3)
    do = mmwt(dz32, w["ro"])
    segs = range(sb)
    d = [split2(do[s * SB_ROWS : (s + 1) * SB_ROWS]) for s in segs]
    dp = [nt3_narrow(d2, v2) for d2, v2 in zip(d, v)]
    ds = [split2(p * (x - router_reduce(p * x, jnp.add))) for p, x in zip(probs, dp)]
    dq = jnp.concatenate([nn3_short(s2, k2) for s2, k2 in zip(ds, k)], 0) * SCALE
    q = [split2(q[s * SB_ROWS : (s + 1) * SB_ROWS]) for s in segs]
    dk = jnp.concatenate([gather_rows(tn3_short(s2, q2)) for s2, q2 in zip(ds, q)], 0)
    dv = jnp.concatenate([gather_rows(tn3_short(split2(p), d2)) for p, d2 in zip(probs, d)], 0)
    rows[1] += colsum(dq)
    dq2 = split2(dq)
    dsend = dz3 + mmwt(dq2, w["rq"])
    dk2 = split2(dk)
    dv2 = split2(dv)
    rows[2] += colsum(dv)
    g["rk"][...] += tn3(buf2, dk2)
    g["rv"][...] += tn3(buf2, dv2)
    dbuf = mmwt(dk2, w["rk"]) + mmwt(dv2, w["rv"])
    rows[0] += colsum(dbuf)
    dbuf2 = split2(dbuf)
    g["so"][...] += tn3(o2, dbuf2)
    return dsend, mmwt(dbuf2, w["so"]), (dq, dz3, du, dz4)


def recv_squares(layer):
    return [12 * layer + k for k in (7, 9, 10, 8, 11)]


def seg_block(sb, rows=SB_ROWS, width=D):
    return pl.BlockSpec((sb, rows, width), lambda i: (i, 0, 0))


MERGE = pl.BlockSpec((2, D, D), lambda i: (12, 0, 0))


def pack_spec(sb):
    return seg_block(sb, PACK, HALF)


def recv_fwd_kernel(sb, send_ref, o_ref, *refs):
    w = {n: refs[i][...] for i, n in enumerate(RECV_W)}
    vec_ref, mvec_ref, mw_ref, out_ref = refs[7:11]
    y, _, saved = recv_forward(send_ref[...].reshape(sb * SB_ROWS, D), unpack_block(o_ref, sb), w, vec_ref[...])
    for ref, x in zip(refs[11:], saved):
        ref[...] = x
    mvec = mvec_ref[...]
    wide, _, _, _ = merge_rows(y, sb // 2, mvec)
    out_ref[...] = (mmw(split2(wide), mw_ref[...].reshape(2 * D, D)) + mvec[4:5]).reshape(sb // 2, SB_ROWS, D)


def recv_fwd(send, o, model, mvec, sb):
    squares = recv_squares(0)
    n = send.shape[0]
    return pl.pallas_call(
        functools.partial(recv_fwd_kernel, sb),
        grid=(n // sb,),
        in_specs=[seg_block(sb), pack_spec(sb)] + weight_specs(squares, 1, 0) + [whole((8, D)), MERGE],
        out_specs=[seg_block(sb // 2)] + kept_specs(sb),
        out_shape=[jax.ShapeDtypeStruct((n // 2, SB_ROWS, D), F32)]
        + [jax.ShapeDtypeStruct((n * SB_ROWS, k), F32) for k in KEPT_WIDTHS],
        compiler_params=params_spec(),
        name="recv_fwd",
    )(send, o, *weight_args(model, squares, 1), mvec, model[0])


def recv_bwd_kernel(sb, send_ref, o_ref, dx_ref, *refs):
    saved = [ref[...] for ref in refs[:6]]
    refs = refs[6:]
    w = {n: refs[i][...] for i, n in enumerate(RECV_W)}
    vec_ref, mvec_ref, mw_ref = refs[7:10]
    g_mat, dsend_ref, do_ref, rows_ref, dmv_ref = refs[11:16]
    later, accs, dmw_ref, sems = refs[16:20], refs[20:23], refs[23], refs[24]
    g = dict(zip(RECV_G, tuple(accs) + (rows_ref,)))

    @pl.when(pl.program_id(0) == 0)
    def _():
        for ref in list(g.values()) + [dmw_ref, dmv_ref]:
            ref[...] = jnp.zeros(ref.shape, F32)

    vec = vec_ref[...]
    y, kept = recv_restore(send_ref[...].reshape(sb * SB_ROWS, D), unpack_block(o_ref, sb), w, vec, saved)
    pairs = sb // 2
    wide, unit, inv, gain = merge_rows(y, pairs, mvec_ref[...])
    dx = dx_ref[...].reshape(pairs * SB_ROWS, D)
    dmv_ref[4] += colsum(dx)
    dx2 = split2(dx)
    dmw_ref[...] += tn3(split2(wide), dx2).reshape(2, D, D)
    dn = mmwt(dx2, mw_ref[...].reshape(2 * D, D))
    part = colsum(dn * unit)
    dmv_ref[0] += part[:, :D]
    dmv_ref[1] += part[:, D:]
    part = colsum(dn)
    dmv_ref[2] += part[:, :D]
    dmv_ref[3] += part[:, D:]
    dwide = norm_bwd(dn, unit, inv, gain)
    left = dwide[:, :D].reshape(pairs, 1, SB_ROWS, D)
    right = dwide[:, D:].reshape(pairs, 1, SB_ROWS, D)
    dy = jnp.concatenate([left, right], 1).reshape(sb * SB_ROWS, D)
    dsend, do, grads = recv_backward(dy, kept, w, vec, g)
    put(later, grads)
    dsend_ref[...] = dsend.reshape(sb, SB_ROWS, D)
    pack_block(do_ref, do, sb)
    recv_flush(accs, [(dmw_ref, 24)], 0, g_mat, sems)


RECV_ACC = [pltpu.VMEM((D, D), F32)] * 3


def recv_flush(accs, more, layer, g_mat, sems):
    flush(
        pl.program_id(0), pl.num_programs(0) - 1, list(accs) + [m for m, _ in more],
        recv_squares(layer)[:3] + [at for _, at in more], [], 0, g_mat, None, sems,
    )


def recv_bwd(send, o, dx, kept, model, mvec, sb, g_mat, parts):
    n = send.shape[0]
    squares = recv_squares(0)
    shapes = [(11, 8, D), (5, 8, D)]
    specs = [seg_block(sb), pack_spec(sb), seg_block(sb // 2)] + kept_specs(sb)
    specs += weight_specs(squares, 1, 0) + [whole((8, D)), MERGE]
    return pl.pallas_call(
        functools.partial(recv_bwd_kernel, sb),
        grid=(n // sb,),
        in_specs=specs + [ANY],
        out_specs=[ANY, seg_block(sb), tall_spec(sb)] + [whole(s) for s in shapes] + row_specs(sb, LATER_WIDTHS),
        out_shape=pack_shapes()[:1]
        + [jax.ShapeDtypeStruct((n, SB_ROWS, D), F32), jax.ShapeDtypeStruct((tall_rows(n, parts), HALF), F32)]
        + [jax.ShapeDtypeStruct(s, F32) for s in shapes]
        + row_shapes(n, LATER_WIDTHS),
        input_output_aliases={len(specs): 0},
        scratch_shapes=RECV_ACC + [pltpu.VMEM((2, D, D), F32), pltpu.SemaphoreType.DMA((4,))],
        compiler_params=params_spec(),
        name="recv_bwd",
    )(send, o, dx, *kept, *weight_args(model, squares, 1), mvec, model[0], g_mat)


def tail_kernel(sb, send_ref, o_ref, tgt_ref, kept_ref, scale_ref, mean_ref, *refs):
    w = {n: refs[i][...] for i, n in enumerate(RECV_W)}
    vec_ref, head_ref, g_mat, g_feed, dsend_ref, do_ref, rows_ref, dhead_ref = refs[7:15]
    saved, later, accs, sems = refs[15:18], refs[18:22], refs[22:25], refs[25]
    g = dict(zip(RECV_G, tuple(accs) + (rows_ref,)))

    @pl.when(pl.program_id(0) == 0)
    def _():
        for ref in list(g.values()) + [dhead_ref]:
            ref[...] = jnp.zeros(ref.shape, F32)

    vec = vec_ref[...]
    rows = sb * SB_ROWS
    y, kept, (_, mixed, _, z3, u, _) = recv_forward(
        send_ref[...].reshape(rows, D), unpack_block(o_ref, sb), w, vec
    )
    head = head_ref[...]
    y2 = split2(y)
    scale = jnp.broadcast_to(scale_ref[...][None], (sb, SB_ROWS, PPAD)).reshape(rows, PPAD)
    mean = jnp.broadcast_to(mean_ref[...][None], (sb, SB_ROWS, PPAD)).reshape(rows, PPAD)
    misfit = mmwt(y2, head) * scale + mean - tgt_ref[...].reshape(rows, PPAD)
    put(saved, (mixed, z3, u))
    dpred = kept_ref[...].reshape(rows, PPAD) * misfit * scale
    dpred2 = split2(dpred)
    dhead_ref[...] += tn3(dpred2, y2)
    dy = mmw(dpred2, head)
    dsend, do, grads = recv_backward(dy, kept, w, vec, g)
    put(later, grads)
    dsend_ref[...] = dsend.reshape(sb, SB_ROWS, D)
    pack_block(do_ref, do, sb)
    recv_flush(accs, [], 1, g_mat, sems)


def tail(send, o, tgt, kept, scale, mean, model, head, sb, parts):
    n = send.shape[0]
    squares = recv_squares(1)
    shapes = [(11, 8, D), (PPAD, D)]
    return pl.pallas_call(
        functools.partial(tail_kernel, sb),
        grid=(n // sb,),
        in_specs=[seg_block(sb), pack_spec(sb), seg_block(sb, SB_ROWS, PPAD), seg_block(sb, SB_ROWS, PPAD)]
        + [whole((SB_ROWS, PPAD))] * 2
        + weight_specs(squares, 3, 1)
        + [whole((PPAD, D))],
        out_specs=[ANY] * 2 + [seg_block(sb), tall_spec(sb)] + [whole(s) for s in shapes]
        + row_specs(sb, (D, D, FF) + LATER_WIDTHS),
        out_shape=pack_shapes()
        + [jax.ShapeDtypeStruct((n, SB_ROWS, D), F32), jax.ShapeDtypeStruct((tall_rows(n, parts), HALF), F32)]
        + [jax.ShapeDtypeStruct(s, F32) for s in shapes]
        + row_shapes(n, (D, D, FF) + LATER_WIDTHS),
        scratch_shapes=RECV_ACC + [pltpu.SemaphoreType.DMA((3,))],
        compiler_params=params_spec(),
        name="tail",
    )(send, o, tgt, kept, scale, mean, *weight_args(model, squares, 3), head)


SEND_W = ("sq", "sk", "sv")


def send_project(dim2, r_rows, w, vec):
    r2 = split2(r_rows)
    sb = r_rows.shape[0] // RPAD
    k = mmw(dim2, w["sk"])
    v = mmw(dim2, w["sv"]) + vec[11:12]
    q = (mmw(r2, w["sq"]) + vec[10:11]) * SCALE
    k = [split2(k[s * SB_ROWS : (s + 1) * SB_ROWS]) for s in range(sb)]
    v = [split2(v[s * SB_ROWS : (s + 1) * SB_ROWS]) for s in range(sb)]
    q = [split2(spread_rows(q[s * RPAD : (s + 1) * RPAD])) for s in range(sb)]
    return r2, k, v, q


def send_fwd_kernel(sb, dim_ref, r_ref, here_ref, *refs):
    w = {n: refs[i][...] for i, n in enumerate(SEND_W)}
    vec_ref, o_ref = refs[3:]
    dim2 = split2(dim_ref[...].reshape(sb * SB_ROWS, D))
    _, k, v, q = send_project(dim2, r_ref[...].reshape(sb * RPAD, D), w, vec_ref[...])
    here = here_ref[...] > 0.5
    scores = [jnp.where(here, nt3_narrow(k2, q2), negative) for k2, q2 in zip(k, q)]
    tops = [jnp.max(sc, 0, keepdims=True) for sc in scores]
    probs = [jnp.where(here, jnp.exp(sc - top), 0.0) for sc, top in zip(scores, tops)]
    totals = [jnp.sum(p, 0, keepdims=True) for p in probs]
    safe = [jnp.where(t > 0.0, t, 1.0) for t in totals]
    mixed = [gather_rows(tn3_short(split2(p / t), v2)) for p, t, v2 in zip(probs, safe, v)]
    for s in range(sb):
        lse = jnp.where(totals[s] > 0.0, tops[s] + jnp.log(safe[s]), negative)
        o_ref[s] = pack_rows(mixed[s], lse)


def send_squares(layer):
    return [12 * layer + k for k in (4, 5, 6)]


def send_fwd(dim, routers, here, model, layer, sb, npad):
    squares = send_squares(layer)
    n = dim.shape[0]
    return pl.pallas_call(
        functools.partial(send_fwd_kernel, sb),
        grid=(n // sb,),
        in_specs=[seg_block(sb), seg_block(sb, RPAD), whole((SB_ROWS, HALF))]
        + weight_specs(squares, None, layer),
        out_specs=pack_spec(sb),
        out_shape=jax.ShapeDtypeStruct((npad, PACK, HALF), F32),
        compiler_params=params_spec(),
        name="send_fwd",
    )(dim, routers, here, *weight_args(model, squares, None))


def send_bwd_kernel(sb, layer, dim_ref, dpart_ref, r_ref, o_ref, do_ref, here_ref, *refs):
    w = {n: refs[i][...] for i, n in enumerate(SEND_W)}
    vec_ref = refs[3]
    g_mat, ddim_ref, dr_ref, rows = refs[5:9]
    dsq_ref, dsk_ref, dsv_ref, sems = refs[9:13]

    @pl.when(pl.program_id(0) == 0)
    def _():
        for ref in (dsq_ref, dsk_ref, dsv_ref, rows):
            ref[...] = jnp.zeros(ref.shape, F32)

    dim2 = split2(dim_ref[...].reshape(sb * SB_ROWS, D))
    r2, k, v, q = send_project(dim2, r_ref[...].reshape(sb * RPAD, D), w, vec_ref[...])
    here = (here_ref[...] > 0.5) & valid_lane(SB_ROWS)
    segs = range(sb)
    scores = [nt3_narrow(k2, q2) for k2, q2 in zip(k, q)]
    probs = [jnp.where(here, jnp.exp(scores[s] - o_ref[s][2 * ROUT : 2 * ROUT + 1]), 0.0) for s in segs]
    dwide = [spread_rows(unpack_rows(do_ref[s * TALL : (s + 1) * TALL])) for s in segs]
    owide = [
        jnp.broadcast_to(unpack_rows(o_ref[s])[:, None, :], (RPAD, HEADS, D)).reshape(RPAD * HEADS, D) for s in segs
    ]
    e = [split2(a * b) for a, b in zip(dwide, owide)]
    d = [split2(a) for a in dwide]
    one_row = jnp.ones((8, D), BF)
    means = [(dots(one_row, e2[0], 1, 1) + dots(one_row, e2[1], 1, 1))[0:1] for e2 in e]
    dp = [nt3_narrow(v2, d2) for v2, d2 in zip(v, d)]
    ds = [split2(p * (x - mean)) for p, x, mean in zip(probs, dp, means)]
    dk = jnp.concatenate([nn3_short(s2, q2) for s2, q2 in zip(ds, q)], 0)
    dv = jnp.concatenate([nn3_short(split2(p), d2) for p, d2 in zip(probs, d)], 0)
    dq = jnp.concatenate([gather_rows(tn3_short(s2, k2)) for s2, k2 in zip(ds, k)], 0) * SCALE
    dk2 = split2(dk)
    dv2 = split2(dv)
    rows[1] += colsum(dv)
    dsk_ref[...] += tn3(dim2, dk2)
    dsv_ref[...] += tn3(dim2, dv2)
    out = dpart_ref[...].reshape(sb * SB_ROWS, D) + mmwt(dk2, w["sk"]) + mmwt(dv2, w["sv"])
    ddim_ref[...] = out.reshape(sb, SB_ROWS, D)
    rows[0] += colsum(dq)
    dq2 = split2(dq)
    dsq_ref[...] += tn3(r2, dq2)
    dr_ref[...] = mmwt(dq2, w["sq"]).reshape(sb, RPAD, D)
    flush(
        pl.program_id(0), pl.num_programs(0) - 1, [dsq_ref, dsk_ref, dsv_ref], send_squares(layer), [], 0, g_mat, None,
        sems,
    )


def send_bwd(dim, dpart, routers, o, do, here, model, layer, sb, g_mat):
    n = dim.shape[0]
    squares = send_squares(layer)
    specs = [seg_block(sb), seg_block(sb), seg_block(sb, RPAD), pack_spec(sb), tall_spec(sb), whole((SB_ROWS, HALF))]
    specs += weight_specs(squares, None, layer)
    return pl.pallas_call(
        functools.partial(send_bwd_kernel, sb, layer),
        grid=(n // sb,),
        in_specs=specs + [ANY],
        out_specs=[ANY, seg_block(sb), seg_block(sb, RPAD), whole((2, 8, D))],
        out_shape=pack_shapes()[:1]
        + [jax.ShapeDtypeStruct((n, SB_ROWS, D), F32), jax.ShapeDtypeStruct((n, RPAD, D), F32)]
        + [jax.ShapeDtypeStruct((2, 8, D), F32)],
        input_output_aliases={len(specs): 0},
        scratch_shapes=[pltpu.VMEM((D, D), F32)] * 3 + [pltpu.SemaphoreType.DMA((3,))],
        compiler_params=params_spec(),
        name="send_bwd",
    )(dim, dpart, routers, o, do, here, *weight_args(model, squares, None), g_mat)

MESH = pl.DeviceIdType.MESH


def grid_sizes():
    nf = lax.axis_size("fsdp")
    nx = 1
    while 2 * nx * nx < nf:
        nx *= 2
    return lax.axis_size("dp") // 2, nf // nx, nx


class Place:
    def __init__(self):
        self.ny, self.nz, self.nx = grid_sizes()
        dp, fs = lax.axis_index("dp"), lax.axis_index("fsdp")
        self.core, self.y = lax.rem(dp, 2), lax.div(dp, 2)
        self.x, self.z = lax.rem(fs, self.nx), lax.div(fs, self.nx)

    def at(self, y=None, core=None, z=None, x=None):
        y = self.y if y is None else y
        core = self.core if core is None else core
        z = self.z if z is None else z
        x = self.x if x is None else x
        return (y * 2 + core, z * self.nx + x)

    def other(self):
        return 1 - self.core

    def next_x(self, k):
        return lax.rem(self.x + k, self.nx)

    def next_y(self, k):
        return lax.rem(self.y + k, self.ny)

    def next_z(self, k):
        return lax.rem(self.z + k, self.nz)

    def neighbours(self):
        out = [self.at(core=self.other())]
        out += [self.at(x=self.next_x(k)) for k in range(1, self.nx)]
        out += [self.at(y=self.next_y(k)) for k in range(1, self.ny)]
        out += [self.at(z=self.next_z(k)) for k in range(1, self.nz)]
        return out


def greet(devices):
    barrier = pltpu.get_barrier_semaphore()
    for device in devices:
        pl.semaphore_signal(barrier, inc=1, device_id=device, device_id_type=MESH)
    pl.semaphore_wait(barrier, len(devices))


def remote(src, dst, send, recv, device):
    return pltpu.make_async_remote_copy(
        src_ref=src, dst_ref=dst, send_sem=send, recv_sem=recv, device_id=device, device_id_type=MESH
    )


def gather_kernel(n, *refs):
    shards, outs = refs[:n], refs[n : 2 * n]
    send, recv, local = refs[2 * n :]
    me = Place()
    y, c, z, x = me.y, me.core, me.z, me.x
    m = me.nx
    greet(me.neighbours())
    slot = [0]

    def push(src, dst, device):
        copy = remote(src, dst, send.at[slot[0]], recv.at[slot[0]], device)
        slot[0] += 1
        copy.start()
        return copy

    def finish(copies):
        for copy in copies:
            copy.wait()

    own = [pltpu.make_async_copy(shards[j], outs[j].at[y, c, z, x], local.at[j]) for j in range(n)]
    for copy in own:
        copy.start()

    def along_z(j):
        return [push(shards[j], outs[j].at[y, c, z, x], me.at(z=me.next_z(k))) for k in range(1, me.nz)]

    first = along_z(0)
    finish(own)
    base = slot[0]

    def rest(by_core):
        slot[0] = base
        sibling = me.at(core=1 - by_core)
        shared = []

        def second(j):
            piece = outs[j].at[y, by_core, :, x]
            out = []
            for k in range(1, m):
                out.append(push(piece, piece, me.at(x=me.next_x(k)) if by_core == 0 else me.at(y=me.next_y(k))))
            shared.append(push(piece, piece, sibling))
            return out

        def third(j):
            wide = outs[j].at[y, by_core] if by_core == 0 else outs[j].at[:, by_core, :, x]
            out = []
            for k in range(1, m):
                out.append(push(wide, wide, me.at(y=me.next_y(k)) if by_core == 0 else me.at(x=me.next_x(k))))
            for k in range(1, m):
                piece = outs[j].at[y, by_core, :, me.next_x(k)] if by_core == 0 else outs[j].at[me.next_y(k), by_core, :, x]
                shared.append(push(piece, piece, sibling))
            return out

        def fourth(j):
            for k in range(1, m):
                wide = outs[j].at[me.next_y(k), by_core] if by_core == 0 else outs[j].at[:, by_core, :, me.next_x(k)]
                shared.append(push(wide, wide, sibling))

        one, two, three = {0: first}, {}, {}
        for t in range(n + 2):
            if t < n:
                finish(one[t])
                if t + 1 < n:
                    one[t + 1] = along_z(t + 1)
            if 0 < t <= n:
                finish(two[t - 1])
            if t < n:
                two[t] = second(t)
            if t > 1:
                finish(three[t - 2])
            if 0 < t <= n:
                three[t - 1] = third(t - 1)
            if t > 1:
                fourth(t - 2)
        finish(shared)

    for by_core in (0, 1):
        pl.when(c == by_core)(functools.partial(rest, by_core))


def gather_all(shards):
    ny, nz, nx = grid_sizes()
    n = len(shards)
    count = n * ((nz - 1) + (nx - 1) + 1 + (nx - 1) * 3)
    return pl.pallas_call(
        functools.partial(gather_kernel, n),
        in_specs=[ANY] * n,
        out_specs=[ANY] * n,
        out_shape=[jax.ShapeDtypeStruct((ny, 2, nz, nx) + s.shape, s.dtype) for s in shards],
        scratch_shapes=[pltpu.SemaphoreType.DMA((count,)), pltpu.SemaphoreType.DMA((count,)), pltpu.SemaphoreType.DMA((n,))],
        compiler_params=pltpu.CompilerParams(collective_id=0, has_side_effects=True, vmem_limit_bytes=VMEM_LIMIT),
        name="gather_all",
    )(*shards)


def row_chunks(rows):
    count = max(1, rows // 40)
    if rows % 8:
        count = 1
    cuts = [rows // 8 * k // count * 8 for k in range(count)] + [rows]
    return [(a, b - a) for a, b in zip(cuts, cuts[1:])]


def scatter_kernel(shapes, *refs):
    n = len(shapes)
    chunks = [(j, a, b) for j, s in enumerate(shapes) for a, b in row_chunks(s[0])]
    total = len(chunks)
    grads, tile_ref = refs[:n], refs[n]
    outs, stat_ref = refs[n + 1 : 2 * n + 1], refs[2 * n + 1]
    bufs = refs[2 * n + 2 :]
    acc, r1, r2, r3, r4 = (bufs[i * total : (i + 1) * total] for i in range(5))
    tp, tz, send, recv, local = bufs[5 * total :]
    me = Place()
    y, c, z, x = me.y, me.core, me.z, me.x
    ny, nz, nx, m = me.ny, me.nz, me.nx, me.nx
    plane = plane_peers(me)
    greet([p for p, _ in plane] + [me.at(z=me.next_z(k)) for k in range(1, nz)])
    slot = [0]

    def push(src, dst, device):
        copy = remote(src, dst, send.at[slot[0]], recv.at[slot[0]], device)
        slot[0] += 1
        copy.start()
        return copy

    def finish(copies):
        for copy in copies:
            copy.wait()

    def rest(by_core):
        slot[0] = 0
        sibling = me.at(core=1 - by_core)

        def one(i):
            j, a, b = chunks[i]
            out = []
            for k in range(nx):
                out.append(push(grads[j].at[:, 1 - by_core, :, k, pl.ds(a, b)], r1[i].at[:, k], sibling))
                copy = pltpu.make_async_copy(grads[j].at[:, by_core, :, k, pl.ds(a, b)], acc[i].at[:, k], local.at[i * nx + k])
                copy.start()
                out.append(copy)
            return out

        def add1(i):
            def body(k, carry):
                at = (lax.div(k, nx * nz), lax.rem(lax.div(k, nz), nx), lax.rem(k, nz))
                acc[i][at] = acc[i][at] + r1[i][at]
                return carry

            lax.fori_loop(0, ny * nx * nz, body, 0)

        def two(i):
            if by_core == 0:
                return [push(acc[i].at[:, me.next_x(k)], r2[i].at[k - 1], me.at(x=me.next_x(k))) for k in range(1, m)]
            return [push(acc[i].at[me.next_y(k)], r2[i].at[k - 1], me.at(y=me.next_y(k))) for k in range(1, m)]

        def add2(i):
            def body(k, carry):
                a, b = lax.div(k, nz), lax.rem(k, nz)
                at = (a, x, b) if by_core == 0 else (y, a, b)
                value = acc[i][at]
                for q in range(m - 1):
                    value = value + r2[i][q, a, b]
                acc[i][at] = value
                return carry

            lax.fori_loop(0, m * nz, body, 0)

        def three(i):
            if by_core == 0:
                return [push(acc[i].at[me.next_y(k), x], r3[i].at[k - 1], me.at(y=me.next_y(k))) for k in range(1, m)]
            return [push(acc[i].at[y, me.next_x(k)], r3[i].at[k - 1], me.at(x=me.next_x(k))) for k in range(1, m)]

        def add3(i):
            def body(k, carry):
                value = acc[i][y, x, k]
                for q in range(m - 1):
                    value = value + r3[i][q, k]
                acc[i][y, x, k] = value
                return carry

            lax.fori_loop(0, nz, body, 0)

        def four(i):
            return [push(acc[i].at[y, x, me.next_z(k)], r4[i].at[k - 1], me.at(z=me.next_z(k))) for k in range(1, nz)]

        def end(i):
            j, a, b = chunks[i]
            value = acc[i][y, x, z]
            for k in range(nz - 1):
                value = value + r4[i][k]
            outs[j][a : a + b] = value
            sq = colsum_any(value * value)
            return sq[:, :HALF] + sq[:, HALF:]

        squares = jnp.zeros((8, HALF), F32)
        ahead = 3
        p1, p2, p3, p4 = {i: one(i) for i in range(min(ahead, total))}, {}, {}, {}
        for t in range(total + 3):
            if t < total:
                finish(p1[t])
                if t + ahead < total:
                    p1[t + ahead] = one(t + ahead)
                add1(t)
                p2[t] = two(t)
            if 0 <= t - 1 < total:
                finish(p2[t - 1])
                add2(t - 1)
                p3[t - 1] = three(t - 1)
            if 0 <= t - 2 < total:
                finish(p3[t - 2])
                add3(t - 2)
                p4[t - 2] = four(t - 2)
            if 0 <= t - 3 < total:
                finish(p4[t - 3])
                squares = squares + end(t - 3)
        tp[(y * 2 + by_core) * nx + x] = jnp.concatenate([squares, tile_ref[...]], 0)

    for by_core in (0, 1):
        pl.when(c == by_core)(functools.partial(rest, by_core))

    slot[0] = total * (nx + 2 * (m - 1) + nz - 1)
    mine = tp.at[(y * 2 + c) * nx + x]
    finish([push(mine, mine, p) for p, _ in plane])
    tz[z] = functools.reduce(jnp.add, [tp[k] for k in range(2 * ny * nx)])
    finish([push(tz.at[z], tz.at[z], me.at(z=me.next_z(k))) for k in range(1, nz)])
    stat_ref[...] = functools.reduce(jnp.add, [tz[k] for k in range(nz)])


def plane_peers(me):
    out = []
    for k in range(1, 2 * me.ny * me.nx):
        dc, dy, dx = k % 2, k // 2 % me.ny, k // (2 * me.ny)
        out.append((me.at(core=lax.rem(me.core + dc, 2), y=lax.rem(me.y + dy, me.ny), x=lax.rem(me.x + dx, me.nx)), k))
    return out


def colsum_any(x):
    rows = x.shape[0]
    even = rows // 8 * 8
    out = colsum(x[:even]) if even else jnp.zeros((8, x.shape[1]), F32)
    if rows > even:
        out = out + jnp.pad(x[even:], ((0, 8 - rows + even), (0, 0)))
    return out


def scatter_sum(grads, tile):
    ny, nz, nx = grid_sizes()
    n = len(grads)
    shapes = [g.shape[-2:] for g in grads]
    pieces = [(b, s[1]) for s in shapes for _, b in row_chunks(s[0])]
    total = len(pieces)
    count = total * (nx + (nx - 1) * 2 + nz - 1) + 2 * ny * nx - 1 + nz - 1

    def buffers(*lead):
        return [pltpu.VMEM(lead + s, F32) for s in pieces]

    return pl.pallas_call(
        functools.partial(scatter_kernel, shapes),
        in_specs=[ANY] * n + [INVMEM],
        out_specs=[INVMEM] * (n + 1),
        out_shape=[jax.ShapeDtypeStruct(s, F32) for s in shapes] + [jax.ShapeDtypeStruct((16, HALF), F32)],
        scratch_shapes=buffers(ny, nx, nz)
        + buffers(ny, nx, nz)
        + buffers(nx - 1, nx, nz)
        + buffers(nx - 1, nz)
        + buffers(nz - 1)
        + [pltpu.VMEM((2 * ny * nx, 16, HALF), F32), pltpu.VMEM((nz, 16, HALF), F32)]
        + [pltpu.SemaphoreType.DMA((count,)), pltpu.SemaphoreType.DMA((count,)), pltpu.SemaphoreType.DMA((total * nx,))],
        compiler_params=pltpu.CompilerParams(collective_id=1, has_side_effects=True, vmem_limit_bytes=VMEM_LIMIT),
        name="scatter_sum",
    )(*grads, tile)


def group_part(ref, who, per):
    return ref.at[pl.ds(pl.multiple_of(who * per, per), per)]


def group_out(per, in_ref, got, send, recv, local):
    nf = lax.axis_size("fsdp")
    dp, f = lax.axis_index("dp"), lax.axis_index("fsdp")
    copies = [pltpu.make_async_copy(group_part(in_ref, f, per), got.at[f], local)]
    for k in range(1, nf):
        p = lax.rem(f + k, nf)
        copies.append(remote(group_part(in_ref, p, per), got.at[f], send.at[k - 1], recv.at[k - 1], (dp, p)))
    return copies


def group_back(per, result, out_ref, send, recv, local):
    nf = lax.axis_size("fsdp")
    dp, f = lax.axis_index("dp"), lax.axis_index("fsdp")
    copies = [pltpu.make_async_copy(result, group_part(out_ref, f, per), local)]
    for k in range(1, nf):
        p = lax.rem(f + k, nf)
        copies.append(remote(result, group_part(out_ref, f, per), send.at[nf - 2 + k], recv.at[nf - 2 + k], (dp, p)))
    return copies


def greet_group():
    nf = lax.axis_size("fsdp")
    dp, f = lax.axis_index("dp"), lax.axis_index("fsdp")
    greet([(dp, lax.rem(f + k, nf)) for k in range(1, nf)])


def start_all(copies):
    for copy in copies:
        copy.start()


def wait_all(copies):
    for copy in copies:
        copy.wait()


def stats_kernel(per, in_ref, out_ref, got, result, send, recv, local):
    nf = lax.axis_size("fsdp")
    greet_group()
    copies = group_out(per, in_ref, got, send, recv, local)
    start_all(copies)
    wait_all(copies)
    row = lax.broadcasted_iota(jnp.int32, (PACK, HALF), 0)
    lane = lax.broadcasted_iota(jnp.int32, (PACK, HALF), 1)
    router = jnp.where(row < ROUT, row, row - ROUT)
    chosen = (lane // 8 == router) & (row < 2 * ROUT)
    src = lax.broadcasted_iota(jnp.int32, (HALF, D), 0)
    dst = lax.broadcasted_iota(jnp.int32, (HALF, D), 1)
    widen = jnp.where(src % 8 == dst // 32, 1.0, 0.0).astype(BF)

    def one(s, carry):
        lse = [got[d, s, 2 * ROUT : 2 * ROUT + 1, :] for d in range(nf)]
        top = functools.reduce(jnp.maximum, lse)
        total = top + jnp.log(functools.reduce(jnp.add, [jnp.exp(l - top) for l in lse]))
        out = jnp.where(row == 2 * ROUT, total, 0.0)
        share = jnp.concatenate([jnp.where(chosen, jnp.exp(l - total), 0.0) for l in lse], 0)
        wide = mmw(split2(share), widen)
        for d in range(nf):
            w = wide[d * PACK : (d + 1) * PACK]
            w = jnp.where(row < ROUT, w[:, :HALF], w[:, HALF:])
            out = out + jnp.where(row < 2 * ROUT, w * got[d, s], 0.0)
        result[s] = out
        return carry

    lax.fori_loop(0, per, one, 0)
    copies = group_back(per, result, out_ref, send, recv, local)
    start_all(copies)
    wait_all(copies)


def sum_kernel(per, turn, in_ref, x_ref, mixed_ref, z_ref, u_ref, dq_ref, dz3_ref, du_ref, dz4_ref, vec_ref, *refs):
    out_ref, rq, ro, up, down, got, result, send, recv, local = refs
    step = pl.program_id(0)

    @pl.when(step == 0)
    def _():
        greet_group()
        start_all(group_out(per, in_ref, got, send, recv, local))
        for ref in (rq, ro, up, down):
            ref[...] = jnp.zeros(ref.shape, F32)

    @pl.when(step == turn)
    def _():
        wait_all(group_out(per, in_ref, got, send, recv, local))
        result[...] = functools.reduce(jnp.add, [got[d] for d in range(lax.axis_size("fsdp"))])
        start_all(group_back(per, result, out_ref, send, recv, local))

    rq[...] += tn3(split2(x_ref[...]), split2(dq_ref[...]))
    ro[...] += tn3(split2(mixed_ref[...]), split2(dz3_ref[...]))
    g, _, _ = norm_fwd(z_ref[...], vec_ref[16:17], vec_ref[17:18])
    up[...] += tn3(split2(g), split2(du_ref[...]))
    u = u_ref[...]
    down[...] += tn3(split2(u * gelu_cdf(u)), split2(dz4_ref[...]))

    @pl.when(step == pl.num_programs(0) - 1)
    def _():
        wait_all(group_back(per, result, out_ref, send, recv, local))


def group_scratch(part, nf):
    return [
        pltpu.VMEM((nf,) + part, F32),
        pltpu.VMEM(part, F32),
        pltpu.SemaphoreType.DMA((2 * nf - 2,)),
        pltpu.SemaphoreType.DMA((2 * nf - 2,)),
        pltpu.SemaphoreType.DMA,
    ]


def group_params(cid):
    return pltpu.CompilerParams(collective_id=cid, has_side_effects=True, vmem_limit_bytes=VMEM_LIMIT)


def group_stats(packed, cid):
    nf = lax.axis_size("fsdp")
    per = packed.shape[0] // nf
    return pl.pallas_call(
        functools.partial(stats_kernel, per),
        in_specs=[ANY],
        out_specs=ANY,
        out_shape=jax.ShapeDtypeStruct(packed.shape, F32),
        scratch_shapes=group_scratch((per, PACK, HALF), nf),
        compiler_params=group_params(cid),
        name="group_stats",
    )(packed)


def group_sum(packed, work, vecs, layer, cid):
    nf = lax.axis_size("fsdp")
    per = packed.shape[0] // nf
    rows = 480
    steps = work[0].shape[0] // rows
    shapes = [(D, D), (D, D), (D, FF), (FF, D)]
    return pl.pallas_call(
        functools.partial(sum_kernel, per, steps - steps // 4),
        grid=(steps,),
        in_specs=[ANY] + [pl.BlockSpec((rows, w.shape[1]), lambda i: (i, 0)) for w in work] + [pick((24, D), layer)],
        out_specs=[ANY] + [whole(s) for s in shapes],
        out_shape=[jax.ShapeDtypeStruct(packed.shape, F32)] + [jax.ShapeDtypeStruct(s, F32) for s in shapes],
        scratch_shapes=group_scratch((per, HALF), nf),
        compiler_params=group_params(cid),
        name="group_sum",
    )(packed, *work, vecs)

LAYER_AT = SEGLEN + 1 + SEG
MERGE_AT = LAYER_AT + 46
HEAD_AT = MERGE_AT + 5
ROUTER_AT = HEAD_AT + PRED
VROWS = NVEC + 20


def own_size(devices):
    own = NVEC * D // devices
    return own, -(-own // D)


def prepare_kernel(nfeed, ser_ref, obs_ref, tgt_ref, mask_ref, count_ref, mat_ref, feed_ref, vec_ref, *outs):
    pieces, tgt, kept, scale_ref, mean_ref, here_ref, tile_ref, mat_o, feed_o, vec_o = outs
    for src, dst in ((mat_ref, mat_o), (feed_ref, feed_o), (vec_ref, vec_o)):
        rows = dst.shape[0]
        left, right = src[pl.ds(0, rows, stride=2), :], src[pl.ds(1, rows, stride=2), :]
        dst[...] = jnp.concatenate([left, right], 1).astype(BF)
    nv = ser_ref.shape[0]
    series, seen = ser_ref[...], obs_ref[...].astype(F32)
    counted = jnp.maximum(jnp.sum(seen, -1, keepdims=True), 1.0)
    mean = jnp.sum(seen * series, -1, keepdims=True) / counted
    center = (series - mean) * seen
    scale = jnp.sqrt(jnp.sum(center * center, -1, keepdims=True) / counted + norm_eps)
    slot = lax.axis_index("fsdp") * nv + lax.broadcasted_iota(jnp.int32, (nv, HALF), 0)
    here = jnp.where(slot < count_ref[0], 1.0, 0.0)
    here_ref[...] = here
    scale_ref[...] = jnp.broadcast_to(scale, (nv, PPAD))
    mean_ref[...] = jnp.broadcast_to(mean, (nv, PPAD))
    mask = mask_ref[...].astype(F32) * here[:, :1]
    tile_ref[...] = jnp.broadcast_to(jnp.sum(jnp.sum(mask, 0, keepdims=True), -1, keepdims=True), (8, HALF)) * (1.0 / (8 * HALF))
    lane = lax.broadcasted_iota(jnp.int32, (nv, PPAD), 1)

    def cut(x, dst):
        x = jnp.concatenate([x, jnp.zeros((nv, PPAD - 12), F32)], 1)
        for s in range(dst.shape[0]):
            dst[s] = jnp.where(lane < 12, x[:, 12 * s : 12 * s + PPAD], 0.0)

    cut(center / scale, pieces)
    cut(tgt_ref[...], tgt)
    cut(mask * (2.0 / (1 << 20)), kept)


def prepare(series, observed, targets, target_mask, counts, matrices, feed, vectors):
    nv = series.shape[0]
    shapes = [((SEG, nv, PPAD), F32), ((SEG // 2, nv, PPAD), F32), ((SEG // 2, nv, PPAD), F32), ((nv, PPAD), F32), ((nv, PPAD), F32)]
    shapes += [((nv, HALF), F32), ((8, HALF), F32)]
    shapes += [((x.shape[0] // 2, D), BF) for x in (matrices, feed, vectors)]
    return pl.pallas_call(
        functools.partial(prepare_kernel, 0),
        grid=(1,),
        in_specs=[whole(x.shape) for x in (series, observed, targets, target_mask)]
        + [pl.BlockSpec(memory_space=pltpu.SMEM)]
        + [whole(x.shape) for x in (matrices, feed, vectors)],
        out_specs=[whole(s) for s, _ in shapes],
        out_shape=[jax.ShapeDtypeStruct(s, t) for s, t in shapes],
        compiler_params=pltpu.CompilerParams(vmem_limit_bytes=VMEM_LIMIT),
        name="prepare",
    )(series, observed, targets, target_mask, counts, matrices, feed, vectors)


def unpack_kernel(devices, own, vec_ref, vecs, mvec, emb, place, head, r0, r1, flat):
    flat[...] = jnp.zeros(flat.shape, F32)
    rows = vec_ref.shape[1]
    lane = lax.broadcasted_iota(jnp.int32, (rows, D), 1)
    for d in range(devices):
        at, shift = divmod(own * d, D)
        block = vec_ref[d].astype(F32)
        if shift:
            block = pltpu.roll(block, shift, 1)
            flat[at + 1 : at + 1 + rows] += jnp.where(lane < shift, block, 0.0)
            block = jnp.where(lane >= shift, block, 0.0)
        flat[at : at + rows] += block

    def padded(at, count, total):
        return jnp.concatenate([flat[at : at + count], jnp.zeros((total - count, D), F32)], 0)

    for l in range(2):
        vecs[l] = padded(LAYER_AT + 23 * l, 23, 24)
    mvec[...] = padded(MERGE_AT, 5, 8)
    emb[...] = padded(0, SEGLEN, 16).astype(BF)
    head[...] = padded(HEAD_AT, PRED, PPAD).astype(BF)
    for s in range(SEG):
        place[s] = flat[SEGLEN + 1 + s : SEGLEN + 2 + s] + flat[SEGLEN : SEGLEN + 1]
        r0[s] = padded(ROUTER_AT + ROUT * s, ROUT, RPAD)
    for s in range(SEG // 2):
        r1[s] = padded(ROUTER_AT + ROUT * (SEG + s), ROUT, RPAD)


def unpack_vectors(gathered, own):
    devices, rows, _ = gathered.shape
    shapes = [((2, 24, D), F32), ((8, D), F32), ((16, D), BF), ((SEG, 1, D), F32), ((PPAD, D), BF)]
    shapes += [((SEG, RPAD, D), F32), ((SEG // 2, RPAD, D), F32)]
    return pl.pallas_call(
        functools.partial(unpack_kernel, devices, own),
        grid=(1,),
        in_specs=[whole(gathered.shape)],
        out_specs=[whole(s) for s, _ in shapes],
        out_shape=[jax.ShapeDtypeStruct(s, t) for s, t in shapes],
        scratch_shapes=[pltpu.VMEM((VROWS + 24, D), F32)],
        compiler_params=pltpu.CompilerParams(vmem_limit_bytes=VMEM_LIMIT),
        name="unpack_vectors",
    )(gathered)


def assemble_kernel(devices, own, demb, dplace, *refs):
    (rt0, rs0, rr0, rt1, rs1, rr1, dmv, dhead, dr0, dr1), out, flat = refs[:10], refs[10], refs[11]
    flat[...] = jnp.zeros(flat.shape, F32)
    flat[0:SEGLEN] = demb[0:SEGLEN]
    place = jnp.sum(dplace[...].reshape(SEG, VB, D), 1)
    flat[SEGLEN : SEGLEN + 1] = jnp.sum(place, 0, keepdims=True)
    flat[SEGLEN + 1 : SEGLEN + 1 + SEG] = place
    at = LAYER_AT
    for ref in (rt0, rs0, rr0, rt1, rs1, rr1, dmv):
        count = ref.shape[0]
        flat[at : at + count] = jnp.sum(ref[...], 1)
        at += count
    flat[HEAD_AT : HEAD_AT + PRED] = dhead[0:PRED]
    for s in range(SEG):
        flat[ROUTER_AT + ROUT * s : ROUTER_AT + ROUT * (s + 1)] = dr0[s][:ROUT]
    for s in range(SEG // 2):
        flat[ROUTER_AT + ROUT * (SEG + s) : ROUTER_AT + ROUT * (SEG + s + 1)] = dr1[s][:ROUT]
    rows = out.shape[1]
    lane = lax.broadcasted_iota(jnp.int32, (rows, D), 1)
    inside = lax.broadcasted_iota(jnp.int32, (rows, D), 0) * D + lane < own
    for d in range(devices):
        at, shift = divmod(own * d, D)
        block = flat[at : at + rows]
        if shift:
            block = jnp.where(lane < D - shift, pltpu.roll(block, D - shift, 1), pltpu.roll(flat[at + 1 : at + 1 + rows], D - shift, 1))
        out[d] = jnp.where(inside, block, 0.0)


def assemble_vectors(parts, devices):
    own, rows = own_size(devices)
    return pl.pallas_call(
        functools.partial(assemble_kernel, devices, own),
        grid=(1,),
        in_specs=[whole(p.shape) for p in parts],
        out_specs=whole((devices, rows, D)),
        out_shape=jax.ShapeDtypeStruct((devices, rows, D), F32),
        scratch_shapes=[pltpu.VMEM((VROWS + 24, D), F32)],
        compiler_params=pltpu.CompilerParams(vmem_limit_bytes=VMEM_LIMIT),
        name="assemble_vectors",
    )(*parts)


def adam_update(weight, first_moment, second_moment, gradient):
    first_new = beta_one * first_moment + (1.0 - beta_one) * gradient
    second_new = beta_two * second_moment + (1.0 - beta_two) * gradient * gradient
    corrected = (
        first_new
        / (1.0 - beta_one**step_count)
        / (jnp.sqrt(second_new / (1.0 - beta_two**step_count)) + adam_eps)
    )
    return (weight - learn_rate * (corrected + weight_decay * weight), first_new, second_new)


def gradient_parts(ready, model, extras, up_rows, group_stats, group_sum, nf, devices):
    pieces, tgt, kept, scale, mean, here = ready
    mvec, emb, place, head, routers0, routers1 = extras
    sb0, sb1, sf0, sf1, st = 12, 10, 20, 10, 10
    rf, rb = 20, 20
    half = SEG // 2
    dim0, kept0 = time_fwd(True, pieces, (emb, place), model, 0, SEG)
    o0 = send_fwd(dim0, routers0, here, model, 0, sf0, -(-SEG // nf) * nf)
    o0 = group_stats(o0, 2)
    x1, *saved = recv_fwd(dim0, o0, model, mvec, rf)
    dim1, kept1 = time_fwd(False, x1, (), model, 1, half)
    o1 = send_fwd(dim1, routers1, here, model, 1, sf1, -(-half // nf) * nf)
    o1 = group_stats(o1, 3)
    vecs = model[3]
    g_mat, g_feed, ddim1, do1, rr1, dhead, *work = tail(dim1, o1, tgt, kept, scale, mean, model, head, st, nf)
    do1, *later = group_sum(do1, [dim1.reshape(-1, D)] + work, vecs, 1, 4)
    g_mat, ddim1, dr1, rs1 = send_bwd(dim1, ddim1, routers1, o1, do1, here, model, 1, sb1, g_mat)
    g_mat, g_feed, rt1, dx1 = time_bwd(
        False, x1, (), ddim1, kept1, model, 1, half, later, (g_mat, g_feed), up_rows
    )
    g_mat, ddim0, do0, rr0, dmv, *work = recv_bwd(dim0, o0, dx1, saved, model, mvec, rb, g_mat, nf)
    work = [dim0.reshape(-1, D), saved[1], saved[3], saved[4]] + work
    do0, *later = group_sum(do0, work, vecs, 0, 5)
    g_mat, ddim0, dr0, rs0 = send_bwd(dim0, ddim0, routers0, o0, do0, here, model, 0, sb0, g_mat)
    g_mat, g_feed, rt0, demb, dplace = time_bwd(
        True, pieces, (emb, place), ddim0, kept0, model, 0, SEG, later, (g_mat, g_feed), up_rows
    )
    g_vec = assemble_vectors((demb, dplace, rt0, rs0, rr0, rt1, rs1, rr1, dmv, dhead, dr0, dr1), devices)
    return g_mat, g_feed, g_vec


def on_device(series, observed, targets, target_mask, counts, matrices, feed_weights, vectors, matrices_first, matrices_second, feed_first, feed_second, vectors_first, vectors_second):
    nf = lax.axis_size("fsdp")
    nd = lax.axis_size("dp")
    devices = nf * nd
    own, vec_rows = own_size(devices)
    out = prepare(
        series[0],
        observed[0],
        targets[0],
        target_mask[0],
        counts,
        matrices.reshape(-1, HALF),
        feed_weights.reshape(-1, HALF),
        jnp.pad(vectors, (0, vec_rows * D - own)).reshape(-1, HALF),
    )
    ready, tile, shards = out[:6], out[6], out[7:]
    square, feed, vecs = gather_all(shards)
    square = square.reshape(NSQ, D, D)
    feed = feed.reshape(-1, D)
    up = feed[: 4 * FF].reshape(4, D, FF)
    down = feed.reshape(8, FF, D)
    vecs, *extras = unpack_vectors(vecs.reshape(devices, vec_rows, D), own)
    up_rows = feed_weights.shape[0] // FF
    g_mat, g_feed, g_vec = gradient_parts(ready, (square, up, down, vecs), extras, up_rows, group_stats, group_sum, nf, devices)
    ny, nz, nx = grid_sizes()
    lead = (ny, 2, nz, nx)
    s_mat, s_feed, s_vec, sums = scatter_sum([g.reshape(lead + (-1, D)) for g in (g_mat, g_feed, g_vec)], tile)
    is_up = lax.axis_index("dp") * 2 < nd
    halves_of = s_feed.reshape(2, up_rows, D)
    s_feed = jnp.where(is_up, jnp.concatenate([halves_of[0], halves_of[1]], 1).reshape(-1), s_feed.reshape(-1))
    grads = (s_mat.reshape(-1), s_feed, s_vec.reshape(-1)[:own])
    upscale = (1 << 20) / jnp.maximum(jnp.sum(sums[8:]), 1.0)
    grad_norm = jnp.sqrt(jnp.sum(sums[:8])) * upscale
    factor = upscale * (clip_norm / jnp.maximum(grad_norm, clip_norm))
    new = (
        adam_update(matrices, matrices_first, matrices_second, grads[0] * factor)
        + adam_update(feed_weights, feed_first, feed_second, grads[1] * factor)
        + adam_update(vectors, vectors_first, vectors_second, grads[2] * factor)
    )
    return (grad_norm,) + new


def solution(mesh):
    both = P(("dp", "fsdp"))
    data = P("dp", "fsdp", None)
    return jax.shard_map(
        on_device,
        mesh=mesh,
        in_specs=(data,) * 4 + (P("dp"),) + (both,) * 9,
        out_specs=(P(),) + (both,) * 9,
        check_vma=False,
    )
```

```python
import functools
import jax
import jax.numpy as jnp
from jax import lax
from jax.experimental import pallas as pl
from jax.experimental.pallas import tpu as pltpu
from jax.sharding import PartitionSpec as P

D = 256
HEADS = 8
FF = 512
ROUT = 10
RPAD = 16
SEGLEN = 12
PRED = 12
PPAD = 16
SEG = 60
NSQ = 26
NVEC = 1036
HALF = 128
VB = 8
UNROLL = 8
UNROLL_BACK = 8

BF = jnp.bfloat16
F32 = jnp.float32
SCALE = (D // HEADS) ** (-0.5)
negative = -1e30
norm_eps = 1e-05
beta_one = 0.9
beta_two = 0.999
adam_eps = 1e-08
weight_decay = 0.01
learn_rate = 0.2
clip_norm = 0.01
step_count = 10.0
VMEM_LIMIT = 60 << 20


ANY = pl.BlockSpec(memory_space=pl.ANY)
INVMEM = pl.BlockSpec(memory_space=pltpu.VMEM)


def split2(x):
    hi = x.astype(BF)
    return hi, (x - hi.astype(F32)).astype(BF)


def dots(a, b, ca, cb):
    return lax.dot_general(a, b, (((ca,), (cb,)), ((), ())), preferred_element_type=F32)


def mmw(x2, w):
    return dots(x2[0], w, 1, 0) + dots(x2[1], w, 1, 0)


def mmwt(x2, w):
    return dots(x2[0], w, 1, 1) + dots(x2[1], w, 1, 1)


def rows2(a2):
    return jnp.concatenate([a2[0], a2[1]], 0)


def nn3(a2, b2):
    m = a2[0].shape[0]
    both = dots(rows2(a2), b2[0], 1, 0)
    return both[:m] + both[m:] + dots(a2[0], b2[1], 1, 0)


def nt3(a2, b2):
    m = a2[0].shape[0]
    both = dots(rows2(a2), b2[0], 1, 1)
    return both[:m] + both[m:] + dots(a2[0], b2[1], 1, 1)


def tn3(a2, b2):
    n = b2[0].shape[1]
    both = dots(a2[0], jnp.concatenate([b2[0], b2[1]], 1), 0, 0)
    return both[:, :n] + both[:, n:] + dots(a2[1], b2[0], 0, 0)


def tn3_short(a2, b2):
    return dots(jnp.concatenate([a2[0], a2[0], a2[1]], 0), jnp.concatenate([b2[0], b2[1], b2[0]], 0), 0, 0)


def nn3_short(a2, b2):
    return dots(jnp.concatenate([a2[0], a2[0], a2[1]], 1), jnp.concatenate([b2[0], b2[1], b2[0]], 0), 1, 0)


def corner(r, m, n):
    return r[:m, :n] + r[m:, :n] + r[:m, n:]


def nn3_narrow(a2, b2):
    r = dots(rows2(a2), jnp.concatenate([b2[0], b2[1]], 1), 1, 0)
    return corner(r, a2[0].shape[0], b2[0].shape[1])


def nt3_narrow(a2, b2):
    return corner(dots(rows2(a2), rows2(b2), 1, 1), a2[0].shape[0], b2[0].shape[0])


def norm_fwd(z, gain, bias):
    center = z - jnp.mean(z, -1, keepdims=True)
    inv = lax.rsqrt(jnp.mean(center * center, -1, keepdims=True) + norm_eps)
    unit = center * inv
    return unit * gain + bias, unit, inv


def norm_bwd(dy, unit, inv, gain):
    t = dy * gain
    return inv * (t - jnp.mean(t, -1, keepdims=True) - unit * jnp.mean(t * unit, -1, keepdims=True))


def colsum(x):
    return jnp.sum(x.reshape(x.shape[0] // 8, 8, x.shape[1]), 0)


def gelu_cdf(u):
    return 0.5 + 0.5 * lax.erf(u * 0.7071067811865476)


def gelu_slope(u, cdf):
    return cdf + u * (jnp.exp(-0.5 * u * u) * 0.3989422804014327)


def halves(x):
    return x[:, :HALF], x[:, HALF:]


def lane_head(rows):
    return lax.broadcasted_iota(jnp.int32, (rows, HALF), 1) // 32


def spread_heads(x, zero):
    head = lane_head(x.shape[0])
    return jnp.concatenate([jnp.where(head == h, x, zero) for h in range(4)], 0)


def gather_heads(x, group):
    head = lane_head(group)
    out = x[3 * group :]
    for h in range(3):
        out = jnp.where(head == h, x[h * group : (h + 1) * group], out)
    return out


def ones_heads(group, count):
    row = lax.broadcasted_iota(jnp.int32, (4 * group, HALF), 0)
    lane = lax.broadcasted_iota(jnp.int32, (4 * group, HALF), 1)
    return jnp.where((row // group == lane // 32) & (row % group < count), 1.0, 0.0).astype(BF)


def group_max(s, group, count):
    lane = lax.broadcasted_iota(jnp.int32, (s.shape[0], HALF), 1)
    outs = []
    for t in range(s.shape[1] // HALF):
        part = s[:, t * HALF : (t + 1) * HALF]
        top = None
        for g in range(HALF // group):
            here = (lane // group == g)
            best = jnp.max(jnp.where((lane // group == g) & (lane % group < count), part, negative), -1, keepdims=True)
            top = jnp.broadcast_to(best, part.shape) if top is None else jnp.where(here, best, top)
        outs.append(jnp.where(lane % group < count, part - top, negative))
    return jnp.concatenate(outs, 1)


def time_parts(units, group, ref):
    return [split2(ref[c, pl.ds(v, group, stride=VB), :]) for c, v in units]


def spread2(x2):
    zero = jnp.zeros((), BF)
    return spread_heads(x2[0], zero), spread_heads(x2[1], zero)


def time_attend(units, group, count, q_s, k_s, v_s, o_s, p_s, l_s):
    q = time_parts(units, group, q_s)
    k = [spread2(x2) for x2 in time_parts(units, group, k_s)]
    scores = [
        dots(jnp.concatenate(q2, 1), jnp.concatenate([k2[0], k2[0]], 1), 1, 1) + dots(q2[0], k2[1], 1, 1)
        for q2, k2 in zip(q, k)
    ]
    probs = [jnp.exp(group_max(s, group, count)) for s in scores]
    probs2 = [split2(p) for p in probs]
    w = [spread2(x2) for x2 in time_parts(units, group, v_s)]
    ones = ones_heads(group, count)
    both = [dots(rows2(p2), jnp.concatenate([w2[0], ones], 1), 1, 0) for p2, w2 in zip(probs2, w)]
    both = [b[:group] + b[group:] for b in both]
    inv = [1.0 / b[:, HALF:] for b in both]
    mixed = [(b[:, :HALF] + dots(p2[0], w2[1], 1, 0)) * i for b, p2, w2, i in zip(both, probs2, w, inv)]
    for (c, v), o, p, i in zip(units, mixed, probs, inv):
        o_s[c, pl.ds(v, group, stride=VB), :] = o
        p_s[c, v] = p
        l_s[c, v] = i


def time_attend_back(units, group, count, q_s, k_s, v_s, o_s, p_s, l_s, do_s, dq_s, dk_s, dv_s):
    d = [do_s[c, pl.ds(v, group, stride=VB), :] * l_s[c, v] for c, v in units]
    e2 = [split2(x * o_s[c, pl.ds(v, group, stride=VB), :]) for x, (c, v) in zip(d, units)]
    d2 = [split2(x) for x in d]
    w = [spread2(x2) for x2 in time_parts(units, group, v_s)]
    ones = -ones_heads(group, count)
    both = [
        dots(
            jnp.concatenate([jnp.concatenate([a[0], b[0]], 1), jnp.concatenate([a[1], b[1]], 1)], 0),
            jnp.concatenate([w2[0], ones], 1),
            1,
            1,
        )
        for a, b, w2 in zip(d2, e2, w)
    ]
    dp = [b[:group] + b[group:] + dots(a[0], w2[1], 1, 1) for b, a, w2 in zip(both, d2, w)]
    probs = [p_s[c, v] for c, v in units]
    s2 = [split2(p * x) for p, x in zip(probs, dp)]
    p2 = [split2(p) for p in probs]
    k = [spread2(x2) for x2 in time_parts(units, group, k_s)]
    dq = [nn3_narrow(a, k2) for a, k2 in zip(s2, k)]
    q = time_parts(units, group, q_s)
    dk = [gather_heads(tn3_short(a, q2), group) for a, q2 in zip(s2, q)]
    dv = [gather_heads(tn3_short(a, x), group) for a, x in zip(p2, d2)]
    for (c, v), x, y, z in zip(units, dq, dk, dv):
        at = pl.ds(v, group, stride=VB)
        dq_s[c, at, :] = x
        dk_s[c, at, :] = y
        dv_s[c, at, :] = z


def store_halves(ref, x):
    rows = x.shape[0]
    ref[0, :rows, :] = x[:, :HALF]
    ref[1, :rows, :] = x[:, HALF:]


def load_halves(ref, rows):
    return jnp.concatenate([ref[0, :rows, :], ref[1, :rows, :]], 1)


def zero_tail(ref, rows):
    tail = ref.shape[1] - rows
    ref[:, rows:, :] = jnp.zeros((2, tail, HALF), F32)


def time_forward(x, w, vec, count, group, kept):
    q_s, k_s, v_s, o_s, p_s, l_s, z1_s, u_s, z2_s = kept
    rows = count * VB
    x2 = split2(x)
    store_halves(q_s, (mmw(x2, w["q"]) + vec[0:1]) * SCALE)
    store_halves(k_s, mmw(x2, w["k"]))
    store_halves(v_s, mmw(x2, w["v"]) + vec[1:2])
    for ref in (q_s, k_s, v_s):
        zero_tail(ref, rows)

    def some(i, carry):
        units = [(c, i * UNROLL + k) for k in range(UNROLL) for c in range(2)]
        time_attend(units, group, count, q_s, k_s, v_s, o_s, p_s, l_s)
        return carry

    lax.fori_loop(0, VB // UNROLL, some, 0)
    z1 = x + mmw(split2(load_halves(o_s, rows)), w["o"]) + vec[2:3]
    z1_s[...] = z1
    h, _, _ = norm_fwd(z1, vec[3:4], vec[4:5])
    u = mmw(split2(h), w["up"]) + jnp.concatenate([vec[5:6], vec[6:7]], 1)
    u_s[...] = u
    z2 = h + mmw(split2(u * gelu_cdf(u)), w["down"]) + vec[7:8]
    z2_s[...] = z2
    return norm_fwd(z2, vec[8:9], vec[9:10])[0]


def embed_block(pieces, emb, place):
    return mmw(split2(pieces), emb) + place


TIME_W = ("q", "k", "v", "o", "up", "down")


def time_fwd_kernel(first, count, group, *refs):
    if first:
        x_ref, emb_ref, place_ref = refs[:3]
        refs = refs[3:]
    else:
        x_ref = refs[0]
        refs = refs[1:]
    w = {name: refs[i][...] for i, name in enumerate(TIME_W)}
    vec_ref, y_ref = refs[6:8]
    rows = count * VB
    if first:
        place = jnp.broadcast_to(place_ref[...], (count, VB, D)).reshape(rows, D)
        x = embed_block(x_ref[...].reshape(rows, 16), emb_ref[...], place)
    else:
        x = x_ref[...].reshape(rows, D)
    y = time_forward(x, w, vec_ref[...], count, group, refs[8:])
    y_ref[...] = y.reshape(count, VB, D)


def whole(shape):
    return pl.BlockSpec(shape, lambda i: (0,) * len(shape))


def params_spec():
    return pltpu.CompilerParams(vmem_limit_bytes=VMEM_LIMIT)


def pick(shape, index):
    return pl.BlockSpec((None,) + shape, lambda i: (index,) + (0,) * len(shape))


def weight_specs(squares, feed, layer):
    specs = [pick((D, D), k) for k in squares]
    if feed is not None:
        specs += [pick((D, FF), feed), pick((FF, D), 4 + feed)]
    return specs + [pick((24, D), layer)]


def weight_args(model, squares, feed):
    square, up, down, vecs = model
    return [square] * len(squares) + ([up, down] if feed is not None else []) + [vecs]


def flush(step, last, accs, mat_at, feeds, up_rows, g_mat, g_feed, sems):
    @pl.when(step == last)
    def _():
        copies = []

        def add(src, dst):
            copies.append(pltpu.make_async_copy(src, dst, sems.at[len(copies)]))

        for acc, at in zip(accs, mat_at):
            add(acc, g_mat.at[pl.ds(at, acc.shape[0])] if len(acc.shape) == 3 else g_mat.at[at])
        for up_acc, down_acc, feed_at in feeds:
            for k in range(D // up_rows):
                for half in range(2):
                    base = 2 * D * feed_at + (2 * k + half) * up_rows
                    add(up_acc.at[pl.ds(k * up_rows, up_rows), pl.ds(half * D, D)], g_feed.at[pl.ds(base, up_rows)])
            add(down_acc, g_feed.at[pl.ds(4 * FF + feed_at * FF, FF)])
        for copy in copies:
            copy.start()
        for copy in copies:
            copy.wait()


def pack_shapes():
    return [jax.ShapeDtypeStruct((NSQ, D, D), F32), jax.ShapeDtypeStruct((8 * FF, D), F32)]


def flush_count(mats, feeds, up_rows):
    return mats + feeds * (2 * D // up_rows + 1 if up_rows else 0)


def time_kept(count, group, nb):
    pad, rows = group * VB, count * VB
    shapes = [(2, pad, HALF)] * 4 + [(2, VB, group, 4 * group), (2, VB, group, HALF), (rows, D), (rows, FF), (rows, D)]
    specs = [pl.BlockSpec((None,) + s, lambda i, n=len(s): (i,) + (0,) * n) for s in shapes]
    return specs, [jax.ShapeDtypeStruct((nb,) + s, F32) for s in shapes]


def time_fwd(first, x, extra, model, layer, count):
    squares = [12 * layer + k for k in range(4)]
    group = 64 if count > 32 else 32
    nv = x.shape[1]
    width = x.shape[2]
    specs = [pl.BlockSpec((count, VB, width), lambda i: (0, i, 0))]
    if first:
        specs += [whole((16, D)), whole((count, 1, D))]
    kept_specs, kept_shapes = time_kept(count, group, nv // VB)
    out = pl.pallas_call(
        functools.partial(time_fwd_kernel, first, count, group),
        grid=(nv // VB,),
        in_specs=specs + weight_specs(squares, 2 * layer, layer),
        out_specs=[pl.BlockSpec((count, VB, D), lambda i: (0, i, 0))] + kept_specs,
        out_shape=[jax.ShapeDtypeStruct((count, nv, D), F32)] + kept_shapes,
        compiler_params=params_spec(),
        name="time_fwd",
    )(x, *extra, *weight_args(model, squares, 2 * layer))
    return out[0], out[1:]


def time_bwd_kernel(first, count, group, layer, up_rows, *refs):
    if first:
        x_ref, emb_ref, place_ref = refs[:3]
        refs = refs[3:]
    else:
        x_ref = refs[0]
        refs = refs[1:]
    dy_ref = refs[0]
    q_s, k_s, v_s, o_s, p_s, l_s, z1_s, u_s, z2_s = refs[1:10]
    w = {name: refs[10 + i][...] for i, name in enumerate(TIME_W)}
    vec_ref = refs[16]
    later = refs[17:21]
    g_mat, g_feed = refs[23:25]
    outs = refs[25:]
    n_out = 3 if first else 2
    tail = outs[1:n_out]
    accs = outs[n_out : n_out + 6]
    sems = outs[n_out + 6]
    g = dict(zip(TIME_W + ("rows",), tuple(accs) + (outs[0],)))
    do_s, dq_s, dk_s, dv_s = outs[n_out + 7 :]
    rows = count * VB
    step = pl.program_id(0)

    @pl.when(step == 0)
    def _():
        for ref in list(g.values()) + (list(tail) if first else []):
            ref[...] = jnp.zeros(ref.shape, F32)

    vec = vec_ref[...]
    if first:
        place = jnp.broadcast_to(place_ref[...], (count, VB, D)).reshape(rows, D)
        pieces = x_ref[...].reshape(rows, 16)
        x = embed_block(pieces, emb_ref[...], place)
    else:
        x = x_ref[...].reshape(rows, D)
    x2 = split2(x)
    mixed = load_halves(o_s, rows)
    h, unit1, inv1 = norm_fwd(z1_s[...], vec[3:4], vec[4:5])
    u = u_s[...]
    cdf = gelu_cdf(u)
    _, unit2, inv2 = norm_fwd(z2_s[...], vec[8:9], vec[9:10])
    dy = dy_ref[...].reshape(rows, D)
    g["rows"][8] += colsum(dy * unit2)
    g["rows"][9] += colsum(dy)
    dz2 = norm_bwd(dy, unit2, inv2, vec[8:9])
    g["rows"][7] += colsum(dz2)
    dz22 = split2(dz2)
    g["down"][...] += tn3(split2(u * cdf), dz22)
    du = mmwt(dz22, w["down"]) * gelu_slope(u, cdf)
    g["rows"][5] += colsum(du[:, :D])
    g["rows"][6] += colsum(du[:, D:])
    du2 = split2(du)
    g["up"][...] += tn3(split2(h), du2)
    dh = dz2 + mmwt(du2, w["up"])
    g["rows"][3] += colsum(dh * unit1)
    g["rows"][4] += colsum(dh)
    dz1 = norm_bwd(dh, unit1, inv1, vec[3:4])
    g["rows"][2] += colsum(dz1)
    dz12 = split2(dz1)
    g["o"][...] += tn3(split2(mixed), dz12)
    store_halves(do_s, mmwt(dz12, w["o"]))
    zero_tail(do_s, rows)

    def some(i, carry):
        units = [(c, i * UNROLL_BACK + k) for k in range(UNROLL_BACK) for c in range(2)]
        time_attend_back(units, group, count, q_s, k_s, v_s, o_s, p_s, l_s, do_s, dq_s, dk_s, dv_s)
        return carry

    lax.fori_loop(0, VB // UNROLL_BACK, some, 0)
    dq = load_halves(dq_s, rows) * SCALE
    g["rows"][0] += colsum(dq)
    dq2 = split2(dq)
    g["q"][...] += tn3(x2, dq2)
    dx = dz1 + mmwt(dq2, w["q"])
    dk2 = split2(load_halves(dk_s, rows))
    g["k"][...] += tn3(x2, dk2)
    dx = dx + mmwt(dk2, w["k"])
    dv = load_halves(dv_s, rows)
    g["rows"][1] += colsum(dv)
    dv2 = split2(dv)
    g["v"][...] += tn3(x2, dv2)
    dx = dx + mmwt(dv2, w["v"])
    if first:
        tail[0][...] += tn3(split2(pieces), split2(dx))
        tail[1][...] += dx
    else:
        tail[0][...] = dx.reshape(count, VB, D)
    flush(
        step, pl.num_programs(0) - 1, list(accs[:4]) + list(later[:2]), [12 * layer + k for k in (0, 1, 2, 3, 8, 11)],
        [(accs[4], accs[5], 2 * layer), (later[2], later[3], 2 * layer + 1)], up_rows, g_mat, g_feed, sems,
    )


def time_bwd(first, x, extra, dy, kept, model, layer, count, later, packs, up_rows):
    group = 64 if count > 32 else 32
    nv = x.shape[1]
    width = x.shape[2]
    pad = group * VB
    squares = [12 * layer + k for k in range(4)]
    block = pl.BlockSpec((count, VB, D), lambda i: (0, i, 0))
    specs = [pl.BlockSpec((count, VB, width), lambda i: (0, i, 0))]
    if first:
        specs += [whole((16, D)), whole((count, 1, D))]
    specs += [block] + time_kept(count, group, nv // VB)[0] + weight_specs(squares, 2 * layer, layer)
    specs += [whole((D, D)), whole((D, D)), whole((D, FF)), whole((FF, D))]
    grad_shapes = [(10, 8, D)] + ([(16, D), (count * VB, D)] if first else [])
    out_specs = [ANY] * 2 + [whole(s) for s in grad_shapes]
    out_shape = pack_shapes() + [jax.ShapeDtypeStruct(s, F32) for s in grad_shapes]
    if not first:
        out_specs.append(block)
        out_shape.append(jax.ShapeDtypeStruct((count, nv, D), F32))
    return pl.pallas_call(
        functools.partial(time_bwd_kernel, first, count, group, layer, up_rows),
        grid=(nv // VB,),
        in_specs=specs + [ANY] * 2,
        out_specs=out_specs,
        out_shape=out_shape,
        input_output_aliases={len(specs): 0, len(specs) + 1: 1},
        scratch_shapes=[pltpu.VMEM((D, D), F32)] * 4
        + [pltpu.VMEM((D, FF), F32), pltpu.VMEM((FF, D), F32), pltpu.SemaphoreType.DMA((flush_count(6, 2, up_rows),))]
        + [pltpu.VMEM((2, pad, HALF), F32)] * 4,
        compiler_params=params_spec(),
        name="time_bwd",
    )(x, *extra, dy, *kept, *weight_args(model, squares, 2 * layer), *later, *packs)

SB_ROWS = 64


def head_rows():
    sub = lax.broadcasted_iota(jnp.int32, (8, D), 0)
    lane = lax.broadcasted_iota(jnp.int32, (8, D), 1)
    return jnp.where(sub == lane // 32, 1.0, 0.0).astype(F32)


def spread_rows(x):
    wide = jnp.broadcast_to(x[:, None, :], (RPAD, HEADS, D)) * head_rows()[None]
    return wide.reshape(RPAD * HEADS, D)


def gather_rows(x):
    return jnp.sum(x.reshape(RPAD, HEADS, D) * head_rows()[None], 1)


PACK = 24


def pack_rows(x, last=None):
    last = jnp.zeros((1, HALF), F32) if last is None else last
    return jnp.concatenate([x[:ROUT, :HALF], x[:ROUT, HALF:], last, jnp.zeros((PACK - 2 * ROUT - 1, HALF), F32)], 0)


def unpack_rows(x):
    x = jnp.concatenate([x[:ROUT], x[ROUT : 2 * ROUT]], 1)
    return jnp.concatenate([x, jnp.zeros((RPAD - ROUT, D), F32)], 0)


def unpack_block(ref, sb):
    return jnp.concatenate([unpack_rows(ref[s]) for s in range(sb)], 0)


TALL = 2 * ROUT


def tall_spec(sb):
    return pl.BlockSpec((sb * TALL, HALF), lambda i: (i, 0))


def tall_rows(n, parts):
    return -(-n * TALL // (8 * parts)) * 8 * parts


def pack_block(ref, x, sb):
    for s in range(sb):
        rows = x[s * RPAD : s * RPAD + ROUT]
        ref[s * TALL : (s + 1) * TALL] = jnp.concatenate([rows[:, :HALF], rows[:, HALF:]], 0)


def valid_lane(rows):
    return lax.broadcasted_iota(jnp.int32, (rows, HALF), 1) < ROUT * HEADS


def router_reduce(x, op):
    for shift in (8, 16, 32, 64):
        x = op(x, pltpu.roll(x, shift, 1))
    return x


def merge_rows(y, pairs, vec):
    wide = y.reshape(pairs, 2, SB_ROWS, D)
    wide = jnp.concatenate([wide[:, 0].reshape(pairs * SB_ROWS, D), wide[:, 1].reshape(pairs * SB_ROWS, D)], 1)
    gain = jnp.concatenate([vec[0:1], vec[1:2]], 1)
    bias = jnp.concatenate([vec[2:3], vec[3:4]], 1)
    return norm_fwd(wide, gain, bias) + (gain,)


RECV_W = ("so", "rk", "rv", "rq", "ro", "up", "down")


def recv_buffer(o2, w, vec):
    buf2 = split2(mmw(o2, w["so"]) + vec[12:13])
    kb = mmw(buf2, w["rk"])
    vb = mmw(buf2, w["rv"]) + vec[14:15]
    segs = range(kb.shape[0] // RPAD)
    k = [split2(spread_rows(kb[s * RPAD : (s + 1) * RPAD])) for s in segs]
    v = [split2(spread_rows(vb[s * RPAD : (s + 1) * RPAD])) for s in segs]
    return buf2, k, v


def recv_forward(send, o_rows, w, vec):
    sb = send.shape[0] // SB_ROWS
    send2 = split2(send)
    o2 = split2(o_rows)
    buf2, k, v = recv_buffer(o2, w, vec)
    q = (mmw(send2, w["rq"]) + vec[13:14]) * SCALE
    segs = range(sb)
    ok = valid_lane(SB_ROWS)
    scores = [jnp.where(ok, nt3_narrow(split2(q[s * SB_ROWS : (s + 1) * SB_ROWS]), k[s]), negative) for s in segs]
    probs = [jnp.exp(sc - router_reduce(sc, jnp.maximum)) for sc in scores]
    probs = [p / router_reduce(p, jnp.add) for p in probs]
    mixed = jnp.concatenate([nn3_short(split2(p), v2) for p, v2 in zip(probs, v)], 0)
    z3 = send + mmw(split2(mixed), w["ro"]) + vec[15:16]
    g, unit3, inv3 = norm_fwd(z3, vec[16:17], vec[17:18])
    u = mmw(split2(g), w["up"]) + jnp.concatenate([vec[18:19], vec[19:20]], 1)
    cdf = gelu_cdf(u)
    z4 = g + mmw(split2(u * cdf), w["down"]) + vec[20:21]
    y, unit4, inv4 = norm_fwd(z4, vec[21:22], vec[22:23])
    kept = (send2, o2, buf2, mixed, g, unit3, inv3, u, cdf, unit4, inv4, q, k, v, probs)
    return y, kept, (q, mixed, jnp.concatenate(probs, 0), z3, u, z4)


def recv_restore(send, o_rows, w, vec, saved):
    q, mixed, p, z3, u, z4 = saved
    o2 = split2(o_rows)
    buf2, k, v = recv_buffer(o2, w, vec)
    g, unit3, inv3 = norm_fwd(z3, vec[16:17], vec[17:18])
    y, unit4, inv4 = norm_fwd(z4, vec[21:22], vec[22:23])
    probs = [p[s * SB_ROWS : (s + 1) * SB_ROWS] for s in range(send.shape[0] // SB_ROWS)]
    return y, (split2(send), o2, buf2, mixed, g, unit3, inv3, u, gelu_cdf(u), unit4, inv4, q, k, v, probs)


KEPT_WIDTHS = (D, D, HALF, D, FF, D)


def kept_specs(sb):
    return [pl.BlockSpec((sb * SB_ROWS, k), lambda i: (i, 0)) for k in KEPT_WIDTHS]


RECV_G = ("so", "rk", "rv", "rows")
LATER_WIDTHS = (D, D, FF, D)


def row_specs(sb, widths):
    return [pl.BlockSpec((sb * SB_ROWS, k), lambda i: (i, 0)) for k in widths]


def row_shapes(n, widths):
    return [jax.ShapeDtypeStruct((n * SB_ROWS, k), F32) for k in widths]


def put(refs, values):
    for ref, value in zip(refs, values):
        ref[...] = value


def recv_backward(dy, kept, w, vec, g):
    send2, o2, buf2, mixed, gg, unit3, inv3, u, cdf, unit4, inv4, q, k, v, probs = kept
    sb = dy.shape[0] // SB_ROWS
    rows = g["rows"]
    rows[9] += colsum(dy * unit4)
    rows[10] += colsum(dy)
    dz4 = norm_bwd(dy, unit4, inv4, vec[21:22])
    rows[8] += colsum(dz4)
    dz42 = split2(dz4)
    du = mmwt(dz42, w["down"]) * gelu_slope(u, cdf)
    rows[6] += colsum(du[:, :D])
    rows[7] += colsum(du[:, D:])
    du2 = split2(du)
    dg = dz4 + mmwt(du2, w["up"])
    rows[4] += colsum(dg * unit3)
    rows[5] += colsum(dg)
    dz3 = norm_bwd(dg, unit3, inv3, vec[16:17])
    rows[3] += colsum(dz3)
    dz32 = split2(dz3)
    do = mmwt(dz32, w["ro"])
    segs = range(sb)
    d = [split2(do[s * SB_ROWS : (s + 1) * SB_ROWS]) for s in segs]
    dp = [nt3_narrow(d2, v2) for d2, v2 in zip(d, v)]
    ds = [split2(p * (x - router_reduce(p * x, jnp.add))) for p, x in zip(probs, dp)]
    dq = jnp.concatenate([nn3_short(s2, k2) for s2, k2 in zip(ds, k)], 0) * SCALE
    q = [split2(q[s * SB_ROWS : (s + 1) * SB_ROWS]) for s in segs]
    dk = jnp.concatenate([gather_rows(tn3_short(s2, q2)) for s2, q2 in zip(ds, q)], 0)
    dv = jnp.concatenate([gather_rows(tn3_short(split2(p), d2)) for p, d2 in zip(probs, d)], 0)
    rows[1] += colsum(dq)
    dq2 = split2(dq)
    dsend = dz3 + mmwt(dq2, w["rq"])
    dk2 = split2(dk)
    dv2 = split2(dv)
    rows[2] += colsum(dv)
    g["rk"][...] += tn3(buf2, dk2)
    g["rv"][...] += tn3(buf2, dv2)
    dbuf = mmwt(dk2, w["rk"]) + mmwt(dv2, w["rv"])
    rows[0] += colsum(dbuf)
    dbuf2 = split2(dbuf)
    g["so"][...] += tn3(o2, dbuf2)
    return dsend, mmwt(dbuf2, w["so"]), (dq, dz3, du, dz4)


def recv_squares(layer):
    return [12 * layer + k for k in (7, 9, 10, 8, 11)]


def seg_block(sb, rows=SB_ROWS, width=D):
    return pl.BlockSpec((sb, rows, width), lambda i: (i, 0, 0))


MERGE = pl.BlockSpec((2, D, D), lambda i: (12, 0, 0))


def pack_spec(sb):
    return seg_block(sb, PACK, HALF)


def recv_fwd_kernel(sb, send_ref, o_ref, *refs):
    w = {n: refs[i][...] for i, n in enumerate(RECV_W)}
    vec_ref, mvec_ref, mw_ref, out_ref = refs[7:11]
    y, _, saved = recv_forward(send_ref[...].reshape(sb * SB_ROWS, D), unpack_block(o_ref, sb), w, vec_ref[...])
    for ref, x in zip(refs[11:], saved):
        ref[...] = x
    mvec = mvec_ref[...]
    wide, _, _, _ = merge_rows(y, sb // 2, mvec)
    out_ref[...] = (mmw(split2(wide), mw_ref[...].reshape(2 * D, D)) + mvec[4:5]).reshape(sb // 2, SB_ROWS, D)


def recv_fwd(send, o, model, mvec, sb):
    squares = recv_squares(0)
    n = send.shape[0]
    return pl.pallas_call(
        functools.partial(recv_fwd_kernel, sb),
        grid=(n // sb,),
        in_specs=[seg_block(sb), pack_spec(sb)] + weight_specs(squares, 1, 0) + [whole((8, D)), MERGE],
        out_specs=[seg_block(sb // 2)] + kept_specs(sb),
        out_shape=[jax.ShapeDtypeStruct((n // 2, SB_ROWS, D), F32)]
        + [jax.ShapeDtypeStruct((n * SB_ROWS, k), F32) for k in KEPT_WIDTHS],
        compiler_params=params_spec(),
        name="recv_fwd",
    )(send, o, *weight_args(model, squares, 1), mvec, model[0])


def recv_bwd_kernel(sb, send_ref, o_ref, dx_ref, *refs):
    saved = [ref[...] for ref in refs[:6]]
    refs = refs[6:]
    w = {n: refs[i][...] for i, n in enumerate(RECV_W)}
    vec_ref, mvec_ref, mw_ref = refs[7:10]
    g_mat, dsend_ref, do_ref, rows_ref, dmv_ref = refs[11:16]
    later, accs, dmw_ref, sems = refs[16:20], refs[20:23], refs[23], refs[24]
    g = dict(zip(RECV_G, tuple(accs) + (rows_ref,)))

    @pl.when(pl.program_id(0) == 0)
    def _():
        for ref in list(g.values()) + [dmw_ref, dmv_ref]:
            ref[...] = jnp.zeros(ref.shape, F32)

    vec = vec_ref[...]
    y, kept = recv_restore(send_ref[...].reshape(sb * SB_ROWS, D), unpack_block(o_ref, sb), w, vec, saved)
    pairs = sb // 2
    wide, unit, inv, gain = merge_rows(y, pairs, mvec_ref[...])
    dx = dx_ref[...].reshape(pairs * SB_ROWS, D)
    dmv_ref[4] += colsum(dx)
    dx2 = split2(dx)
    dmw_ref[...] += tn3(split2(wide), dx2).reshape(2, D, D)
    dn = mmwt(dx2, mw_ref[...].reshape(2 * D, D))
    part = colsum(dn * unit)
    dmv_ref[0] += part[:, :D]
    dmv_ref[1] += part[:, D:]
    part = colsum(dn)
    dmv_ref[2] += part[:, :D]
    dmv_ref[3] += part[:, D:]
    dwide = norm_bwd(dn, unit, inv, gain)
    left = dwide[:, :D].reshape(pairs, 1, SB_ROWS, D)
    right = dwide[:, D:].reshape(pairs, 1, SB_ROWS, D)
    dy = jnp.concatenate([left, right], 1).reshape(sb * SB_ROWS, D)
    dsend, do, grads = recv_backward(dy, kept, w, vec, g)
    put(later, grads)
    dsend_ref[...] = dsend.reshape(sb, SB_ROWS, D)
    pack_block(do_ref, do, sb)
    recv_flush(accs, [(dmw_ref, 24)], 0, g_mat, sems)


RECV_ACC = [pltpu.VMEM((D, D), F32)] * 3


def recv_flush(accs, more, layer, g_mat, sems):
    flush(
        pl.program_id(0), pl.num_programs(0) - 1, list(accs) + [m for m, _ in more],
        recv_squares(layer)[:3] + [at for _, at in more], [], 0, g_mat, None, sems,
    )


def recv_bwd(send, o, dx, kept, model, mvec, sb, g_mat, parts):
    n = send.shape[0]
    squares = recv_squares(0)
    shapes = [(11, 8, D), (5, 8, D)]
    specs = [seg_block(sb), pack_spec(sb), seg_block(sb // 2)] + kept_specs(sb)
    specs += weight_specs(squares, 1, 0) + [whole((8, D)), MERGE]
    return pl.pallas_call(
        functools.partial(recv_bwd_kernel, sb),
        grid=(n // sb,),
        in_specs=specs + [ANY],
        out_specs=[ANY, seg_block(sb), tall_spec(sb)] + [whole(s) for s in shapes] + row_specs(sb, LATER_WIDTHS),
        out_shape=pack_shapes()[:1]
        + [jax.ShapeDtypeStruct((n, SB_ROWS, D), F32), jax.ShapeDtypeStruct((tall_rows(n, parts), HALF), F32)]
        + [jax.ShapeDtypeStruct(s, F32) for s in shapes]
        + row_shapes(n, LATER_WIDTHS),
        input_output_aliases={len(specs): 0},
        scratch_shapes=RECV_ACC + [pltpu.VMEM((2, D, D), F32), pltpu.SemaphoreType.DMA((4,))],
        compiler_params=params_spec(),
        name="recv_bwd",
    )(send, o, dx, *kept, *weight_args(model, squares, 1), mvec, model[0], g_mat)


def tail_kernel(sb, send_ref, o_ref, tgt_ref, kept_ref, scale_ref, mean_ref, *refs):
    w = {n: refs[i][...] for i, n in enumerate(RECV_W)}
    vec_ref, head_ref, g_mat, g_feed, dsend_ref, do_ref, rows_ref, dhead_ref = refs[7:15]
    saved, later, accs, sems = refs[15:18], refs[18:22], refs[22:25], refs[25]
    g = dict(zip(RECV_G, tuple(accs) + (rows_ref,)))

    @pl.when(pl.program_id(0) == 0)
    def _():
        for ref in list(g.values()) + [dhead_ref]:
            ref[...] = jnp.zeros(ref.shape, F32)

    vec = vec_ref[...]
    rows = sb * SB_ROWS
    y, kept, (_, mixed, _, z3, u, _) = recv_forward(
        send_ref[...].reshape(rows, D), unpack_block(o_ref, sb), w, vec
    )
    head = head_ref[...]
    y2 = split2(y)
    scale = jnp.broadcast_to(scale_ref[...][None], (sb, SB_ROWS, PPAD)).reshape(rows, PPAD)
    mean = jnp.broadcast_to(mean_ref[...][None], (sb, SB_ROWS, PPAD)).reshape(rows, PPAD)
    misfit = mmwt(y2, head) * scale + mean - tgt_ref[...].reshape(rows, PPAD)
    put(saved, (mixed, z3, u))
    dpred = kept_ref[...].reshape(rows, PPAD) * misfit * scale
    dpred2 = split2(dpred)
    dhead_ref[...] += tn3(dpred2, y2)
    dy = mmw(dpred2, head)
    dsend, do, grads = recv_backward(dy, kept, w, vec, g)
    put(later, grads)
    dsend_ref[...] = dsend.reshape(sb, SB_ROWS, D)
    pack_block(do_ref, do, sb)
    recv_flush(accs, [], 1, g_mat, sems)


def tail(send, o, tgt, kept, scale, mean, model, head, sb, parts):
    n = send.shape[0]
    squares = recv_squares(1)
    shapes = [(11, 8, D), (PPAD, D)]
    return pl.pallas_call(
        functools.partial(tail_kernel, sb),
        grid=(n // sb,),
        in_specs=[seg_block(sb), pack_spec(sb), seg_block(sb, SB_ROWS, PPAD), seg_block(sb, SB_ROWS, PPAD)]
        + [whole((SB_ROWS, PPAD))] * 2
        + weight_specs(squares, 3, 1)
        + [whole((PPAD, D))],
        out_specs=[ANY] * 2 + [seg_block(sb), tall_spec(sb)] + [whole(s) for s in shapes]
        + row_specs(sb, (D, D, FF) + LATER_WIDTHS),
        out_shape=pack_shapes()
        + [jax.ShapeDtypeStruct((n, SB_ROWS, D), F32), jax.ShapeDtypeStruct((tall_rows(n, parts), HALF), F32)]
        + [jax.ShapeDtypeStruct(s, F32) for s in shapes]
        + row_shapes(n, (D, D, FF) + LATER_WIDTHS),
        scratch_shapes=RECV_ACC + [pltpu.SemaphoreType.DMA((3,))],
        compiler_params=params_spec(),
        name="tail",
    )(send, o, tgt, kept, scale, mean, *weight_args(model, squares, 3), head)


SEND_W = ("sq", "sk", "sv")


def send_project(dim2, r_rows, w, vec):
    r2 = split2(r_rows)
    sb = r_rows.shape[0] // RPAD
    k = mmw(dim2, w["sk"])
    v = mmw(dim2, w["sv"]) + vec[11:12]
    q = (mmw(r2, w["sq"]) + vec[10:11]) * SCALE
    k = [split2(k[s * SB_ROWS : (s + 1) * SB_ROWS]) for s in range(sb)]
    v = [split2(v[s * SB_ROWS : (s + 1) * SB_ROWS]) for s in range(sb)]
    q = [split2(spread_rows(q[s * RPAD : (s + 1) * RPAD])) for s in range(sb)]
    return r2, k, v, q


def send_fwd_kernel(sb, dim_ref, r_ref, here_ref, *refs):
    w = {n: refs[i][...] for i, n in enumerate(SEND_W)}
    vec_ref, o_ref = refs[3:]
    dim2 = split2(dim_ref[...].reshape(sb * SB_ROWS, D))
    _, k, v, q = send_project(dim2, r_ref[...].reshape(sb * RPAD, D), w, vec_ref[...])
    here = here_ref[...] > 0.5
    scores = [jnp.where(here, nt3_narrow(k2, q2), negative) for k2, q2 in zip(k, q)]
    tops = [jnp.max(sc, 0, keepdims=True) for sc in scores]
    probs = [jnp.where(here, jnp.exp(sc - top), 0.0) for sc, top in zip(scores, tops)]
    totals = [jnp.sum(p, 0, keepdims=True) for p in probs]
    safe = [jnp.where(t > 0.0, t, 1.0) for t in totals]
    mixed = [gather_rows(tn3_short(split2(p / t), v2)) for p, t, v2 in zip(probs, safe, v)]
    for s in range(sb):
        lse = jnp.where(totals[s] > 0.0, tops[s] + jnp.log(safe[s]), negative)
        o_ref[s] = pack_rows(mixed[s], lse)


def send_squares(layer):
    return [12 * layer + k for k in (4, 5, 6)]


def send_fwd(dim, routers, here, model, layer, sb, npad):
    squares = send_squares(layer)
    n = dim.shape[0]
    return pl.pallas_call(
        functools.partial(send_fwd_kernel, sb),
        grid=(n // sb,),
        in_specs=[seg_block(sb), seg_block(sb, RPAD), whole((SB_ROWS, HALF))]
        + weight_specs(squares, None, layer),
        out_specs=pack_spec(sb),
        out_shape=jax.ShapeDtypeStruct((npad, PACK, HALF), F32),
        compiler_params=params_spec(),
        name="send_fwd",
    )(dim, routers, here, *weight_args(model, squares, None))


def send_bwd_kernel(sb, layer, dim_ref, dpart_ref, r_ref, o_ref, do_ref, here_ref, *refs):
    w = {n: refs[i][...] for i, n in enumerate(SEND_W)}
    vec_ref = refs[3]
    g_mat, ddim_ref, dr_ref, rows = refs[5:9]
    dsq_ref, dsk_ref, dsv_ref, sems = refs[9:13]

    @pl.when(pl.program_id(0) == 0)
    def _():
        for ref in (dsq_ref, dsk_ref, dsv_ref, rows):
            ref[...] = jnp.zeros(ref.shape, F32)

    dim2 = split2(dim_ref[...].reshape(sb * SB_ROWS, D))
    r2, k, v, q = send_project(dim2, r_ref[...].reshape(sb * RPAD, D), w, vec_ref[...])
    here = (here_ref[...] > 0.5) & valid_lane(SB_ROWS)
    segs = range(sb)
    scores = [nt3_narrow(k2, q2) for k2, q2 in zip(k, q)]
    probs = [jnp.where(here, jnp.exp(scores[s] - o_ref[s][2 * ROUT : 2 * ROUT + 1]), 0.0) for s in segs]
    dwide = [spread_rows(unpack_rows(do_ref[s * TALL : (s + 1) * TALL])) for s in segs]
    owide = [
        jnp.broadcast_to(unpack_rows(o_ref[s])[:, None, :], (RPAD, HEADS, D)).reshape(RPAD * HEADS, D) for s in segs
    ]
    e = [split2(a * b) for a, b in zip(dwide, owide)]
    d = [split2(a) for a in dwide]
    one_row = jnp.ones((8, D), BF)
    means = [(dots(one_row, e2[0], 1, 1) + dots(one_row, e2[1], 1, 1))[0:1] for e2 in e]
    dp = [nt3_narrow(v2, d2) for v2, d2 in zip(v, d)]
    ds = [split2(p * (x - mean)) for p, x, mean in zip(probs, dp, means)]
    dk = jnp.concatenate([nn3_short(s2, q2) for s2, q2 in zip(ds, q)], 0)
    dv = jnp.concatenate([nn3_short(split2(p), d2) for p, d2 in zip(probs, d)], 0)
    dq = jnp.concatenate([gather_rows(tn3_short(s2, k2)) for s2, k2 in zip(ds, k)], 0) * SCALE
    dk2 = split2(dk)
    dv2 = split2(dv)
    rows[1] += colsum(dv)
    dsk_ref[...] += tn3(dim2, dk2)
    dsv_ref[...] += tn3(dim2, dv2)
    out = dpart_ref[...].reshape(sb * SB_ROWS, D) + mmwt(dk2, w["sk"]) + mmwt(dv2, w["sv"])
    ddim_ref[...] = out.reshape(sb, SB_ROWS, D)
    rows[0] += colsum(dq)
    dq2 = split2(dq)
    dsq_ref[...] += tn3(r2, dq2)
    dr_ref[...] = mmwt(dq2, w["sq"]).reshape(sb, RPAD, D)
    flush(
        pl.program_id(0), pl.num_programs(0) - 1, [dsq_ref, dsk_ref, dsv_ref], send_squares(layer), [], 0, g_mat, None,
        sems,
    )


def send_bwd(dim, dpart, routers, o, do, here, model, layer, sb, g_mat):
    n = dim.shape[0]
    squares = send_squares(layer)
    specs = [seg_block(sb), seg_block(sb), seg_block(sb, RPAD), pack_spec(sb), tall_spec(sb), whole((SB_ROWS, HALF))]
    specs += weight_specs(squares, None, layer)
    return pl.pallas_call(
        functools.partial(send_bwd_kernel, sb, layer),
        grid=(n // sb,),
        in_specs=specs + [ANY],
        out_specs=[ANY, seg_block(sb), seg_block(sb, RPAD), whole((2, 8, D))],
        out_shape=pack_shapes()[:1]
        + [jax.ShapeDtypeStruct((n, SB_ROWS, D), F32), jax.ShapeDtypeStruct((n, RPAD, D), F32)]
        + [jax.ShapeDtypeStruct((2, 8, D), F32)],
        input_output_aliases={len(specs): 0},
        scratch_shapes=[pltpu.VMEM((D, D), F32)] * 3 + [pltpu.SemaphoreType.DMA((3,))],
        compiler_params=params_spec(),
        name="send_bwd",
    )(dim, dpart, routers, o, do, here, *weight_args(model, squares, None), g_mat)

MESH = pl.DeviceIdType.MESH


def grid_sizes():
    nf = lax.axis_size("fsdp")
    nx = 1
    while 2 * nx * nx < nf:
        nx *= 2
    return lax.axis_size("dp") // 2, nf // nx, nx


class Place:
    def __init__(self):
        self.ny, self.nz, self.nx = grid_sizes()
        dp, fs = lax.axis_index("dp"), lax.axis_index("fsdp")
        self.core, self.y = lax.rem(dp, 2), lax.div(dp, 2)
        self.x, self.z = lax.rem(fs, self.nx), lax.div(fs, self.nx)

    def at(self, y=None, core=None, z=None, x=None):
        y = self.y if y is None else y
        core = self.core if core is None else core
        z = self.z if z is None else z
        x = self.x if x is None else x
        return (y * 2 + core, z * self.nx + x)

    def other(self):
        return 1 - self.core

    def next_x(self, k):
        return lax.rem(self.x + k, self.nx)

    def next_y(self, k):
        return lax.rem(self.y + k, self.ny)

    def next_z(self, k):
        return lax.rem(self.z + k, self.nz)

    def neighbours(self):
        out = [self.at(core=self.other())]
        out += [self.at(x=self.next_x(k)) for k in range(1, self.nx)]
        out += [self.at(y=self.next_y(k)) for k in range(1, self.ny)]
        out += [self.at(z=self.next_z(k)) for k in range(1, self.nz)]
        return out


def greet(devices):
    barrier = pltpu.get_barrier_semaphore()
    for device in devices:
        pl.semaphore_signal(barrier, inc=1, device_id=device, device_id_type=MESH)
    pl.semaphore_wait(barrier, len(devices))


def remote(src, dst, send, recv, device):
    return pltpu.make_async_remote_copy(
        src_ref=src, dst_ref=dst, send_sem=send, recv_sem=recv, device_id=device, device_id_type=MESH
    )


def gather_chunks(shapes):
    out = []
    for j, (rows, _) in enumerate(shapes):
        cut = rows // 32 * 16 if rows >= 160 else 0
        out += [(j, 0, cut), (j, cut, rows - cut)] if cut else [(j, 0, rows)]
    return out


def gather_kernel(shapes, *refs):
    packs = len(shapes)
    chunks = gather_chunks(shapes)
    n = len(chunks)
    shards = [refs[j].at[pl.ds(a, b)] for j, a, b in chunks]
    send, recv, local = refs[2 * packs :]

    def view(i, *at):
        j, a, b = chunks[i]
        return refs[packs + j].at[at + (slice(None),) * (4 - len(at)) + (pl.ds(a, b),)]

    me = Place()
    y, c, z, x = me.y, me.core, me.z, me.x
    m = me.nx
    greet(me.neighbours())
    slot = [0]

    def push(src, dst, device):
        copy = remote(src, dst, send.at[slot[0]], recv.at[slot[0]], device)
        slot[0] += 1
        copy.start()
        return copy

    def finish(copies):
        for copy in copies:
            copy.wait()

    own = [pltpu.make_async_copy(shards[j], view(j, y, c, z, x), local.at[j]) for j in range(n)]
    for copy in own:
        copy.start()

    def along_z(j):
        return [push(shards[j], view(j, y, c, z, x), me.at(z=me.next_z(k))) for k in range(1, me.nz)]

    first = along_z(0)
    finish(own)
    base = slot[0]

    def rest(by_core):
        slot[0] = base
        sibling = me.at(core=1 - by_core)
        shared = []

        def second(j):
            piece = view(j, y, by_core, slice(None), x)
            out = []
            for k in range(1, m):
                out.append(push(piece, piece, me.at(x=me.next_x(k)) if by_core == 0 else me.at(y=me.next_y(k))))
            shared.append(push(piece, piece, sibling))
            return out

        def third(j):
            wide = view(j, y, by_core) if by_core == 0 else view(j, slice(None), by_core, slice(None), x)
            out = []
            for k in range(1, m):
                out.append(push(wide, wide, me.at(y=me.next_y(k)) if by_core == 0 else me.at(x=me.next_x(k))))
            for k in range(1, m):
                piece = view(j, y, by_core, slice(None), me.next_x(k)) if by_core == 0 else view(j, me.next_y(k), by_core, slice(None), x)
                shared.append(push(piece, piece, sibling))
            return out

        def fourth(j):
            for k in range(1, m):
                wide = view(j, me.next_y(k), by_core) if by_core == 0 else view(j, slice(None), by_core, slice(None), me.next_x(k))
                shared.append(push(wide, wide, sibling))

        one, two, three = {0: first}, {}, {}
        for t in range(n + 2):
            if t < n:
                finish(one[t])
                if t + 1 < n:
                    one[t + 1] = along_z(t + 1)
                two[t] = second(t)
            if 0 < t <= n:
                finish(two[t - 1])
                three[t - 1] = third(t - 1)
            if t > 1:
                finish(three[t - 2])
                fourth(t - 2)
        finish(shared)

    for by_core in (0, 1):
        pl.when(c == by_core)(functools.partial(rest, by_core))


def gather_all(shards):
    ny, nz, nx = grid_sizes()
    shapes = [s.shape for s in shards]
    n, parts = len(shards), len(gather_chunks(shapes))
    count = parts * ((nz - 1) + (nx - 1) + 1 + (nx - 1) * 3)
    return pl.pallas_call(
        functools.partial(gather_kernel, shapes),
        in_specs=[ANY] * n,
        out_specs=[ANY] * n,
        out_shape=[jax.ShapeDtypeStruct((ny, 2, nz, nx) + s.shape, s.dtype) for s in shards],
        scratch_shapes=[pltpu.SemaphoreType.DMA((count,)), pltpu.SemaphoreType.DMA((count,)), pltpu.SemaphoreType.DMA((parts,))],
        compiler_params=pltpu.CompilerParams(collective_id=0, has_side_effects=True, vmem_limit_bytes=VMEM_LIMIT),
        name="gather_all",
    )(*shards)


def row_chunks(rows):
    count = max(1, rows // 40)
    if rows % 8:
        count = 1
    cuts = [rows // 8 * k // count * 8 for k in range(count)] + [rows]
    return [(a, b - a) for a, b in zip(cuts, cuts[1:])]


def scatter_kernel(shapes, *refs):
    n = len(shapes)
    chunks = [(j, a, b) for j, s in enumerate(shapes) for a, b in row_chunks(s[0])]
    total = len(chunks)
    grads, tile_ref = refs[:n], refs[n]
    outs, stat_ref = refs[n + 1 : 2 * n + 1], refs[2 * n + 1]
    bufs = refs[2 * n + 2 :]
    acc, r1, r2, r3, r4 = (bufs[i * total : (i + 1) * total] for i in range(5))
    tp, tz, send, recv, local = bufs[5 * total :]
    me = Place()
    y, c, z, x = me.y, me.core, me.z, me.x
    ny, nz, nx, m = me.ny, me.nz, me.nx, me.nx
    plane = plane_peers(me)
    greet([p for p, _ in plane] + [me.at(z=me.next_z(k)) for k in range(1, nz)])
    slot = [0]

    def push(src, dst, device):
        copy = remote(src, dst, send.at[slot[0]], recv.at[slot[0]], device)
        slot[0] += 1
        copy.start()
        return copy

    def finish(copies):
        for copy in copies:
            copy.wait()

    def rest(by_core):
        slot[0] = 0
        sibling = me.at(core=1 - by_core)

        def one(i):
            j, a, b = chunks[i]
            out = []
            for k in range(nx):
                out.append(push(grads[j].at[:, 1 - by_core, :, k, pl.ds(a, b)], r1[i].at[:, k], sibling))
                copy = pltpu.make_async_copy(grads[j].at[:, by_core, :, k, pl.ds(a, b)], acc[i].at[:, k], local.at[i * nx + k])
                copy.start()
                out.append(copy)
            return out

        def add1(i):
            def body(k, carry):
                at = (lax.div(k, nx * nz), lax.rem(lax.div(k, nz), nx), lax.rem(k, nz))
                acc[i][at] = acc[i][at] + r1[i][at]
                return carry

            lax.fori_loop(0, ny * nx * nz, body, 0)

        def two(i):
            if by_core == 0:
                return [push(acc[i].at[:, me.next_x(k)], r2[i].at[k - 1], me.at(x=me.next_x(k))) for k in range(1, m)]
            return [push(acc[i].at[me.next_y(k)], r2[i].at[k - 1], me.at(y=me.next_y(k))) for k in range(1, m)]

        def add2(i):
            def body(k, carry):
                a, b = lax.div(k, nz), lax.rem(k, nz)
                at = (a, x, b) if by_core == 0 else (y, a, b)
                value = acc[i][at]
                for q in range(m - 1):
                    value = value + r2[i][q, a, b]
                acc[i][at] = value
                return carry

            lax.fori_loop(0, m * nz, body, 0)

        def three(i):
            if by_core == 0:
                return [push(acc[i].at[me.next_y(k), x], r3[i].at[k - 1], me.at(y=me.next_y(k))) for k in range(1, m)]
            return [push(acc[i].at[y, me.next_x(k)], r3[i].at[k - 1], me.at(x=me.next_x(k))) for k in range(1, m)]

        def add3(i):
            def body(k, carry):
                value = acc[i][y, x, k]
                for q in range(m - 1):
                    value = value + r3[i][q, k]
                acc[i][y, x, k] = value
                return carry

            lax.fori_loop(0, nz, body, 0)

        def four(i):
            return [push(acc[i].at[y, x, me.next_z(k)], r4[i].at[k - 1], me.at(z=me.next_z(k))) for k in range(1, nz)]

        def end(i):
            j, a, b = chunks[i]
            value = acc[i][y, x, z]
            for k in range(nz - 1):
                value = value + r4[i][k]
            outs[j][a : a + b] = value
            sq = colsum_any(value * value)
            return sq[:, :HALF] + sq[:, HALF:]

        squares = jnp.zeros((8, HALF), F32)
        ahead = 3
        p1, p2, p3, p4 = {i: one(i) for i in range(min(ahead, total))}, {}, {}, {}
        for t in range(total + 3):
            if t < total:
                finish(p1[t])
                if t + ahead < total:
                    p1[t + ahead] = one(t + ahead)
                add1(t)
                p2[t] = two(t)
            if 0 <= t - 1 < total:
                finish(p2[t - 1])
                add2(t - 1)
                p3[t - 1] = three(t - 1)
            if 0 <= t - 2 < total:
                finish(p3[t - 2])
                add3(t - 2)
                p4[t - 2] = four(t - 2)
            if 0 <= t - 3 < total:
                finish(p4[t - 3])
                squares = squares + end(t - 3)
        tp[(y * 2 + by_core) * nx + x] = jnp.concatenate([squares, tile_ref[...]], 0)

    for by_core in (0, 1):
        pl.when(c == by_core)(functools.partial(rest, by_core))

    slot[0] = total * (nx + 2 * (m - 1) + nz - 1)
    mine = tp.at[(y * 2 + c) * nx + x]
    finish([push(mine, mine, p) for p, _ in plane])
    tz[z] = functools.reduce(jnp.add, [tp[k] for k in range(2 * ny * nx)])
    finish([push(tz.at[z], tz.at[z], me.at(z=me.next_z(k))) for k in range(1, nz)])
    stat_ref[...] = functools.reduce(jnp.add, [tz[k] for k in range(nz)])


def plane_peers(me):
    out = []
    for k in range(1, 2 * me.ny * me.nx):
        dc, dy, dx = k % 2, k // 2 % me.ny, k // (2 * me.ny)
        out.append((me.at(core=lax.rem(me.core + dc, 2), y=lax.rem(me.y + dy, me.ny), x=lax.rem(me.x + dx, me.nx)), k))
    return out


def colsum_any(x):
    rows = x.shape[0]
    even = rows // 8 * 8
    out = colsum(x[:even]) if even else jnp.zeros((8, x.shape[1]), F32)
    if rows > even:
        out = out + jnp.pad(x[even:], ((0, 8 - rows + even), (0, 0)))
    return out


def scatter_sum(grads, tile):
    ny, nz, nx = grid_sizes()
    n = len(grads)
    shapes = [g.shape[-2:] for g in grads]
    pieces = [(b, s[1]) for s in shapes for _, b in row_chunks(s[0])]
    total = len(pieces)
    count = total * (nx + (nx - 1) * 2 + nz - 1) + 2 * ny * nx - 1 + nz - 1

    def buffers(*lead):
        return [pltpu.VMEM(lead + s, F32) for s in pieces]

    return pl.pallas_call(
        functools.partial(scatter_kernel, shapes),
        in_specs=[ANY] * n + [INVMEM],
        out_specs=[INVMEM] * (n + 1),
        out_shape=[jax.ShapeDtypeStruct(s, F32) for s in shapes] + [jax.ShapeDtypeStruct((16, HALF), F32)],
        scratch_shapes=buffers(ny, nx, nz)
        + buffers(ny, nx, nz)
        + buffers(nx - 1, nx, nz)
        + buffers(nx - 1, nz)
        + buffers(nz - 1)
        + [pltpu.VMEM((2 * ny * nx, 16, HALF), F32), pltpu.VMEM((nz, 16, HALF), F32)]
        + [pltpu.SemaphoreType.DMA((count,)), pltpu.SemaphoreType.DMA((count,)), pltpu.SemaphoreType.DMA((total * nx,))],
        compiler_params=pltpu.CompilerParams(collective_id=1, has_side_effects=True, vmem_limit_bytes=VMEM_LIMIT),
        name="scatter_sum",
    )(*grads, tile)


def group_part(ref, who, per):
    return ref.at[pl.ds(pl.multiple_of(who * per, per), per)]


def group_out(per, in_ref, got, send, recv, local):
    nf = lax.axis_size("fsdp")
    dp, f = lax.axis_index("dp"), lax.axis_index("fsdp")
    copies = [pltpu.make_async_copy(group_part(in_ref, f, per), got.at[f], local)]
    for k in range(1, nf):
        p = lax.rem(f + k, nf)
        copies.append(remote(group_part(in_ref, p, per), got.at[f], send.at[k - 1], recv.at[k - 1], (dp, p)))
    return copies


def group_back(per, result, out_ref, send, recv, local):
    nf = lax.axis_size("fsdp")
    dp, f = lax.axis_index("dp"), lax.axis_index("fsdp")
    copies = [pltpu.make_async_copy(result, group_part(out_ref, f, per), local)]
    for k in range(1, nf):
        p = lax.rem(f + k, nf)
        copies.append(remote(result, group_part(out_ref, f, per), send.at[nf - 2 + k], recv.at[nf - 2 + k], (dp, p)))
    return copies


def greet_group():
    nf = lax.axis_size("fsdp")
    dp, f = lax.axis_index("dp"), lax.axis_index("fsdp")
    greet([(dp, lax.rem(f + k, nf)) for k in range(1, nf)])


def start_all(copies):
    for copy in copies:
        copy.start()


def wait_all(copies):
    for copy in copies:
        copy.wait()


def stats_kernel(per, in_ref, out_ref, got, result, send, recv, local):
    nf = lax.axis_size("fsdp")
    greet_group()
    copies = group_out(per, in_ref, got, send, recv, local)
    start_all(copies)
    wait_all(copies)
    row = lax.broadcasted_iota(jnp.int32, (PACK, HALF), 0)
    lane = lax.broadcasted_iota(jnp.int32, (PACK, HALF), 1)
    router = jnp.where(row < ROUT, row, row - ROUT)
    chosen = (lane // 8 == router) & (row < 2 * ROUT)
    src = lax.broadcasted_iota(jnp.int32, (HALF, D), 0)
    dst = lax.broadcasted_iota(jnp.int32, (HALF, D), 1)
    widen = jnp.where(src % 8 == dst // 32, 1.0, 0.0).astype(BF)

    def one(s, carry):
        lse = [got[d, s, 2 * ROUT : 2 * ROUT + 1, :] for d in range(nf)]
        top = functools.reduce(jnp.maximum, lse)
        total = top + jnp.log(functools.reduce(jnp.add, [jnp.exp(l - top) for l in lse]))
        out = jnp.where(row == 2 * ROUT, total, 0.0)
        share = jnp.concatenate([jnp.where(chosen, jnp.exp(l - total), 0.0) for l in lse], 0)
        wide = mmw(split2(share), widen)
        for d in range(nf):
            w = wide[d * PACK : (d + 1) * PACK]
            w = jnp.where(row < ROUT, w[:, :HALF], w[:, HALF:])
            out = out + jnp.where(row < 2 * ROUT, w * got[d, s], 0.0)
        result[s] = out
        return carry

    lax.fori_loop(0, per, one, 0)
    copies = group_back(per, result, out_ref, send, recv, local)
    start_all(copies)
    wait_all(copies)


def sum_kernel(per, turn, in_ref, x_ref, mixed_ref, z_ref, u_ref, dq_ref, dz3_ref, du_ref, dz4_ref, vec_ref, *refs):
    out_ref, rq, ro, up, down, got, result, send, recv, local = refs
    step = pl.program_id(0)

    @pl.when(step == 0)
    def _():
        greet_group()
        start_all(group_out(per, in_ref, got, send, recv, local))
        for ref in (rq, ro, up, down):
            ref[...] = jnp.zeros(ref.shape, F32)

    @pl.when(step == turn)
    def _():
        wait_all(group_out(per, in_ref, got, send, recv, local))
        result[...] = functools.reduce(jnp.add, [got[d] for d in range(lax.axis_size("fsdp"))])
        start_all(group_back(per, result, out_ref, send, recv, local))

    rq[...] += tn3(split2(x_ref[...]), split2(dq_ref[...]))
    ro[...] += tn3(split2(mixed_ref[...]), split2(dz3_ref[...]))
    g, _, _ = norm_fwd(z_ref[...], vec_ref[16:17], vec_ref[17:18])
    up[...] += tn3(split2(g), split2(du_ref[...]))
    u = u_ref[...]
    down[...] += tn3(split2(u * gelu_cdf(u)), split2(dz4_ref[...]))

    @pl.when(step == pl.num_programs(0) - 1)
    def _():
        wait_all(group_back(per, result, out_ref, send, recv, local))


def group_scratch(part, nf):
    return [
        pltpu.VMEM((nf,) + part, F32),
        pltpu.VMEM(part, F32),
        pltpu.SemaphoreType.DMA((2 * nf - 2,)),
        pltpu.SemaphoreType.DMA((2 * nf - 2,)),
        pltpu.SemaphoreType.DMA,
    ]


def group_params(cid):
    return pltpu.CompilerParams(collective_id=cid, has_side_effects=True, vmem_limit_bytes=VMEM_LIMIT)


def group_stats(packed, cid):
    nf = lax.axis_size("fsdp")
    per = packed.shape[0] // nf
    return pl.pallas_call(
        functools.partial(stats_kernel, per),
        in_specs=[ANY],
        out_specs=ANY,
        out_shape=jax.ShapeDtypeStruct(packed.shape, F32),
        scratch_shapes=group_scratch((per, PACK, HALF), nf),
        compiler_params=group_params(cid),
        name="group_stats",
    )(packed)


def group_sum(packed, work, vecs, layer, cid):
    nf = lax.axis_size("fsdp")
    per = packed.shape[0] // nf
    rows = 480
    steps = work[0].shape[0] // rows
    shapes = [(D, D), (D, D), (D, FF), (FF, D)]
    return pl.pallas_call(
        functools.partial(sum_kernel, per, steps - steps // 4),
        grid=(steps,),
        in_specs=[ANY] + [pl.BlockSpec((rows, w.shape[1]), lambda i: (i, 0)) for w in work] + [pick((24, D), layer)],
        out_specs=[ANY] + [whole(s) for s in shapes],
        out_shape=[jax.ShapeDtypeStruct(packed.shape, F32)] + [jax.ShapeDtypeStruct(s, F32) for s in shapes],
        scratch_shapes=group_scratch((per, HALF), nf),
        compiler_params=group_params(cid),
        name="group_sum",
    )(packed, *work, vecs)

LAYER_AT = SEGLEN + 1 + SEG
MERGE_AT = LAYER_AT + 46
HEAD_AT = MERGE_AT + 5
ROUTER_AT = HEAD_AT + PRED
VROWS = NVEC + 20


def own_size(devices):
    own = NVEC * D // devices
    return own, -(-own // D)


def prepare_kernel(nfeed, ser_ref, obs_ref, tgt_ref, mask_ref, count_ref, mat_ref, feed_ref, vec_ref, *outs):
    pieces, tgt, kept, scale_ref, mean_ref, here_ref, tile_ref, mat_o, feed_o, vec_o = outs
    for src, dst in ((mat_ref, mat_o), (feed_ref, feed_o), (vec_ref, vec_o)):
        rows = dst.shape[0]
        left, right = src[pl.ds(0, rows, stride=2), :], src[pl.ds(1, rows, stride=2), :]
        dst[...] = jnp.concatenate([left, right], 1).astype(BF)
    nv = ser_ref.shape[0]
    series, seen = ser_ref[...], obs_ref[...].astype(F32)
    counted = jnp.maximum(jnp.sum(seen, -1, keepdims=True), 1.0)
    mean = jnp.sum(seen * series, -1, keepdims=True) / counted
    center = (series - mean) * seen
    scale = jnp.sqrt(jnp.sum(center * center, -1, keepdims=True) / counted + norm_eps)
    slot = lax.axis_index("fsdp") * nv + lax.broadcasted_iota(jnp.int32, (nv, HALF), 0)
    here = jnp.where(slot < count_ref[0], 1.0, 0.0)
    here_ref[...] = here
    scale_ref[...] = jnp.broadcast_to(scale, (nv, PPAD))
    mean_ref[...] = jnp.broadcast_to(mean, (nv, PPAD))
    mask = mask_ref[...].astype(F32) * here[:, :1]
    tile_ref[...] = jnp.broadcast_to(jnp.sum(jnp.sum(mask, 0, keepdims=True), -1, keepdims=True), (8, HALF)) * (1.0 / (8 * HALF))
    lane = lax.broadcasted_iota(jnp.int32, (nv, PPAD), 1)

    def cut(x, dst):
        x = jnp.concatenate([x, jnp.zeros((nv, PPAD - 12), F32)], 1)
        for s in range(dst.shape[0]):
            dst[s] = jnp.where(lane < 12, x[:, 12 * s : 12 * s + PPAD], 0.0)

    cut(center / scale, pieces)
    cut(tgt_ref[...], tgt)
    cut(mask * (2.0 / (1 << 20)), kept)


def prepare(series, observed, targets, target_mask, counts, matrices, feed, vectors):
    nv = series.shape[0]
    shapes = [((SEG, nv, PPAD), F32), ((SEG // 2, nv, PPAD), F32), ((SEG // 2, nv, PPAD), F32), ((nv, PPAD), F32), ((nv, PPAD), F32)]
    shapes += [((nv, HALF), F32), ((8, HALF), F32)]
    shapes += [((x.shape[0] // 2, D), BF) for x in (matrices, feed, vectors)]
    return pl.pallas_call(
        functools.partial(prepare_kernel, 0),
        grid=(1,),
        in_specs=[whole(x.shape) for x in (series, observed, targets, target_mask)]
        + [pl.BlockSpec(memory_space=pltpu.SMEM)]
        + [whole(x.shape) for x in (matrices, feed, vectors)],
        out_specs=[whole(s) for s, _ in shapes],
        out_shape=[jax.ShapeDtypeStruct(s, t) for s, t in shapes],
        compiler_params=pltpu.CompilerParams(vmem_limit_bytes=VMEM_LIMIT),
        name="prepare",
    )(series, observed, targets, target_mask, counts, matrices, feed, vectors)


def unpack_kernel(devices, own, vec_ref, vecs, mvec, emb, place, head, r0, r1, flat):
    flat[...] = jnp.zeros(flat.shape, F32)
    rows = vec_ref.shape[1]
    lane = lax.broadcasted_iota(jnp.int32, (rows, D), 1)
    for d in range(devices):
        at, shift = divmod(own * d, D)
        block = vec_ref[d].astype(F32)
        if shift:
            block = pltpu.roll(block, shift, 1)
            flat[at + 1 : at + 1 + rows] += jnp.where(lane < shift, block, 0.0)
            block = jnp.where(lane >= shift, block, 0.0)
        flat[at : at + rows] += block

    def padded(at, count, total):
        return jnp.concatenate([flat[at : at + count], jnp.zeros((total - count, D), F32)], 0)

    for l in range(2):
        vecs[l] = padded(LAYER_AT + 23 * l, 23, 24)
    mvec[...] = padded(MERGE_AT, 5, 8)
    emb[...] = padded(0, SEGLEN, 16).astype(BF)
    head[...] = padded(HEAD_AT, PRED, PPAD).astype(BF)
    for s in range(SEG):
        place[s] = flat[SEGLEN + 1 + s : SEGLEN + 2 + s] + flat[SEGLEN : SEGLEN + 1]
        r0[s] = padded(ROUTER_AT + ROUT * s, ROUT, RPAD)
    for s in range(SEG // 2):
        r1[s] = padded(ROUTER_AT + ROUT * (SEG + s), ROUT, RPAD)


def unpack_vectors(gathered, own):
    devices, rows, _ = gathered.shape
    shapes = [((2, 24, D), F32), ((8, D), F32), ((16, D), BF), ((SEG, 1, D), F32), ((PPAD, D), BF)]
    shapes += [((SEG, RPAD, D), F32), ((SEG // 2, RPAD, D), F32)]
    return pl.pallas_call(
        functools.partial(unpack_kernel, devices, own),
        grid=(1,),
        in_specs=[whole(gathered.shape)],
        out_specs=[whole(s) for s, _ in shapes],
        out_shape=[jax.ShapeDtypeStruct(s, t) for s, t in shapes],
        scratch_shapes=[pltpu.VMEM((VROWS + 24, D), F32)],
        compiler_params=pltpu.CompilerParams(vmem_limit_bytes=VMEM_LIMIT),
        name="unpack_vectors",
    )(gathered)


def assemble_kernel(devices, own, demb, dplace, *refs):
    (rt0, rs0, rr0, rt1, rs1, rr1, dmv, dhead, dr0, dr1), out, flat = refs[:10], refs[10], refs[11]
    flat[...] = jnp.zeros(flat.shape, F32)
    flat[0:SEGLEN] = demb[0:SEGLEN]
    place = jnp.sum(dplace[...].reshape(SEG, VB, D), 1)
    flat[SEGLEN : SEGLEN + 1] = jnp.sum(place, 0, keepdims=True)
    flat[SEGLEN + 1 : SEGLEN + 1 + SEG] = place
    at = LAYER_AT
    for ref in (rt0, rs0, rr0, rt1, rs1, rr1, dmv):
        count = ref.shape[0]
        flat[at : at + count] = jnp.sum(ref[...], 1)
        at += count
    flat[HEAD_AT : HEAD_AT + PRED] = dhead[0:PRED]
    for s in range(SEG):
        flat[ROUTER_AT + ROUT * s : ROUTER_AT + ROUT * (s + 1)] = dr0[s][:ROUT]
    for s in range(SEG // 2):
        flat[ROUTER_AT + ROUT * (SEG + s) : ROUTER_AT + ROUT * (SEG + s + 1)] = dr1[s][:ROUT]
    rows = out.shape[1]
    lane = lax.broadcasted_iota(jnp.int32, (rows, D), 1)
    inside = lax.broadcasted_iota(jnp.int32, (rows, D), 0) * D + lane < own
    for d in range(devices):
        at, shift = divmod(own * d, D)
        block = flat[at : at + rows]
        if shift:
            block = jnp.where(lane < D - shift, pltpu.roll(block, D - shift, 1), pltpu.roll(flat[at + 1 : at + 1 + rows], D - shift, 1))
        out[d] = jnp.where(inside, block, 0.0)


def assemble_vectors(parts, devices):
    own, rows = own_size(devices)
    return pl.pallas_call(
        functools.partial(assemble_kernel, devices, own),
        grid=(1,),
        in_specs=[whole(p.shape) for p in parts],
        out_specs=whole((devices, rows, D)),
        out_shape=jax.ShapeDtypeStruct((devices, rows, D), F32),
        scratch_shapes=[pltpu.VMEM((VROWS + 24, D), F32)],
        compiler_params=pltpu.CompilerParams(vmem_limit_bytes=VMEM_LIMIT),
        name="assemble_vectors",
    )(*parts)


def adam_update(weight, first_moment, second_moment, gradient):
    first_new = beta_one * first_moment + (1.0 - beta_one) * gradient
    second_new = beta_two * second_moment + (1.0 - beta_two) * gradient * gradient
    corrected = (
        first_new
        / (1.0 - beta_one**step_count)
        / (jnp.sqrt(second_new / (1.0 - beta_two**step_count)) + adam_eps)
    )
    return (weight - learn_rate * (corrected + weight_decay * weight), first_new, second_new)


def adam_kernel(up_rows, s_mat, s_feed, sums, *refs):
    old, new, norm_ref, scratch = refs[:6], refs[6:12], refs[12], refs[13:]

    def add_up(x):
        return jnp.sum(jnp.sum(x, 0, keepdims=True), -1, keepdims=True)

    upscale = (1 << 20) / jnp.maximum(add_up(sums[8:]), 1.0)
    norm = jnp.sqrt(add_up(sums[:8])) * upscale
    factor = upscale * (clip_norm / jnp.maximum(norm, clip_norm))
    norm_ref[0:1] = jnp.broadcast_to(norm, (1, HALF))
    norm_ref[1:2] = jnp.broadcast_to(factor, (1, HALF))

    def spread(src, dst):
        rows = src.shape[0]
        value = src[...] * factor
        dst[pl.ds(0, rows, stride=2), :] = value[:, :HALF]
        dst[pl.ds(1, rows, stride=2), :] = value[:, HALF:]

    spread(s_mat, scratch[0])
    up = lax.axis_index("dp") * 2 < lax.axis_size("dp")
    pl.when(jnp.logical_not(up))(lambda: spread(s_feed, scratch[1]))

    @pl.when(up)
    def _():
        for half in range(2):
            value = s_feed[half * up_rows : (half + 1) * up_rows] * factor
            scratch[1][pl.ds(2 * half, up_rows, stride=4), :] = value[:, :HALF]
            scratch[1][pl.ds(2 * half + 1, up_rows, stride=4), :] = value[:, HALF:]

    for k in range(2):
        values = adam_update(*[ref[...] for ref in old[3 * k : 3 * k + 3]], scratch[k][...])
        for ref, value in zip(new[3 * k : 3 * k + 3], values):
            ref[...] = value


def adam_packs(s_mat, s_feed, sums, old, up_rows):
    args = [s_mat, s_feed, sums] + old
    outs = [x.shape for x in old] + [(8, HALF)]
    return pl.pallas_call(
        functools.partial(adam_kernel, up_rows),
        grid=(1,),
        in_specs=[whole(x.shape) for x in args],
        out_specs=[whole(s) for s in outs],
        out_shape=[jax.ShapeDtypeStruct(s, F32) for s in outs],
        scratch_shapes=[pltpu.VMEM(old[0].shape, F32), pltpu.VMEM(old[3].shape, F32)],
        compiler_params=params_spec(),
        name="adam_packs",
    )(*args)


def gradient_parts(ready, model, extras, up_rows, group_stats, group_sum, nf, devices):
    pieces, tgt, kept, scale, mean, here = ready
    mvec, emb, place, head, routers0, routers1 = extras
    sb0, sb1, sf0, sf1, st = 12, 10, 20, 10, 10
    rf, rb = 20, 20
    half = SEG // 2
    dim0, kept0 = time_fwd(True, pieces, (emb, place), model, 0, SEG)
    o0 = send_fwd(dim0, routers0, here, model, 0, sf0, -(-SEG // nf) * nf)
    o0 = group_stats(o0, 2)
    x1, *saved = recv_fwd(dim0, o0, model, mvec, rf)
    dim1, kept1 = time_fwd(False, x1, (), model, 1, half)
    o1 = send_fwd(dim1, routers1, here, model, 1, sf1, -(-half // nf) * nf)
    o1 = group_stats(o1, 3)
    vecs = model[3]
    g_mat, g_feed, ddim1, do1, rr1, dhead, *work = tail(dim1, o1, tgt, kept, scale, mean, model, head, st, nf)
    do1, *later = group_sum(do1, [dim1.reshape(-1, D)] + work, vecs, 1, 4)
    g_mat, ddim1, dr1, rs1 = send_bwd(dim1, ddim1, routers1, o1, do1, here, model, 1, sb1, g_mat)
    g_mat, g_feed, rt1, dx1 = time_bwd(
        False, x1, (), ddim1, kept1, model, 1, half, later, (g_mat, g_feed), up_rows
    )
    g_mat, ddim0, do0, rr0, dmv, *work = recv_bwd(dim0, o0, dx1, saved, model, mvec, rb, g_mat, nf)
    work = [dim0.reshape(-1, D), saved[1], saved[3], saved[4]] + work
    do0, *later = group_sum(do0, work, vecs, 0, 5)
    g_mat, ddim0, dr0, rs0 = send_bwd(dim0, ddim0, routers0, o0, do0, here, model, 0, sb0, g_mat)
    g_mat, g_feed, rt0, demb, dplace = time_bwd(
        True, pieces, (emb, place), ddim0, kept0, model, 0, SEG, later, (g_mat, g_feed), up_rows
    )
    g_vec = assemble_vectors((demb, dplace, rt0, rs0, rr0, rt1, rs1, rr1, dmv, dhead, dr0, dr1), devices)
    return g_mat, g_feed, g_vec


def on_device(series, observed, targets, target_mask, counts, matrices, feed_weights, vectors, matrices_first, matrices_second, feed_first, feed_second, vectors_first, vectors_second):
    nf = lax.axis_size("fsdp")
    nd = lax.axis_size("dp")
    devices = nf * nd
    own, vec_rows = own_size(devices)
    out = prepare(
        series[0],
        observed[0],
        targets[0],
        target_mask[0],
        counts,
        matrices.reshape(-1, HALF),
        feed_weights.reshape(-1, HALF),
        jnp.pad(vectors, (0, vec_rows * D - own)).reshape(-1, HALF),
    )
    ready, tile, shards = out[:6], out[6], out[7:]
    square, feed, vecs = gather_all(shards)
    square = square.reshape(NSQ, D, D)
    feed = feed.reshape(-1, D)
    up = feed[: 4 * FF].reshape(4, D, FF)
    down = feed.reshape(8, FF, D)
    vecs, *extras = unpack_vectors(vecs.reshape(devices, vec_rows, D), own)
    up_rows = feed_weights.shape[0] // FF
    g_mat, g_feed, g_vec = gradient_parts(ready, (square, up, down, vecs), extras, up_rows, group_stats, group_sum, nf, devices)
    ny, nz, nx = grid_sizes()
    lead = (ny, 2, nz, nx)
    s_mat, s_feed, s_vec, sums = scatter_sum([g.reshape(lead + (-1, D)) for g in (g_mat, g_feed, g_vec)], tile)
    old = [matrices, matrices_first, matrices_second, feed_weights, feed_first, feed_second]
    *new, norm = adam_packs(s_mat, s_feed, sums, [x.reshape(-1, HALF) for x in old], up_rows)
    vec_new = adam_update(vectors, vectors_first, vectors_second, s_vec.reshape(-1)[:own] * norm[1, 0])
    return (norm[0, 0], *[x.reshape(-1) for x in new], *vec_new)


def solution(mesh):
    both = P(("dp", "fsdp"))
    data = P("dp", "fsdp", None)
    return jax.shard_map(
        on_device,
        mesh=mesh,
        in_specs=(data,) * 4 + (P("dp"),) + (both,) * 9,
        out_specs=(P(),) + (both,) * 9,
        check_vma=False,
    )
```

```python
import functools
import jax
import jax.numpy as jnp
from jax import lax
from jax.experimental import pallas as pl
from jax.experimental.pallas import tpu as pltpu
from jax.sharding import PartitionSpec as P

D = 256
HEADS = 8
FF = 512
ROUT = 10
RPAD = 16
SEGLEN = 12
PRED = 12
PPAD = 16
SEG = 60
NSQ = 26
NVEC = 1036
HALF = 128
VB = 8
UNROLL = 8
UNROLL_BACK = 8

BF = jnp.bfloat16
F32 = jnp.float32
SCALE = (D // HEADS) ** (-0.5)
negative = -1e30
norm_eps = 1e-05
beta_one = 0.9
beta_two = 0.999
adam_eps = 1e-08
weight_decay = 0.01
learn_rate = 0.2
clip_norm = 0.01
step_count = 10.0
VMEM_LIMIT = 60 << 20


ANY = pl.BlockSpec(memory_space=pl.ANY)
INVMEM = pl.BlockSpec(memory_space=pltpu.VMEM)


def split2(x):
    hi = x.astype(BF)
    return hi, (x - hi.astype(F32)).astype(BF)


def dots(a, b, ca, cb):
    return lax.dot_general(a, b, (((ca,), (cb,)), ((), ())), preferred_element_type=F32)


def mmw(x2, w):
    return dots(x2[0], w, 1, 0) + dots(x2[1], w, 1, 0)


def mmwt(x2, w):
    return dots(x2[0], w, 1, 1) + dots(x2[1], w, 1, 1)


def rows2(a2):
    return jnp.concatenate([a2[0], a2[1]], 0)


def nn3(a2, b2):
    m = a2[0].shape[0]
    both = dots(rows2(a2), b2[0], 1, 0)
    return both[:m] + both[m:] + dots(a2[0], b2[1], 1, 0)


def nt3(a2, b2):
    m = a2[0].shape[0]
    both = dots(rows2(a2), b2[0], 1, 1)
    return both[:m] + both[m:] + dots(a2[0], b2[1], 1, 1)


def tn3(a2, b2):
    n = b2[0].shape[1]
    both = dots(a2[0], jnp.concatenate([b2[0], b2[1]], 1), 0, 0)
    return both[:, :n] + both[:, n:] + dots(a2[1], b2[0], 0, 0)


def tn3_short(a2, b2):
    return dots(jnp.concatenate([a2[0], a2[0], a2[1]], 0), jnp.concatenate([b2[0], b2[1], b2[0]], 0), 0, 0)


def nn3_short(a2, b2):
    return dots(jnp.concatenate([a2[0], a2[0], a2[1]], 1), jnp.concatenate([b2[0], b2[1], b2[0]], 0), 1, 0)


def corner(r, m, n):
    return r[:m, :n] + r[m:, :n] + r[:m, n:]


def nn3_narrow(a2, b2):
    r = dots(rows2(a2), jnp.concatenate([b2[0], b2[1]], 1), 1, 0)
    return corner(r, a2[0].shape[0], b2[0].shape[1])


def nt3_narrow(a2, b2):
    return corner(dots(rows2(a2), rows2(b2), 1, 1), a2[0].shape[0], b2[0].shape[0])


def norm_fwd(z, gain, bias):
    center = z - jnp.mean(z, -1, keepdims=True)
    inv = lax.rsqrt(jnp.mean(center * center, -1, keepdims=True) + norm_eps)
    unit = center * inv
    return unit * gain + bias, unit, inv


def norm_bwd(dy, unit, inv, gain):
    t = dy * gain
    return inv * (t - jnp.mean(t, -1, keepdims=True) - unit * jnp.mean(t * unit, -1, keepdims=True))


def colsum(x):
    return jnp.sum(x.reshape(x.shape[0] // 8, 8, x.shape[1]), 0)


def gelu_cdf(u):
    return 0.5 + 0.5 * lax.erf(u * 0.7071067811865476)


def gelu_slope(u, cdf):
    return cdf + u * (jnp.exp(-0.5 * u * u) * 0.3989422804014327)


def halves(x):
    return x[:, :HALF], x[:, HALF:]


def lane_head(rows):
    return lax.broadcasted_iota(jnp.int32, (rows, HALF), 1) // 32


def spread_heads(x, zero):
    head = lane_head(x.shape[0])
    return jnp.concatenate([jnp.where(head == h, x, zero) for h in range(4)], 0)


def gather_heads(x, group):
    head = lane_head(group)
    out = x[3 * group :]
    for h in range(3):
        out = jnp.where(head == h, x[h * group : (h + 1) * group], out)
    return out


def ones_heads(group, count):
    row = lax.broadcasted_iota(jnp.int32, (4 * group, HALF), 0)
    lane = lax.broadcasted_iota(jnp.int32, (4 * group, HALF), 1)
    return jnp.where((row // group == lane // 32) & (row % group < count), 1.0, 0.0).astype(BF)


def group_max(s, group, count):
    lane = lax.broadcasted_iota(jnp.int32, (s.shape[0], HALF), 1)
    outs = []
    for t in range(s.shape[1] // HALF):
        part = s[:, t * HALF : (t + 1) * HALF]
        top = None
        for g in range(HALF // group):
            here = (lane // group == g)
            best = jnp.max(jnp.where((lane // group == g) & (lane % group < count), part, negative), -1, keepdims=True)
            top = jnp.broadcast_to(best, part.shape) if top is None else jnp.where(here, best, top)
        outs.append(jnp.where(lane % group < count, part - top, negative))
    return jnp.concatenate(outs, 1)


def time_parts(units, group, ref):
    return [split2(ref[c, pl.ds(v, group, stride=VB), :]) for c, v in units]


def spread2(x2):
    zero = jnp.zeros((), BF)
    return spread_heads(x2[0], zero), spread_heads(x2[1], zero)


def time_attend(units, group, count, q_s, k_s, v_s, o_s, p_s, l_s):
    q = time_parts(units, group, q_s)
    k = [spread2(x2) for x2 in time_parts(units, group, k_s)]
    scores = [
        dots(jnp.concatenate(q2, 1), jnp.concatenate([k2[0], k2[0]], 1), 1, 1) + dots(q2[0], k2[1], 1, 1)
        for q2, k2 in zip(q, k)
    ]
    probs = [jnp.exp(group_max(s, group, count)) for s in scores]
    probs2 = [split2(p) for p in probs]
    w = [spread2(x2) for x2 in time_parts(units, group, v_s)]
    ones = ones_heads(group, count)
    both = [dots(rows2(p2), jnp.concatenate([w2[0], ones], 1), 1, 0) for p2, w2 in zip(probs2, w)]
    both = [b[:group] + b[group:] for b in both]
    inv = [1.0 / b[:, HALF:] for b in both]
    mixed = [(b[:, :HALF] + dots(p2[0], w2[1], 1, 0)) * i for b, p2, w2, i in zip(both, probs2, w, inv)]
    for (c, v), o, p, i in zip(units, mixed, probs, inv):
        o_s[c, pl.ds(v, group, stride=VB), :] = o
        p_s[c, v] = p
        l_s[c, v] = i


def time_attend_back(units, group, count, q_s, k_s, v_s, o_s, p_s, l_s, do_s, dq_s, dk_s, dv_s):
    d = [do_s[c, pl.ds(v, group, stride=VB), :] * l_s[c, v] for c, v in units]
    e2 = [split2(x * o_s[c, pl.ds(v, group, stride=VB), :]) for x, (c, v) in zip(d, units)]
    d2 = [split2(x) for x in d]
    w = [spread2(x2) for x2 in time_parts(units, group, v_s)]
    ones = -ones_heads(group, count)
    both = [
        dots(
            jnp.concatenate([jnp.concatenate([a[0], b[0]], 1), jnp.concatenate([a[1], b[1]], 1)], 0),
            jnp.concatenate([w2[0], ones], 1),
            1,
            1,
        )
        for a, b, w2 in zip(d2, e2, w)
    ]
    dp = [b[:group] + b[group:] + dots(a[0], w2[1], 1, 1) for b, a, w2 in zip(both, d2, w)]
    probs = [p_s[c, v] for c, v in units]
    s2 = [split2(p * x) for p, x in zip(probs, dp)]
    p2 = [split2(p) for p in probs]
    k = [spread2(x2) for x2 in time_parts(units, group, k_s)]
    dq = [nn3_narrow(a, k2) for a, k2 in zip(s2, k)]
    q = time_parts(units, group, q_s)
    dk = [gather_heads(tn3_short(a, q2), group) for a, q2 in zip(s2, q)]
    dv = [gather_heads(tn3_short(a, x), group) for a, x in zip(p2, d2)]
    for (c, v), x, y, z in zip(units, dq, dk, dv):
        at = pl.ds(v, group, stride=VB)
        dq_s[c, at, :] = x
        dk_s[c, at, :] = y
        dv_s[c, at, :] = z


def store_halves(ref, x):
    rows = x.shape[0]
    ref[0, :rows, :] = x[:, :HALF]
    ref[1, :rows, :] = x[:, HALF:]


def load_halves(ref, rows):
    return jnp.concatenate([ref[0, :rows, :], ref[1, :rows, :]], 1)


def zero_tail(ref, rows):
    tail = ref.shape[1] - rows
    ref[:, rows:, :] = jnp.zeros((2, tail, HALF), F32)


def time_forward(x, w, vec, count, group, kept):
    q_s, k_s, v_s, o_s, p_s, l_s, z1_s, u_s, z2_s = kept
    rows = count * VB
    x2 = split2(x)
    store_halves(q_s, (mmw(x2, w["q"]) + vec[0:1]) * SCALE)
    store_halves(k_s, mmw(x2, w["k"]))
    store_halves(v_s, mmw(x2, w["v"]) + vec[1:2])
    for ref in (q_s, k_s, v_s):
        zero_tail(ref, rows)

    def some(i, carry):
        units = [(c, i * UNROLL + k) for k in range(UNROLL) for c in range(2)]
        time_attend(units, group, count, q_s, k_s, v_s, o_s, p_s, l_s)
        return carry

    lax.fori_loop(0, VB // UNROLL, some, 0)
    z1 = x + mmw(split2(load_halves(o_s, rows)), w["o"]) + vec[2:3]
    z1_s[...] = z1
    h, _, _ = norm_fwd(z1, vec[3:4], vec[4:5])
    u = mmw(split2(h), w["up"]) + jnp.concatenate([vec[5:6], vec[6:7]], 1)
    u_s[...] = u
    z2 = h + mmw(split2(u * gelu_cdf(u)), w["down"]) + vec[7:8]
    z2_s[...] = z2
    return norm_fwd(z2, vec[8:9], vec[9:10])[0]


def embed_block(pieces, emb, place):
    return mmw(split2(pieces), emb) + place


TIME_W = ("q", "k", "v", "o", "up", "down")


def time_fwd_kernel(first, count, group, *refs):
    if first:
        x_ref, emb_ref, place_ref = refs[:3]
        refs = refs[3:]
    else:
        x_ref = refs[0]
        refs = refs[1:]
    w = {name: refs[i][...] for i, name in enumerate(TIME_W)}
    vec_ref, y_ref = refs[6:8]
    rows = count * VB
    if first:
        place = jnp.broadcast_to(place_ref[...], (count, VB, D)).reshape(rows, D)
        x = embed_block(x_ref[...].reshape(rows, 16), emb_ref[...], place)
    else:
        x = x_ref[...].reshape(rows, D)
    y = time_forward(x, w, vec_ref[...], count, group, refs[8:])
    y_ref[...] = y.reshape(count, VB, D)


def whole(shape):
    return pl.BlockSpec(shape, lambda i: (0,) * len(shape))


def params_spec():
    return pltpu.CompilerParams(vmem_limit_bytes=VMEM_LIMIT)


def pick(shape, index):
    return pl.BlockSpec((None,) + shape, lambda i: (index,) + (0,) * len(shape))


def weight_specs(squares, feed, layer):
    specs = [pick((D, D), k) for k in squares]
    if feed is not None:
        specs += [pick((D, FF), feed), pick((FF, D), 4 + feed)]
    return specs + [pick((24, D), layer)]


def weight_args(model, squares, feed):
    square, up, down, vecs = model
    return [square] * len(squares) + ([up, down] if feed is not None else []) + [vecs]


def flush(step, last, accs, mat_at, feeds, up_rows, g_mat, g_feed, sems):
    @pl.when(step == last)
    def _():
        copies = []

        def add(src, dst):
            copies.append(pltpu.make_async_copy(src, dst, sems.at[len(copies)]))

        for acc, at in zip(accs, mat_at):
            add(acc, g_mat.at[pl.ds(at, acc.shape[0])] if len(acc.shape) == 3 else g_mat.at[at])
        for up_acc, down_acc, feed_at in feeds:
            for k in range(D // up_rows):
                for half in range(2):
                    base = 2 * D * feed_at + (2 * k + half) * up_rows
                    add(up_acc.at[pl.ds(k * up_rows, up_rows), pl.ds(half * D, D)], g_feed.at[pl.ds(base, up_rows)])
            add(down_acc, g_feed.at[pl.ds(4 * FF + feed_at * FF, FF)])
        for copy in copies:
            copy.start()
        for copy in copies:
            copy.wait()


def pack_shapes():
    return [jax.ShapeDtypeStruct((NSQ, D, D), F32), jax.ShapeDtypeStruct((8 * FF, D), F32)]


def flush_count(mats, feeds, up_rows):
    return mats + feeds * (2 * D // up_rows + 1 if up_rows else 0)


def time_kept(count, group, nb):
    pad, rows = group * VB, count * VB
    shapes = [(2, pad, HALF)] * 4 + [(2, VB, group, 4 * group), (2, VB, group, HALF), (rows, D), (rows, FF), (rows, D)]
    specs = [pl.BlockSpec((None,) + s, lambda i, n=len(s): (i,) + (0,) * n) for s in shapes]
    return specs, [jax.ShapeDtypeStruct((nb,) + s, F32) for s in shapes]


def time_fwd(first, x, extra, model, layer, count):
    squares = [12 * layer + k for k in range(4)]
    group = 64 if count > 32 else 32
    nv = x.shape[1]
    width = x.shape[2]
    specs = [pl.BlockSpec((count, VB, width), lambda i: (0, i, 0))]
    if first:
        specs += [whole((16, D)), whole((count, 1, D))]
    kept_specs, kept_shapes = time_kept(count, group, nv // VB)
    out = pl.pallas_call(
        functools.partial(time_fwd_kernel, first, count, group),
        grid=(nv // VB,),
        in_specs=specs + weight_specs(squares, 2 * layer, layer),
        out_specs=[pl.BlockSpec((count, VB, D), lambda i: (0, i, 0))] + kept_specs,
        out_shape=[jax.ShapeDtypeStruct((count, nv, D), F32)] + kept_shapes,
        compiler_params=params_spec(),
        name="time_fwd",
    )(x, *extra, *weight_args(model, squares, 2 * layer))
    return out[0], out[1:]


def time_bwd_kernel(first, count, group, layer, up_rows, *refs):
    if first:
        x_ref, emb_ref, place_ref = refs[:3]
        refs = refs[3:]
    else:
        x_ref = refs[0]
        refs = refs[1:]
    dy_ref = refs[0]
    q_s, k_s, v_s, o_s, p_s, l_s, z1_s, u_s, z2_s = refs[1:10]
    w = {name: refs[10 + i][...] for i, name in enumerate(TIME_W)}
    vec_ref = refs[16]
    later = refs[17:21]
    g_mat, g_feed = refs[23:25]
    outs = refs[25:]
    n_out = 3 if first else 2
    tail = outs[1:n_out]
    accs = outs[n_out : n_out + 6]
    sems = outs[n_out + 6]
    g = dict(zip(TIME_W + ("rows",), tuple(accs) + (outs[0],)))
    do_s, dq_s, dk_s, dv_s = outs[n_out + 7 :]
    rows = count * VB
    step = pl.program_id(0)

    @pl.when(step == 0)
    def _():
        for ref in list(g.values()) + (list(tail) if first else []):
            ref[...] = jnp.zeros(ref.shape, F32)

    vec = vec_ref[...]
    if first:
        place = jnp.broadcast_to(place_ref[...], (count, VB, D)).reshape(rows, D)
        pieces = x_ref[...].reshape(rows, 16)
        x = embed_block(pieces, emb_ref[...], place)
    else:
        x = x_ref[...].reshape(rows, D)
    x2 = split2(x)
    mixed = load_halves(o_s, rows)
    h, unit1, inv1 = norm_fwd(z1_s[...], vec[3:4], vec[4:5])
    u = u_s[...]
    cdf = gelu_cdf(u)
    _, unit2, inv2 = norm_fwd(z2_s[...], vec[8:9], vec[9:10])
    dy = dy_ref[...].reshape(rows, D)
    g["rows"][8] += colsum(dy * unit2)
    g["rows"][9] += colsum(dy)
    dz2 = norm_bwd(dy, unit2, inv2, vec[8:9])
    g["rows"][7] += colsum(dz2)
    dz22 = split2(dz2)
    g["down"][...] += tn3(split2(u * cdf), dz22)
    du = mmwt(dz22, w["down"]) * gelu_slope(u, cdf)
    g["rows"][5] += colsum(du[:, :D])
    g["rows"][6] += colsum(du[:, D:])
    du2 = split2(du)
    g["up"][...] += tn3(split2(h), du2)
    dh = dz2 + mmwt(du2, w["up"])
    g["rows"][3] += colsum(dh * unit1)
    g["rows"][4] += colsum(dh)
    dz1 = norm_bwd(dh, unit1, inv1, vec[3:4])
    g["rows"][2] += colsum(dz1)
    dz12 = split2(dz1)
    g["o"][...] += tn3(split2(mixed), dz12)
    store_halves(do_s, mmwt(dz12, w["o"]))
    zero_tail(do_s, rows)

    def some(i, carry):
        units = [(c, i * UNROLL_BACK + k) for k in range(UNROLL_BACK) for c in range(2)]
        time_attend_back(units, group, count, q_s, k_s, v_s, o_s, p_s, l_s, do_s, dq_s, dk_s, dv_s)
        return carry

    lax.fori_loop(0, VB // UNROLL_BACK, some, 0)
    dq = load_halves(dq_s, rows) * SCALE
    g["rows"][0] += colsum(dq)
    dq2 = split2(dq)
    g["q"][...] += tn3(x2, dq2)
    dx = dz1 + mmwt(dq2, w["q"])
    dk2 = split2(load_halves(dk_s, rows))
    g["k"][...] += tn3(x2, dk2)
    dx = dx + mmwt(dk2, w["k"])
    dv = load_halves(dv_s, rows)
    g["rows"][1] += colsum(dv)
    dv2 = split2(dv)
    g["v"][...] += tn3(x2, dv2)
    dx = dx + mmwt(dv2, w["v"])
    if first:
        tail[0][...] += tn3(split2(pieces), split2(dx))
        tail[1][...] += dx
    else:
        tail[0][...] = dx.reshape(count, VB, D)
    flush(
        step, pl.num_programs(0) - 1, list(accs[:4]) + list(later[:2]), [12 * layer + k for k in (0, 1, 2, 3, 8, 11)],
        [(accs[4], accs[5], 2 * layer), (later[2], later[3], 2 * layer + 1)], up_rows, g_mat, g_feed, sems,
    )


def time_bwd(first, x, extra, dy, kept, model, layer, count, later, packs, up_rows):
    group = 64 if count > 32 else 32
    nv = x.shape[1]
    width = x.shape[2]
    pad = group * VB
    squares = [12 * layer + k for k in range(4)]
    block = pl.BlockSpec((count, VB, D), lambda i: (0, i, 0))
    specs = [pl.BlockSpec((count, VB, width), lambda i: (0, i, 0))]
    if first:
        specs += [whole((16, D)), whole((count, 1, D))]
    specs += [block] + time_kept(count, group, nv // VB)[0] + weight_specs(squares, 2 * layer, layer)
    specs += [whole((D, D)), whole((D, D)), whole((D, FF)), whole((FF, D))]
    grad_shapes = [(10, 8, D)] + ([(16, D), (count * VB, D)] if first else [])
    out_specs = [ANY] * 2 + [whole(s) for s in grad_shapes]
    out_shape = pack_shapes() + [jax.ShapeDtypeStruct(s, F32) for s in grad_shapes]
    if not first:
        out_specs.append(block)
        out_shape.append(jax.ShapeDtypeStruct((count, nv, D), F32))
    return pl.pallas_call(
        functools.partial(time_bwd_kernel, first, count, group, layer, up_rows),
        grid=(nv // VB,),
        in_specs=specs + [ANY] * 2,
        out_specs=out_specs,
        out_shape=out_shape,
        input_output_aliases={len(specs): 0, len(specs) + 1: 1},
        scratch_shapes=[pltpu.VMEM((D, D), F32)] * 4
        + [pltpu.VMEM((D, FF), F32), pltpu.VMEM((FF, D), F32), pltpu.SemaphoreType.DMA((flush_count(6, 2, up_rows),))]
        + [pltpu.VMEM((2, pad, HALF), F32)] * 4,
        compiler_params=params_spec(),
        name="time_bwd",
    )(x, *extra, dy, *kept, *weight_args(model, squares, 2 * layer), *later, *packs)

SB_ROWS = 64


def head_rows():
    sub = lax.broadcasted_iota(jnp.int32, (8, D), 0)
    lane = lax.broadcasted_iota(jnp.int32, (8, D), 1)
    return jnp.where(sub == lane // 32, 1.0, 0.0).astype(F32)


def spread_rows(x):
    wide = jnp.broadcast_to(x[:, None, :], (RPAD, HEADS, D)) * head_rows()[None]
    return wide.reshape(RPAD * HEADS, D)


def gather_rows(x):
    return jnp.sum(x.reshape(RPAD, HEADS, D) * head_rows()[None], 1)


PACK = 24


def pack_rows(x, last=None):
    last = jnp.zeros((1, HALF), F32) if last is None else last
    return jnp.concatenate([x[:ROUT, :HALF], x[:ROUT, HALF:], last, jnp.zeros((PACK - 2 * ROUT - 1, HALF), F32)], 0)


def unpack_rows(x):
    x = jnp.concatenate([x[:ROUT], x[ROUT : 2 * ROUT]], 1)
    return jnp.concatenate([x, jnp.zeros((RPAD - ROUT, D), F32)], 0)


def unpack_block(ref, sb):
    return jnp.concatenate([unpack_rows(ref[s]) for s in range(sb)], 0)


TALL = 2 * ROUT


def tall_spec(sb):
    return pl.BlockSpec((sb * TALL, HALF), lambda i: (i, 0))


def tall_rows(n, parts):
    return -(-n * TALL // (8 * parts)) * 8 * parts


def pack_block(ref, x, sb):
    for s in range(sb):
        rows = x[s * RPAD : s * RPAD + ROUT]
        ref[s * TALL : (s + 1) * TALL] = jnp.concatenate([rows[:, :HALF], rows[:, HALF:]], 0)


def valid_lane(rows):
    return lax.broadcasted_iota(jnp.int32, (rows, HALF), 1) < ROUT * HEADS


def router_reduce(x, op):
    for shift in (8, 16, 32, 64):
        x = op(x, pltpu.roll(x, shift, 1))
    return x


def merge_rows(y, pairs, vec):
    wide = y.reshape(pairs, 2, SB_ROWS, D)
    wide = jnp.concatenate([wide[:, 0].reshape(pairs * SB_ROWS, D), wide[:, 1].reshape(pairs * SB_ROWS, D)], 1)
    gain = jnp.concatenate([vec[0:1], vec[1:2]], 1)
    bias = jnp.concatenate([vec[2:3], vec[3:4]], 1)
    return norm_fwd(wide, gain, bias) + (gain,)


RECV_W = ("so", "rk", "rv", "rq", "ro", "up", "down")


def recv_buffer(o2, w, vec):
    buf2 = split2(mmw(o2, w["so"]) + vec[12:13])
    kb = mmw(buf2, w["rk"])
    vb = mmw(buf2, w["rv"]) + vec[14:15]
    segs = range(kb.shape[0] // RPAD)
    k = [split2(spread_rows(kb[s * RPAD : (s + 1) * RPAD])) for s in segs]
    v = [split2(spread_rows(vb[s * RPAD : (s + 1) * RPAD])) for s in segs]
    return buf2, k, v


def recv_forward(send, o_rows, w, vec):
    sb = send.shape[0] // SB_ROWS
    send2 = split2(send)
    o2 = split2(o_rows)
    buf2, k, v = recv_buffer(o2, w, vec)
    q = (mmw(send2, w["rq"]) + vec[13:14]) * SCALE
    segs = range(sb)
    ok = valid_lane(SB_ROWS)
    scores = [jnp.where(ok, nt3_narrow(split2(q[s * SB_ROWS : (s + 1) * SB_ROWS]), k[s]), negative) for s in segs]
    probs = [jnp.exp(sc - router_reduce(sc, jnp.maximum)) for sc in scores]
    probs = [p / router_reduce(p, jnp.add) for p in probs]
    mixed = jnp.concatenate([nn3_short(split2(p), v2) for p, v2 in zip(probs, v)], 0)
    z3 = send + mmw(split2(mixed), w["ro"]) + vec[15:16]
    g, unit3, inv3 = norm_fwd(z3, vec[16:17], vec[17:18])
    u = mmw(split2(g), w["up"]) + jnp.concatenate([vec[18:19], vec[19:20]], 1)
    cdf = gelu_cdf(u)
    z4 = g + mmw(split2(u * cdf), w["down"]) + vec[20:21]
    y, unit4, inv4 = norm_fwd(z4, vec[21:22], vec[22:23])
    kept = (send2, o2, buf2, mixed, g, unit3, inv3, u, cdf, unit4, inv4, q, k, v, probs)
    return y, kept, (q, mixed, jnp.concatenate(probs, 0), z3, u, z4)


def recv_restore(send, o_rows, w, vec, saved):
    q, mixed, p, z3, u, z4 = saved
    o2 = split2(o_rows)
    buf2, k, v = recv_buffer(o2, w, vec)
    g, unit3, inv3 = norm_fwd(z3, vec[16:17], vec[17:18])
    y, unit4, inv4 = norm_fwd(z4, vec[21:22], vec[22:23])
    probs = [p[s * SB_ROWS : (s + 1) * SB_ROWS] for s in range(send.shape[0] // SB_ROWS)]
    return y, (split2(send), o2, buf2, mixed, g, unit3, inv3, u, gelu_cdf(u), unit4, inv4, q, k, v, probs)


KEPT_WIDTHS = (D, D, HALF, D, FF, D)


def kept_specs(sb):
    return [pl.BlockSpec((sb * SB_ROWS, k), lambda i: (i, 0)) for k in KEPT_WIDTHS]


RECV_G = ("so", "rk", "rv", "rows")
LATER_WIDTHS = (D, D, FF, D)


def row_specs(sb, widths):
    return [pl.BlockSpec((sb * SB_ROWS, k), lambda i: (i, 0)) for k in widths]


def row_shapes(n, widths):
    return [jax.ShapeDtypeStruct((n * SB_ROWS, k), F32) for k in widths]


def put(refs, values):
    for ref, value in zip(refs, values):
        ref[...] = value


def recv_backward(dy, kept, w, vec, g):
    send2, o2, buf2, mixed, gg, unit3, inv3, u, cdf, unit4, inv4, q, k, v, probs = kept
    sb = dy.shape[0] // SB_ROWS
    rows = g["rows"]
    rows[9] += colsum(dy * unit4)
    rows[10] += colsum(dy)
    dz4 = norm_bwd(dy, unit4, inv4, vec[21:22])
    rows[8] += colsum(dz4)
    dz42 = split2(dz4)
    du = mmwt(dz42, w["down"]) * gelu_slope(u, cdf)
    rows[6] += colsum(du[:, :D])
    rows[7] += colsum(du[:, D:])
    du2 = split2(du)
    dg = dz4 + mmwt(du2, w["up"])
    rows[4] += colsum(dg * unit3)
    rows[5] += colsum(dg)
    dz3 = norm_bwd(dg, unit3, inv3, vec[16:17])
    rows[3] += colsum(dz3)
    dz32 = split2(dz3)
    do = mmwt(dz32, w["ro"])
    segs = range(sb)
    d = [split2(do[s * SB_ROWS : (s + 1) * SB_ROWS]) for s in segs]
    dp = [nt3_narrow(d2, v2) for d2, v2 in zip(d, v)]
    ds = [split2(p * (x - router_reduce(p * x, jnp.add))) for p, x in zip(probs, dp)]
    dq = jnp.concatenate([nn3_short(s2, k2) for s2, k2 in zip(ds, k)], 0) * SCALE
    q = [split2(q[s * SB_ROWS : (s + 1) * SB_ROWS]) for s in segs]
    dk = jnp.concatenate([gather_rows(tn3_short(s2, q2)) for s2, q2 in zip(ds, q)], 0)
    dv = jnp.concatenate([gather_rows(tn3_short(split2(p), d2)) for p, d2 in zip(probs, d)], 0)
    rows[1] += colsum(dq)
    dq2 = split2(dq)
    dsend = dz3 + mmwt(dq2, w["rq"])
    dk2 = split2(dk)
    dv2 = split2(dv)
    rows[2] += colsum(dv)
    g["rk"][...] += tn3(buf2, dk2)
    g["rv"][...] += tn3(buf2, dv2)
    dbuf = mmwt(dk2, w["rk"]) + mmwt(dv2, w["rv"])
    rows[0] += colsum(dbuf)
    dbuf2 = split2(dbuf)
    g["so"][...] += tn3(o2, dbuf2)
    return dsend, mmwt(dbuf2, w["so"]), (dq, dz3, du, dz4)


def recv_squares(layer):
    return [12 * layer + k for k in (7, 9, 10, 8, 11)]


def seg_block(sb, rows=SB_ROWS, width=D):
    return pl.BlockSpec((sb, rows, width), lambda i: (i, 0, 0))


MERGE = pl.BlockSpec((2, D, D), lambda i: (12, 0, 0))


def pack_spec(sb):
    return seg_block(sb, PACK, HALF)


def recv_fwd_kernel(sb, send_ref, o_ref, *refs):
    w = {n: refs[i][...] for i, n in enumerate(RECV_W)}
    vec_ref, mvec_ref, mw_ref, out_ref = refs[7:11]
    y, _, saved = recv_forward(send_ref[...].reshape(sb * SB_ROWS, D), unpack_block(o_ref, sb), w, vec_ref[...])
    for ref, x in zip(refs[11:], saved):
        ref[...] = x
    mvec = mvec_ref[...]
    wide, _, _, _ = merge_rows(y, sb // 2, mvec)
    out_ref[...] = (mmw(split2(wide), mw_ref[...].reshape(2 * D, D)) + mvec[4:5]).reshape(sb // 2, SB_ROWS, D)


def recv_fwd(send, o, model, mvec, sb):
    squares = recv_squares(0)
    n = send.shape[0]
    return pl.pallas_call(
        functools.partial(recv_fwd_kernel, sb),
        grid=(n // sb,),
        in_specs=[seg_block(sb), pack_spec(sb)] + weight_specs(squares, 1, 0) + [whole((8, D)), MERGE],
        out_specs=[seg_block(sb // 2)] + kept_specs(sb),
        out_shape=[jax.ShapeDtypeStruct((n // 2, SB_ROWS, D), F32)]
        + [jax.ShapeDtypeStruct((n * SB_ROWS, k), F32) for k in KEPT_WIDTHS],
        compiler_params=params_spec(),
        name="recv_fwd",
    )(send, o, *weight_args(model, squares, 1), mvec, model[0])


def recv_bwd_kernel(sb, send_ref, o_ref, dx_ref, *refs):
    saved = [ref[...] for ref in refs[:6]]
    refs = refs[6:]
    w = {n: refs[i][...] for i, n in enumerate(RECV_W)}
    vec_ref, mvec_ref, mw_ref = refs[7:10]
    g_mat, dsend_ref, do_ref, rows_ref, dmv_ref = refs[11:16]
    later, accs, dmw_ref, sems = refs[16:20], refs[20:23], refs[23], refs[24]
    g = dict(zip(RECV_G, tuple(accs) + (rows_ref,)))

    @pl.when(pl.program_id(0) == 0)
    def _():
        for ref in list(g.values()) + [dmw_ref, dmv_ref]:
            ref[...] = jnp.zeros(ref.shape, F32)

    vec = vec_ref[...]
    y, kept = recv_restore(send_ref[...].reshape(sb * SB_ROWS, D), unpack_block(o_ref, sb), w, vec, saved)
    pairs = sb // 2
    wide, unit, inv, gain = merge_rows(y, pairs, mvec_ref[...])
    dx = dx_ref[...].reshape(pairs * SB_ROWS, D)
    dmv_ref[4] += colsum(dx)
    dx2 = split2(dx)
    dmw_ref[...] += tn3(split2(wide), dx2).reshape(2, D, D)
    dn = mmwt(dx2, mw_ref[...].reshape(2 * D, D))
    part = colsum(dn * unit)
    dmv_ref[0] += part[:, :D]
    dmv_ref[1] += part[:, D:]
    part = colsum(dn)
    dmv_ref[2] += part[:, :D]
    dmv_ref[3] += part[:, D:]
    dwide = norm_bwd(dn, unit, inv, gain)
    left = dwide[:, :D].reshape(pairs, 1, SB_ROWS, D)
    right = dwide[:, D:].reshape(pairs, 1, SB_ROWS, D)
    dy = jnp.concatenate([left, right], 1).reshape(sb * SB_ROWS, D)
    dsend, do, grads = recv_backward(dy, kept, w, vec, g)
    put(later, grads)
    dsend_ref[...] = dsend.reshape(sb, SB_ROWS, D)
    pack_block(do_ref, do, sb)
    recv_flush(accs, [(dmw_ref, 24)], 0, g_mat, sems)


RECV_ACC = [pltpu.VMEM((D, D), F32)] * 3


def recv_flush(accs, more, layer, g_mat, sems):
    flush(
        pl.program_id(0), pl.num_programs(0) - 1, list(accs) + [m for m, _ in more],
        recv_squares(layer)[:3] + [at for _, at in more], [], 0, g_mat, None, sems,
    )


def recv_bwd(send, o, dx, kept, model, mvec, sb, g_mat, parts):
    n = send.shape[0]
    squares = recv_squares(0)
    shapes = [(11, 8, D), (5, 8, D)]
    specs = [seg_block(sb), pack_spec(sb), seg_block(sb // 2)] + kept_specs(sb)
    specs += weight_specs(squares, 1, 0) + [whole((8, D)), MERGE]
    return pl.pallas_call(
        functools.partial(recv_bwd_kernel, sb),
        grid=(n // sb,),
        in_specs=specs + [ANY],
        out_specs=[ANY, seg_block(sb), tall_spec(sb)] + [whole(s) for s in shapes] + row_specs(sb, LATER_WIDTHS),
        out_shape=pack_shapes()[:1]
        + [jax.ShapeDtypeStruct((n, SB_ROWS, D), F32), jax.ShapeDtypeStruct((tall_rows(n, parts), HALF), F32)]
        + [jax.ShapeDtypeStruct(s, F32) for s in shapes]
        + row_shapes(n, LATER_WIDTHS),
        input_output_aliases={len(specs): 0},
        scratch_shapes=RECV_ACC + [pltpu.VMEM((2, D, D), F32), pltpu.SemaphoreType.DMA((4,))],
        compiler_params=params_spec(),
        name="recv_bwd",
    )(send, o, dx, *kept, *weight_args(model, squares, 1), mvec, model[0], g_mat)


def tail_kernel(sb, send_ref, o_ref, tgt_ref, kept_ref, scale_ref, mean_ref, *refs):
    w = {n: refs[i][...] for i, n in enumerate(RECV_W)}
    vec_ref, head_ref, g_mat, g_feed, dsend_ref, do_ref, rows_ref, dhead_ref = refs[7:15]
    saved, later, accs, sems = refs[15:18], refs[18:22], refs[22:25], refs[25]
    g = dict(zip(RECV_G, tuple(accs) + (rows_ref,)))

    @pl.when(pl.program_id(0) == 0)
    def _():
        for ref in list(g.values()) + [dhead_ref]:
            ref[...] = jnp.zeros(ref.shape, F32)

    vec = vec_ref[...]
    rows = sb * SB_ROWS
    y, kept, (_, mixed, _, z3, u, _) = recv_forward(
        send_ref[...].reshape(rows, D), unpack_block(o_ref, sb), w, vec
    )
    head = head_ref[...]
    y2 = split2(y)
    scale = jnp.broadcast_to(scale_ref[...][None], (sb, SB_ROWS, PPAD)).reshape(rows, PPAD)
    mean = jnp.broadcast_to(mean_ref[...][None], (sb, SB_ROWS, PPAD)).reshape(rows, PPAD)
    misfit = mmwt(y2, head) * scale + mean - tgt_ref[...].reshape(rows, PPAD)
    put(saved, (mixed, z3, u))
    dpred = kept_ref[...].reshape(rows, PPAD) * misfit * scale
    dpred2 = split2(dpred)
    dhead_ref[...] += tn3(dpred2, y2)
    dy = mmw(dpred2, head)
    dsend, do, grads = recv_backward(dy, kept, w, vec, g)
    put(later, grads)
    dsend_ref[...] = dsend.reshape(sb, SB_ROWS, D)
    pack_block(do_ref, do, sb)
    recv_flush(accs, [], 1, g_mat, sems)


def tail(send, o, tgt, kept, scale, mean, model, head, sb, parts):
    n = send.shape[0]
    squares = recv_squares(1)
    shapes = [(11, 8, D), (PPAD, D)]
    return pl.pallas_call(
        functools.partial(tail_kernel, sb),
        grid=(n // sb,),
        in_specs=[seg_block(sb), pack_spec(sb), seg_block(sb, SB_ROWS, PPAD), seg_block(sb, SB_ROWS, PPAD)]
        + [whole((SB_ROWS, PPAD))] * 2
        + weight_specs(squares, 3, 1)
        + [whole((PPAD, D))],
        out_specs=[ANY] * 2 + [seg_block(sb), tall_spec(sb)] + [whole(s) for s in shapes]
        + row_specs(sb, (D, D, FF) + LATER_WIDTHS),
        out_shape=pack_shapes()
        + [jax.ShapeDtypeStruct((n, SB_ROWS, D), F32), jax.ShapeDtypeStruct((tall_rows(n, parts), HALF), F32)]
        + [jax.ShapeDtypeStruct(s, F32) for s in shapes]
        + row_shapes(n, (D, D, FF) + LATER_WIDTHS),
        scratch_shapes=RECV_ACC + [pltpu.SemaphoreType.DMA((3,))],
        compiler_params=params_spec(),
        name="tail",
    )(send, o, tgt, kept, scale, mean, *weight_args(model, squares, 3), head)


SEND_W = ("sq", "sk", "sv")


def send_project(dim2, r_rows, w, vec):
    r2 = split2(r_rows)
    sb = r_rows.shape[0] // RPAD
    k = mmw(dim2, w["sk"])
    v = mmw(dim2, w["sv"]) + vec[11:12]
    q = (mmw(r2, w["sq"]) + vec[10:11]) * SCALE
    k = [split2(k[s * SB_ROWS : (s + 1) * SB_ROWS]) for s in range(sb)]
    v = [split2(v[s * SB_ROWS : (s + 1) * SB_ROWS]) for s in range(sb)]
    q = [split2(spread_rows(q[s * RPAD : (s + 1) * RPAD])) for s in range(sb)]
    return r2, k, v, q


def send_fwd_kernel(sb, dim_ref, r_ref, here_ref, *refs):
    w = {n: refs[i][...] for i, n in enumerate(SEND_W)}
    vec_ref, o_ref = refs[3:]
    dim2 = split2(dim_ref[...].reshape(sb * SB_ROWS, D))
    _, k, v, q = send_project(dim2, r_ref[...].reshape(sb * RPAD, D), w, vec_ref[...])
    here = here_ref[...] > 0.5
    scores = [jnp.where(here, nt3_narrow(k2, q2), negative) for k2, q2 in zip(k, q)]
    tops = [jnp.max(sc, 0, keepdims=True) for sc in scores]
    probs = [jnp.where(here, jnp.exp(sc - top), 0.0) for sc, top in zip(scores, tops)]
    totals = [jnp.sum(p, 0, keepdims=True) for p in probs]
    safe = [jnp.where(t > 0.0, t, 1.0) for t in totals]
    mixed = [gather_rows(tn3_short(split2(p / t), v2)) for p, t, v2 in zip(probs, safe, v)]
    for s in range(sb):
        lse = jnp.where(totals[s] > 0.0, tops[s] + jnp.log(safe[s]), negative)
        o_ref[s] = pack_rows(mixed[s], lse)


def send_squares(layer):
    return [12 * layer + k for k in (4, 5, 6)]


def send_fwd(dim, routers, here, model, layer, sb, npad):
    squares = send_squares(layer)
    n = dim.shape[0]
    return pl.pallas_call(
        functools.partial(send_fwd_kernel, sb),
        grid=(n // sb,),
        in_specs=[seg_block(sb), seg_block(sb, RPAD), whole((SB_ROWS, HALF))]
        + weight_specs(squares, None, layer),
        out_specs=pack_spec(sb),
        out_shape=jax.ShapeDtypeStruct((npad, PACK, HALF), F32),
        compiler_params=params_spec(),
        name="send_fwd",
    )(dim, routers, here, *weight_args(model, squares, None))


def send_bwd_kernel(sb, layer, dim_ref, dpart_ref, r_ref, o_ref, do_ref, here_ref, *refs):
    w = {n: refs[i][...] for i, n in enumerate(SEND_W)}
    vec_ref = refs[3]
    g_mat, ddim_ref, dr_ref, rows = refs[5:9]
    dsq_ref, dsk_ref, dsv_ref, sems = refs[9:13]

    @pl.when(pl.program_id(0) == 0)
    def _():
        for ref in (dsq_ref, dsk_ref, dsv_ref, rows):
            ref[...] = jnp.zeros(ref.shape, F32)

    dim2 = split2(dim_ref[...].reshape(sb * SB_ROWS, D))
    r2, k, v, q = send_project(dim2, r_ref[...].reshape(sb * RPAD, D), w, vec_ref[...])
    here = (here_ref[...] > 0.5) & valid_lane(SB_ROWS)
    segs = range(sb)
    scores = [nt3_narrow(k2, q2) for k2, q2 in zip(k, q)]
    probs = [jnp.where(here, jnp.exp(scores[s] - o_ref[s][2 * ROUT : 2 * ROUT + 1]), 0.0) for s in segs]
    dwide = [spread_rows(unpack_rows(do_ref[s * TALL : (s + 1) * TALL])) for s in segs]
    owide = [
        jnp.broadcast_to(unpack_rows(o_ref[s])[:, None, :], (RPAD, HEADS, D)).reshape(RPAD * HEADS, D) for s in segs
    ]
    e = [split2(a * b) for a, b in zip(dwide, owide)]
    d = [split2(a) for a in dwide]
    one_row = jnp.ones((8, D), BF)
    means = [(dots(one_row, e2[0], 1, 1) + dots(one_row, e2[1], 1, 1))[0:1] for e2 in e]
    dp = [nt3_narrow(v2, d2) for v2, d2 in zip(v, d)]
    ds = [split2(p * (x - mean)) for p, x, mean in zip(probs, dp, means)]
    dk = jnp.concatenate([nn3_short(s2, q2) for s2, q2 in zip(ds, q)], 0)
    dv = jnp.concatenate([nn3_short(split2(p), d2) for p, d2 in zip(probs, d)], 0)
    dq = jnp.concatenate([gather_rows(tn3_short(s2, k2)) for s2, k2 in zip(ds, k)], 0) * SCALE
    dk2 = split2(dk)
    dv2 = split2(dv)
    rows[1] += colsum(dv)
    dsk_ref[...] += tn3(dim2, dk2)
    dsv_ref[...] += tn3(dim2, dv2)
    out = dpart_ref[...].reshape(sb * SB_ROWS, D) + mmwt(dk2, w["sk"]) + mmwt(dv2, w["sv"])
    ddim_ref[...] = out.reshape(sb, SB_ROWS, D)
    rows[0] += colsum(dq)
    dq2 = split2(dq)
    dsq_ref[...] += tn3(r2, dq2)
    dr_ref[...] = mmwt(dq2, w["sq"]).reshape(sb, RPAD, D)
    flush(
        pl.program_id(0), pl.num_programs(0) - 1, [dsq_ref, dsk_ref, dsv_ref], send_squares(layer), [], 0, g_mat, None,
        sems,
    )


def send_bwd(dim, dpart, routers, o, do, here, model, layer, sb, g_mat):
    n = dim.shape[0]
    squares = send_squares(layer)
    specs = [seg_block(sb), seg_block(sb), seg_block(sb, RPAD), pack_spec(sb), tall_spec(sb), whole((SB_ROWS, HALF))]
    specs += weight_specs(squares, None, layer)
    return pl.pallas_call(
        functools.partial(send_bwd_kernel, sb, layer),
        grid=(n // sb,),
        in_specs=specs + [ANY],
        out_specs=[ANY, seg_block(sb), seg_block(sb, RPAD), whole((2, 8, D))],
        out_shape=pack_shapes()[:1]
        + [jax.ShapeDtypeStruct((n, SB_ROWS, D), F32), jax.ShapeDtypeStruct((n, RPAD, D), F32)]
        + [jax.ShapeDtypeStruct((2, 8, D), F32)],
        input_output_aliases={len(specs): 0},
        scratch_shapes=[pltpu.VMEM((D, D), F32)] * 3 + [pltpu.SemaphoreType.DMA((3,))],
        compiler_params=params_spec(),
        name="send_bwd",
    )(dim, dpart, routers, o, do, here, *weight_args(model, squares, None), g_mat)

MESH = pl.DeviceIdType.MESH


def grid_sizes():
    nf = lax.axis_size("fsdp")
    nx = 1
    while 2 * nx * nx < nf:
        nx *= 2
    return lax.axis_size("dp") // 2, nf // nx, nx


class Place:
    def __init__(self):
        self.ny, self.nz, self.nx = grid_sizes()
        dp, fs = lax.axis_index("dp"), lax.axis_index("fsdp")
        self.core, self.y = lax.rem(dp, 2), lax.div(dp, 2)
        self.x, self.z = lax.rem(fs, self.nx), lax.div(fs, self.nx)

    def at(self, y=None, core=None, z=None, x=None):
        y = self.y if y is None else y
        core = self.core if core is None else core
        z = self.z if z is None else z
        x = self.x if x is None else x
        return (y * 2 + core, z * self.nx + x)

    def other(self):
        return 1 - self.core

    def next_x(self, k):
        return lax.rem(self.x + k, self.nx)

    def next_y(self, k):
        return lax.rem(self.y + k, self.ny)

    def next_z(self, k):
        return lax.rem(self.z + k, self.nz)

    def neighbours(self):
        out = [self.at(core=self.other())]
        out += [self.at(x=self.next_x(k)) for k in range(1, self.nx)]
        out += [self.at(y=self.next_y(k)) for k in range(1, self.ny)]
        out += [self.at(z=self.next_z(k)) for k in range(1, self.nz)]
        return out


def greet(devices):
    barrier = pltpu.get_barrier_semaphore()
    for device in devices:
        pl.semaphore_signal(barrier, inc=1, device_id=device, device_id_type=MESH)
    pl.semaphore_wait(barrier, len(devices))


def remote(src, dst, send, recv, device):
    return pltpu.make_async_remote_copy(
        src_ref=src, dst_ref=dst, send_sem=send, recv_sem=recv, device_id=device, device_id_type=MESH
    )


def gather_chunks(shapes):
    out = []
    for j, (rows, _) in enumerate(shapes):
        cut = rows // 32 * 16 if rows >= 160 else 0
        out += [(j, 0, cut), (j, cut, rows - cut)] if cut else [(j, 0, rows)]
    return out


def gather_kernel(shapes, *refs):
    packs = len(shapes)
    chunks = gather_chunks(shapes)
    n = len(chunks)
    shards = [refs[j].at[pl.ds(a, b)] for j, a, b in chunks]
    send, recv, local = refs[2 * packs :]

    def view(i, *at):
        j, a, b = chunks[i]
        return refs[packs + j].at[at + (slice(None),) * (4 - len(at)) + (pl.ds(a, b),)]

    me = Place()
    y, c, z, x = me.y, me.core, me.z, me.x
    m = me.nx
    greet(me.neighbours())
    slot = [0]

    def push(src, dst, device):
        copy = remote(src, dst, send.at[slot[0]], recv.at[slot[0]], device)
        slot[0] += 1
        copy.start()
        return copy

    def finish(copies):
        for copy in copies:
            copy.wait()

    own = [pltpu.make_async_copy(shards[j], view(j, y, c, z, x), local.at[j]) for j in range(n)]
    for copy in own:
        copy.start()

    def along_z(j):
        return [push(shards[j], view(j, y, c, z, x), me.at(z=me.next_z(k))) for k in range(1, me.nz)]

    first = along_z(0)
    finish(own)
    base = slot[0]

    def rest(by_core):
        slot[0] = base
        sibling = me.at(core=1 - by_core)
        shared = []

        def second(j):
            piece = view(j, y, by_core, slice(None), x)
            out = []
            for k in range(1, m):
                out.append(push(piece, piece, me.at(x=me.next_x(k)) if by_core == 0 else me.at(y=me.next_y(k))))
            shared.append(push(piece, piece, sibling))
            return out

        def third(j):
            wide = view(j, y, by_core) if by_core == 0 else view(j, slice(None), by_core, slice(None), x)
            out = []
            for k in range(1, m):
                out.append(push(wide, wide, me.at(y=me.next_y(k)) if by_core == 0 else me.at(x=me.next_x(k))))
            for k in range(1, m):
                piece = view(j, y, by_core, slice(None), me.next_x(k)) if by_core == 0 else view(j, me.next_y(k), by_core, slice(None), x)
                shared.append(push(piece, piece, sibling))
            return out

        def fourth(j):
            for k in range(1, m):
                wide = view(j, me.next_y(k), by_core) if by_core == 0 else view(j, slice(None), by_core, slice(None), me.next_x(k))
                shared.append(push(wide, wide, sibling))

        one, two, three = {0: first}, {}, {}
        for t in range(n + 2):
            if t < n:
                finish(one[t])
                if t + 1 < n:
                    one[t + 1] = along_z(t + 1)
                two[t] = second(t)
            if 0 < t <= n:
                finish(two[t - 1])
                three[t - 1] = third(t - 1)
            if t > 1:
                finish(three[t - 2])
                fourth(t - 2)
        finish(shared)

    for by_core in (0, 1):
        pl.when(c == by_core)(functools.partial(rest, by_core))


def gather_all(shards):
    ny, nz, nx = grid_sizes()
    shapes = [s.shape for s in shards]
    n, parts = len(shards), len(gather_chunks(shapes))
    count = parts * ((nz - 1) + (nx - 1) + 1 + (nx - 1) * 3)
    return pl.pallas_call(
        functools.partial(gather_kernel, shapes),
        in_specs=[ANY] * n,
        out_specs=[ANY] * n,
        out_shape=[jax.ShapeDtypeStruct((ny, 2, nz, nx) + s.shape, s.dtype) for s in shards],
        scratch_shapes=[pltpu.SemaphoreType.DMA((count,)), pltpu.SemaphoreType.DMA((count,)), pltpu.SemaphoreType.DMA((parts,))],
        compiler_params=pltpu.CompilerParams(collective_id=0, has_side_effects=True, vmem_limit_bytes=VMEM_LIMIT),
        name="gather_all",
    )(*shards)


def row_chunks(rows):
    count = max(1, rows // 40)
    if rows % 8:
        count = 1
    cuts = [rows // 8 * k // count * 8 for k in range(count)] + [rows]
    return [(a, b - a) for a, b in zip(cuts, cuts[1:])]


def scatter_kernel(shapes, *refs):
    n = len(shapes)
    chunks = [(j, a, b) for j, s in enumerate(shapes) for a, b in row_chunks(s[0])]
    total = len(chunks)
    grads, tile_ref = refs[:n], refs[n]
    outs, stat_ref = refs[n + 1 : 2 * n + 1], refs[2 * n + 1]
    bufs = refs[2 * n + 2 :]
    acc, r1, r2, r3, r4 = (bufs[i * total : (i + 1) * total] for i in range(5))
    tp, tz, send, recv, local = bufs[5 * total :]
    me = Place()
    y, c, z, x = me.y, me.core, me.z, me.x
    ny, nz, nx, m = me.ny, me.nz, me.nx, me.nx
    plane = plane_peers(me)
    greet([p for p, _ in plane] + [me.at(z=me.next_z(k)) for k in range(1, nz)])
    slot = [0]

    def push(src, dst, device):
        copy = remote(src, dst, send.at[slot[0]], recv.at[slot[0]], device)
        slot[0] += 1
        copy.start()
        return copy

    def finish(copies):
        for copy in copies:
            copy.wait()

    def rest(by_core):
        slot[0] = 0
        sibling = me.at(core=1 - by_core)

        def one(i):
            j, a, b = chunks[i]
            out = []
            for k in range(nx):
                out.append(push(grads[j].at[:, 1 - by_core, :, k, pl.ds(a, b)], r1[i].at[:, k], sibling))
                copy = pltpu.make_async_copy(grads[j].at[:, by_core, :, k, pl.ds(a, b)], acc[i].at[:, k], local.at[i * nx + k])
                copy.start()
                out.append(copy)
            return out

        def add1(i):
            def body(k, carry):
                at = (lax.div(k, nx * nz), lax.rem(lax.div(k, nz), nx), lax.rem(k, nz))
                acc[i][at] = acc[i][at] + r1[i][at]
                return carry

            lax.fori_loop(0, ny * nx * nz, body, 0)

        def two(i):
            if by_core == 0:
                return [push(acc[i].at[:, me.next_x(k)], r2[i].at[k - 1], me.at(x=me.next_x(k))) for k in range(1, m)]
            return [push(acc[i].at[me.next_y(k)], r2[i].at[k - 1], me.at(y=me.next_y(k))) for k in range(1, m)]

        def add2(i):
            def body(k, carry):
                a, b = lax.div(k, nz), lax.rem(k, nz)
                at = (a, x, b) if by_core == 0 else (y, a, b)
                value = acc[i][at]
                for q in range(m - 1):
                    value = value + r2[i][q, a, b]
                acc[i][at] = value
                return carry

            lax.fori_loop(0, m * nz, body, 0)

        def three(i):
            if by_core == 0:
                return [push(acc[i].at[me.next_y(k), x], r3[i].at[k - 1], me.at(y=me.next_y(k))) for k in range(1, m)]
            return [push(acc[i].at[y, me.next_x(k)], r3[i].at[k - 1], me.at(x=me.next_x(k))) for k in range(1, m)]

        def add3(i):
            def body(k, carry):
                value = acc[i][y, x, k]
                for q in range(m - 1):
                    value = value + r3[i][q, k]
                acc[i][y, x, k] = value
                return carry

            lax.fori_loop(0, nz, body, 0)

        def four(i):
            return [push(acc[i].at[y, x, me.next_z(k)], r4[i].at[k - 1], me.at(z=me.next_z(k))) for k in range(1, nz)]

        def end(i):
            j, a, b = chunks[i]
            value = acc[i][y, x, z]
            for k in range(nz - 1):
                value = value + r4[i][k]
            outs[j][a : a + b] = value
            sq = colsum_any(value * value)
            return sq[:, :HALF] + sq[:, HALF:]

        squares = jnp.zeros((8, HALF), F32)
        ahead = 3
        p1, p2, p3, p4 = {i: one(i) for i in range(min(ahead, total))}, {}, {}, {}
        for t in range(total + 3):
            if t < total:
                finish(p1[t])
                if t + ahead < total:
                    p1[t + ahead] = one(t + ahead)
                add1(t)
                p2[t] = two(t)
            if 0 <= t - 1 < total:
                finish(p2[t - 1])
                add2(t - 1)
                p3[t - 1] = three(t - 1)
            if 0 <= t - 2 < total:
                finish(p3[t - 2])
                add3(t - 2)
                p4[t - 2] = four(t - 2)
            if 0 <= t - 3 < total:
                finish(p4[t - 3])
                squares = squares + end(t - 3)
        tp[(y * 2 + by_core) * nx + x] = jnp.concatenate([squares, tile_ref[...]], 0)

    for by_core in (0, 1):
        pl.when(c == by_core)(functools.partial(rest, by_core))

    slot[0] = total * (nx + 2 * (m - 1) + nz - 1)
    mine = tp.at[(y * 2 + c) * nx + x]
    finish([push(mine, mine, p) for p, _ in plane])
    tz[z] = functools.reduce(jnp.add, [tp[k] for k in range(2 * ny * nx)])
    finish([push(tz.at[z], tz.at[z], me.at(z=me.next_z(k))) for k in range(1, nz)])
    stat_ref[...] = functools.reduce(jnp.add, [tz[k] for k in range(nz)])


def plane_peers(me):
    out = []
    for k in range(1, 2 * me.ny * me.nx):
        dc, dy, dx = k % 2, k // 2 % me.ny, k // (2 * me.ny)
        out.append((me.at(core=lax.rem(me.core + dc, 2), y=lax.rem(me.y + dy, me.ny), x=lax.rem(me.x + dx, me.nx)), k))
    return out


def colsum_any(x):
    rows = x.shape[0]
    even = rows // 8 * 8
    out = colsum(x[:even]) if even else jnp.zeros((8, x.shape[1]), F32)
    if rows > even:
        out = out + jnp.pad(x[even:], ((0, 8 - rows + even), (0, 0)))
    return out


def scatter_sum(grads, tile):
    ny, nz, nx = grid_sizes()
    n = len(grads)
    shapes = [g.shape[-2:] for g in grads]
    pieces = [(b, s[1]) for s in shapes for _, b in row_chunks(s[0])]
    total = len(pieces)
    count = total * (nx + (nx - 1) * 2 + nz - 1) + 2 * ny * nx - 1 + nz - 1

    def buffers(*lead):
        return [pltpu.VMEM(lead + s, F32) for s in pieces]

    return pl.pallas_call(
        functools.partial(scatter_kernel, shapes),
        in_specs=[ANY] * n + [INVMEM],
        out_specs=[INVMEM] * (n + 1),
        out_shape=[jax.ShapeDtypeStruct(s, F32) for s in shapes] + [jax.ShapeDtypeStruct((16, HALF), F32)],
        scratch_shapes=buffers(ny, nx, nz)
        + buffers(ny, nx, nz)
        + buffers(nx - 1, nx, nz)
        + buffers(nx - 1, nz)
        + buffers(nz - 1)
        + [pltpu.VMEM((2 * ny * nx, 16, HALF), F32), pltpu.VMEM((nz, 16, HALF), F32)]
        + [pltpu.SemaphoreType.DMA((count,)), pltpu.SemaphoreType.DMA((count,)), pltpu.SemaphoreType.DMA((total * nx,))],
        compiler_params=pltpu.CompilerParams(collective_id=1, has_side_effects=True, vmem_limit_bytes=VMEM_LIMIT),
        name="scatter_sum",
    )(*grads, tile)


def group_part(ref, who, per):
    return ref.at[pl.ds(pl.multiple_of(who * per, per), per)]


def group_out(per, in_ref, got, send, recv, local):
    nf = lax.axis_size("fsdp")
    dp, f = lax.axis_index("dp"), lax.axis_index("fsdp")
    copies = [pltpu.make_async_copy(group_part(in_ref, f, per), got.at[f], local)]
    for k in range(1, nf):
        p = lax.rem(f + k, nf)
        copies.append(remote(group_part(in_ref, p, per), got.at[f], send.at[k - 1], recv.at[k - 1], (dp, p)))
    return copies


def group_back(per, result, out_ref, send, recv, local):
    nf = lax.axis_size("fsdp")
    dp, f = lax.axis_index("dp"), lax.axis_index("fsdp")
    copies = [pltpu.make_async_copy(result, group_part(out_ref, f, per), local)]
    for k in range(1, nf):
        p = lax.rem(f + k, nf)
        copies.append(remote(result, group_part(out_ref, f, per), send.at[nf - 2 + k], recv.at[nf - 2 + k], (dp, p)))
    return copies


def greet_group():
    nf = lax.axis_size("fsdp")
    dp, f = lax.axis_index("dp"), lax.axis_index("fsdp")
    greet([(dp, lax.rem(f + k, nf)) for k in range(1, nf)])


def start_all(copies):
    for copy in copies:
        copy.start()


def wait_all(copies):
    for copy in copies:
        copy.wait()


def stats_kernel(per, in_ref, out_ref, got, result, send, recv, local):
    nf = lax.axis_size("fsdp")
    greet_group()
    copies = group_out(per, in_ref, got, send, recv, local)
    start_all(copies)
    wait_all(copies)
    row = lax.broadcasted_iota(jnp.int32, (PACK, HALF), 0)
    lane = lax.broadcasted_iota(jnp.int32, (PACK, HALF), 1)
    router = jnp.where(row < ROUT, row, row - ROUT)
    chosen = (lane // 8 == router) & (row < 2 * ROUT)
    src = lax.broadcasted_iota(jnp.int32, (HALF, D), 0)
    dst = lax.broadcasted_iota(jnp.int32, (HALF, D), 1)
    widen = jnp.where(src % 8 == dst // 32, 1.0, 0.0).astype(BF)

    segs, devs = range(per), range(nf)
    lse = [[got[d, s, 2 * ROUT : 2 * ROUT + 1, :] for d in devs] for s in segs]
    tops = [functools.reduce(jnp.maximum, l) for l in lse]
    totals = [t + jnp.log(functools.reduce(jnp.add, [jnp.exp(x - t) for x in l])) for t, l in zip(tops, lse)]
    shares = [
        jnp.concatenate([jnp.where(chosen, jnp.exp(x - t), 0.0) for x in l], 0) for t, l in zip(totals, lse)
    ]
    wide = [mmw(split2(x), widen) for x in shares]
    outs = []
    for s in segs:
        out = jnp.where(row == 2 * ROUT, totals[s], 0.0)
        for d in devs:
            w = wide[s][d * PACK : (d + 1) * PACK]
            w = jnp.where(row < ROUT, w[:, :HALF], w[:, HALF:])
            out = out + jnp.where(row < 2 * ROUT, w * got[d, s], 0.0)
        outs.append(out)
    for s in segs:
        result[s] = outs[s]
    copies = group_back(per, result, out_ref, send, recv, local)
    start_all(copies)
    wait_all(copies)


def sum_kernel(per, turn, in_ref, x_ref, mixed_ref, z_ref, u_ref, dq_ref, dz3_ref, du_ref, dz4_ref, vec_ref, *refs):
    out_ref, rq, ro, up, down, got, result, send, recv, local = refs
    step = pl.program_id(0)

    @pl.when(step == 0)
    def _():
        greet_group()
        start_all(group_out(per, in_ref, got, send, recv, local))
        for ref in (rq, ro, up, down):
            ref[...] = jnp.zeros(ref.shape, F32)

    @pl.when(step == turn)
    def _():
        wait_all(group_out(per, in_ref, got, send, recv, local))
        result[...] = functools.reduce(jnp.add, [got[d] for d in range(lax.axis_size("fsdp"))])
        start_all(group_back(per, result, out_ref, send, recv, local))

    rq[...] += tn3(split2(x_ref[...]), split2(dq_ref[...]))
    ro[...] += tn3(split2(mixed_ref[...]), split2(dz3_ref[...]))
    g, _, _ = norm_fwd(z_ref[...], vec_ref[16:17], vec_ref[17:18])
    up[...] += tn3(split2(g), split2(du_ref[...]))
    u = u_ref[...]
    down[...] += tn3(split2(u * gelu_cdf(u)), split2(dz4_ref[...]))

    @pl.when(step == pl.num_programs(0) - 1)
    def _():
        wait_all(group_back(per, result, out_ref, send, recv, local))


def group_scratch(part, nf):
    return [
        pltpu.VMEM((nf,) + part, F32),
        pltpu.VMEM(part, F32),
        pltpu.SemaphoreType.DMA((2 * nf - 2,)),
        pltpu.SemaphoreType.DMA((2 * nf - 2,)),
        pltpu.SemaphoreType.DMA,
    ]


def group_params(cid):
    return pltpu.CompilerParams(collective_id=cid, has_side_effects=True, vmem_limit_bytes=VMEM_LIMIT)


def group_stats(packed, cid):
    nf = lax.axis_size("fsdp")
    per = packed.shape[0] // nf
    return pl.pallas_call(
        functools.partial(stats_kernel, per),
        in_specs=[ANY],
        out_specs=ANY,
        out_shape=jax.ShapeDtypeStruct(packed.shape, F32),
        scratch_shapes=group_scratch((per, PACK, HALF), nf),
        compiler_params=group_params(cid),
        name="group_stats",
    )(packed)


def group_sum(packed, work, vecs, layer, cid):
    nf = lax.axis_size("fsdp")
    per = packed.shape[0] // nf
    rows = 480
    steps = work[0].shape[0] // rows
    shapes = [(D, D), (D, D), (D, FF), (FF, D)]
    return pl.pallas_call(
        functools.partial(sum_kernel, per, steps - steps // 4),
        grid=(steps,),
        in_specs=[ANY] + [pl.BlockSpec((rows, w.shape[1]), lambda i: (i, 0)) for w in work] + [pick((24, D), layer)],
        out_specs=[ANY] + [whole(s) for s in shapes],
        out_shape=[jax.ShapeDtypeStruct(packed.shape, F32)] + [jax.ShapeDtypeStruct(s, F32) for s in shapes],
        scratch_shapes=group_scratch((per, HALF), nf),
        compiler_params=group_params(cid),
        name="group_sum",
    )(packed, *work, vecs)

LAYER_AT = SEGLEN + 1 + SEG
MERGE_AT = LAYER_AT + 46
HEAD_AT = MERGE_AT + 5
ROUTER_AT = HEAD_AT + PRED
VROWS = NVEC + 20


def own_size(devices):
    own = NVEC * D // devices
    return own, -(-own // D)


def prepare_kernel(nfeed, ser_ref, obs_ref, tgt_ref, mask_ref, count_ref, mat_ref, feed_ref, vec_ref, *outs):
    pieces, tgt, kept, scale_ref, mean_ref, here_ref, tile_ref, mat_o, feed_o, vec_o = outs
    for src, dst in ((mat_ref, mat_o), (feed_ref, feed_o), (vec_ref, vec_o)):
        rows = dst.shape[0]
        left, right = src[pl.ds(0, rows, stride=2), :], src[pl.ds(1, rows, stride=2), :]
        dst[...] = jnp.concatenate([left, right], 1).astype(BF)
    nv = ser_ref.shape[0]
    series, seen = ser_ref[...], obs_ref[...].astype(F32)
    counted = jnp.maximum(jnp.sum(seen, -1, keepdims=True), 1.0)
    mean = jnp.sum(seen * series, -1, keepdims=True) / counted
    center = (series - mean) * seen
    scale = jnp.sqrt(jnp.sum(center * center, -1, keepdims=True) / counted + norm_eps)
    slot = lax.axis_index("fsdp") * nv + lax.broadcasted_iota(jnp.int32, (nv, HALF), 0)
    here = jnp.where(slot < count_ref[0], 1.0, 0.0)
    here_ref[...] = here
    scale_ref[...] = jnp.broadcast_to(scale, (nv, PPAD))
    mean_ref[...] = jnp.broadcast_to(mean, (nv, PPAD))
    mask = mask_ref[...].astype(F32) * here[:, :1]
    tile_ref[...] = jnp.broadcast_to(jnp.sum(jnp.sum(mask, 0, keepdims=True), -1, keepdims=True), (8, HALF)) * (1.0 / (8 * HALF))
    lane = lax.broadcasted_iota(jnp.int32, (nv, PPAD), 1)

    def cut(x, dst):
        x = jnp.concatenate([x, jnp.zeros((nv, PPAD - 12), F32)], 1)
        for s in range(dst.shape[0]):
            dst[s] = jnp.where(lane < 12, x[:, 12 * s : 12 * s + PPAD], 0.0)

    cut(center / scale, pieces)
    cut(tgt_ref[...], tgt)
    cut(mask * (2.0 / (1 << 20)), kept)


def prepare(series, observed, targets, target_mask, counts, matrices, feed, vectors):
    nv = series.shape[0]
    shapes = [((SEG, nv, PPAD), F32), ((SEG // 2, nv, PPAD), F32), ((SEG // 2, nv, PPAD), F32), ((nv, PPAD), F32), ((nv, PPAD), F32)]
    shapes += [((nv, HALF), F32), ((8, HALF), F32)]
    shapes += [((x.shape[0] // 2, D), BF) for x in (matrices, feed, vectors)]
    return pl.pallas_call(
        functools.partial(prepare_kernel, 0),
        grid=(1,),
        in_specs=[whole(x.shape) for x in (series, observed, targets, target_mask)]
        + [pl.BlockSpec(memory_space=pltpu.SMEM)]
        + [whole(x.shape) for x in (matrices, feed, vectors)],
        out_specs=[whole(s) for s, _ in shapes],
        out_shape=[jax.ShapeDtypeStruct(s, t) for s, t in shapes],
        compiler_params=pltpu.CompilerParams(vmem_limit_bytes=VMEM_LIMIT),
        name="prepare",
    )(series, observed, targets, target_mask, counts, matrices, feed, vectors)


def unpack_kernel(devices, own, vec_ref, vecs, mvec, emb, place, head, r0, r1, flat):
    flat[...] = jnp.zeros(flat.shape, F32)
    rows = vec_ref.shape[1]
    lane = lax.broadcasted_iota(jnp.int32, (rows, D), 1)
    for d in range(devices):
        at, shift = divmod(own * d, D)
        block = vec_ref[d].astype(F32)
        if shift:
            block = pltpu.roll(block, shift, 1)
            flat[at + 1 : at + 1 + rows] += jnp.where(lane < shift, block, 0.0)
            block = jnp.where(lane >= shift, block, 0.0)
        flat[at : at + rows] += block

    def padded(at, count, total):
        return jnp.concatenate([flat[at : at + count], jnp.zeros((total - count, D), F32)], 0)

    for l in range(2):
        vecs[l] = padded(LAYER_AT + 23 * l, 23, 24)
    mvec[...] = padded(MERGE_AT, 5, 8)
    emb[...] = padded(0, SEGLEN, 16).astype(BF)
    head[...] = padded(HEAD_AT, PRED, PPAD).astype(BF)
    for s in range(SEG):
        place[s] = flat[SEGLEN + 1 + s : SEGLEN + 2 + s] + flat[SEGLEN : SEGLEN + 1]
        r0[s] = padded(ROUTER_AT + ROUT * s, ROUT, RPAD)
    for s in range(SEG // 2):
        r1[s] = padded(ROUTER_AT + ROUT * (SEG + s), ROUT, RPAD)


def unpack_vectors(gathered, own):
    devices, rows, _ = gathered.shape
    shapes = [((2, 24, D), F32), ((8, D), F32), ((16, D), BF), ((SEG, 1, D), F32), ((PPAD, D), BF)]
    shapes += [((SEG, RPAD, D), F32), ((SEG // 2, RPAD, D), F32)]
    return pl.pallas_call(
        functools.partial(unpack_kernel, devices, own),
        grid=(1,),
        in_specs=[whole(gathered.shape)],
        out_specs=[whole(s) for s, _ in shapes],
        out_shape=[jax.ShapeDtypeStruct(s, t) for s, t in shapes],
        scratch_shapes=[pltpu.VMEM((VROWS + 24, D), F32)],
        compiler_params=pltpu.CompilerParams(vmem_limit_bytes=VMEM_LIMIT),
        name="unpack_vectors",
    )(gathered)


def assemble_kernel(devices, own, demb, dplace, *refs):
    (rt0, rs0, rr0, rt1, rs1, rr1, dmv, dhead, dr0, dr1), out, flat = refs[:10], refs[10], refs[11]
    flat[...] = jnp.zeros(flat.shape, F32)
    flat[0:SEGLEN] = demb[0:SEGLEN]
    place = jnp.sum(dplace[...].reshape(SEG, VB, D), 1)
    flat[SEGLEN : SEGLEN + 1] = jnp.sum(place, 0, keepdims=True)
    flat[SEGLEN + 1 : SEGLEN + 1 + SEG] = place
    at = LAYER_AT
    for ref in (rt0, rs0, rr0, rt1, rs1, rr1, dmv):
        count = ref.shape[0]
        flat[at : at + count] = jnp.sum(ref[...], 1)
        at += count
    flat[HEAD_AT : HEAD_AT + PRED] = dhead[0:PRED]
    for s in range(SEG):
        flat[ROUTER_AT + ROUT * s : ROUTER_AT + ROUT * (s + 1)] = dr0[s][:ROUT]
    for s in range(SEG // 2):
        flat[ROUTER_AT + ROUT * (SEG + s) : ROUTER_AT + ROUT * (SEG + s + 1)] = dr1[s][:ROUT]
    rows = out.shape[1]
    lane = lax.broadcasted_iota(jnp.int32, (rows, D), 1)
    inside = lax.broadcasted_iota(jnp.int32, (rows, D), 0) * D + lane < own
    for d in range(devices):
        at, shift = divmod(own * d, D)
        block = flat[at : at + rows]
        if shift:
            block = jnp.where(lane < D - shift, pltpu.roll(block, D - shift, 1), pltpu.roll(flat[at + 1 : at + 1 + rows], D - shift, 1))
        out[d] = jnp.where(inside, block, 0.0)


def assemble_vectors(parts, devices):
    own, rows = own_size(devices)
    return pl.pallas_call(
        functools.partial(assemble_kernel, devices, own),
        grid=(1,),
        in_specs=[whole(p.shape) for p in parts],
        out_specs=whole((devices, rows, D)),
        out_shape=jax.ShapeDtypeStruct((devices, rows, D), F32),
        scratch_shapes=[pltpu.VMEM((VROWS + 24, D), F32)],
        compiler_params=pltpu.CompilerParams(vmem_limit_bytes=VMEM_LIMIT),
        name="assemble_vectors",
    )(*parts)


def adam_update(weight, first_moment, second_moment, gradient):
    first_new = beta_one * first_moment + (1.0 - beta_one) * gradient
    second_new = beta_two * second_moment + (1.0 - beta_two) * gradient * gradient
    corrected = (
        first_new
        / (1.0 - beta_one**step_count)
        / (jnp.sqrt(second_new / (1.0 - beta_two**step_count)) + adam_eps)
    )
    return (weight - learn_rate * (corrected + weight_decay * weight), first_new, second_new)


def adam_kernel(up_rows, s_mat, s_feed, sums, *refs):
    old, new, norm_ref, scratch = refs[:6], refs[6:12], refs[12], refs[13:]

    def add_up(x):
        return jnp.sum(jnp.sum(x, 0, keepdims=True), -1, keepdims=True)

    upscale = (1 << 20) / jnp.maximum(add_up(sums[8:]), 1.0)
    norm = jnp.sqrt(add_up(sums[:8])) * upscale
    factor = upscale * (clip_norm / jnp.maximum(norm, clip_norm))
    norm_ref[0:1] = jnp.broadcast_to(norm, (1, HALF))
    norm_ref[1:2] = jnp.broadcast_to(factor, (1, HALF))

    def spread(src, dst):
        rows = src.shape[0]
        value = src[...] * factor
        dst[pl.ds(0, rows, stride=2), :] = value[:, :HALF]
        dst[pl.ds(1, rows, stride=2), :] = value[:, HALF:]

    spread(s_mat, scratch[0])
    up = lax.axis_index("dp") * 2 < lax.axis_size("dp")
    pl.when(jnp.logical_not(up))(lambda: spread(s_feed, scratch[1]))

    @pl.when(up)
    def _():
        for half in range(2):
            value = s_feed[half * up_rows : (half + 1) * up_rows] * factor
            scratch[1][pl.ds(2 * half, up_rows, stride=4), :] = value[:, :HALF]
            scratch[1][pl.ds(2 * half + 1, up_rows, stride=4), :] = value[:, HALF:]

    for k in range(2):
        values = adam_update(*[ref[...] for ref in old[3 * k : 3 * k + 3]], scratch[k][...])
        for ref, value in zip(new[3 * k : 3 * k + 3], values):
            ref[...] = value


def adam_packs(s_mat, s_feed, sums, old, up_rows):
    args = [s_mat, s_feed, sums] + old
    outs = [x.shape for x in old] + [(8, HALF)]
    return pl.pallas_call(
        functools.partial(adam_kernel, up_rows),
        grid=(1,),
        in_specs=[whole(x.shape) for x in args],
        out_specs=[whole(s) for s in outs],
        out_shape=[jax.ShapeDtypeStruct(s, F32) for s in outs],
        scratch_shapes=[pltpu.VMEM(old[0].shape, F32), pltpu.VMEM(old[3].shape, F32)],
        compiler_params=params_spec(),
        name="adam_packs",
    )(*args)


def gradient_parts(ready, model, extras, up_rows, group_stats, group_sum, nf, devices):
    pieces, tgt, kept, scale, mean, here = ready
    mvec, emb, place, head, routers0, routers1 = extras
    sb0, sb1, sf0, sf1, st = 12, 10, 20, 10, 10
    rf, rb = 20, 20
    half = SEG // 2
    dim0, kept0 = time_fwd(True, pieces, (emb, place), model, 0, SEG)
    o0 = send_fwd(dim0, routers0, here, model, 0, sf0, -(-SEG // nf) * nf)
    o0 = group_stats(o0, 2)
    x1, *saved = recv_fwd(dim0, o0, model, mvec, rf)
    dim1, kept1 = time_fwd(False, x1, (), model, 1, half)
    o1 = send_fwd(dim1, routers1, here, model, 1, sf1, -(-half // nf) * nf)
    o1 = group_stats(o1, 3)
    vecs = model[3]
    g_mat, g_feed, ddim1, do1, rr1, dhead, *work = tail(dim1, o1, tgt, kept, scale, mean, model, head, st, nf)
    do1, *later = group_sum(do1, [dim1.reshape(-1, D)] + work, vecs, 1, 4)
    g_mat, ddim1, dr1, rs1 = send_bwd(dim1, ddim1, routers1, o1, do1, here, model, 1, sb1, g_mat)
    g_mat, g_feed, rt1, dx1 = time_bwd(
        False, x1, (), ddim1, kept1, model, 1, half, later, (g_mat, g_feed), up_rows
    )
    g_mat, ddim0, do0, rr0, dmv, *work = recv_bwd(dim0, o0, dx1, saved, model, mvec, rb, g_mat, nf)
    work = [dim0.reshape(-1, D), saved[1], saved[3], saved[4]] + work
    do0, *later = group_sum(do0, work, vecs, 0, 5)
    g_mat, ddim0, dr0, rs0 = send_bwd(dim0, ddim0, routers0, o0, do0, here, model, 0, sb0, g_mat)
    g_mat, g_feed, rt0, demb, dplace = time_bwd(
        True, pieces, (emb, place), ddim0, kept0, model, 0, SEG, later, (g_mat, g_feed), up_rows
    )
    g_vec = assemble_vectors((demb, dplace, rt0, rs0, rr0, rt1, rs1, rr1, dmv, dhead, dr0, dr1), devices)
    return g_mat, g_feed, g_vec


def on_device(series, observed, targets, target_mask, counts, matrices, feed_weights, vectors, matrices_first, matrices_second, feed_first, feed_second, vectors_first, vectors_second):
    nf = lax.axis_size("fsdp")
    nd = lax.axis_size("dp")
    devices = nf * nd
    own, vec_rows = own_size(devices)
    out = prepare(
        series[0],
        observed[0],
        targets[0],
        target_mask[0],
        counts,
        matrices.reshape(-1, HALF),
        feed_weights.reshape(-1, HALF),
        jnp.pad(vectors, (0, vec_rows * D - own)).reshape(-1, HALF),
    )
    ready, tile, shards = out[:6], out[6], out[7:]
    square, feed, vecs = gather_all(shards)
    square = square.reshape(NSQ, D, D)
    feed = feed.reshape(-1, D)
    up = feed[: 4 * FF].reshape(4, D, FF)
    down = feed.reshape(8, FF, D)
    vecs, *extras = unpack_vectors(vecs.reshape(devices, vec_rows, D), own)
    up_rows = feed_weights.shape[0] // FF
    g_mat, g_feed, g_vec = gradient_parts(ready, (square, up, down, vecs), extras, up_rows, group_stats, group_sum, nf, devices)
    ny, nz, nx = grid_sizes()
    lead = (ny, 2, nz, nx)
    s_mat, s_feed, s_vec, sums = scatter_sum([g.reshape(lead + (-1, D)) for g in (g_mat, g_feed, g_vec)], tile)
    old = [matrices, matrices_first, matrices_second, feed_weights, feed_first, feed_second]
    *new, norm = adam_packs(s_mat, s_feed, sums, [x.reshape(-1, HALF) for x in old], up_rows)
    vec_new = adam_update(vectors, vectors_first, vectors_second, s_vec.reshape(-1)[:own] * norm[1, 0])
    return (norm[0, 0], *[x.reshape(-1) for x in new], *vec_new)


def solution(mesh):
    both = P(("dp", "fsdp"))
    data = P("dp", "fsdp", None)
    return jax.shard_map(
        on_device,
        mesh=mesh,
        in_specs=(data,) * 4 + (P("dp"),) + (both,) * 9,
        out_specs=(P(),) + (both,) * 9,
        check_vma=False,
    )
```
